32 devices in a mesh: seq: 8 (over z, core), batch: 4 (over y, x).
Axes of the slice: x: 2, y: 2, z: 4, core: 2. Of those that a mesh axis runs over, the one named last changes fastest.
Arguments:
- inputs: bfloat16 [8, 1024, 512], P('batch', 'seq'), may hold values from -6 to 6
- lengths: int32 [8], P('batch'), may hold values from 200 to 1024, as said below
- norm_gain: float32 [512], replicated, may hold values from 0.25 to 1.75
- norm_shift: float32 [512], replicated, may hold values from -3 to 3
- log_step: float32 [512], replicated, may hold values from -6.9 to -2.3
- decay_rate: float32 [32, 512], replicated, may hold values from 0.2 to 0.8
- rotation: float32 [32, 512], replicated, may hold values from 0.5 to 100
- drive_real: float32 [32, 512], replicated, may hold values from -5 to 5
- drive_imag: float32 [32, 512], replicated, may hold values from -5 to 5
- read_real: float32 [32, 512], replicated, may hold values from -3 to 3
- read_imag: float32 [32, 512], replicated, may hold values from -3 to 3
- skip_gain: float32 [512], replicated, may hold values from -4 to 4
- glu_weight: bfloat16 [512, 1024], replicated, may hold values from -0.25 to 0.25
- glu_bias: float32 [1024], replicated, may hold values from -3 to 3
- out_cotangent: bfloat16 [8, 1024, 512], P('batch', 'seq'), may hold values from -6 to 6
Outputs:
- out: bfloat16 [8, 1024, 512], P('batch', 'seq')
- grad_inputs: float32 [8, 1024, 512], P('batch', 'seq')
- grad_norm_gain: float32 [512], replicated
- grad_norm_shift: float32 [512], replicated
- grad_log_step: float32 [512], replicated
- grad_decay_rate: float32 [32, 512], replicated
- grad_rotation: float32 [32, 512], replicated
- grad_drive_real: float32 [32, 512], replicated
- grad_drive_imag: float32 [32, 512], replicated
- grad_read_real: float32 [32, 512], replicated
- grad_read_imag: float32 [32, 512], replicated
- grad_skip_gain: float32 [512], replicated
- grad_glu_weight: float32 [512, 1024], replicated
- grad_glu_bias: float32 [1024], replicated
The draws below stay inside these ranges and needn't reach their ends.
Inputs may be any that keep to these rules, and one draw needn't show every extreme that they name: `lengths`: each of the 8 sequences has its own true length; at least one sequence, at a place drawn from the seed, has length 1024.
All inputs are finite; a program needn't handle non-finite values.
Results may differ from the reference program's by a relative error of at most 0.0074.
Values sent between devices are 32-bit elements; how exact they have to be, the bound alone decides.
No kernel may reach another device: no remote copies, remote signals or barrier semaphores. Data moves between devices by JAX's collectives and lax.ppermute only.
A program may use at most 128 MiB of HBM per device.

```python
import math
from functools import partial
import jax
import jax.numpy as jnp
from jax import lax

D = 512
MODES = 32
L = 1024
MINLEN = 200
SEQS = 8


def draw_lengths(key, part):
    length_key = jax.random.fold_in(key, 11)
    pick_key = jax.random.fold_in(key, 23)
    drawn = jax.random.randint(length_key, (SEQS,), MINLEN, L + 1)
    chosen = jax.random.randint(pick_key, (), 0, SEQS)
    return jnp.where(jnp.arange(SEQS) == chosen, L, drawn).astype(jnp.int32)


def block_scale(stream_key, extent, cuts, least, top_value):
    def one(dim, parts):
        draws = jax.random.uniform(jax.random.fold_in(jax.random.fold_in(stream_key, 6), dim), (parts,), jnp.float32, least / len(cuts), top_value / len(cuts))
        return jnp.repeat(jnp.exp(draws), extent[dim] // parts).reshape((-1,) + (1,) * (len(extent) - dim - 1))

    gain = one(*cuts[0])
    for cut in cuts[1:]:
        gain = gain * one(*cut)
    return gain


def bell_draw(stream_key, extent, spread, bound, split=(), kind=jnp.bfloat16):
    values = jax.random.normal(stream_key, extent, jnp.float32) * spread
    if len(split) > 0:
        values = block_scale(stream_key, extent, split, -0.22, 0.18) * values
    return jnp.clip(values, min=-bound, max=bound).astype(kind)


def setup_inputs(seed: int = 0) -> dict:
    key_list = jax.random.split(jax.random.key(seed), 16)
    return {
        "inputs": bell_draw(key_list[0], (SEQS, L, D), 1.0, 6.0, ((0, 4), (1, 8))),
        "lengths": draw_lengths(jax.random.fold_in(key_list[15], 71), 0),
        "norm_gain": jnp.clip(1.0 + 0.15 * jax.random.normal(key_list[2], (D,), jnp.float32), 0.25, 1.75),
        "norm_shift": bell_draw(key_list[3], (D,), 0.5, 3.0, (), jnp.float32),
        "log_step": jnp.clip(jax.random.uniform(key_list[4], (D,), jnp.float32, -6.9, -2.3), -6.9, -2.3),
        "decay_rate": jnp.clip(jnp.exp(jax.random.uniform(key_list[5], (MODES, D), jnp.float32, math.log(0.2), math.log(0.8))), 0.2, 0.8),
        "rotation": jnp.clip(jax.random.uniform(key_list[6], (MODES, D), jnp.float32, 0.5, 100.0), 0.5, 100.0),
        "drive_real": bell_draw(key_list[7], (MODES, D), 1.0, 5.0, (), jnp.float32),
        "drive_imag": bell_draw(key_list[8], (MODES, D), 1.0, 5.0, (), jnp.float32),
        "read_real": bell_draw(key_list[9], (MODES, D), 0.5, 3.0, (), jnp.float32),
        "read_imag": bell_draw(key_list[10], (MODES, D), 0.5, 3.0, (), jnp.float32),
        "skip_gain": bell_draw(key_list[11], (D,), 1.0, 4.0, (), jnp.float32),
        "glu_weight": bell_draw(key_list[12], (D, 2 * D), D ** -0.5, 0.25),
        "glu_bias": bell_draw(key_list[13], (2 * D,), 0.5, 3.0, (), jnp.float32),
        "out_cotangent": bell_draw(key_list[14], (SEQS, L, D), 1.0, 6.0, ((0, 4), (1, 8))),
    }


highest = lax.Precision.HIGHEST
epsilon = 1e-05

@jax.custom_vjp
def low(v):
    return lax.optimization_barrier(v.astype(jnp.bfloat16)).astype(jnp.float32)

@jax.custom_vjp
def low_back(v):
    return v

def low_keep(v):
    return (low(v), None)

def low_pass(kept, grad):
    return (grad,)

def back_keep(v):
    return (v, None)

def back_low(kept, grad):
    return (low(grad),)
low.defvjp(low_keep, low_pass)
low_back.defvjp(back_keep, back_low)

def kernel_part(log_step, decay_rate, rotation, drive_real, drive_imag, read_real, read_imag, freq_angle, parity_sign, seq_span):
    step_size = jnp.exp(log_step)[None, :]
    log_mag = -step_size * decay_rate
    turn_rate = step_size * rotation
    far_mag = jnp.exp(seq_span * log_mag)
    far_angle = seq_span * turn_rate
    sign_col = parity_sign[None, :, None]
    one_real = 1.0 - sign_col * (far_mag * jnp.cos(far_angle))[:, None, :]
    one_imag = -sign_col * (far_mag * jnp.sin(far_angle))[:, None, :]
    decay_gap = (-jnp.expm1(log_mag))[:, None, :]
    magnitude = jnp.exp(log_mag)[:, None, :]
    phase_up = turn_rate[:, None, :] + freq_angle[None, :, None]
    phase_down = freq_angle[None, :, None] - turn_rate[:, None, :]
    up_real = decay_gap + 2.0 * magnitude * jnp.sin(0.5 * phase_up) ** 2
    up_imag = -magnitude * jnp.sin(phase_up)
    down_real = decay_gap + 2.0 * magnitude * jnp.sin(0.5 * phase_down) ** 2
    down_imag = -magnitude * jnp.sin(phase_down)
    up_norm = up_real * up_real + up_imag * up_imag
    down_norm = down_real * down_real + down_imag * down_imag
    prod_real = read_real * drive_real - read_imag * drive_imag
    prod_imag = read_real * drive_imag + read_imag * drive_real
    first_real = step_size * prod_real
    first_imag = step_size * prod_imag
    second_real = first_real * drive_real - first_imag * drive_imag
    second_imag = first_real * drive_imag + first_imag * drive_real

    def resolve(coef_real, coef_imag):
        num_real = coef_real[:, None, :] * one_real - coef_imag[:, None, :] * one_imag
        num_imag = coef_real[:, None, :] * one_imag + coef_imag[:, None, :] * one_real
        part_real = (num_real * up_real + num_imag * up_imag) / up_norm + (num_real * down_real - num_imag * down_imag) / down_norm
        part_imag = (num_imag * up_real - num_real * up_imag) / up_norm - (num_real * down_imag + num_imag * down_real) / down_norm
        return (lax.optimization_barrier(jnp.sum(part_real, axis=0)), lax.optimization_barrier(jnp.sum(part_imag, axis=0)))
    lead_real, lead_imag = resolve(first_real, first_imag)
    liquid_real, liquid_imag = resolve(second_real, second_imag)
    return (lead_real, lead_imag, liquid_real, liquid_imag)

def kernel_table(log_step, mode_params):
    freq_ids = jnp.arange(L + 1, dtype=jnp.int32)
    freq_angle = freq_ids.astype(jnp.float32) * (-math.pi / L)
    parity_sign = 1.0 - 2.0 * (freq_ids % 2).astype(jnp.float32)
    blocks = tuple((entry.reshape(MODES // 2, 2, D) for entry in mode_params))

    def add_block(carry, block):
        block_parts = kernel_part(log_step, *block, freq_angle, parity_sign, float(L))
        return (tuple((carried_sum + block_sum for carried_sum, block_sum in zip(carry, block_parts))), None)
    blank = jnp.zeros((L + 1, D), jnp.float32)
    totals, unused_out = lax.scan(jax.checkpoint(add_block), (blank, blank, blank, blank), blocks)
    return totals

def forward(lengths, values, norm_gain, norm_shift, log_step, decay_rate, rotation, drive_real, drive_imag, read_real, read_imag, skip_gain, glu_weight, glu_bias):
    valid_mask = (jnp.arange(L, dtype=jnp.int32)[None, :] < lengths[:, None]).astype(jnp.float32)[:, :, None]
    tok_count = jnp.sum(valid_mask)
    average = lax.optimization_barrier(jnp.sum(valid_mask * values, axis=(0, 1))) / tok_count
    centered = values - average
    variance = lax.optimization_barrier(jnp.sum(valid_mask * centered * centered, axis=(0, 1))) / tok_count
    normed = centered * lax.rsqrt(variance + epsilon)
    mixed_in = (norm_gain * normed + norm_shift) * valid_mask
    earlier = jnp.concatenate([jnp.zeros_like(mixed_in[:, :1]), mixed_in[:, :-1]], axis=1)
    liquid = mixed_in * earlier
    lead_real, lead_imag, liquid_real, liquid_imag = kernel_table(log_step, (decay_rate, rotation, drive_real, drive_imag, read_real, read_imag))
    lead_freq = lead_real + 1j * lead_imag
    liquid_freq = liquid_real + 1j * liquid_imag

    def per_sequence(items):
        mixed_row, liquid_row, value_row = items
        spec_sum = lead_freq * jnp.fft.rfft(mixed_row, n=2 * L, axis=0) + liquid_freq * jnp.fft.rfft(liquid_row, n=2 * L, axis=0)
        response = jnp.fft.irfft(spec_sum, n=2 * L, axis=0)[:L] + skip_gain * mixed_row
        activated = low(jax.nn.gelu(response))
        joined = low_back(jnp.dot(activated, glu_weight, precision=highest) + glu_bias)
        return value_row + joined[:, :D] * jax.nn.sigmoid(joined[:, D:])
    return lax.map(jax.checkpoint(per_sequence), (mixed_in, liquid, values))

def reference(inputs, lengths, norm_gain, norm_shift, log_step, decay_rate, rotation, drive_real, drive_imag, read_real, read_imag, skip_gain, glu_weight, glu_bias, out_cotangent):
    primal, pull_back = jax.vjp(partial(forward, lengths), inputs.astype(jnp.float32), norm_gain, norm_shift, log_step, decay_rate, rotation, drive_real, drive_imag, read_real, read_imag, skip_gain, glu_weight.astype(jnp.float32), glu_bias)
    grads = pull_back(out_cotangent.astype(jnp.float32))
    return (primal.astype(jnp.bfloat16), grads[0], grads[1], grads[2], grads[3], grads[4], grads[5], grads[6], grads[7], grads[8], grads[9], grads[10], grads[11], grads[12])
```

```python
import functools
import math

import jax
import jax.numpy as jnp
from jax import lax
from jax.experimental import pallas as pl
from jax.experimental.pallas import tpu as pltpu
from jax.sharding import Mesh
from jax.sharding import PartitionSpec as P


EPS = 1e-05
LANES = 128
ALL = ("batch", "z", "core")
SMEM = pl.BlockSpec(memory_space=pltpu.SMEM)
VMEM = pl.BlockSpec(memory_space=pltpu.VMEM)
f32 = jnp.float32
bf16 = jnp.bfloat16


def mm(a, b):
    return jnp.dot(a, b, preferred_element_type=f32)


def halves(x):
    hi = x.astype(bf16)
    return hi, (x - hi.astype(f32)).astype(bf16)


def lane_ids(shape):
    return lax.broadcasted_iota(jnp.int32, shape, len(shape) - 1)


def swap_blocks(tiles, width):
    tiles = list(tiles)
    block = lane_ids(tiles[0].shape) // width
    step = 1
    while step < len(tiles):
        low = (block & step) == 0
        for a in range(len(tiles)):
            if a & step == 0:
                first, second = tiles[a], tiles[a + step]
                tiles[a] = jnp.where(low, first, pltpu.roll(second, step * width, second.ndim - 1))
                tiles[a + step] = jnp.where(
                    low, pltpu.roll(first, LANES - step * width, first.ndim - 1), second
                )
        step *= 2
    return tiles


def fold_matrix(dims):
    rows = lax.broadcasted_iota(jnp.int32, (LANES, LANES), 0) % dims.chans
    cols = lax.broadcasted_iota(jnp.int32, (LANES, LANES), 1) % dims.chans
    return (rows == cols).astype(f32).astype(bf16)


def fold(row, dims):
    shift = dims.chans
    while shift < LANES:
        row = row + pltpu.roll(row, shift, 1)
        shift *= 2
    return row


class Dims:
    def __init__(self, inputs_shape, modes, mesh_shape):
        self.seqs, self.places, self.width = inputs_shape
        self.ni = mesh_shape["batch"]
        self.nz = mesh_shape["z"]
        self.nj = mesh_shape["z"] * mesh_shape["core"]
        self.devices = self.ni * self.nj
        self.length = self.places * self.nj
        self.chans = self.width // self.devices
        self.groups = LANES // self.chans
        self.all_seqs = self.seqs * self.ni
        self.modes = modes
        self.mode_rows = -(-modes // self.groups)
        self.small_rows = -(-(6 * self.mode_rows + 4) // 8) * 8
        self.piece_width = self.seqs * self.chans
        self.place_groups = LANES // self.piece_width
        self.piece_rows = self.places // self.place_groups
        self.units = self.width * 2 * self.width // (8 * LANES) // self.devices
        self.fast = (
            self.piece_width * self.ni == LANES
            and self.piece_rows % 8 == 0
            and self.nj == self.groups
            and self.small_rows == 32
        )


def pack_tokens(read, write, dims):
    for tile in range(dims.width // LANES):
        parts = []
        for g in range(dims.place_groups):
            for b in range(dims.seqs):
                parts.append(read(b, g * dims.piece_rows, tile * LANES))
        parts = swap_blocks(parts, dims.chans)
        for e in range(dims.groups):
            write(tile * dims.groups + e, parts[e])


def unpack_tokens(read, write, dims):
    for tile in range(dims.width // LANES):
        parts = [read(tile * dims.groups + e) for e in range(dims.groups)]
        parts = swap_blocks(parts, dims.chans)
        for g in range(dims.place_groups):
            for b in range(dims.seqs):
                write(b, g * dims.piece_rows, tile * LANES, parts[g * dims.seqs + b])


def pack_kernel(dims, x_ref, out_ref):
    rows = dims.piece_rows

    def read(b, row, lane):
        return x_ref[b, row : row + rows, lane : lane + LANES].astype(f32)

    def write(piece, value):
        out_ref[piece] = value

    pack_tokens(read, write, dims)


def unpack_channels(ref, out, dims):
    if not dims.fast:
        out[...] = ref[...]
        return
    rows = dims.piece_rows
    for j in range(dims.nj):
        parts = [ref[i * dims.nj + j] for i in range(dims.ni)]
        parts = swap_blocks(parts, dims.piece_width)
        for g in range(dims.place_groups):
            at = j * dims.places + g * rows
            out[at : at + rows, :] = parts[g]


def pack_channels(read, out_ref, dims):
    rows = dims.piece_rows
    if not dims.fast:
        step = dims.places
        for j in range(dims.nj):
            out_ref[j * step : (j + 1) * step, :] = read(j * step, step)
        return
    for j in range(dims.nj):
        parts = [read(j * dims.places + g * rows, rows) for g in range(dims.place_groups)]
        parts = swap_blocks(parts, dims.piece_width)
        for i in range(dims.ni):
            out_ref[i * dims.nj + j] = parts[i]


def mode_constants(par_ref, dims):
    m = dims.mode_rows
    decay, rotation, dr, di, rr, ri = [par_ref[p * m : (p + 1) * m, :] for p in range(6)]
    step = jnp.exp(par_ref[6 * m : 6 * m + 1, :])
    log_mag = -step * decay
    turn = step * rotation
    c1r = step * (rr * dr - ri * di)
    c1i = step * (rr * di + ri * dr)
    c2r = c1r * dr - c1i * di
    c2i = c1r * di + c1i * dr
    return step, log_mag, turn, (c1r, c1i, c2r, c2i), (decay, rotation, dr, di, rr, ri)


def tables_kernel(
    dims, par_ref, fhi_ref, flo_ref, spec_ref, zr_ref, zi_ref, vec_ref, kt, kcat
):
    n = dims.length
    m = dims.mode_rows
    outer = n // 32

    def some_columns(ct, _):
        at = pl.multiple_of(ct * LANES, LANES)
        odd = 2 * (lax.broadcasted_iota(jnp.int32, (outer, LANES), 1) + at) + 1
        row = lax.broadcasted_iota(jnp.int32, (outer, LANES), 0)
        turn = ((64 * row * odd) & (8 * n - 1)).astype(f32) * (math.pi / (4 * n))
        ec, es = jnp.cos(turn), jnp.sin(turn)
        odd = 2 * (lax.broadcasted_iota(jnp.int32, (32, LANES), 1) + at) + 1
        row = 2 * lax.broadcasted_iota(jnp.int32, (32, LANES), 0) + 1
        turn = ((row * odd) & (8 * n - 1)).astype(f32) * (math.pi / (4 * n))
        qc, qs = jnp.cos(turn), jnp.sin(turn)
        for a in range(outer):
            pc, ps = ec[a : a + 1], es[a : a + 1]
            hi, lo = halves(pc * qc - ps * qs)
            fhi_ref[a * 32 : a * 32 + 32, pl.ds(at, LANES)] = hi
            flo_ref[a * 32 : a * 32 + 32, pl.ds(at, LANES)] = lo
            hi, lo = halves(ps * qc + pc * qs)
            fhi_ref[n + a * 32 : n + a * 32 + 32, pl.ds(at, LANES)] = hi
            flo_ref[n + a * 32 : n + a * 32 + 32, pl.ds(at, LANES)] = lo
        return 0

    lax.fori_loop(0, n // LANES, some_columns, 0)

    step, log_mag, turn, coefs, _ = mode_constants(par_ref, dims)
    c1r, c1i, c2r, c2i = coefs
    mag8 = jnp.exp(8.0 * log_mag)
    l8r = mag8 * jnp.cos(8.0 * turn)
    l8i = mag8 * jnp.sin(8.0 * turn)
    sub = lax.broadcasted_iota(jnp.int32, (8, LANES), 0).astype(f32)
    start = []
    for r in range(m):
        mag = jnp.exp(sub * log_mag[r : r + 1])
        ang = sub * turn[r : r + 1]
        start.append((mag * jnp.cos(ang), mag * jnp.sin(ang)))
        zr_ref[8 * r : 8 * r + 8, :] = start[r][0]
        zi_ref[8 * r : 8 * r + 8, :] = start[r][1]
    for p, value in enumerate((l8r, l8i, c1r, c1i, c2r, c2i)):
        vec_ref[p * m : (p + 1) * m, :] = value

    def wide(x, r):
        return jnp.broadcast_to(x[r : r + 1], (8, LANES))

    consts = [
        tuple(wide(x, r) for x in (l8r, l8i, 2 * c1r, 2 * c1i, 2 * c2r, 2 * c2i)) for r in range(m)
    ]

    def time_step(t, zs):
        at = pl.multiple_of(t * 8, 8)
        k1 = jnp.zeros((8, LANES), f32)
        k2 = jnp.zeros((8, LANES), f32)
        out = []
        for r in range(m):
            zr, zi = zs[2 * r], zs[2 * r + 1]
            ar, ai, b1r, b1i, b2r, b2i = consts[r]
            k1 = k1 + (b1r * zr - b1i * zi)
            k2 = k2 + (b2r * zr - b2i * zi)
            out += [zr * ar - zi * ai, zr * ai + zi * ar]
        kt[pl.ds(at, 8), 0:LANES] = k1
        kt[pl.ds(at, 8), LANES : 2 * LANES] = k2
        return tuple(out)

    lax.fori_loop(0, n // 8, time_step, tuple(v for pair in start for v in pair), unroll=2)

    group = fold_matrix(dims)
    block = 256

    def fold_rows(b, _):
        at = pl.multiple_of(b * block, block)
        for p in range(2):
            hi, lo = halves(kt[pl.ds(at, block), p * LANES : (p + 1) * LANES])
            hi, lo = halves(mm(hi, group) + mm(lo, group))
            kcat[pl.ds(at, block), p * LANES : (p + 1) * LANES] = hi
            kcat[pl.ds(at, block), (2 + p) * LANES : (3 + p) * LANES] = lo
        return 0

    lax.fori_loop(0, n // block, fold_rows, 0)

    def spectrum(b, _):
        at = pl.multiple_of(b * block, block)
        below = pl.multiple_of(n + b * block, block)
        ck = three(fhi_ref, flo_ref, at, block, kcat, 2)
        sk = three(fhi_ref, flo_ref, below, block, kcat, 2)
        ch, sh = half_turn(fhi_ref, flo_ref, at, below, block)
        re = (ch * ck + sh * sk) * (1.0 / n)
        im = (sh * ck - ch * sk) * (1.0 / n)
        spec_ref[pl.ds(at, block), 0:LANES] = re[:, :LANES]
        spec_ref[pl.ds(at, block), LANES : 2 * LANES] = im[:, :LANES]
        spec_ref[pl.ds(at, block), 2 * LANES : 3 * LANES] = re[:, LANES:]
        spec_ref[pl.ds(at, block), 3 * LANES : 4 * LANES] = im[:, LANES:]
        return 0

    lax.fori_loop(0, n // block, spectrum, 0)


def half_turn(fhi_ref, flo_ref, at, below, block):
    def column(start):
        hi = fhi_ref[pl.ds(start, block), 0:LANES].astype(f32)
        lo = flo_ref[pl.ds(start, block), 0:LANES].astype(f32)
        return (hi + lo)[:, 0:1]

    return column(at), column(below)


def three(fhi_ref, flo_ref, at, block, cat, count):
    wide = count * LANES
    both = mm(fhi_ref[pl.ds(at, block), :], cat[...])
    low = mm(flo_ref[pl.ds(at, block), :], cat[:, :wide])
    return both[:, :wide] + both[:, wide:] + low


def lane_lengths(meta_ref, lens_ref, dims):
    lane = lane_ids((1, LANES)) // dims.chans
    row = jnp.zeros((1, LANES), jnp.int32)
    total = jnp.int32(0)
    for s in range(dims.all_seqs):
        source = s // dims.seqs
        if dims.fast:
            source = lax.rem(meta_ref[0] - source + dims.ni, dims.ni)
        value = lens_ref[source, s % dims.seqs]
        total = total + value
        row = jnp.where(lane == s, value, row)
    return row, total.astype(f32)


def valid_rows(at, rows, lens):
    return ((lax.broadcasted_iota(jnp.int32, (rows, LANES), 0) + at) < lens).astype(f32)


def forward_kernel(
    dims,
    meta_ref,
    lens_ref,
    r_ref,
    par_ref,
    fhi_ref,
    flo_ref,
    spec_ref,
    send_ref,
    mixed_ref,
    normed_ref,
    seen_ref,
    stat_ref,
    x_sc,
    mix_sc,
    cat,
    ycat_r,
    ycat_i,
):
    n = dims.length
    m = dims.mode_rows
    lens, total = lane_lengths(meta_ref, lens_ref, dims)
    unpack_channels(r_ref, x_sc, dims)
    rows = 64

    def add_up(b, acc):
        at = pl.multiple_of(b * rows, rows)
        x = x_sc[pl.ds(at, rows), :] * valid_rows(at, rows, lens)
        return acc + jnp.sum(x.reshape(rows // 8, 8, LANES), axis=0)

    zero = jnp.zeros((8, LANES), f32)
    acc = lax.fori_loop(0, n // rows, add_up, zero)
    average = fold(jnp.sum(acc, axis=0, keepdims=True), dims) / total

    def add_squares(b, acc):
        at = pl.multiple_of(b * rows, rows)
        x = (x_sc[pl.ds(at, rows), :] - average) * valid_rows(at, rows, lens)
        return acc + jnp.sum((x * x).reshape(rows // 8, 8, LANES), axis=0)

    acc = lax.fori_loop(0, n // rows, add_squares, zero)
    variance = fold(jnp.sum(acc, axis=0, keepdims=True), dims) / total
    inv = lax.rsqrt(variance + EPS)
    gain = par_ref[6 * m + 1 : 6 * m + 2, :]
    shift = par_ref[6 * m + 2 : 6 * m + 3, :]
    skip = par_ref[6 * m + 3 : 6 * m + 4, :]
    stat_ref[...] = jnp.broadcast_to(inv, (8, LANES))
    mix_sc[0:8, :] = zero

    def normalize(b, _):
        at = pl.multiple_of(b * rows, rows)
        normed = (x_sc[pl.ds(at, rows), :] - average) * inv
        mixed = (gain * normed + shift) * valid_rows(at, rows, lens)
        normed_ref[pl.ds(at, rows), :] = normed
        mixed_ref[pl.ds(at, rows), :] = mixed
        mix_sc[pl.ds(pl.multiple_of(at + 8, 8), rows), :] = mixed
        return 0

    lax.fori_loop(0, n // rows, normalize, 0)
    for b in range(n // rows):
        at = b * rows
        mixed = mix_sc[at + 8 : at + 8 + rows, :]
        liquid = mixed * mix_sc[at + 7 : at + 7 + rows, :]
        for p, value in enumerate((mixed, liquid)):
            hi, lo = halves(value)
            cat[at : at + rows, p * LANES : (p + 1) * LANES] = hi
            cat[at : at + rows, (2 + p) * LANES : (3 + p) * LANES] = lo
    block = 256

    def transform(b, _):
        at = pl.multiple_of(b * block, block)
        below = pl.multiple_of(n + b * block, block)
        re = three(fhi_ref, flo_ref, at, block, cat, 2)
        im = -three(fhi_ref, flo_ref, below, block, cat, 2)
        m_re, m_im, l_re, l_im = re[:, :LANES], im[:, :LANES], re[:, LANES:], im[:, LANES:]
        for p, value in enumerate((m_re, m_im, l_re, l_im)):
            seen_ref[pl.ds(at, block), p * LANES : (p + 1) * LANES] = value
        kr, ki, qr, qi = [spec_ref[pl.ds(at, block), p * LANES : (p + 1) * LANES] for p in range(4)]
        y_re = kr * m_re - ki * m_im + qr * l_re - qi * l_im
        y_im = kr * m_im + ki * m_re + qr * l_im + qi * l_re
        for ref, value in ((ycat_r, y_re), (ycat_i, -y_im)):
            hi, lo = halves(value)
            ref[pl.ds(at, block), 0:LANES] = hi
            ref[pl.ds(at, block), LANES : 2 * LANES] = lo
        return 0

    lax.fori_loop(0, n // block, transform, 0)

    def back(b, _):
        at = pl.multiple_of(b * block, block)
        below = pl.multiple_of(n + b * block, block)
        out = three(fhi_ref, flo_ref, at, block, ycat_r, 1)
        out = out + three(fhi_ref, flo_ref, below, block, ycat_i, 1)
        x_sc[pl.ds(at, block), :] = out + skip * mixed_ref[pl.ds(at, block), :]
        return 0

    lax.fori_loop(0, n // block, back, 0)
    pack_channels(lambda at, size: x_sc[at : at + size, :], send_ref, dims)


def gate_kernel(
    dims,
    meta_ref,
    r_ref,
    x_ref,
    w_ref,
    b_ref,
    ct_ref,
    send_ref,
    out_ref,
    wsend_ref,
    wkeep_ref,
    resp,
    act,
    joined,
    gj,
    gact,
):
    tokens = dims.seqs * dims.places
    width = dims.width
    places = dims.places

    if dims.fast:

        def write(b, row, lane, value):
            at = b * places + row
            resp[at : at + dims.piece_rows, lane : lane + LANES] = value

        unpack_tokens(lambda piece: r_ref[piece], write, dims)
    else:
        resp[...] = r_ref[...]
    c0 = math.sqrt(2.0 / math.pi)
    c1 = 0.044715
    rows = 32

    def gelu(b, _):
        at = pl.multiple_of(b * rows, rows)
        r = resp[pl.ds(at, rows), :]
        t = jnp.tanh(c0 * (r + c1 * r * r * r))
        act[pl.ds(at, rows), :] = (0.5 * r * (1.0 + t)).astype(bf16)
        slope = 0.5 * (1.0 + t) + 0.5 * r * (1.0 - t * t) * (c0 * (1.0 + 3.0 * c1 * r * r))
        resp[pl.ds(at, rows), :] = slope
        return 0

    lax.fori_loop(0, tokens // rows, gelu, 0)
    joined[...] = mm(act[...], w_ref[...])
    bias = b_ref[...]
    half = min(16, places)
    for b in range(dims.seqs):

        def gate(k, sums):
            at = pl.multiple_of(k * half, half)
            tok = pl.multiple_of(b * places + k * half, half)
            value = joined[pl.ds(tok, half), :width] + bias[:, :width]
            s = jax.nn.sigmoid(joined[pl.ds(tok, half), width:] + bias[:, width:])
            x = x_ref[b, pl.ds(at, half), :].astype(f32)
            g = ct_ref[b, pl.ds(at, half), :].astype(f32)
            out_ref[b, pl.ds(at, half), :] = (x + value * s).astype(bf16)
            gs = g * s
            first = gs.astype(bf16)
            second = (gs * value * (1.0 - s)).astype(bf16)
            gj[pl.ds(tok, half), :width] = first
            gj[pl.ds(tok, half), width:] = second
            first = jnp.sum(first.astype(f32).reshape(half // 8, 8, width), axis=0)
            second = jnp.sum(second.astype(f32).reshape(half // 8, 8, width), axis=0)
            return sums[0] + first, sums[1] + second

        if b == 0:
            zero = jnp.zeros((8, width), f32)
            sums = (zero, zero)
        sums = lax.fori_loop(0, places // half, gate, sums)
    gact[...] = lax.dot_general(
        gj[...], w_ref[...], (((1,), (1,)), ((), ())), preferred_element_type=f32
    )
    if dims.fast:

        def read(b, row, lane):
            at = b * places + row
            value = gact[at : at + dims.piece_rows, lane : lane + LANES]
            return value * resp[at : at + dims.piece_rows, lane : lane + LANES]

        def put(piece, value):
            send_ref[piece] = value

        pack_tokens(read, put, dims)
    else:
        send_ref[...] = gact[...] * resp[...]
    weight = lax.dot_general(
        act[...], gj[...], (((0,), (0,)), ((), ())), preferred_element_type=f32
    )
    joined_rows = jnp.concatenate([jnp.sum(s, axis=0, keepdims=True) for s in sums], axis=1)
    unit_rows = dims.units * 8 * LANES // (2 * width)
    tiles = 2 * width // LANES
    bias_rows = jnp.concatenate(
        [joined_rows[:, t * LANES : (t + 1) * LANES] for t in range(tiles)], axis=0
    )
    core = meta_ref[1]
    for side in range(2):
        part = weight[side * (width // 2) : (side + 1) * (width // 2), :]
        for ref, mine in ((wkeep_ref, side), (wsend_ref, 1 - side)):

            @pl.when(core == mine)
            def _():
                for i in range(dims.ni):
                    for z in range(dims.nz):
                        ref[i, z, dims.units, :, :] = bias_rows
                        if unit_rows % 8 == 0:
                            at = (i * dims.nz + z) * unit_rows
                            for rb in range(unit_rows // 8):
                                for t in range(tiles):
                                    ref[i, z, rb * tiles + t, :, :] = part[
                                        at + rb * 8 : at + rb * 8 + 8, t * LANES : (t + 1) * LANES
                                    ]
                        else:
                            first = (i * dims.nz + z) * dims.units
                            for u in range(dims.units):
                                rb, t = divmod(first + u, tiles)
                                ref[i, z, u, :, :] = part[
                                    rb * 8 : rb * 8 + 8, t * LANES : (t + 1) * LANES
                                ]


def backward_kernel(
    dims,
    meta_ref,
    lens_ref,
    r_ref,
    par_ref,
    fhi_ref,
    flo_ref,
    spec_ref,
    mixed_ref,
    normed_ref,
    seen_ref,
    stat_ref,
    zr_ref,
    zi_ref,
    vec_ref,
    send_ref,
    small_ref,
    g_sc,
    mix_sc,
    up_sc,
    cat,
    ycat_r,
    ycat_i,
    back_sc,
    dk,
):
    n = dims.length
    m = dims.mode_rows
    lens, total = lane_lengths(meta_ref, lens_ref, dims)
    unpack_channels(r_ref, g_sc, dims)
    gain = par_ref[6 * m + 1 : 6 * m + 2, :]
    skip = par_ref[6 * m + 3 : 6 * m + 4, :]
    inv = stat_ref[0:1, :]
    rows = 64
    zero = jnp.zeros((8, LANES), f32)
    mix_sc[0:8, :] = zero
    up_sc[n : n + 8, :] = zero

    def gather(b, acc):
        at = pl.multiple_of(b * rows, rows)
        g = g_sc[pl.ds(at, rows), :]
        mixed = mixed_ref[pl.ds(at, rows), :]
        mix_sc[pl.ds(pl.multiple_of(at + 8, 8), rows), :] = mixed
        hi, lo = halves(g)
        cat[pl.ds(at, rows), 0:LANES] = hi
        cat[pl.ds(at, rows), LANES : 2 * LANES] = lo
        return acc + jnp.sum((g * mixed).reshape(rows // 8, 8, LANES), axis=0)

    skip_acc = lax.fori_loop(0, n // rows, gather, zero)
    block = 256

    def transform(b, _):
        at = pl.multiple_of(b * block, block)
        below = pl.multiple_of(n + b * block, block)
        re = three(fhi_ref, flo_ref, at, block, cat, 1)
        im = -three(fhi_ref, flo_ref, below, block, cat, 1)
        ch, sh = half_turn(fhi_ref, flo_ref, at, below, block)
        kr, ki, qr, qi = [spec_ref[pl.ds(at, block), p * LANES : (p + 1) * LANES] for p in range(4)]
        mr, mi, lr, li = [seen_ref[pl.ds(at, block), p * LANES : (p + 1) * LANES] for p in range(4)]
        outs = [(kr * re + ki * im, kr * im - ki * re), (qr * re + qi * im, qr * im - qi * re)]
        gr = (re * ch + im * sh) * (1.0 / n)
        gi = (im * ch - re * sh) * (1.0 / n)
        for a, b_ in ((mr, mi), (lr, li)):
            outs.append((a * gr + b_ * gi, a * gi - b_ * gr))
        for p, (y_re, y_im) in enumerate(outs):
            for ref, value in ((ycat_r, y_re), (ycat_i, -y_im)):
                hi, lo = halves(value)
                ref[pl.ds(at, block), p * LANES : (p + 1) * LANES] = hi
                ref[pl.ds(at, block), (4 + p) * LANES : (5 + p) * LANES] = lo
        return 0

    lax.fori_loop(0, n // block, transform, 0)
    group = fold_matrix(dims)

    def back(b, _):
        at = pl.multiple_of(b * block, block)
        below = pl.multiple_of(n + b * block, block)
        out = three(fhi_ref, flo_ref, at, block, ycat_r, 4)
        out = out + three(fhi_ref, flo_ref, below, block, ycat_i, 4)
        back_sc[pl.ds(at, block), :] = out[:, : 2 * LANES]
        for p in range(2):
            hi, lo = halves(out[:, (2 + p) * LANES : (3 + p) * LANES])
            dk[pl.ds(at, block), p * LANES : (p + 1) * LANES] = mm(hi, group) + mm(lo, group)
        return 0

    lax.fori_loop(0, n // block, back, 0)

    step, log_mag, turn, _, params = mode_constants(par_ref, dims)
    decay, rotation, dr, di, rr, ri = params
    l8r, l8i, c1r, c1i, c2r, c2i = [vec_ref[p * m : (p + 1) * m, :] for p in range(6)]
    sub = lax.broadcasted_iota(jnp.int32, (8, LANES), 0).astype(f32)
    sums = [[] for _ in range(8)]
    for first in range(0, m, 2):
        some = range(first, min(m, first + 2))
        ratio = [
            (
                jnp.broadcast_to(l8r[r : r + 1], (8, LANES)),
                jnp.broadcast_to(l8i[r : r + 1], (8, LANES)),
            )
            for r in some
        ]

        def mode_step(t, carry):
            at = pl.multiple_of(t * 8, 8)
            d1 = dk[pl.ds(at, 8), 0:LANES]
            d2 = dk[pl.ds(at, 8), LANES : 2 * LANES]
            place = sub + (t * 8).astype(f32)
            e1 = d1 * place
            e2 = d2 * place
            out = []
            for k, (ar, ai) in enumerate(ratio):
                zr, zi, *acc = carry[10 * k : 10 * (k + 1)]
                out += [zr * ar - zi * ai, zr * ai + zi * ar]
                for q, d in enumerate((d1, d2, e1, e2)):
                    out += [acc[2 * q] + d * zr, acc[2 * q + 1] + d * zi]
            return tuple(out)

        carry = []
        for r in some:
            carry += [zr_ref[8 * r : 8 * r + 8, :], zi_ref[8 * r : 8 * r + 8, :]] + [zero] * 8
        carry = lax.fori_loop(0, n // 8, mode_step, tuple(carry), unroll=2)
        for k in range(len(ratio)):
            for q in range(8):
                sums[q].append(jnp.sum(carry[10 * k + 2 + q], axis=0, keepdims=True))
    a1r, a1i, a2r, a2i, e1r, e1i, e2r, e2i = [
        jnp.concatenate(s, axis=0) if len(s) > 1 else s[0] for s in sums
    ]
    btr = c1r * e1r - c1i * e1i + c2r * e2r - c2i * e2i
    bti = c1r * e1i + c1i * e1r + c2r * e2i + c2i * e2r
    d2r = dr * dr - di * di
    d2i = 2.0 * dr * di
    erd = step * (a1r * dr - a1i * di + a2r * d2r - a2i * d2i)
    eri = step * (a1r * di + a1i * dr + a2r * d2i + a2i * d2r)
    tr = a1r + 2.0 * (a2r * dr - a2i * di)
    ti = a1i + 2.0 * (a2r * di + a2i * dr)
    edr = step * (rr * tr - ri * ti)
    edi = step * (rr * ti + ri * tr)
    by_step = 2.0 * (c1r * a1r - c1i * a1i + c2r * a2r - c2i * a2i) + 2.0 * step * (
        -decay * btr - rotation * bti
    )
    small_ref[...] = jnp.zeros_like(small_ref)
    answers = (-2.0 * step * btr, -2.0 * step * bti, 2.0 * edr, -2.0 * edi, 2.0 * erd, -2.0 * eri)
    for p, value in enumerate(answers):
        small_ref[p * m : (p + 1) * m, :] = value

    def spread(b, _):
        at = pl.multiple_of(b * rows, rows)
        up_sc[pl.ds(at, rows), :] = (
            back_sc[pl.ds(at, rows), LANES : 2 * LANES] * mixed_ref[pl.ds(at, rows), :]
        )
        return 0

    lax.fori_loop(0, n // rows, spread, 0)
    gain_acc, shift_acc = zero, zero
    for b in range(n // rows):
        at = b * rows
        masked = (
            back_sc[at : at + rows, 0:LANES]
            + skip * g_sc[at : at + rows, :]
            + back_sc[at : at + rows, LANES : 2 * LANES] * mix_sc[at + 7 : at + 7 + rows, :]
            + up_sc[at + 1 : at + 1 + rows, :]
        ) * valid_rows(at, rows, lens)
        g_sc[at : at + rows, :] = masked
        shift_acc = shift_acc + jnp.sum(masked.reshape(rows // 8, 8, LANES), axis=0)
        scaled = masked * normed_ref[at : at + rows, :]
        gain_acc = gain_acc + jnp.sum(scaled.reshape(rows // 8, 8, LANES), axis=0)

    def whole(acc):
        return fold(jnp.sum(acc, axis=0, keepdims=True), dims)

    gain_sum, shift_sum, skip_sum = whole(gain_acc), whole(shift_acc), whole(skip_acc)
    step_sum = fold(jnp.sum(by_step, axis=0, keepdims=True), dims)
    for p, value in enumerate((step_sum, gain_sum, shift_sum, skip_sum)):
        small_ref[6 * m + p : 6 * m + p + 1, :] = value
    scale = gain * inv
    shift_mean = shift_sum / total
    gain_mean = gain_sum / total

    def read(at, size):
        value = g_sc[at : at + size, :] - shift_mean - normed_ref[at : at + size, :] * gain_mean
        return value * scale * valid_rows(at, size, lens)

    pack_channels(read, send_ref, dims)


def finish_kernel(
    dims, meta_ref, r_ref, ct_ref, mine_ref, other_ref, grad_ref, weight_ref, *small_refs
):
    rows = dims.piece_rows

    def write(b, row, lane, value):
        ct = ct_ref[b, row : row + rows, lane : lane + LANES].astype(f32)
        grad_ref[b, row : row + rows, lane : lane + LANES] = value + ct

    unpack_tokens(lambda piece: r_ref[piece], write, dims)
    core = meta_ref[1]
    tiles = 2 * dims.width // LANES
    per = dims.units // tiles
    m = dims.mode_rows
    half_rows = dims.width // 2
    for mine, ref in ((True, mine_ref), (False, other_ref)):
        base = (core if mine else 1 - core) * half_rows
        for i in range(dims.ni):
            for z in range(dims.nz):
                for rb in range(per):
                    at = base + ((i * dims.nz + z) * per + rb) * 8
                    at = pl.multiple_of(at, 8)
                    for t in range(tiles):
                        weight_ref[pl.ds(at, 8), t * LANES : (t + 1) * LANES] = ref[
                            i, z, rb * tiles + t
                        ]
    first = core == 0
    for i in range(dims.ni):
        parts = []
        for z in range(dims.nz):
            a = mine_ref[i, z, dims.units :].reshape(dims.small_rows, LANES)
            b = other_ref[i, z, dims.units :].reshape(dims.small_rows, LANES)
            parts += [jnp.where(first, a, b), jnp.where(first, b, a)]
        parts = swap_blocks(parts, dims.chans)
        cols = slice(i * LANES, (i + 1) * LANES)
        for q in range(dims.groups):
            for p in range(6):
                for r in range(m):
                    at = r * dims.groups + q
                    small_refs[p][at : at + 1, cols] = parts[q][p * m + r : p * m + r + 1, :]
        for p in range(4):
            small_refs[6 + p][:, cols] = parts[0][6 * m + p : 6 * m + p + 1, :]


def call(kernel, out_shape, in_specs, scratch, limit):
    outs = jax.tree.map(lambda _: VMEM, out_shape)
    return pl.pallas_call(
        kernel,
        out_shape=out_shape,
        in_specs=in_specs,
        out_specs=outs,
        scratch_shapes=scratch,
        compiler_params=pltpu.CompilerParams(vmem_limit_bytes=limit << 20),
    )


def shape(*dims, dtype=f32):
    return jax.ShapeDtypeStruct(dims, dtype)


def local(
    mesh_shape,
    inputs,
    lengths,
    norm_gain,
    norm_shift,
    log_step,
    decay_rate,
    rotation,
    drive_real,
    drive_imag,
    read_real,
    read_imag,
    skip_gain,
    glu_weight,
    glu_bias,
    out_cotangent,
):
    modes = decay_rate.shape[0]
    dims = Dims(inputs.shape, modes, mesh_shape)
    n, nd, m, hc = dims.length, dims.devices, dims.mode_rows, dims.chans
    core = lax.axis_index("core")
    owner = lax.axis_index(ALL)
    meta = jnp.stack([lax.axis_index("batch"), core]).astype(jnp.int32)

    def exchange(x):
        return lax.all_to_all(x, ALL, 0, 0, tiled=True)

    def to_channels(x):
        x = x.reshape(dims.seqs, dims.places, nd, hc).transpose(2, 1, 0, 3)
        x = exchange(x.reshape(nd, dims.places, dims.piece_width))
        x = x.reshape(dims.ni, dims.nj, dims.places, dims.piece_width).transpose(1, 2, 0, 3)
        x = x.reshape(n, dims.all_seqs * hc)
        return jnp.pad(x, ((0, 0), (0, LANES - x.shape[1])))

    def to_tokens(x):
        x = x[:, : dims.all_seqs * hc].reshape(dims.nj, dims.places, dims.ni, dims.piece_width)
        x = exchange(x.transpose(2, 0, 1, 3).reshape(nd, dims.places, dims.piece_width))
        x = x.reshape(nd, dims.places, dims.seqs, hc).transpose(2, 1, 0, 3)
        return x.reshape(dims.seqs * dims.places, dims.width)

    if dims.fast:
        others = [
            lax.ppermute(lengths, "batch", [(i, (i + s) % dims.ni) for i in range(dims.ni)])
            for s in range(1, dims.ni)
        ]
        lens = jnp.stack([lengths] + others)
    else:
        lens = lax.all_gather(lengths, "batch", tiled=True).reshape(dims.ni, dims.seqs)

    table = jnp.stack([decay_rate, rotation, drive_real, drive_imag, read_real, read_imag])
    table = lax.dynamic_slice_in_dim(table, owner * hc, hc, 2)
    table = jnp.pad(table, ((0, 0), (0, m * dims.groups - modes), (0, 0)))
    table = table.reshape(6 * m, LANES)
    rest = jnp.stack([log_step, norm_gain, norm_shift, skip_gain])
    rest = lax.dynamic_slice_in_dim(rest, owner * hc, hc, 1)
    params = jnp.concatenate([table, jnp.tile(rest, (1, dims.groups))], axis=0)

    pieces = shape(nd, dims.piece_rows, LANES) if dims.fast else shape(n, LANES)
    tokens = dims.seqs * dims.places
    token_pieces = shape(nd, dims.piece_rows, LANES) if dims.fast else shape(tokens, dims.width)
    bind = functools.partial

    fhi, flo, spec, zr, zi, vec = call(
        bind(tables_kernel, dims),
        (
            shape(2 * n, n, dtype=bf16),
            shape(2 * n, n, dtype=bf16),
            shape(n, 4 * LANES),
            shape(8 * m, LANES),
            shape(8 * m, LANES),
            shape(6 * m, LANES),
        ),
        [VMEM],
        [
            pltpu.VMEM((n, 2 * LANES), f32),
            pltpu.VMEM((n, 4 * LANES), bf16),
        ],
        32,
    )(params)

    if dims.fast:
        packed = call(bind(pack_kernel, dims), pieces, [VMEM], [], 8)(inputs)
        received = exchange(packed)
    else:
        received = to_channels(inputs.astype(f32))

    send, mixed, normed, seen, stat = call(
        bind(forward_kernel, dims),
        (pieces, shape(n, LANES), shape(n, LANES), shape(n, 4 * LANES), shape(8, LANES)),
        [SMEM, SMEM] + [VMEM] * 5,
        [
            pltpu.VMEM((n, LANES), f32),
            pltpu.VMEM((n + 8, LANES), f32),
            pltpu.VMEM((n, 4 * LANES), bf16),
            pltpu.VMEM((n, 2 * LANES), bf16),
            pltpu.VMEM((n, 2 * LANES), bf16),
        ],
        40,
    )(meta, lens, received, params, fhi, flo, spec)

    received = exchange(send) if dims.fast else to_tokens(send)
    part = shape(dims.ni, dims.nz, dims.units + 1, 8, LANES)
    send, result, wsend, wkeep = call(
        bind(gate_kernel, dims),
        (token_pieces, shape(*inputs.shape, dtype=bf16), part, part),
        [SMEM] + [VMEM] * 5,
        [
            pltpu.VMEM((tokens, dims.width), f32),
            pltpu.VMEM((tokens, dims.width), bf16),
            pltpu.VMEM((tokens, 2 * dims.width), f32),
            pltpu.VMEM((tokens, 2 * dims.width), bf16),
            pltpu.VMEM((tokens, dims.width), f32),
        ],
        32,
    )(meta, received, inputs, glu_weight, glu_bias.reshape(1, -1), out_cotangent)

    received = exchange(send) if dims.fast else to_channels(
        send.reshape(dims.seqs, dims.places, dims.width)
    )
    swap = [(0, 1), (1, 0)]
    part = wkeep + lax.ppermute(wsend, "core", swap)
    part = jnp.sum(lax.all_to_all(part, "batch", 0, 0, tiled=True), axis=0)
    part = jnp.sum(lax.all_to_all(part, "z", 0, 0, tiled=True), axis=0)

    send, small = call(
        bind(backward_kernel, dims),
        (pieces, shape(dims.small_rows, LANES)),
        [SMEM, SMEM] + [VMEM] * 12,
        [
            pltpu.VMEM((n, LANES), f32),
            pltpu.VMEM((n + 8, LANES), f32),
            pltpu.VMEM((n + 8, LANES), f32),
            pltpu.VMEM((n, 2 * LANES), bf16),
            pltpu.VMEM((n, 8 * LANES), bf16),
            pltpu.VMEM((n, 8 * LANES), bf16),
            pltpu.VMEM((n, 2 * LANES), f32),
            pltpu.VMEM((n, 2 * LANES), f32),
        ],
        48,
    )(meta, lens, received, params, fhi, flo, spec, mixed, normed, seen, stat, zr, zi, vec)

    received = exchange(send) if dims.fast else to_tokens(send)
    bias_grad = part[dims.units].reshape(-1)
    gathered = jnp.concatenate([part[: dims.units], small.reshape(-1, 8, LANES)], axis=0)
    for axis, size in (("z", dims.nz), ("batch", dims.ni)):
        gathered = jnp.broadcast_to(gathered[None], (size,) + gathered.shape)
        gathered = lax.all_to_all(gathered, axis, 0, 0, tiled=True)
    other = lax.ppermute(gathered, "core", swap)

    if dims.fast:
        outs = call(
            bind(finish_kernel, dims),
            (shape(*inputs.shape), shape(dims.width, 2 * dims.width))
            + (shape(modes, dims.width),) * 6
            + (shape(1, dims.width),) * 4,
            [SMEM] + [VMEM] * 4,
            [],
            32,
        )(meta, received, out_cotangent, gathered, other)
        grad_in, weight_grad = outs[:2]
        mode_grads = outs[2:8]
        chan_grads = [x.reshape(-1) for x in outs[8:]]
    else:
        grad_in = out_cotangent.astype(f32) + received.reshape(inputs.shape)
        both = jnp.where(core == 0, jnp.stack([gathered, other]), jnp.stack([other, gathered]))
        units = both[:, :, :, : dims.units].reshape(dims.width // 8, -1, 8, LANES)
        weight_grad = units.transpose(0, 2, 1, 3).reshape(dims.width, -1)
        rows = both[:, :, :, dims.units :].transpose(1, 2, 0, 3, 4, 5)
        rows = rows.reshape(nd, dims.small_rows, dims.groups, hc)
        table = rows[:, : 6 * m].reshape(nd, 6, m * dims.groups, hc).transpose(1, 2, 0, 3)
        mode_grads = list(table.reshape(6, m * dims.groups, dims.width)[:, :modes])
        rest = rows[:, 6 * m : 6 * m + 4, 0].transpose(1, 0, 2).reshape(4, dims.width)
        chan_grads = list(rest)
    step_grad, gain_grad, shift_grad, skip_grad = chan_grads
    return (
        result,
        grad_in,
        gain_grad,
        shift_grad,
        step_grad,
        *mode_grads,
        skip_grad,
        weight_grad,
        bias_grad,
    )


def solution(mesh):
    batch = mesh.shape["batch"]
    fine = Mesh(mesh.devices.reshape(-1, 2, batch), ("z", "core", "batch"))
    tokens = P("batch", ("z", "core"), None)
    return jax.shard_map(
        functools.partial(local, dict(fine.shape)),
        mesh=fine,
        in_specs=(tokens, P("batch")) + (P(),) * 12 + (tokens,),
        out_specs=(tokens, tokens) + (P(),) * 12,
        check_vma=False,
    )
```

```python
import functools
import math

import jax
import jax.numpy as jnp
from jax import lax
from jax.experimental import pallas as pl
from jax.experimental.pallas import tpu as pltpu
from jax.sharding import Mesh
from jax.sharding import PartitionSpec as P


EPS = 1e-05
LANES = 128
ALL = ("batch", "z", "core")
SMEM = pl.BlockSpec(memory_space=pltpu.SMEM)
VMEM = pl.BlockSpec(memory_space=pltpu.VMEM)
f32 = jnp.float32
bf16 = jnp.bfloat16


def mm(a, b):
    return jnp.dot(a, b, preferred_element_type=f32)


def halves(x):
    hi = x.astype(bf16)
    return hi, (x - hi.astype(f32)).astype(bf16)


def lane_ids(shape):
    return lax.broadcasted_iota(jnp.int32, shape, len(shape) - 1)


def swap_blocks(tiles, width):
    tiles = list(tiles)
    block = lane_ids(tiles[0].shape) // width
    step = 1
    while step < len(tiles):
        low = (block & step) == 0
        for a in range(len(tiles)):
            if a & step == 0:
                first, second = tiles[a], tiles[a + step]
                tiles[a] = jnp.where(low, first, pltpu.roll(second, step * width, second.ndim - 1))
                tiles[a + step] = jnp.where(
                    low, pltpu.roll(first, LANES - step * width, first.ndim - 1), second
                )
        step *= 2
    return tiles


def fold_matrix(dims):
    rows = lax.broadcasted_iota(jnp.int32, (LANES, LANES), 0) % dims.chans
    cols = lax.broadcasted_iota(jnp.int32, (LANES, LANES), 1) % dims.chans
    return (rows == cols).astype(f32).astype(bf16)


def fold(row, dims):
    shift = dims.chans
    while shift < LANES:
        row = row + pltpu.roll(row, shift, 1)
        shift *= 2
    return row


class Dims:
    def __init__(self, inputs_shape, modes, mesh_shape):
        self.seqs, self.places, self.width = inputs_shape
        self.ni = mesh_shape["batch"]
        self.nz = mesh_shape["z"]
        self.nj = mesh_shape["z"] * mesh_shape["core"]
        self.devices = self.ni * self.nj
        self.length = self.places * self.nj
        self.chans = self.width // self.devices
        self.groups = LANES // self.chans
        self.all_seqs = self.seqs * self.ni
        self.modes = modes
        self.mode_rows = -(-modes // self.groups)
        self.small_rows = -(-(6 * self.mode_rows + 4) // 8) * 8
        self.piece_width = self.seqs * self.chans
        self.place_groups = LANES // self.piece_width
        self.piece_rows = self.places // self.place_groups
        self.units = self.width * 2 * self.width // (8 * LANES) // self.devices
        self.fast = (
            self.piece_width * self.ni == LANES
            and self.piece_rows % 8 == 0
            and self.nj == self.groups
            and self.small_rows == 32
        )


def pack_tokens(read, write, dims):
    for tile in range(dims.width // LANES):
        parts = []
        for g in range(dims.place_groups):
            for b in range(dims.seqs):
                parts.append(read(b, g * dims.piece_rows, tile * LANES))
        parts = swap_blocks(parts, dims.chans)
        for e in range(dims.groups):
            write(tile * dims.groups + e, parts[e])


def unpack_tokens(read, write, dims):
    for tile in range(dims.width // LANES):
        parts = [read(tile * dims.groups + e) for e in range(dims.groups)]
        parts = swap_blocks(parts, dims.chans)
        for g in range(dims.place_groups):
            for b in range(dims.seqs):
                write(b, g * dims.piece_rows, tile * LANES, parts[g * dims.seqs + b])


def pack_kernel(dims, x_ref, out_ref):
    rows = dims.piece_rows

    def read(b, row, lane):
        return x_ref[b, row : row + rows, lane : lane + LANES].astype(f32)

    def write(piece, value):
        out_ref[piece] = value

    pack_tokens(read, write, dims)


def unpack_channels(ref, out, dims):
    if not dims.fast:
        out[...] = ref[...]
        return
    rows = dims.piece_rows
    for j in range(dims.nj):
        parts = [ref[i * dims.nj + j] for i in range(dims.ni)]
        parts = swap_blocks(parts, dims.piece_width)
        for g in range(dims.place_groups):
            at = j * dims.places + g * rows
            out[at : at + rows, :] = parts[g]


def pack_channels(read, out_ref, dims):
    rows = dims.piece_rows
    if not dims.fast:
        step = dims.places
        for j in range(dims.nj):
            out_ref[j * step : (j + 1) * step, :] = read(j * step, step)
        return
    for j in range(dims.nj):
        parts = [read(j * dims.places + g * rows, rows) for g in range(dims.place_groups)]
        parts = swap_blocks(parts, dims.piece_width)
        for i in range(dims.ni):
            out_ref[i * dims.nj + j] = parts[i]


def mode_constants(par_ref, dims):
    m = dims.mode_rows
    decay, rotation, dr, di, rr, ri = [par_ref[p * m : (p + 1) * m, :] for p in range(6)]
    step = jnp.exp(par_ref[6 * m : 6 * m + 1, :])
    log_mag = -step * decay
    turn = step * rotation
    c1r = step * (rr * dr - ri * di)
    c1i = step * (rr * di + ri * dr)
    c2r = c1r * dr - c1i * di
    c2i = c1r * di + c1i * dr
    return step, log_mag, turn, (c1r, c1i, c2r, c2i), (decay, rotation, dr, di, rr, ri)


def tables_kernel(
    dims, par_ref, fhi_ref, flo_ref, spec_ref, zr_ref, zi_ref, vec_ref, kt, kcat
):
    n = dims.length
    m = dims.mode_rows
    outer = n // 32

    def some_columns(ct, _):
        at = pl.multiple_of(ct * LANES, LANES)
        odd = 2 * (lax.broadcasted_iota(jnp.int32, (outer, LANES), 1) + at) + 1
        row = lax.broadcasted_iota(jnp.int32, (outer, LANES), 0)
        turn = ((64 * row * odd) & (8 * n - 1)).astype(f32) * (math.pi / (4 * n))
        ec, es = jnp.cos(turn), jnp.sin(turn)
        odd = 2 * (lax.broadcasted_iota(jnp.int32, (32, LANES), 1) + at) + 1
        row = 2 * lax.broadcasted_iota(jnp.int32, (32, LANES), 0) + 1
        turn = ((row * odd) & (8 * n - 1)).astype(f32) * (math.pi / (4 * n))
        qc, qs = jnp.cos(turn), jnp.sin(turn)
        for a in range(outer):
            pc, ps = ec[a : a + 1], es[a : a + 1]
            hi, lo = halves(pc * qc - ps * qs)
            fhi_ref[a * 32 : a * 32 + 32, pl.ds(at, LANES)] = hi
            flo_ref[a * 32 : a * 32 + 32, pl.ds(at, LANES)] = lo
            hi, lo = halves(ps * qc + pc * qs)
            fhi_ref[n + a * 32 : n + a * 32 + 32, pl.ds(at, LANES)] = hi
            flo_ref[n + a * 32 : n + a * 32 + 32, pl.ds(at, LANES)] = lo
        return 0

    lax.fori_loop(0, n // LANES, some_columns, 0)

    step, log_mag, turn, coefs, _ = mode_constants(par_ref, dims)
    c1r, c1i, c2r, c2i = coefs
    mag8 = jnp.exp(8.0 * log_mag)
    l8r = mag8 * jnp.cos(8.0 * turn)
    l8i = mag8 * jnp.sin(8.0 * turn)
    sub = lax.broadcasted_iota(jnp.int32, (8, LANES), 0).astype(f32)
    start = []
    for r in range(m):
        mag = jnp.exp(sub * log_mag[r : r + 1])
        ang = sub * turn[r : r + 1]
        start.append((mag * jnp.cos(ang), mag * jnp.sin(ang)))
        zr_ref[8 * r : 8 * r + 8, :] = start[r][0]
        zi_ref[8 * r : 8 * r + 8, :] = start[r][1]
    for p, value in enumerate((l8r, l8i, c1r, c1i, c2r, c2i)):
        vec_ref[p * m : (p + 1) * m, :] = value

    def wide(x, r):
        return jnp.broadcast_to(x[r : r + 1], (8, LANES))

    consts = [
        tuple(wide(x, r) for x in (l8r, l8i, 2 * c1r, 2 * c1i, 2 * c2r, 2 * c2i)) for r in range(m)
    ]

    def time_step(t, zs):
        at = pl.multiple_of(t * 8, 8)
        k1 = jnp.zeros((8, LANES), f32)
        k2 = jnp.zeros((8, LANES), f32)
        out = []
        for r in range(m):
            zr, zi = zs[2 * r], zs[2 * r + 1]
            ar, ai, b1r, b1i, b2r, b2i = consts[r]
            k1 = k1 + (b1r * zr - b1i * zi)
            k2 = k2 + (b2r * zr - b2i * zi)
            out += [zr * ar - zi * ai, zr * ai + zi * ar]
        kt[pl.ds(at, 8), 0:LANES] = k1
        kt[pl.ds(at, 8), LANES : 2 * LANES] = k2
        return tuple(out)

    lax.fori_loop(0, n // 8, time_step, tuple(v for pair in start for v in pair), unroll=2)

    group = fold_matrix(dims)
    block = 256

    def fold_rows(b, _):
        at = pl.multiple_of(b * block, block)
        for p in range(2):
            hi, lo = halves(kt[pl.ds(at, block), p * LANES : (p + 1) * LANES])
            hi, lo = halves(mm(hi, group) + mm(lo, group))
            kcat[pl.ds(at, block), p * LANES : (p + 1) * LANES] = hi
            kcat[pl.ds(at, block), (2 + p) * LANES : (3 + p) * LANES] = lo
        return 0

    lax.fori_loop(0, n // block, fold_rows, 0)

    def spectrum(b, _):
        at = pl.multiple_of(b * block, block)
        below = pl.multiple_of(n + b * block, block)
        ck = three(fhi_ref, flo_ref, at, block, kcat, 2)
        sk = three(fhi_ref, flo_ref, below, block, kcat, 2)
        ch, sh = half_turn(fhi_ref, flo_ref, at, below, block)
        re = (ch * ck + sh * sk) * (1.0 / n)
        im = (sh * ck - ch * sk) * (1.0 / n)
        spec_ref[pl.ds(at, block), 0:LANES] = re[:, :LANES]
        spec_ref[pl.ds(at, block), LANES : 2 * LANES] = im[:, :LANES]
        spec_ref[pl.ds(at, block), 2 * LANES : 3 * LANES] = re[:, LANES:]
        spec_ref[pl.ds(at, block), 3 * LANES : 4 * LANES] = im[:, LANES:]
        return 0

    lax.fori_loop(0, n // block, spectrum, 0)


def half_turn(fhi_ref, flo_ref, at, below, block):
    def column(start):
        hi = fhi_ref[pl.ds(start, block), 0:LANES].astype(f32)
        lo = flo_ref[pl.ds(start, block), 0:LANES].astype(f32)
        return (hi + lo)[:, 0:1]

    return column(at), column(below)


def three(fhi_ref, flo_ref, at, block, cat, count):
    wide = count * LANES
    both = mm(fhi_ref[pl.ds(at, block), :], cat[...])
    low = mm(flo_ref[pl.ds(at, block), :], cat[:, :wide])
    return both[:, :wide] + both[:, wide:] + low


def lane_lengths(meta_ref, lens_ref, dims):
    lane = lane_ids((1, LANES)) // dims.chans
    row = jnp.zeros((1, LANES), jnp.int32)
    total = jnp.int32(0)
    for s in range(dims.all_seqs):
        source = s // dims.seqs
        if dims.fast:
            source = lax.rem(meta_ref[0] - source + dims.ni, dims.ni)
        value = lens_ref[source, s % dims.seqs]
        total = total + value
        row = jnp.where(lane == s, value, row)
    return row, total.astype(f32)


def valid_rows(at, rows, lens):
    return ((lax.broadcasted_iota(jnp.int32, (rows, LANES), 0) + at) < lens).astype(f32)


def forward_kernel(
    dims,
    meta_ref,
    lens_ref,
    r_ref,
    par_ref,
    fhi_ref,
    flo_ref,
    spec_ref,
    send_ref,
    mixed_ref,
    normed_ref,
    seen_ref,
    stat_ref,
    x_sc,
    mix_sc,
    cat,
    ycat_r,
    ycat_i,
):
    n = dims.length
    m = dims.mode_rows
    lens, total = lane_lengths(meta_ref, lens_ref, dims)
    unpack_channels(r_ref, x_sc, dims)
    rows = 64

    def add_up(b, acc):
        at = pl.multiple_of(b * rows, rows)
        x = x_sc[pl.ds(at, rows), :] * valid_rows(at, rows, lens)
        return acc + jnp.sum(x.reshape(rows // 8, 8, LANES), axis=0)

    zero = jnp.zeros((8, LANES), f32)
    acc = lax.fori_loop(0, n // rows, add_up, zero)
    average = fold(jnp.sum(acc, axis=0, keepdims=True), dims) / total

    def add_squares(b, acc):
        at = pl.multiple_of(b * rows, rows)
        x = (x_sc[pl.ds(at, rows), :] - average) * valid_rows(at, rows, lens)
        return acc + jnp.sum((x * x).reshape(rows // 8, 8, LANES), axis=0)

    acc = lax.fori_loop(0, n // rows, add_squares, zero)
    variance = fold(jnp.sum(acc, axis=0, keepdims=True), dims) / total
    inv = lax.rsqrt(variance + EPS)
    gain = par_ref[6 * m + 1 : 6 * m + 2, :]
    shift = par_ref[6 * m + 2 : 6 * m + 3, :]
    skip = par_ref[6 * m + 3 : 6 * m + 4, :]
    stat_ref[...] = jnp.broadcast_to(inv, (8, LANES))
    mix_sc[0:8, :] = zero

    def normalize(b, _):
        at = pl.multiple_of(b * rows, rows)
        normed = (x_sc[pl.ds(at, rows), :] - average) * inv
        mixed = (gain * normed + shift) * valid_rows(at, rows, lens)
        normed_ref[pl.ds(at, rows), :] = normed
        mixed_ref[pl.ds(at, rows), :] = mixed
        mix_sc[pl.ds(pl.multiple_of(at + 8, 8), rows), :] = mixed
        return 0

    lax.fori_loop(0, n // rows, normalize, 0)
    for b in range(n // rows):
        at = b * rows
        mixed = mix_sc[at + 8 : at + 8 + rows, :]
        liquid = mixed * mix_sc[at + 7 : at + 7 + rows, :]
        for p, value in enumerate((mixed, liquid)):
            hi, lo = halves(value)
            cat[at : at + rows, p * LANES : (p + 1) * LANES] = hi
            cat[at : at + rows, (2 + p) * LANES : (3 + p) * LANES] = lo
    block = 256

    def transform(b, _):
        at = pl.multiple_of(b * block, block)
        below = pl.multiple_of(n + b * block, block)
        re = three(fhi_ref, flo_ref, at, block, cat, 2)
        im = -three(fhi_ref, flo_ref, below, block, cat, 2)
        m_re, m_im, l_re, l_im = re[:, :LANES], im[:, :LANES], re[:, LANES:], im[:, LANES:]
        for p, value in enumerate((m_re, m_im, l_re, l_im)):
            seen_ref[pl.ds(at, block), p * LANES : (p + 1) * LANES] = value
        kr, ki, qr, qi = [spec_ref[pl.ds(at, block), p * LANES : (p + 1) * LANES] for p in range(4)]
        y_re = kr * m_re - ki * m_im + qr * l_re - qi * l_im
        y_im = kr * m_im + ki * m_re + qr * l_im + qi * l_re
        for ref, value in ((ycat_r, y_re), (ycat_i, -y_im)):
            hi, lo = halves(value)
            ref[pl.ds(at, block), 0:LANES] = hi
            ref[pl.ds(at, block), LANES : 2 * LANES] = lo
        return 0

    lax.fori_loop(0, n // block, transform, 0)

    def back(b, _):
        at = pl.multiple_of(b * block, block)
        below = pl.multiple_of(n + b * block, block)
        out = three(fhi_ref, flo_ref, at, block, ycat_r, 1)
        out = out + three(fhi_ref, flo_ref, below, block, ycat_i, 1)
        x_sc[pl.ds(at, block), :] = out + skip * mixed_ref[pl.ds(at, block), :]
        return 0

    lax.fori_loop(0, n // block, back, 0)
    pack_channels(lambda at, size: x_sc[at : at + size, :], send_ref, dims)


def gate_kernel(
    dims,
    meta_ref,
    r_ref,
    x_ref,
    w_ref,
    b_ref,
    ct_ref,
    send_ref,
    out_ref,
    wsend_ref,
    wkeep_ref,
    resp,
    act,
    joined,
    gj,
    gact,
    weight,
):
    tokens = dims.seqs * dims.places
    width = dims.width
    places = dims.places

    if dims.fast:

        def write(b, row, lane, value):
            at = b * places + row
            resp[at : at + dims.piece_rows, lane : lane + LANES] = value

        unpack_tokens(lambda piece: r_ref[piece], write, dims)
    else:
        resp[...] = r_ref[...]
    c0 = math.sqrt(2.0 / math.pi)
    c1 = 0.044715
    rows = 32

    def gelu(b, _):
        at = pl.multiple_of(b * rows, rows)
        r = resp[pl.ds(at, rows), :]
        t = jnp.tanh(c0 * (r + c1 * r * r * r))
        act[pl.ds(at, rows), :] = (0.5 * r * (1.0 + t)).astype(bf16)
        slope = 0.5 * (1.0 + t) + 0.5 * r * (1.0 - t * t) * (c0 * (1.0 + 3.0 * c1 * r * r))
        resp[pl.ds(at, rows), :] = slope
        return 0

    lax.fori_loop(0, tokens // rows, gelu, 0)
    joined[...] = mm(act[...], w_ref[...])
    bias = b_ref[...]
    half = min(16, places)
    for b in range(dims.seqs):

        def gate(k, sums):
            at = pl.multiple_of(k * half, half)
            tok = pl.multiple_of(b * places + k * half, half)
            value = joined[pl.ds(tok, half), :width] + bias[:, :width]
            s = jax.nn.sigmoid(joined[pl.ds(tok, half), width:] + bias[:, width:])
            x = x_ref[b, pl.ds(at, half), :].astype(f32)
            g = ct_ref[b, pl.ds(at, half), :].astype(f32)
            out_ref[b, pl.ds(at, half), :] = (x + value * s).astype(bf16)
            gs = g * s
            first = gs.astype(bf16)
            second = (gs * value * (1.0 - s)).astype(bf16)
            gj[pl.ds(tok, half), :width] = first
            gj[pl.ds(tok, half), width:] = second
            first = jnp.sum(first.astype(f32).reshape(half // 8, 8, width), axis=0)
            second = jnp.sum(second.astype(f32).reshape(half // 8, 8, width), axis=0)
            return sums[0] + first, sums[1] + second

        if b == 0:
            zero = jnp.zeros((8, width), f32)
            sums = (zero, zero)
        sums = lax.fori_loop(0, places // half, gate, sums)
    gact[...] = lax.dot_general(
        gj[...], w_ref[...], (((1,), (1,)), ((), ())), preferred_element_type=f32
    )
    if dims.fast:

        def read(b, row, lane):
            at = b * places + row
            value = gact[at : at + dims.piece_rows, lane : lane + LANES]
            return value * resp[at : at + dims.piece_rows, lane : lane + LANES]

        def put(piece, value):
            send_ref[piece] = value

        pack_tokens(read, put, dims)
    else:
        send_ref[...] = gact[...] * resp[...]
    weight[...] = lax.dot_general(
        act[...], gj[...], (((0,), (0,)), ((), ())), preferred_element_type=f32
    )
    joined_rows = jnp.concatenate([jnp.sum(s, axis=0, keepdims=True) for s in sums], axis=1)
    tiles = 2 * width // LANES
    bias_rows = jnp.concatenate(
        [joined_rows[:, t * LANES : (t + 1) * LANES] for t in range(tiles)], axis=0
    )
    for ref, core in ((wkeep_ref, meta_ref[1]), (wsend_ref, 1 - meta_ref[1])):
        for i in range(dims.ni):
            for z in range(dims.nz):
                ref[i, z, dims.units, :, :] = bias_rows
                owner = ((core * dims.ni) + (meta_ref[0] ^ i)) * dims.nz + (meta_ref[2] ^ z)
                for u in range(dims.units):
                    if dims.units % tiles == 0:
                        row = owner * (dims.units // tiles) + u // tiles
                        cols = slice((u % tiles) * LANES, (u % tiles + 1) * LANES)
                    else:
                        unit = owner * dims.units + u
                        row = unit // tiles
                        cols = pl.ds(pl.multiple_of(unit % tiles * LANES, LANES), LANES)
                    ref[i, z, u, :, :] = weight[pl.ds(pl.multiple_of(row * 8, 8), 8), cols]


def backward_kernel(
    dims,
    meta_ref,
    lens_ref,
    r_ref,
    par_ref,
    fhi_ref,
    flo_ref,
    spec_ref,
    mixed_ref,
    normed_ref,
    seen_ref,
    stat_ref,
    zr_ref,
    zi_ref,
    vec_ref,
    send_ref,
    small_ref,
    g_sc,
    mix_sc,
    up_sc,
    cat,
    ycat_r,
    ycat_i,
    back_sc,
    dk,
):
    n = dims.length
    m = dims.mode_rows
    lens, total = lane_lengths(meta_ref, lens_ref, dims)
    unpack_channels(r_ref, g_sc, dims)
    gain = par_ref[6 * m + 1 : 6 * m + 2, :]
    skip = par_ref[6 * m + 3 : 6 * m + 4, :]
    inv = stat_ref[0:1, :]
    rows = 64
    zero = jnp.zeros((8, LANES), f32)
    mix_sc[0:8, :] = zero
    up_sc[n : n + 8, :] = zero

    def gather(b, acc):
        at = pl.multiple_of(b * rows, rows)
        g = g_sc[pl.ds(at, rows), :]
        mixed = mixed_ref[pl.ds(at, rows), :]
        mix_sc[pl.ds(pl.multiple_of(at + 8, 8), rows), :] = mixed
        hi, lo = halves(g)
        cat[pl.ds(at, rows), 0:LANES] = hi
        cat[pl.ds(at, rows), LANES : 2 * LANES] = lo
        return acc + jnp.sum((g * mixed).reshape(rows // 8, 8, LANES), axis=0)

    skip_acc = lax.fori_loop(0, n // rows, gather, zero)
    block = 256

    def transform(b, _):
        at = pl.multiple_of(b * block, block)
        below = pl.multiple_of(n + b * block, block)
        re = three(fhi_ref, flo_ref, at, block, cat, 1)
        im = -three(fhi_ref, flo_ref, below, block, cat, 1)
        ch, sh = half_turn(fhi_ref, flo_ref, at, below, block)
        kr, ki, qr, qi = [spec_ref[pl.ds(at, block), p * LANES : (p + 1) * LANES] for p in range(4)]
        mr, mi, lr, li = [seen_ref[pl.ds(at, block), p * LANES : (p + 1) * LANES] for p in range(4)]
        outs = [(kr * re + ki * im, kr * im - ki * re), (qr * re + qi * im, qr * im - qi * re)]
        gr = (re * ch + im * sh) * (1.0 / n)
        gi = (im * ch - re * sh) * (1.0 / n)
        for a, b_ in ((mr, mi), (lr, li)):
            outs.append((a * gr + b_ * gi, a * gi - b_ * gr))
        for p, (y_re, y_im) in enumerate(outs):
            for ref, value in ((ycat_r, y_re), (ycat_i, -y_im)):
                hi, lo = halves(value)
                ref[pl.ds(at, block), p * LANES : (p + 1) * LANES] = hi
                ref[pl.ds(at, block), (4 + p) * LANES : (5 + p) * LANES] = lo
        return 0

    lax.fori_loop(0, n // block, transform, 0)
    group = fold_matrix(dims)

    def back(b, _):
        at = pl.multiple_of(b * block, block)
        below = pl.multiple_of(n + b * block, block)
        out = three(fhi_ref, flo_ref, at, block, ycat_r, 4)
        out = out + three(fhi_ref, flo_ref, below, block, ycat_i, 4)
        back_sc[pl.ds(at, block), :] = out[:, : 2 * LANES]
        for p in range(2):
            hi, lo = halves(out[:, (2 + p) * LANES : (3 + p) * LANES])
            dk[pl.ds(at, block), p * LANES : (p + 1) * LANES] = mm(hi, group) + mm(lo, group)
        return 0

    lax.fori_loop(0, n // block, back, 0)

    step, log_mag, turn, _, params = mode_constants(par_ref, dims)
    decay, rotation, dr, di, rr, ri = params
    l8r, l8i, c1r, c1i, c2r, c2i = [vec_ref[p * m : (p + 1) * m, :] for p in range(6)]
    sub = lax.broadcasted_iota(jnp.int32, (8, LANES), 0).astype(f32)
    sums = [[] for _ in range(8)]
    for first in range(0, m, 2):
        some = range(first, min(m, first + 2))
        ratio = [
            (
                jnp.broadcast_to(l8r[r : r + 1], (8, LANES)),
                jnp.broadcast_to(l8i[r : r + 1], (8, LANES)),
            )
            for r in some
        ]

        def mode_step(t, carry):
            at = pl.multiple_of(t * 8, 8)
            d1 = dk[pl.ds(at, 8), 0:LANES]
            d2 = dk[pl.ds(at, 8), LANES : 2 * LANES]
            place = sub + (t * 8).astype(f32)
            e1 = d1 * place
            e2 = d2 * place
            out = []
            for k, (ar, ai) in enumerate(ratio):
                zr, zi, *acc = carry[10 * k : 10 * (k + 1)]
                out += [zr * ar - zi * ai, zr * ai + zi * ar]
                for q, d in enumerate((d1, d2, e1, e2)):
                    out += [acc[2 * q] + d * zr, acc[2 * q + 1] + d * zi]
            return tuple(out)

        carry = []
        for r in some:
            carry += [zr_ref[8 * r : 8 * r + 8, :], zi_ref[8 * r : 8 * r + 8, :]] + [zero] * 8
        carry = lax.fori_loop(0, n // 8, mode_step, tuple(carry), unroll=2)
        for k in range(len(ratio)):
            for q in range(8):
                sums[q].append(jnp.sum(carry[10 * k + 2 + q], axis=0, keepdims=True))
    a1r, a1i, a2r, a2i, e1r, e1i, e2r, e2i = [
        jnp.concatenate(s, axis=0) if len(s) > 1 else s[0] for s in sums
    ]
    btr = c1r * e1r - c1i * e1i + c2r * e2r - c2i * e2i
    bti = c1r * e1i + c1i * e1r + c2r * e2i + c2i * e2r
    d2r = dr * dr - di * di
    d2i = 2.0 * dr * di
    erd = step * (a1r * dr - a1i * di + a2r * d2r - a2i * d2i)
    eri = step * (a1r * di + a1i * dr + a2r * d2i + a2i * d2r)
    tr = a1r + 2.0 * (a2r * dr - a2i * di)
    ti = a1i + 2.0 * (a2r * di + a2i * dr)
    edr = step * (rr * tr - ri * ti)
    edi = step * (rr * ti + ri * tr)
    by_step = 2.0 * (c1r * a1r - c1i * a1i + c2r * a2r - c2i * a2i) + 2.0 * step * (
        -decay * btr - rotation * bti
    )
    small_ref[...] = jnp.zeros_like(small_ref)
    answers = (-2.0 * step * btr, -2.0 * step * bti, 2.0 * edr, -2.0 * edi, 2.0 * erd, -2.0 * eri)
    for p, value in enumerate(answers):
        small_ref[p * m : (p + 1) * m, :] = value

    def spread(b, _):
        at = pl.multiple_of(b * rows, rows)
        up_sc[pl.ds(at, rows), :] = (
            back_sc[pl.ds(at, rows), LANES : 2 * LANES] * mixed_ref[pl.ds(at, rows), :]
        )
        return 0

    lax.fori_loop(0, n // rows, spread, 0)
    gain_acc, shift_acc = zero, zero
    for b in range(n // rows):
        at = b * rows
        masked = (
            back_sc[at : at + rows, 0:LANES]
            + skip * g_sc[at : at + rows, :]
            + back_sc[at : at + rows, LANES : 2 * LANES] * mix_sc[at + 7 : at + 7 + rows, :]
            + up_sc[at + 1 : at + 1 + rows, :]
        ) * valid_rows(at, rows, lens)
        g_sc[at : at + rows, :] = masked
        shift_acc = shift_acc + jnp.sum(masked.reshape(rows // 8, 8, LANES), axis=0)
        scaled = masked * normed_ref[at : at + rows, :]
        gain_acc = gain_acc + jnp.sum(scaled.reshape(rows // 8, 8, LANES), axis=0)

    def whole(acc):
        return fold(jnp.sum(acc, axis=0, keepdims=True), dims)

    gain_sum, shift_sum, skip_sum = whole(gain_acc), whole(shift_acc), whole(skip_acc)
    step_sum = fold(jnp.sum(by_step, axis=0, keepdims=True), dims)
    for p, value in enumerate((step_sum, gain_sum, shift_sum, skip_sum)):
        small_ref[6 * m + p : 6 * m + p + 1, :] = value
    scale = gain * inv
    shift_mean = shift_sum / total
    gain_mean = gain_sum / total

    def read(at, size):
        value = g_sc[at : at + size, :] - shift_mean - normed_ref[at : at + size, :] * gain_mean
        return value * scale * valid_rows(at, size, lens)

    pack_channels(read, send_ref, dims)


def finish_kernel(dims, meta_ref, r_ref, ct_ref, *refs):
    rows = dims.piece_rows
    ni, nz = dims.ni, dims.nz
    weights = refs[:ni], refs[ni : 2 * ni]
    smalls = refs[2 * ni], refs[2 * ni + 1]
    grad_ref, weight_ref, *small_refs = refs[2 * ni + 2 :]

    def write(b, row, lane, value):
        ct = ct_ref[b, row : row + rows, lane : lane + LANES].astype(f32)
        grad_ref[b, row : row + rows, lane : lane + LANES] = value + ct

    unpack_tokens(lambda piece: r_ref[piece], write, dims)
    tiles = 2 * dims.width // LANES
    per = dims.units // tiles
    m = dims.mode_rows
    me, core, me_z = meta_ref[0], meta_ref[1], meta_ref[2]
    for half, side in ((0, core), (1, 1 - core)):
        for i in range(ni):
            for z in range(nz):
                owner = (side * ni + (me ^ i)) * nz + (me_z ^ z)
                for rb in range(per):
                    at = pl.multiple_of((owner * per + rb) * 8, 8)
                    for t in range(tiles):
                        cols = slice(t * LANES, (t + 1) * LANES)
                        weight_ref[pl.ds(at, 8), cols] = weights[half][i][z, rb * tiles + t]
    first = core == 0
    for i in range(ni):
        parts = []
        for z in range(nz):
            a = smalls[0][i, me_z ^ z].reshape(dims.small_rows, LANES)
            b = smalls[1][i, me_z ^ z].reshape(dims.small_rows, LANES)
            parts += [jnp.where(first, a, b), jnp.where(first, b, a)]
        parts = swap_blocks(parts, dims.chans)
        cols = pl.ds(pl.multiple_of((me ^ i) * LANES, LANES), LANES)
        for q in range(dims.groups):
            for p in range(6):
                for r in range(m):
                    at = r * dims.groups + q
                    small_refs[p][at : at + 1, cols] = parts[q][p * m + r : p * m + r + 1, :]
        for p in range(4):
            small_refs[6 + p][:, cols] = parts[0][6 * m + p : 6 * m + p + 1, :]


def call(kernel, out_shape, in_specs, scratch, limit):
    outs = jax.tree.map(lambda _: VMEM, out_shape)
    return pl.pallas_call(
        kernel,
        out_shape=out_shape,
        in_specs=in_specs,
        out_specs=outs,
        scratch_shapes=scratch,
        compiler_params=pltpu.CompilerParams(vmem_limit_bytes=limit << 20),
    )


def shape(*dims, dtype=f32):
    return jax.ShapeDtypeStruct(dims, dtype)


def local(
    mesh_shape,
    inputs,
    lengths,
    norm_gain,
    norm_shift,
    log_step,
    decay_rate,
    rotation,
    drive_real,
    drive_imag,
    read_real,
    read_imag,
    skip_gain,
    glu_weight,
    glu_bias,
    out_cotangent,
):
    modes = decay_rate.shape[0]
    dims = Dims(inputs.shape, modes, mesh_shape)
    n, nd, m, hc = dims.length, dims.devices, dims.mode_rows, dims.chans
    core = lax.axis_index("core")
    owner = lax.axis_index(ALL)
    meta = jnp.stack([lax.axis_index("batch"), core, lax.axis_index("z")]).astype(jnp.int32)

    def exchange(x):
        return lax.all_to_all(x, ALL, 0, 0, tiled=True)

    def to_channels(x):
        x = x.reshape(dims.seqs, dims.places, nd, hc).transpose(2, 1, 0, 3)
        x = exchange(x.reshape(nd, dims.places, dims.piece_width))
        x = x.reshape(dims.ni, dims.nj, dims.places, dims.piece_width).transpose(1, 2, 0, 3)
        x = x.reshape(n, dims.all_seqs * hc)
        return jnp.pad(x, ((0, 0), (0, LANES - x.shape[1])))

    def to_tokens(x):
        x = x[:, : dims.all_seqs * hc].reshape(dims.nj, dims.places, dims.ni, dims.piece_width)
        x = exchange(x.transpose(2, 0, 1, 3).reshape(nd, dims.places, dims.piece_width))
        x = x.reshape(nd, dims.places, dims.seqs, hc).transpose(2, 1, 0, 3)
        return x.reshape(dims.seqs * dims.places, dims.width)

    table = jnp.stack([decay_rate, rotation, drive_real, drive_imag, read_real, read_imag])
    table = lax.dynamic_slice_in_dim(table, owner * hc, hc, 2)
    table = jnp.pad(table, ((0, 0), (0, m * dims.groups - modes), (0, 0)))
    table = table.reshape(6 * m, LANES)
    rest = jnp.stack([log_step, norm_gain, norm_shift, skip_gain])
    rest = lax.dynamic_slice_in_dim(rest, owner * hc, hc, 1)
    params = jnp.concatenate([table, jnp.tile(rest, (1, dims.groups))], axis=0)

    pieces = shape(nd, dims.piece_rows, LANES) if dims.fast else shape(n, LANES)
    tokens = dims.seqs * dims.places
    token_pieces = shape(nd, dims.piece_rows, LANES) if dims.fast else shape(tokens, dims.width)
    bind = functools.partial

    fhi, flo, spec, zr, zi, vec = call(
        bind(tables_kernel, dims),
        (
            shape(2 * n, n, dtype=bf16),
            shape(2 * n, n, dtype=bf16),
            shape(n, 4 * LANES),
            shape(8 * m, LANES),
            shape(8 * m, LANES),
            shape(6 * m, LANES),
        ),
        [VMEM],
        [
            pltpu.VMEM((n, 2 * LANES), f32),
            pltpu.VMEM((n, 4 * LANES), bf16),
        ],
        8,
    )(params)

    if dims.fast:
        packed = call(bind(pack_kernel, dims), pieces, [VMEM], [], 4)(inputs)
        packed, lengths = lax.optimization_barrier((packed, lengths))
        received = exchange(packed)
    else:
        received = to_channels(inputs.astype(f32))

    if dims.fast:
        others = [
            lax.ppermute(lengths, "batch", [(i, (i + s) % dims.ni) for i in range(dims.ni)])
            for s in range(1, dims.ni)
        ]
        lens = jnp.stack([lengths] + others)
    else:
        lens = lax.all_gather(lengths, "batch", tiled=True).reshape(dims.ni, dims.seqs)

    send, mixed, normed, seen, stat = call(
        bind(forward_kernel, dims),
        (pieces, shape(n, LANES), shape(n, LANES), shape(n, 4 * LANES), shape(8, LANES)),
        [SMEM, SMEM] + [VMEM] * 5,
        [
            pltpu.VMEM((n, LANES), f32),
            pltpu.VMEM((n + 8, LANES), f32),
            pltpu.VMEM((n, 4 * LANES), bf16),
            pltpu.VMEM((n, 2 * LANES), bf16),
            pltpu.VMEM((n, 2 * LANES), bf16),
        ],
        10,
    )(meta, lens, received, params, fhi, flo, spec)

    received = exchange(send) if dims.fast else to_tokens(send)
    part = shape(dims.ni, dims.nz, dims.units + 1, 8, LANES)
    send, result, wsend, wkeep = call(
        bind(gate_kernel, dims),
        (token_pieces, shape(*inputs.shape, dtype=bf16), part, part),
        [SMEM] + [VMEM] * 5,
        [
            pltpu.VMEM((tokens, dims.width), f32),
            pltpu.VMEM((tokens, dims.width), bf16),
            pltpu.VMEM((tokens, 2 * dims.width), f32),
            pltpu.VMEM((tokens, 2 * dims.width), bf16),
            pltpu.VMEM((tokens, dims.width), f32),
            pltpu.VMEM((dims.width, 2 * dims.width), f32),
        ],
        14,
    )(meta, received, inputs, glu_weight, glu_bias.reshape(1, -1), out_cotangent)

    received = exchange(send) if dims.fast else to_channels(
        send.reshape(dims.seqs, dims.places, dims.width)
    )
    def swap(x, axis, by):
        return lax.ppermute(x, axis, [(i, i ^ by) for i in range(lax.axis_size(axis))])

    def total(pieces, axis):
        got = [swap(piece, axis, s) for s, piece in enumerate(pieces) if s > 0]
        return sum(got, pieces[0])

    def everyone(x, axis, size):
        return [x] + [swap(x, axis, s) for s in range(1, size)]

    other = swap(wsend, "core", 1)
    part = total([wkeep[i] + other[i] for i in range(dims.ni)], "batch")
    received, part = lax.optimization_barrier((received, part))
    part = total([part[z] for z in range(dims.nz)], "z")

    send, small = call(
        bind(backward_kernel, dims),
        (pieces, shape(dims.small_rows, LANES)),
        [SMEM, SMEM] + [VMEM] * 12,
        [
            pltpu.VMEM((n, LANES), f32),
            pltpu.VMEM((n + 8, LANES), f32),
            pltpu.VMEM((n + 8, LANES), f32),
            pltpu.VMEM((n, 2 * LANES), bf16),
            pltpu.VMEM((n, 8 * LANES), bf16),
            pltpu.VMEM((n, 8 * LANES), bf16),
            pltpu.VMEM((n, 2 * LANES), f32),
            pltpu.VMEM((n, 2 * LANES), f32),
        ],
        16,
    )(meta, lens, received, params, fhi, flo, spec, mixed, normed, seen, stat, zr, zi, vec)

    received = exchange(send) if dims.fast else to_tokens(send)
    bias_grad = part[dims.units].reshape(-1)
    plane = everyone(jnp.stack(everyone(part[: dims.units], "z", dims.nz)), "batch", dims.ni)
    plane_too = [swap(x, "core", 1) for x in plane]
    small = jnp.stack(everyone(small.reshape(-1, 8, LANES), "z", dims.nz))
    small = jnp.stack(everyone(small, "batch", dims.ni))
    small_too = swap(small, "core", 1)

    if dims.fast:
        outs = call(
            bind(finish_kernel, dims),
            (shape(*inputs.shape), shape(dims.width, 2 * dims.width))
            + (shape(modes, dims.width),) * 6
            + (shape(1, dims.width),) * 4,
            [SMEM] + [VMEM] * (4 + 2 * dims.ni),
            [],
            6,
        )(meta, received, out_cotangent, *plane, *plane_too, small, small_too)
        grad_in, weight_grad = outs[:2]
        mode_grads = outs[2:8]
        chan_grads = [x.reshape(-1) for x in outs[8:]]
    else:
        grad_in = out_cotangent.astype(f32) + received.reshape(inputs.shape)

        def in_order(mine, other):
            both = jnp.where(core == 0, jnp.stack([mine, other]), jnp.stack([other, mine]))
            both = jnp.take(both, meta[0] ^ jnp.arange(dims.ni), axis=1)
            return jnp.take(both, meta[2] ^ jnp.arange(dims.nz), axis=2)

        units = in_order(jnp.stack(plane), jnp.stack(plane_too))
        units = units.reshape(dims.width // 8, -1, 8, LANES)
        weight_grad = units.transpose(0, 2, 1, 3).reshape(dims.width, -1)
        rows = in_order(small, small_too).transpose(1, 2, 0, 3, 4, 5)
        rows = rows.reshape(nd, dims.small_rows, dims.groups, hc)
        table = rows[:, : 6 * m].reshape(nd, 6, m * dims.groups, hc).transpose(1, 2, 0, 3)
        mode_grads = list(table.reshape(6, m * dims.groups, dims.width)[:, :modes])
        rest = rows[:, 6 * m : 6 * m + 4, 0].transpose(1, 0, 2).reshape(4, dims.width)
        chan_grads = list(rest)
    step_grad, gain_grad, shift_grad, skip_grad = chan_grads
    return (
        result,
        grad_in,
        gain_grad,
        shift_grad,
        step_grad,
        *mode_grads,
        skip_grad,
        weight_grad,
        bias_grad,
    )


def solution(mesh):
    batch = mesh.shape["batch"]
    fine = Mesh(mesh.devices.reshape(-1, 2, batch), ("z", "core", "batch"))
    tokens = P("batch", ("z", "core"), None)
    return jax.shard_map(
        functools.partial(local, dict(fine.shape)),
        mesh=fine,
        in_specs=(tokens, P("batch")) + (P(),) * 12 + (tokens,),
        out_specs=(tokens, tokens) + (P(),) * 12,
        check_vma=False,
    )
```

```python
import functools
import math

import jax
import jax.numpy as jnp
from jax import lax
from jax.experimental import pallas as pl
from jax.experimental.pallas import tpu as pltpu
from jax.sharding import Mesh
from jax.sharding import PartitionSpec as P


EPS = 1e-05
LANES = 128
ALL = ("batch", "z", "core")
SMEM = pl.BlockSpec(memory_space=pltpu.SMEM)
VMEM = pl.BlockSpec(memory_space=pltpu.VMEM)
HBM = pl.BlockSpec(memory_space=pltpu.HBM)
ANY = pl.BlockSpec(memory_space=pl.ANY)
DMA = pltpu.SemaphoreType.DMA
ROWS = 64
STEP = 16
copy = pltpu.make_async_copy
f32 = jnp.float32
bf16 = jnp.bfloat16


def mm(a, b):
    return jnp.dot(a, b, preferred_element_type=f32)


def halves(x):
    hi = x.astype(bf16)
    return hi, (x - hi.astype(f32)).astype(bf16)


def lane_ids(shape):
    return lax.broadcasted_iota(jnp.int32, shape, len(shape) - 1)


def swap_blocks(tiles, width):
    tiles = list(tiles)
    block = lane_ids(tiles[0].shape) // width
    step = 1
    while step < len(tiles):
        low = (block & step) == 0
        for a in range(len(tiles)):
            if a & step == 0:
                first, second = tiles[a], tiles[a + step]
                tiles[a] = jnp.where(low, first, pltpu.roll(second, step * width, second.ndim - 1))
                tiles[a + step] = jnp.where(
                    low, pltpu.roll(first, LANES - step * width, first.ndim - 1), second
                )
        step *= 2
    return tiles


def fold_matrix(dims):
    rows = lax.broadcasted_iota(jnp.int32, (LANES, LANES), 0) % dims.chans
    cols = lax.broadcasted_iota(jnp.int32, (LANES, LANES), 1) % dims.chans
    return (rows == cols).astype(f32).astype(bf16)


def fold(row, dims):
    shift = dims.chans
    while shift < LANES:
        row = row + pltpu.roll(row, shift, 1)
        shift *= 2
    return row


class Dims:
    def __init__(self, inputs_shape, modes, mesh_shape):
        self.seqs, self.places, self.width = inputs_shape
        self.ni = mesh_shape["batch"]
        self.nz = mesh_shape["z"]
        self.nj = mesh_shape["z"] * mesh_shape["core"]
        self.devices = self.ni * self.nj
        self.length = self.places * self.nj
        self.quarter = self.length // 4
        self.chans = self.width // self.devices
        self.groups = LANES // self.chans
        self.all_seqs = self.seqs * self.ni
        self.modes = modes
        self.mode_rows = -(-modes // self.groups)
        self.small_rows = -(-(6 * self.mode_rows + 4) // 8) * 8
        self.piece_width = self.seqs * self.chans
        self.place_groups = LANES // self.piece_width
        self.piece_rows = self.places // self.place_groups
        self.units = self.width * 2 * self.width // (8 * LANES) // self.devices
        self.fast = (
            self.piece_width * self.ni == LANES
            and self.piece_rows % 8 == 0
            and self.nj == self.groups
            and self.small_rows == 32
            and self.place_groups == 4
        )


def each(count, body, unroll=True):
    lax.fori_loop(0, count, lambda k, _: body(k), None, unroll=unroll)


def class_rows(b, g, dims):
    return pl.ds(b * dims.places + g, dims.piece_rows, stride=4)


def pack_tokens(read, write, dims, done=None):
    def some(tile):
        parts = []
        for g in range(4):
            for b in range(dims.seqs):
                parts.append(read(tile, class_rows(b, g, dims)))
        parts = swap_blocks(parts, dims.chans)
        for e in range(dims.groups):
            write(tile * dims.groups + e, parts[e])
        if done is not None:
            done(tile)

    each(dims.width // LANES, some)


def unpack_tokens(ref, out, dims, unroll=True):
    def some(tile):
        parts = [ref[tile * dims.groups + e] for e in range(dims.groups)]
        parts = swap_blocks(parts, dims.chans)
        for g in range(4):
            for b in range(dims.seqs):
                out[tile, class_rows(b, g, dims), :] = parts[g * dims.seqs + b]

    each(dims.width // LANES, some, unroll)


def pack_kernel(dims, x_ref, out_ref, wide):
    for b in range(dims.seqs):
        for t in range(dims.width // LANES):
            wide[t, b * dims.places : (b + 1) * dims.places, :] = x_ref[b, :, lanes(t)].astype(f32)

    def write(piece, value):
        out_ref[piece] = value

    pack_tokens(lambda tile, rows: wide[tile, rows, :], write, dims)


def unpack_channels(ref, out, dims):
    rows = dims.piece_rows
    if not dims.fast:
        for r in range(4):
            out[r] = ref[r * dims.quarter : (r + 1) * dims.quarter, :]
        return

    def some(j):
        parts = [ref[i * dims.nj + j] for i in range(dims.ni)]
        parts = swap_blocks(parts, dims.piece_width)
        for g in range(4):
            out[g, pl.ds(pl.multiple_of(j * rows, rows), rows), :] = parts[g]

    each(dims.nj, some)


def pack_channels(read, send, send_hbm, sem, dims):
    rows = dims.piece_rows
    if not dims.fast:
        for r in range(4):
            for at in range(0, dims.quarter, ROWS):
                start = r * dims.quarter + at
                send[start : start + ROWS, :] = read(r, at, ROWS)
        whole = copy(send, send_hbm, sem.at[0])
        whole.start()
        whole.wait()
        return

    def piece_copy(p):
        return copy(send.at[p], send_hbm.at[p], sem.at[p])

    def some(j):
        at = pl.multiple_of(j * rows, rows)
        parts = swap_blocks([read(g, at, rows) for g in range(4)], dims.piece_width)
        for i in range(dims.ni):
            send[i * dims.nj + j] = parts[i]
            piece_copy(i * dims.nj + j).start()

    each(dims.nj, some)
    each(dims.devices, lambda p: piece_copy(p).wait())


def mode_constants(par_ref, dims):
    m = dims.mode_rows
    decay, rotation, dr, di, rr, ri = [par_ref[p * m : (p + 1) * m, :] for p in range(6)]
    step = jnp.exp(par_ref[6 * m : 6 * m + 1, :])
    log_mag = -step * decay
    turn = step * rotation
    c1r = step * (rr * dr - ri * di)
    c1i = step * (rr * di + ri * dr)
    c2r = c1r * dr - c1i * di
    c2i = c1r * di + c1i * dr
    return step, log_mag, turn, (c1r, c1i, c2r, c2i), (decay, rotation, dr, di, rr, ri)


def tables_kernel(dims, par_ref, tab_hbm, tw_hbm, spec_hbm, zr_ref, zi_ref, vec_ref, *scratch):
    tab, tw, spec, cat, wave, sem_out, sem_spec = scratch
    n, m, q = dims.length, dims.mode_rows, dims.quarter

    def angles(b, _):
        at = pl.multiple_of(b * ROWS, ROWS)
        row = 2 * (lax.broadcasted_iota(jnp.int32, (ROWS, q), 0) + at) + 1
        col = 2 * lax.broadcasted_iota(jnp.int32, (ROWS, q), 1) + 1
        turn = ((row * col) & (8 * q - 1)).astype(f32) * (math.pi / (4 * q))
        for first, value in ((0, jnp.cos(turn)), (q, jnp.sin(turn))):
            for part, half in enumerate(halves(value)):
                tab[part, pl.ds(pl.multiple_of(first + at, ROWS), ROWS), :] = half
        row = 2 * (lax.broadcasted_iota(jnp.int32, (ROWS, LANES), 0) + at) + 1
        turn = row.astype(f32) * (math.pi / (2 * n))
        cos, sin = jnp.cos(turn), jnp.sin(turn)
        for p, value in enumerate((cos, sin, 1.0 - 2.0 * sin * sin, 2.0 * cos * sin)):
            tw[p, pl.ds(at, ROWS), :] = value
        return 0

    lax.fori_loop(0, q // ROWS, angles, 0)
    outs = [copy(tab, tab_hbm, sem_out.at[0]), copy(tw, tw_hbm, sem_out.at[1])]
    for out in outs:
        out.start()

    step, log_mag, turn, coefs, _ = mode_constants(par_ref, dims)
    c1r, c1i, c2r, c2i = coefs
    mag = jnp.exp(log_mag)
    l1r, l1i = mag * jnp.cos(turn), mag * jnp.sin(turn)
    mag = jnp.exp(8.0 * log_mag)
    l32r, l32i = mag * jnp.cos(8.0 * turn), mag * jnp.sin(8.0 * turn)
    for _ in range(2):
        l32r, l32i = l32r * l32r - l32i * l32i, 2.0 * l32r * l32i
    for p, value in enumerate((l32r, l32i, c1r, c1i, c2r, c2i)):
        vec_ref[p * m : (p + 1) * m, :] = value
    sub = 4.0 * lax.broadcasted_iota(jnp.int32, (8, LANES), 0).astype(f32)

    def wide(x, k):
        return jnp.broadcast_to(x[k : k + 1], (8, LANES))

    for k in range(m):
        mag = jnp.exp(sub * log_mag[k : k + 1])
        zr, zi = mag * jnp.cos(sub * turn[k : k + 1]), mag * jnp.sin(sub * turn[k : k + 1])
        for r in range(4):
            zr_ref[r, 8 * k : 8 * k + 8, :] = zr
            zi_ref[r, 8 * k : 8 * k + 8, :] = zi
            ar, ai = wide(l1r, k), wide(l1i, k)
            zr, zi = zr * ar - zi * ai, zr * ai + zi * ar
    consts = [
        tuple(wide(x, k) for x in (l32r, l32i, 2 * c1r, 2 * c1i, 2 * c2r, 2 * c2i)) for k in range(m)
    ]
    group = fold_matrix(dims)
    for r in range(4):

        def time_step(t, zs):
            at = pl.multiple_of(t * 8, 8)
            k1 = jnp.zeros((8, LANES), f32)
            k2 = jnp.zeros((8, LANES), f32)
            out = []
            for k in range(m):
                zr, zi = zs[2 * k], zs[2 * k + 1]
                ar, ai, b1r, b1i, b2r, b2i = consts[k]
                k1 = k1 + (b1r * zr - b1i * zi)
                k2 = k2 + (b2r * zr - b2i * zi)
                out += [zr * ar - zi * ai, zr * ai + zi * ar]
            wave[pl.ds(at, 8), lanes(0)] = k1
            wave[pl.ds(at, 8), lanes(1)] = k2
            return tuple(out)

        start = []
        for k in range(m):
            start += [zr_ref[r, 8 * k : 8 * k + 8, :], zi_ref[r, 8 * k : 8 * k + 8, :]]
        lax.fori_loop(0, q // 8, time_step, tuple(start), unroll=4)
        for p in range(2):
            hi, lo = halves(wave[0:q, lanes(p)])
            hi, lo = halves(mm(hi, group) + mm(lo, group))
            cat[r, :, lanes(p)] = hi
            cat[r, :, lanes(2 + p)] = lo

    forth(tab, cat, wave, 2, dims)

    def spectrum(b, _):
        at = pl.multiple_of(b * STEP, STEP)
        for p in range(2):
            for k, (re, im) in enumerate(butterfly(wave, tw, at, p, dims)):
                spec[k, pl.ds(at, STEP), lanes(2 * p)] = re * (1.0 / n)
                spec[k, pl.ds(at, STEP), lanes(2 * p + 1)] = im * (1.0 / n)
        return 0

    lax.fori_loop(0, q // STEP, spectrum, 0)
    outs += [copy(spec.at[k], spec_hbm.at[k], sem_spec.at[k]) for k in range(4)]
    for out in outs[2:]:
        out.start()
    for out in outs:
        out.wait()


def lanes(p):
    return slice(p * LANES, (p + 1) * LANES)


def forth(tab, cat, wave, count, dims):
    wide = count * LANES
    rows = 2 * dims.quarter

    def one(r, _):
        both = mm(tab[0], cat[r])
        low = mm(tab[1], cat[r, :, :wide])
        out = both[:, :wide] + both[:, wide:] + low
        wave[pl.ds(pl.multiple_of(r * rows, rows), rows), 0:wide] = out
        return 0

    lax.fori_loop(0, 4, one, 0)


def twiddles(tw, at):
    c1, s1, c2, s2 = [tw[p, pl.ds(at, STEP), :] for p in range(4)]
    return (c2, s2), (c1, s1), None, (c1, -s1)


def times(a, b):
    if b is None:
        return a
    return a[0] * b[0] - a[1] * b[1], a[0] * b[1] + a[1] * b[0]


def plus(a, b):
    return a[0] + b[0], a[1] + b[1]


def minus(a, b):
    return a[0] - b[0], a[1] - b[1]


def turned(a):
    return -a[1], a[0]


def butterfly(wave, tw, at, p, dims):
    rows = dims.quarter
    parts = []
    for r, twiddle in enumerate(twiddles(tw, at)):
        re = wave[pl.ds(pl.multiple_of(2 * r * rows + at, STEP), STEP), lanes(p)]
        im = wave[pl.ds(pl.multiple_of((2 * r + 1) * rows + at, STEP), STEP), lanes(p)]
        parts.append(times((re, -im), twiddle))
    even, odd = plus(parts[0], parts[2]), plus(parts[1], parts[3])
    even_too, odd_too = minus(parts[0], parts[2]), turned(minus(parts[1], parts[3]))
    return plus(even, odd), minus(even_too, odd_too), minus(even, odd), plus(even_too, odd_too)


def unbutterfly(parts, tw, at, back_r, back_i, p, count):
    even, odd = plus(parts[0], parts[2]), plus(parts[1], parts[3])
    even_too, odd_too = minus(parts[0], parts[2]), turned(minus(parts[1], parts[3]))
    sums = plus(even, odd), plus(even_too, odd_too), minus(even, odd), minus(even_too, odd_too)
    for r, twiddle in enumerate(twiddles(tw, at)):
        if twiddle is not None:
            twiddle = twiddle[0], -twiddle[1]
        re, im = times(sums[r], twiddle)
        for ref, value in ((back_r, re), (back_i, -im)):
            hi, lo = halves(value)
            ref[r, pl.ds(at, STEP), lanes(p)] = hi
            ref[r, pl.ds(at, STEP), lanes(count + p)] = lo


def back(tab, back_r, back_i, r, count, dims):
    q = dims.quarter
    wide = count * LANES
    both = mm(tab[0, :q], back_r[r]) + mm(tab[0, q:], back_i[r])
    low = mm(tab[1, :q], back_r[r, :, :wide]) + mm(tab[1, q:], back_i[r, :, :wide])
    return both[:, :wide] + both[:, wide:] + low


def column_sums(x):
    return jnp.sum(x.reshape(x.shape[0] // 8, 8, LANES), axis=0)


def lane_lengths(meta_ref, lens_refs, dims):
    lane = lane_ids((1, LANES)) // dims.chans
    row = jnp.zeros((1, LANES), jnp.int32)
    total = jnp.int32(0)
    for s in range(dims.all_seqs):
        source = s // dims.seqs
        value = lens_refs[source][s % dims.seqs]
        total = total + value
        row = jnp.where(lane == s ^ (meta_ref[0] * dims.seqs), value, row)
    return row, total.astype(f32)


def valid_rows(r, at, rows, lens):
    places = 4 * (lax.broadcasted_iota(jnp.int32, (rows, LANES), 0) + at) + r
    return (places < lens).astype(f32)


def forward_kernel(dims, meta_ref, r_ref, par_ref, tab_hbm, tw_hbm, spec_hbm, *rest):
    lens_refs, rest = rest[: dims.ni], rest[dims.ni :]
    (send_hbm, mixed_hbm, normed_hbm, seen_hbm, stat_ref), rest = rest[:5], rest[5:]
    tab, tw, spec, seen, x_sc, mix_sc, normed_sc, cat, wave, back_r, back_i, send = rest[:12]
    sem_tab, sem_spec, sem_seen, sem_out, sem_send = rest[12:]
    m, q = dims.mode_rows, dims.quarter
    ins = [copy(tab_hbm, tab, sem_tab.at[0]), copy(tw_hbm, tw, sem_tab.at[1])]
    ins += [copy(spec_hbm.at[k], spec.at[k], sem_spec.at[k]) for k in range(4)]
    for one in ins:
        one.start()
    lens, total = lane_lengths(meta_ref, lens_refs, dims)
    unpack_channels(r_ref, x_sc, dims)
    classes = range(4)

    def add_up(b, acc):
        at = pl.multiple_of(b * ROWS, ROWS)
        for r in classes:
            acc = acc + column_sums(x_sc[r, pl.ds(at, ROWS), :] * valid_rows(r, at, ROWS, lens))
        return acc

    zero = jnp.zeros((8, LANES), f32)
    acc = lax.fori_loop(0, q // ROWS, add_up, zero)
    average = fold(jnp.sum(acc, axis=0, keepdims=True), dims) / total

    def add_squares(b, acc):
        at = pl.multiple_of(b * ROWS, ROWS)
        for r in classes:
            x = (x_sc[r, pl.ds(at, ROWS), :] - average) * valid_rows(r, at, ROWS, lens)
            acc = acc + column_sums(x * x)
        return acc

    acc = lax.fori_loop(0, q // ROWS, add_squares, zero)
    variance = fold(jnp.sum(acc, axis=0, keepdims=True), dims) / total
    inv = lax.rsqrt(variance + EPS)
    gain = par_ref[6 * m + 1 : 6 * m + 2, :]
    shift = par_ref[6 * m + 2 : 6 * m + 3, :]
    skip = par_ref[6 * m + 3 : 6 * m + 4, :]
    stat_ref[0:1, :] = inv
    stat_ref[1:2, :] = jnp.broadcast_to(total, (1, LANES))
    stat_ref[2:3, :] = lens.astype(f32)
    stat_ref[3:8, :] = jnp.zeros((5, LANES), f32)
    first_row = lax.broadcasted_iota(jnp.int32, (ROWS, LANES), 0) == 0

    def normalize(b, last):
        at = pl.multiple_of(b * ROWS, ROWS)
        mixed = []
        for r in classes:
            normed = (x_sc[r, pl.ds(at, ROWS), :] - average) * inv
            mixed.append((gain * normed + shift) * valid_rows(r, at, ROWS, lens))
            normed_sc[r, pl.ds(at, ROWS), :] = normed
            mix_sc[r, pl.ds(at, ROWS), :] = mixed[r]
        earlier = jnp.where(first_row, last, pltpu.roll(mixed[3], 1, 0))
        for r in classes:
            liquid = mixed[r] * (earlier if r == 0 else mixed[r - 1])
            for p, value in enumerate((mixed[r], liquid)):
                hi, lo = halves(value)
                cat[r, pl.ds(at, ROWS), lanes(p)] = hi
                cat[r, pl.ds(at, ROWS), lanes(2 + p)] = lo
        return mixed[3][ROWS - 1 :, :]

    lax.fori_loop(0, q // ROWS, normalize, jnp.zeros((1, LANES), f32))
    outs = [copy(mix_sc, mixed_hbm, sem_out.at[0]), copy(normed_sc, normed_hbm, sem_out.at[1])]
    for out in outs:
        out.start()
    for one in ins:
        one.wait()
    forth(tab, cat, wave, 2, dims)

    def multiply(b, _):
        at = pl.multiple_of(b * STEP, STEP)
        mixed = butterfly(wave, tw, at, 0, dims)
        liquid = butterfly(wave, tw, at, 1, dims)
        parts = []
        for k in range(4):
            for p, value in enumerate(mixed[k] + liquid[k]):
                seen[k, pl.ds(at, STEP), lanes(p)] = value
            kr, ki, lr, li = [spec[k, pl.ds(at, STEP), lanes(p)] for p in range(4)]
            parts.append(plus(times(mixed[k], (kr, ki)), times(liquid[k], (lr, li))))
        unbutterfly(parts, tw, at, back_r, back_i, 0, 1)
        return 0

    lax.fori_loop(0, q // STEP, multiply, 0)
    outs += [copy(seen.at[k], seen_hbm.at[k], sem_seen.at[k]) for k in range(4)]
    for out in outs[2:]:
        out.start()

    def respond(r, _):
        x_sc[r] = back(tab, back_r, back_i, r, 1, dims) + skip * mix_sc[r]
        return 0

    lax.fori_loop(0, 4, respond, 0)
    pack_channels(
        lambda r, at, size: x_sc[r, pl.ds(at, size), :], send, send_hbm, sem_send, dims
    )
    for out in outs:
        out.wait()


def gate_kernel(dims, r_ref, x_ref, w_ref, b_ref, ct_ref, send_hbm, out_ref, act_hbm, gj_hbm, bias_ref, *scratch):
    resp, act, joined, gj, gact, send, sem_out, sem_send = scratch
    tokens = dims.seqs * dims.places
    width = dims.width
    places = dims.places

    tiles = range(width // LANES)
    if dims.fast:
        unpack_tokens(r_ref, resp, dims)
    else:
        for t in tiles:
            resp[t] = r_ref[:, lanes(t)]
    c0 = math.sqrt(2.0 / math.pi)
    c1 = 0.044715
    rows = 32

    def gelu(b, _):
        at = pl.multiple_of(b * rows, rows)
        for tile in tiles:
            r = resp[tile, pl.ds(at, rows), :]
            t = jnp.tanh(c0 * (r + c1 * r * r * r))
            act[pl.ds(at, rows), lanes(tile)] = (0.5 * r * (1.0 + t)).astype(bf16)
            slope = 0.5 * (1.0 + t) + 0.5 * r * (1.0 - t * t) * (c0 * (1.0 + 3.0 * c1 * r * r))
            resp[tile, pl.ds(at, rows), :] = slope
        return 0

    lax.fori_loop(0, tokens // rows, gelu, 0)
    outs = [copy(act, act_hbm, sem_out.at[0]), copy(gj, gj_hbm, sem_out.at[1])]
    outs[0].start()
    joined[...] = mm(act[...], w_ref[...])
    bias = b_ref[...]
    half = min(16, places)
    for b in range(dims.seqs):

        def gate(k, sums):
            at = pl.multiple_of(k * half, half)
            tok = pl.multiple_of(b * places + k * half, half)
            value = joined[pl.ds(tok, half), :width] + bias[:, :width]
            s = jax.nn.sigmoid(joined[pl.ds(tok, half), width:] + bias[:, width:])
            x = x_ref[b, pl.ds(at, half), :].astype(f32)
            g = ct_ref[b, pl.ds(at, half), :].astype(f32)
            out_ref[b, pl.ds(at, half), :] = (x + value * s).astype(bf16)
            gs = g * s
            first = gs.astype(bf16)
            second = (gs * value * (1.0 - s)).astype(bf16)
            gj[pl.ds(tok, half), :width] = first
            gj[pl.ds(tok, half), width:] = second
            first = jnp.sum(first.astype(f32).reshape(half // 8, 8, width), axis=0)
            second = jnp.sum(second.astype(f32).reshape(half // 8, 8, width), axis=0)
            return sums[0] + first, sums[1] + second

        if b == 0:
            zero = jnp.zeros((8, width), f32)
            sums = (zero, zero)
        sums = lax.fori_loop(0, places // half, gate, sums)
    outs[1].start()
    grad = lax.dot_general(
        gj[...], w_ref[...], (((1,), (1,)), ((), ())), preferred_element_type=f32
    )
    for t in tiles:
        gact[t] = grad[:, lanes(t)]
    if dims.fast:

        def read(tile, rows):
            return gact[tile, rows, :] * resp[tile, rows, :]

        def put(piece, value):
            send[piece] = value

        def tile_copy(tile):
            some = pl.ds(tile * dims.groups, dims.groups)
            return copy(send.at[some], send_hbm.at[some], sem_send.at[tile])

        pack_tokens(read, put, dims, lambda tile: tile_copy(tile).start())
        outs += [tile_copy(tile) for tile in tiles]
    else:
        for t in tiles:
            send[:, lanes(t)] = gact[t] * resp[t]
        outs.append(copy(send, send_hbm, sem_send.at[0]))
        outs[-1].start()
    sums = [jnp.sum(s, axis=0, keepdims=True) for s in sums]
    for p, total in enumerate(sums):
        for t in range(width // LANES):
            row = p * (width // LANES) + t
            bias_ref[row : row + 1, :] = total[:, lanes(t)]
    for out in outs:
        out.wait()


def weight_kernel(dims, meta_ref, act_hbm, gj_hbm, bias_ref, wsend_hbm, wkeep_hbm, *scratch):
    act, gj, weight, wsend, wkeep, sem_in, sem_out = scratch
    ins = [copy(act_hbm, act, sem_in.at[0]), copy(gj_hbm, gj, sem_in.at[1])]
    for each in ins:
        each.start()
    for each in ins:
        each.wait()
    tiles = 2 * dims.width // LANES
    half = dims.width // 2
    outs = []
    other = 1 - meta_ref[1]
    weight[...] = lax.dot_general(
        act[...], gj[...], (((0,), (0,)), ((), ())), preferred_element_type=f32
    )
    for k, (ref, hbm, core) in enumerate(
        ((wsend, wsend_hbm, other), (wkeep, wkeep_hbm, meta_ref[1]))
    ):
        for i in range(dims.ni):
            for z in range(dims.nz):
                ref[i, z, dims.units, :, :] = bias_ref[...]
                owner = ((core * dims.ni) + (meta_ref[0] ^ i)) * dims.nz + (meta_ref[2] ^ z)
                for u in range(dims.units):
                    if dims.units % tiles == 0:
                        row = owner * (dims.units // tiles) + u // tiles
                        cols = lanes(u % tiles)
                    else:
                        unit = owner * dims.units + u
                        row = unit // tiles
                        cols = pl.ds(pl.multiple_of(unit % tiles * LANES, LANES), LANES)
                    ref[i, z, u, :, :] = weight[pl.ds(pl.multiple_of(row * 8, 8), 8), cols]
            outs.append(copy(ref.at[i], hbm.at[i], sem_out.at[k, i]))
            outs[-1].start()
    for out in outs:
        out.wait()


def backward_kernel(dims, r_ref, par_ref, *rest):
    ins_hbm, (stat_ref, send_hbm, grad_hbm, sums_ref) = rest[:5], rest[5:9]
    tab, tw, spec, grads, mix_sc, normed_sc, g_sc, up_sc, cat, wave, back_r, back_i = rest[9:21]
    lead_sc, liquid_sc, send, sem_in, sem_spec, sem_send, sem_grad = rest[21:]
    tab_hbm, tw_hbm, spec_hbm, mixed_hbm, normed_hbm = ins_hbm
    m, q = dims.mode_rows, dims.quarter
    ins = [
        copy(mixed_hbm, mix_sc, sem_in.at[0]),
        copy(tab_hbm, tab, sem_in.at[1]),
        copy(tw_hbm, tw, sem_in.at[2]),
        copy(normed_hbm, normed_sc, sem_in.at[3]),
    ]
    for k in range(4):
        ins.append(copy(spec_hbm.at[k], spec.at[k], sem_spec.at[k]))
    for one in ins:
        one.start()
    unpack_channels(r_ref, g_sc, dims)
    gain = par_ref[6 * m + 1 : 6 * m + 2, :]
    skip = par_ref[6 * m + 3 : 6 * m + 4, :]
    inv = stat_ref[0:1, :]
    total = stat_ref[1:2, :]
    lens = stat_ref[2:3, :].astype(jnp.int32)
    zero = jnp.zeros((8, LANES), f32)
    classes = range(4)
    ins[0].wait()

    def gather(b, acc):
        at = pl.multiple_of(b * ROWS, ROWS)
        for r in classes:
            g = g_sc[r, pl.ds(at, ROWS), :]
            hi, lo = halves(g)
            cat[r, pl.ds(at, ROWS), lanes(0)] = hi
            cat[r, pl.ds(at, ROWS), lanes(1)] = lo
            acc = acc + column_sums(g * mix_sc[r, pl.ds(at, ROWS), :])
        return acc

    skip_acc = lax.fori_loop(0, q // ROWS, gather, zero)
    for one in ins[1:]:
        one.wait()
    forth(tab, cat, wave, 1, dims)

    def multiply(b, _):
        at = pl.multiple_of(b * STEP, STEP)
        grad = butterfly(wave, tw, at, 0, dims)
        for k in range(4):
            for p in range(2):
                grads[k, pl.ds(at, STEP), lanes(p)] = grad[k][p]
        for p in range(2):
            products(grad, spec, tw, at, back_r, back_i, p)
        return 0

    lax.fori_loop(0, q // STEP, multiply, 0)
    out = copy(grads, grad_hbm, sem_grad)
    out.start()

    def pull(r, _):
        value = back(tab, back_r, back_i, r, 2, dims)
        lead_sc[r] = value[:, lanes(0)]
        liquid_sc[r] = value[:, lanes(1)]
        up_sc[r] = value[:, lanes(1)] * mix_sc[r]
        return 0

    lax.fori_loop(0, 4, pull, 0)

    row = lax.broadcasted_iota(jnp.int32, (ROWS, LANES), 0)
    blank = jnp.zeros((1, LANES), f32)
    gain_acc, shift_acc = zero, zero
    for at in range(0, q, ROWS):
        rows = slice(at, at + ROWS)
        for r in classes:
            if r == 0:
                before = blank if at == 0 else mix_sc[3, at - 1 : at, :]
                earlier = jnp.where(row == 0, before, pltpu.roll(mix_sc[3, rows, :], 1, 0))
            else:
                earlier = mix_sc[r - 1, rows, :]
            if r == 3:
                after = blank if at + ROWS == q else up_sc[0, at + ROWS : at + ROWS + 1, :]
                up = jnp.where(row == ROWS - 1, after, pltpu.roll(up_sc[0, rows, :], ROWS - 1, 0))
            else:
                up = up_sc[r + 1, rows, :]
            masked = lead_sc[r, rows, :] + skip * g_sc[r, rows, :] + liquid_sc[r, rows, :] * earlier
            masked = (masked + up) * valid_rows(r, at, ROWS, lens)
            g_sc[r, rows, :] = masked
            gain_acc = gain_acc + column_sums(masked * normed_sc[r, rows, :])
            shift_acc = shift_acc + column_sums(masked)

    def whole(acc):
        return fold(jnp.sum(acc, axis=0, keepdims=True), dims)

    gain_sum, shift_sum, skip_sum = whole(gain_acc), whole(shift_acc), whole(skip_acc)
    scale = gain * inv
    shift_mean = shift_sum / total
    gain_mean = gain_sum / total

    def read(r, at, size):
        normed = normed_sc[r, pl.ds(at, size), :]
        value = g_sc[r, pl.ds(at, size), :] - shift_mean - normed * gain_mean
        return value * scale * valid_rows(r, at, size, lens)

    sums_ref[...] = jnp.zeros_like(sums_ref)
    for p, value in enumerate((gain_sum, shift_sum, skip_sum)):
        sums_ref[p : p + 1, :] = value
    pack_channels(read, send, send_hbm, sem_send, dims)
    out.wait()


def products(grad, ref, tw, at, back_r, back_i, p):
    parts = []
    for k in range(4):
        re = ref[k, pl.ds(at, STEP), lanes(2 * p)]
        im = ref[k, pl.ds(at, STEP), lanes(2 * p + 1)]
        parts.append(times(grad[k], (re, -im)))
    unbutterfly(parts, tw, at, back_r, back_i, p, 2)


def modes_kernel(dims, par_ref, tab_hbm, tw_hbm, seen_hbm, grad_hbm, sums_ref, *rest):
    zr_ref, zi_ref, vec_ref, small_ref, tab, tw, seen, grads, back_r, back_i, dk, sem = rest
    n, m, q = dims.length, dims.mode_rows, dims.quarter
    sources = tw_hbm, seen_hbm, grad_hbm, tab_hbm
    ins = [copy(a, b, sem.at[k]) for k, (a, b) in enumerate(zip(sources, (tw, seen, grads, tab)))]
    for one in ins:
        one.start()
    for one in ins[:3]:
        one.wait()
    zero = jnp.zeros((8, LANES), f32)
    classes = range(4)

    def multiply(b, _):
        at = pl.multiple_of(b * STEP, STEP)
        grad = [tuple(grads[k, pl.ds(at, STEP), lanes(p)] for p in range(2)) for k in range(4)]
        for p in range(2):
            products(grad, seen, tw, at, back_r, back_i, p)
        return 0

    lax.fori_loop(0, q // STEP, multiply, 0)
    ins[3].wait()
    group = fold_matrix(dims)

    def pull(r, _):
        value = back(tab, back_r, back_i, r, 2, dims) * (1.0 / n)
        for p in range(2):
            hi, lo = halves(value[:, lanes(p)])
            dk[r, :, lanes(p)] = mm(hi, group) + mm(lo, group)
        return 0

    lax.fori_loop(0, 4, pull, 0)

    step, log_mag, turn, _, params = mode_constants(par_ref, dims)
    decay, rotation, dr, di, rr, ri = params
    l32r, l32i, c1r, c1i, c2r, c2i = [vec_ref[p * m : (p + 1) * m, :] for p in range(6)]
    sub = 4.0 * lax.broadcasted_iota(jnp.int32, (8, LANES), 0).astype(f32)
    sums = [[] for _ in range(8)]
    for first in range(0, m, 2):
        some = range(first, min(m, first + 2))
        ratio = [
            (
                jnp.broadcast_to(l32r[k : k + 1], (8, LANES)),
                jnp.broadcast_to(l32i[k : k + 1], (8, LANES)),
            )
            for k in some
        ]
        sofar = [zero] * (8 * len(ratio))
        for r in classes:

            def mode_step(t, carry):
                at = pl.multiple_of(t * 8, 8)
                d1 = dk[r, pl.ds(at, 8), lanes(0)]
                d2 = dk[r, pl.ds(at, 8), lanes(1)]
                place = sub + (32 * t + r).astype(f32)
                e1 = d1 * place
                e2 = d2 * place
                out = []
                for k, (ar, ai) in enumerate(ratio):
                    zr, zi, *acc = carry[10 * k : 10 * (k + 1)]
                    out += [zr * ar - zi * ai, zr * ai + zi * ar]
                    for p, d in enumerate((d1, d2, e1, e2)):
                        out += [acc[2 * p] + d * zr, acc[2 * p + 1] + d * zi]
                return tuple(out)

            carry = []
            for at, k in enumerate(some):
                carry += [zr_ref[r, 8 * k : 8 * k + 8, :], zi_ref[r, 8 * k : 8 * k + 8, :]]
                carry += sofar[8 * at : 8 * at + 8]
            carry = lax.fori_loop(0, q // 8, mode_step, tuple(carry), unroll=4)
            sofar = [v for k in range(len(ratio)) for v in carry[10 * k + 2 : 10 * k + 10]]
        for k in range(len(ratio)):
            for p in range(8):
                sums[p].append(jnp.sum(sofar[8 * k + p], axis=0, keepdims=True))
    a1r, a1i, a2r, a2i, e1r, e1i, e2r, e2i = [
        jnp.concatenate(s, axis=0) if len(s) > 1 else s[0] for s in sums
    ]
    btr = c1r * e1r - c1i * e1i + c2r * e2r - c2i * e2i
    bti = c1r * e1i + c1i * e1r + c2r * e2i + c2i * e2r
    d2r = dr * dr - di * di
    d2i = 2.0 * dr * di
    erd = step * (a1r * dr - a1i * di + a2r * d2r - a2i * d2i)
    eri = step * (a1r * di + a1i * dr + a2r * d2i + a2i * d2r)
    tr = a1r + 2.0 * (a2r * dr - a2i * di)
    ti = a1i + 2.0 * (a2r * di + a2i * dr)
    edr = step * (rr * tr - ri * ti)
    edi = step * (rr * ti + ri * tr)
    by_step = 2.0 * (c1r * a1r - c1i * a1i + c2r * a2r - c2i * a2i) + 2.0 * step * (
        -decay * btr - rotation * bti
    )
    small_ref[...] = jnp.zeros_like(small_ref)
    answers = (-2.0 * step * btr, -2.0 * step * bti, 2.0 * edr, -2.0 * edi, 2.0 * erd, -2.0 * eri)
    for p, value in enumerate(answers):
        small_ref[p * m : (p + 1) * m, :] = value
    small_ref[6 * m : 6 * m + 1, :] = fold(jnp.sum(by_step, axis=0, keepdims=True), dims)
    small_ref[6 * m + 1 : 6 * m + 4, :] = sums_ref[0:3, :]


def first_add_kernel(dims, keep_hbm, other_hbm, *refs):
    out_refs, (keep, other, sem) = refs[: dims.ni], refs[dims.ni :]
    ins = []
    for i in range(dims.ni):
        ins.append(copy(keep_hbm.at[i], keep.at[i], sem.at[0, i]))
        ins.append(copy(other_hbm.at[i], other.at[i], sem.at[1, i]))
    for each in ins:
        each.start()
    for i in range(dims.ni):
        ins[2 * i].wait()
        ins[2 * i + 1].wait()
        out_refs[i][...] = keep[i] + other[i]


def add_kernel(count, *refs):
    for p, out_ref in enumerate(refs[count:]):
        total = refs[0][p]
        for ref in refs[1:count]:
            total = total + ref[p]
        out_ref[...] = total


def last_add_kernel(dims, count, *refs):
    rows_ref, bias_ref = refs[count:]
    tiles = 2 * dims.width // LANES

    def unit(u):
        total = refs[0][u]
        for ref in refs[1:count]:
            total = total + ref[u]
        return total

    for u in range(dims.units):
        if dims.fast:
            rb, t = divmod(u, tiles)
            rows_ref[rb * 8 : rb * 8 + 8, lanes(t)] = unit(u)
        else:
            rows_ref[u * 8 : u * 8 + 8, :] = unit(u)
    bias = unit(dims.units)
    for t in range(tiles):
        bias_ref[:, lanes(t)] = bias[t : t + 1, :]


def stack_kernel(meta_at, meta_ref, *refs):
    out_ref = refs[-1]
    for s, ref in enumerate(refs[:-1]):
        out_ref[meta_ref[meta_at] ^ s] = ref[...]


def finish_kernel(dims, meta_ref, r_ref, ct_ref, *refs):
    ni, nz, m = dims.ni, dims.nz, dims.mode_rows
    planes = refs[:ni], refs[ni : 2 * ni]
    smalls = refs[2 * ni : 3 * ni], refs[3 * ni : 4 * ni]
    grad_ref, weight_ref, *small_refs, grad, sem = refs[4 * ni :]
    me, core = meta_ref[0], meta_ref[1]
    per = dims.width // 2 // ni
    copies = []
    for half, side in ((0, core), (1, 1 - core)):
        for i in range(ni):
            at = pl.multiple_of((side * ni + (me ^ i)) * per, per)
            target = weight_ref.at[pl.ds(at, per), :]
            copies.append(copy(planes[half][i], target, sem.at[half, i]))
            copies[-1].start()
    unpack_tokens(r_ref, grad, dims, False)
    for b in range(dims.seqs):
        for t in range(dims.width // LANES):
            value = grad[t, b * dims.places : (b + 1) * dims.places, :]
            grad_ref[b, :, lanes(t)] = value + ct_ref[b, :, lanes(t)].astype(f32)
    first = core == 0
    for i in range(ni):
        parts = []
        for z in range(nz):
            a, b = smalls[0][i][z], smalls[1][i][z]
            parts += [jnp.where(first, a, b), jnp.where(first, b, a)]
        parts = swap_blocks(parts, dims.chans)
        cols = pl.ds(pl.multiple_of((me ^ i) * LANES, LANES), LANES)
        for q in range(dims.groups):
            for p in range(6):
                small_refs[p][q * m : q * m + m, cols] = parts[q][p * m : p * m + m, :]
        for p in range(4):
            small_refs[6 + p][:, cols] = parts[0][6 * m + p : 6 * m + p + 1, :]
    for one in copies:
        one.wait()


def call(kernel, out_shape, in_specs, scratch, limit, us, out_specs=None):
    cost = pl.CostEstimate(flops=int(us * 1.1e9), bytes_accessed=int(us * 3e6), transcendentals=0)
    if out_specs is None:
        out_specs = jax.tree.map(lambda _: VMEM, out_shape)
    else:
        out_shape = tuple(
            pltpu.HBM(out.shape, out.dtype) if spec is HBM else out
            for out, spec in zip(out_shape, out_specs)
        )

    def run(*args):
        args = [
            pltpu.with_memory_space_constraint(x, pltpu.HBM) if spec is HBM else x
            for x, spec in zip(args, in_specs)
        ]
        return pl.pallas_call(
            kernel,
            out_shape=out_shape,
            in_specs=in_specs,
            out_specs=out_specs,
            scratch_shapes=scratch,
            compiler_params=pltpu.CompilerParams(vmem_limit_bytes=limit << 20),
            cost_estimate=cost,
        )(*args)

    return run


def shape(*dims, dtype=f32):
    return jax.ShapeDtypeStruct(dims, dtype)


def local(
    mesh_shape,
    inputs,
    lengths,
    norm_gain,
    norm_shift,
    log_step,
    decay_rate,
    rotation,
    drive_real,
    drive_imag,
    read_real,
    read_imag,
    skip_gain,
    glu_weight,
    glu_bias,
    out_cotangent,
):
    modes = decay_rate.shape[0]
    dims = Dims(inputs.shape, modes, mesh_shape)
    n, nd, m, hc = dims.length, dims.devices, dims.mode_rows, dims.chans
    core = lax.axis_index("core")
    owner = lax.axis_index(ALL)
    meta = jnp.stack([lax.axis_index("batch"), core, lax.axis_index("z")]).astype(jnp.int32)

    def exchange(x):
        return lax.all_to_all(x, ALL, 0, 0, tiled=True)

    some = dims.places // 4

    def to_channels(x):
        x = x.reshape(dims.seqs, some, 4, nd, hc).transpose(3, 2, 1, 0, 4)
        x = exchange(x.reshape(nd, dims.places, dims.piece_width))
        x = x.reshape(dims.ni, dims.nj, 4, some, dims.piece_width).transpose(2, 1, 3, 0, 4)
        x = x.reshape(n, dims.all_seqs * hc)
        return jnp.pad(x, ((0, 0), (0, LANES - x.shape[1])))

    def to_tokens(x):
        x = x[:, : dims.all_seqs * hc].reshape(4, dims.nj, some, dims.ni, dims.piece_width)
        x = x.transpose(3, 1, 0, 2, 4).reshape(nd, dims.places, dims.piece_width)
        x = exchange(x).reshape(nd, 4, some, dims.seqs, hc).transpose(3, 2, 1, 0, 4)
        return x.reshape(dims.seqs * dims.places, dims.width)

    table = jnp.stack([decay_rate, rotation, drive_real, drive_imag, read_real, read_imag])
    table = lax.dynamic_slice_in_dim(table, owner * hc, hc, 2)
    table = jnp.pad(table, ((0, 0), (0, m * dims.groups - modes), (0, 0)))
    table = table.reshape(6, dims.groups, m, hc).transpose(0, 2, 1, 3).reshape(6 * m, LANES)
    rest = jnp.stack([log_step, norm_gain, norm_shift, skip_gain])
    rest = lax.dynamic_slice_in_dim(rest, owner * hc, hc, 1)
    params = jnp.concatenate([table, jnp.tile(rest, (1, dims.groups))], axis=0)
    params, meta = lax.optimization_barrier((params, meta))

    pieces = (nd, dims.piece_rows, LANES) if dims.fast else (n, LANES)
    tokens = dims.seqs * dims.places
    token_pieces = (nd, dims.piece_rows, LANES) if dims.fast else (tokens, dims.width)
    bind = functools.partial
    q = dims.quarter
    tab = (2, 2 * q, q)
    tw = (4, q, LANES)
    four = (4, q, 4 * LANES)
    plain = (4, q, LANES)
    by_tile = (dims.width // LANES, dims.seqs * dims.places, LANES)

    def vmem(*sizes, dtype=f32):
        return pltpu.VMEM(sizes, dtype)

    if dims.fast:
        packed = call(
            bind(pack_kernel, dims), shape(*pieces), [VMEM], [vmem(*by_tile)], 4, 1.5
        )(inputs)
        received = exchange(packed)
    else:
        received = to_channels(inputs.astype(f32))

    tables, twiddle, spec, zr, zi, vec = call(
        bind(tables_kernel, dims),
        (
            shape(*tab, dtype=bf16),
            shape(*tw),
            shape(*four),
            shape(4, 8 * m, LANES),
            shape(4, 8 * m, LANES),
            shape(6 * m, LANES),
        ),
        [VMEM],
        [
            vmem(*tab, dtype=bf16),
            vmem(*tw),
            vmem(*four),
            vmem(*four, dtype=bf16),
            vmem(2 * n, 2 * LANES),
            DMA((2,)),
            DMA((4,)),
        ],
        12,
        6,
        (HBM, HBM, HBM, VMEM, VMEM, VMEM),
    )(params)

    def swap(x, axis, by):
        return lax.ppermute(x, axis, [(i, i ^ by) for i in range(lax.axis_size(axis))])

    def everyone(x, axis, size):
        return [x] + [swap(x, axis, s) for s in range(1, size)]

    lengths, vec = lax.optimization_barrier((lengths, vec))
    lens = everyone(lengths, "batch", dims.ni)
    send, mixed, normed, seen, stat = call(
        bind(forward_kernel, dims),
        (shape(*pieces), shape(*plain), shape(*plain), shape(*four), shape(8, LANES)),
        [SMEM, VMEM, VMEM, HBM, HBM, HBM] + [SMEM] * dims.ni,
        [
            vmem(*tab, dtype=bf16),
            vmem(*tw),
            vmem(*four),
            vmem(*four),
            vmem(*plain),
            vmem(*plain),
            vmem(*plain),
            vmem(*four, dtype=bf16),
            vmem(2 * n, 2 * LANES),
            vmem(4, q, 2 * LANES, dtype=bf16),
            vmem(4, q, 2 * LANES, dtype=bf16),
            vmem(*pieces),
            DMA((2,)),
            DMA((4,)),
            DMA((4,)),
            DMA((2,)),
            DMA((pieces[0],)),
        ],
        18,
        7,
        (HBM, HBM, HBM, HBM, VMEM),
    )(meta, received, params, tables, twiddle, spec, *lens)

    received = exchange(send) if dims.fast else to_tokens(send)
    wide = (tokens, dims.width)
    wider = (tokens, 2 * dims.width)
    unit = (dims.units + 1, 8, LANES)
    part = (dims.ni, dims.nz) + unit
    tiles = 2 * dims.width // LANES
    send, result, act, gj, bias = call(
        bind(gate_kernel, dims),
        (
            shape(*token_pieces),
            shape(*inputs.shape, dtype=bf16),
            shape(*wide, dtype=bf16),
            shape(*wider, dtype=bf16),
            shape(tiles, LANES),
        ),
        [VMEM] * 5,
        [
            vmem(*by_tile),
            vmem(*wide, dtype=bf16),
            vmem(*wider),
            vmem(*wider, dtype=bf16),
            vmem(*by_tile),
            vmem(*token_pieces),
            DMA((2,)),
            DMA((max(1, dims.width // LANES),)),
        ],
        8,
        4,
        (HBM, VMEM, HBM, HBM, VMEM),
    )(received, inputs, glu_weight, glu_bias.reshape(1, -1), out_cotangent)
    received = exchange(send) if dims.fast else to_channels(
        send.reshape(dims.seqs, dims.places, dims.width)
    )

    wsend, wkeep = call(
        bind(weight_kernel, dims),
        (shape(*part), shape(*part)),
        [SMEM, HBM, HBM, VMEM],
        [
            vmem(*wide, dtype=bf16),
            vmem(*wider, dtype=bf16),
            vmem(dims.width, 2 * dims.width),
            vmem(*part),
            vmem(*part),
            DMA((2,)),
            DMA((2, dims.ni)),
        ],
        14,
        3,
        (HBM, HBM),
    )(meta, act, gj, bias)
    parts = call(
        bind(first_add_kernel, dims),
        (shape(dims.nz, *unit),) * dims.ni,
        [HBM, ANY],
        [vmem(*part), vmem(*part), DMA((2, dims.ni))],
        5,
        0.1,
    )(wkeep, swap(wsend, "core", 1))
    parts = [parts[0]] + [swap(parts[s], "batch", s) for s in range(1, dims.ni)]
    parts = call(
        bind(add_kernel, dims.ni), (shape(*unit),) * dims.nz, [VMEM] * dims.ni, [], 2, 0.1
    )(*parts)
    received, parts = lax.optimization_barrier((received, parts))
    parts = [parts[0]] + [swap(parts[s], "z", s) for s in range(1, dims.nz)]

    send, grads, sums = call(
        bind(backward_kernel, dims),
        (shape(*pieces), shape(4, q, 2 * LANES), shape(8, LANES)),
        [VMEM, VMEM] + [HBM] * 5 + [VMEM],
        [
            vmem(*tab, dtype=bf16),
            vmem(*tw),
            vmem(*four),
            vmem(4, q, 2 * LANES),
            vmem(*plain),
            vmem(*plain),
            vmem(*plain),
            vmem(*plain),
            vmem(4, q, 2 * LANES, dtype=bf16),
            vmem(2 * n, LANES),
            vmem(*four, dtype=bf16),
            vmem(*four, dtype=bf16),
            vmem(*plain),
            vmem(*plain),
            vmem(*pieces),
            DMA((4,)),
            DMA((4,)),
            DMA((pieces[0],)),
            DMA(()),
        ],
        16,
        9,
        (HBM, HBM, VMEM),
    )(received, params, tables, twiddle, spec, mixed, normed, stat)

    send, parts = lax.optimization_barrier((send, parts))
    rows = (dims.width // nd, 2 * dims.width) if dims.fast else (dims.units * 8, LANES)
    rows, bias_grad = call(
        bind(last_add_kernel, dims, dims.nz),
        (shape(*rows), shape(1, 2 * dims.width)),
        [VMEM] * dims.nz,
        [],
        2,
        0.7,
    )(*parts)

    def stacked(x):
        pieces = everyone(x, "z", dims.nz)
        return call(
            bind(stack_kernel, 2),
            shape(dims.nz, *x.shape),
            [SMEM] + [VMEM] * dims.nz,
            [],
            2,
            0.7,
        )(meta, *pieces)

    planes = stacked(rows)
    received = exchange(send) if dims.fast else to_tokens(send)
    sums, planes = lax.optimization_barrier((sums, planes))
    planes = planes.reshape(dims.nz * rows.shape[0], rows.shape[1])
    planes = everyone(planes, "batch", dims.ni)
    planes_too = [swap(x, "core", 1) for x in planes]

    small = call(
        bind(modes_kernel, dims),
        shape(dims.small_rows, LANES),
        [VMEM] + [HBM] * 4 + [VMEM] * 4,
        [
            vmem(*tab, dtype=bf16),
            vmem(*tw),
            vmem(*four),
            vmem(4, q, 2 * LANES),
            vmem(*four, dtype=bf16),
            vmem(*four, dtype=bf16),
            vmem(4, q, 2 * LANES),
            DMA((4,)),
        ],
        12,
        6,
    )(params, tables, twiddle, seen, grads, sums, zr, zi, vec)
    smalls = everyone(stacked(small), "batch", dims.ni)
    smalls_too = [swap(x, "core", 1) for x in smalls]

    if dims.fast:
        outs = call(
            bind(finish_kernel, dims),
            (shape(*inputs.shape), shape(dims.width, 2 * dims.width))
            + (shape(modes, dims.width),) * 6
            + (shape(1, dims.width),) * 4,
            [SMEM] + [VMEM] * 2 + [ANY] * (2 * dims.ni) + [VMEM] * (2 * dims.ni),
            [vmem(*by_tile), DMA((2, dims.ni))],
            4,
            4,
            (VMEM, HBM) + (VMEM,) * 10,
        )(meta, received, out_cotangent, *planes, *planes_too, *smalls, *smalls_too)
        grad_in, weight_grad = outs[:2]
        mode_grads = outs[2:8]
        chan_grads = [x.reshape(-1) for x in outs[8:]]
    else:
        grad_in = out_cotangent.astype(f32) + received.reshape(inputs.shape)

        def in_order(mine, other):
            both = jnp.where(core == 0, jnp.stack([mine, other]), jnp.stack([other, mine]))
            return jnp.take(both, meta[0] ^ jnp.arange(dims.ni), axis=1)

        units = in_order(jnp.stack(planes), jnp.stack(planes_too))
        units = units.reshape(dims.width // 8, -1, 8, LANES)
        weight_grad = units.transpose(0, 2, 1, 3).reshape(dims.width, -1)
        rows = in_order(jnp.stack(smalls), jnp.stack(smalls_too)).transpose(1, 2, 0, 3, 4)
        rows = rows.reshape(nd, dims.small_rows, dims.groups, hc)
        table = rows[:, : 6 * m].reshape(nd, 6, m, dims.groups, hc).transpose(1, 3, 2, 0, 4)
        mode_grads = list(table.reshape(6, m * dims.groups, dims.width)[:, :modes])
        rest = rows[:, 6 * m : 6 * m + 4, 0].transpose(1, 0, 2).reshape(4, dims.width)
        chan_grads = list(rest)
    step_grad, gain_grad, shift_grad, skip_grad = chan_grads
    return (
        result,
        grad_in,
        gain_grad,
        shift_grad,
        step_grad,
        *mode_grads,
        skip_grad,
        weight_grad,
        bias_grad.reshape(-1),
    )


def solution(mesh):
    batch = mesh.shape["batch"]
    fine = Mesh(mesh.devices.reshape(-1, 2, batch), ("z", "core", "batch"))
    tokens = P("batch", ("z", "core"), None)
    return jax.shard_map(
        functools.partial(local, dict(fine.shape)),
        mesh=fine,
        in_specs=(tokens, P("batch")) + (P(),) * 12 + (tokens,),
        out_specs=(tokens, tokens) + (P(),) * 12,
        check_vma=False,
    )
```

```python
import functools
import math

import jax
import jax.numpy as jnp
from jax import lax
from jax.experimental import pallas as pl
from jax.experimental.pallas import tpu as pltpu
from jax.sharding import Mesh
from jax.sharding import PartitionSpec as P


EPS = 1e-05
LANES = 128
ALL = ("batch", "z", "core")
SMEM = pl.BlockSpec(memory_space=pltpu.SMEM)
VMEM = pl.BlockSpec(memory_space=pltpu.VMEM)
HBM = pl.BlockSpec(memory_space=pltpu.HBM)
ANY = pl.BlockSpec(memory_space=pl.ANY)
DMA = pltpu.SemaphoreType.DMA
ROWS = 64
STEP = 16
PER = ROWS // STEP
copy = pltpu.make_async_copy
f32 = jnp.float32
bf16 = jnp.bfloat16


def mm(a, b):
    return jnp.dot(a, b, preferred_element_type=f32)


def halves(x):
    hi = x.astype(bf16)
    return hi, (x - hi.astype(f32)).astype(bf16)


def lane_ids(shape):
    return lax.broadcasted_iota(jnp.int32, shape, len(shape) - 1)


def swap_blocks(tiles, width):
    tiles = list(tiles)
    block = lane_ids(tiles[0].shape) // width
    step = 1
    while step < len(tiles):
        low = (block & step) == 0
        for a in range(len(tiles)):
            if a & step == 0:
                first, second = tiles[a], tiles[a + step]
                tiles[a] = jnp.where(low, first, pltpu.roll(second, step * width, second.ndim - 1))
                tiles[a + step] = jnp.where(
                    low, pltpu.roll(first, LANES - step * width, first.ndim - 1), second
                )
        step *= 2
    return tiles


def fold_matrix(dims):
    rows = lax.broadcasted_iota(jnp.int32, (LANES, LANES), 0) % dims.chans
    cols = lax.broadcasted_iota(jnp.int32, (LANES, LANES), 1) % dims.chans
    return (rows == cols).astype(f32).astype(bf16)


def fold(row, dims):
    shift = dims.chans
    while shift < LANES:
        row = row + pltpu.roll(row, shift, 1)
        shift *= 2
    return row


class Dims:
    def __init__(self, inputs_shape, modes, mesh_shape):
        self.seqs, self.places, self.width = inputs_shape
        self.ni = mesh_shape["batch"]
        self.nz = mesh_shape["z"]
        self.nj = mesh_shape["z"] * mesh_shape["core"]
        self.devices = self.ni * self.nj
        self.length = self.places * self.nj
        self.quarter = self.length // 4
        self.chans = self.width // self.devices
        self.groups = LANES // self.chans
        self.all_seqs = self.seqs * self.ni
        self.modes = modes
        self.mode_rows = -(-modes // self.groups)
        self.small_rows = -(-(6 * self.mode_rows + 4) // 8) * 8
        self.piece_width = self.seqs * self.chans
        self.place_groups = LANES // self.piece_width
        self.piece_rows = self.places // self.place_groups
        self.units = self.width * 2 * self.width // (8 * LANES) // self.devices
        self.fast = (
            self.piece_width * self.ni == LANES
            and self.piece_rows % 8 == 0
            and self.nj == self.groups
            and self.small_rows == 32
            and self.place_groups == 4
        )


def each(count, body, unroll=True):
    lax.fori_loop(0, count, lambda k, _: body(k), None, unroll=unroll)


def class_rows(b, g, dims):
    return pl.ds(b * dims.places + g, dims.piece_rows, stride=4)


def pack_tokens(read, write, dims, done=None):
    def some(tile):
        parts = []
        for g in range(4):
            for b in range(dims.seqs):
                parts.append(read(tile, class_rows(b, g, dims)))
        parts = swap_blocks(parts, dims.chans)
        for e in range(dims.groups):
            write(tile * dims.groups + e, parts[e])
        if done is not None:
            done(tile)

    each(dims.width // LANES, some)


def unpack_tokens(ref, out, dims, unroll=True):
    def some(tile):
        parts = [ref[tile * dims.groups + e] for e in range(dims.groups)]
        parts = swap_blocks(parts, dims.chans)
        for g in range(4):
            for b in range(dims.seqs):
                out[tile, class_rows(b, g, dims), :] = parts[g * dims.seqs + b]

    each(dims.width // LANES, some, unroll)


def pack_kernel(dims, x_ref, out_ref, wide):
    for b in range(dims.seqs):
        for t in range(dims.width // LANES):
            wide[t, b * dims.places : (b + 1) * dims.places, :] = x_ref[b, :, lanes(t)].astype(f32)

    def write(piece, value):
        out_ref[piece] = value

    pack_tokens(lambda tile, rows: wide[tile, rows, :], write, dims)


def unpack_channels(ref, out, dims):
    rows = dims.piece_rows
    if not dims.fast:
        for r in range(4):
            out[r] = ref[r * dims.quarter : (r + 1) * dims.quarter, :]
        return

    def some(j):
        parts = [ref[i * dims.nj + j] for i in range(dims.ni)]
        parts = swap_blocks(parts, dims.piece_width)
        for g in range(4):
            out[g, pl.ds(pl.multiple_of(j * rows, rows), rows), :] = parts[g]

    each(dims.nj, some)


def pack_channels(read, send, send_hbm, sem, dims):
    rows = dims.piece_rows
    if not dims.fast:
        for r in range(4):
            for at in range(0, dims.quarter, ROWS):
                start = r * dims.quarter + at
                send[start : start + ROWS, :] = read(r, at, ROWS)
        whole = copy(send, send_hbm, sem.at[0])
        whole.start()
        whole.wait()
        return

    def pieces(j):
        return copy(send.at[:, j], send_hbm.at[:, j], sem.at[j])

    for j in range(dims.nj):
        parts = swap_blocks([read(g, j * rows, rows) for g in range(4)], dims.piece_width)
        for i in range(dims.ni):
            send[i, j] = parts[i]
        pieces(j).start()
    for j in range(dims.nj):
        pieces(j).wait()


def mode_constants(par_ref, dims):
    m = dims.mode_rows
    decay, rotation, dr, di, rr, ri = [par_ref[p * m : (p + 1) * m, :] for p in range(6)]
    step = jnp.exp(par_ref[6 * m : 6 * m + 1, :])
    log_mag = -step * decay
    turn = step * rotation
    c1r = step * (rr * dr - ri * di)
    c1i = step * (rr * di + ri * dr)
    c2r = c1r * dr - c1i * di
    c2i = c1r * di + c1i * dr
    return step, log_mag, turn, (c1r, c1i, c2r, c2i), (decay, rotation, dr, di, rr, ri)


def tables_kernel(
    dims, par_ref, tab_hbm, inv_hbm, tw_hbm, spec_hbm, zr_ref, zi_ref, vec_ref, *scratch
):
    tab, inv, tw, spec, cat, wave, sem_out, sem_spec = scratch
    n, m, q = dims.length, dims.mode_rows, dims.quarter

    def angles(b, _):
        at = pl.multiple_of(b * ROWS, ROWS)
        row = 2 * (lax.broadcasted_iota(jnp.int32, (ROWS, q), 0) + at) + 1
        col = 2 * lax.broadcasted_iota(jnp.int32, (ROWS, q), 1) + 1
        turn = ((row * col) & (8 * q - 1)).astype(f32) * (math.pi / (4 * q))
        for first, value in ((0, jnp.cos(turn)), (q, jnp.sin(turn))):
            for part, half in enumerate(halves(value)):
                tab[part, pl.ds(pl.multiple_of(first + at, ROWS), ROWS), :] = half
                inv[part, pl.ds(at, ROWS), first : first + q] = half
        row = 2 * (lax.broadcasted_iota(jnp.int32, (ROWS, LANES), 0) + at) + 1
        turn = row.astype(f32) * (math.pi / (2 * n))
        cos, sin = jnp.cos(turn), jnp.sin(turn)
        for p, value in enumerate((cos, sin, 1.0 - 2.0 * sin * sin, 2.0 * cos * sin)):
            tw[p, pl.ds(at, ROWS), :] = value
        return 0

    lax.fori_loop(0, q // ROWS, angles, 0)
    outs = [copy(tab, tab_hbm, sem_out.at[0]), copy(tw, tw_hbm, sem_out.at[1])]
    outs.append(copy(inv, inv_hbm, sem_out.at[2]))
    for out in outs:
        out.start()

    step, log_mag, turn, coefs, _ = mode_constants(par_ref, dims)
    c1r, c1i, c2r, c2i = coefs
    mag = jnp.exp(log_mag)
    l1r, l1i = mag * jnp.cos(turn), mag * jnp.sin(turn)
    mag = jnp.exp(8.0 * log_mag)
    l32r, l32i = mag * jnp.cos(8.0 * turn), mag * jnp.sin(8.0 * turn)
    for _ in range(2):
        l32r, l32i = l32r * l32r - l32i * l32i, 2.0 * l32r * l32i
    for p, value in enumerate((l32r, l32i, c1r, c1i, c2r, c2i)):
        vec_ref[p * m : (p + 1) * m, :] = value
    sub = 4.0 * lax.broadcasted_iota(jnp.int32, (8, LANES), 0).astype(f32)

    def wide(x, k):
        return jnp.broadcast_to(x[k : k + 1], (8, LANES))

    for k in range(m):
        mag = jnp.exp(sub * log_mag[k : k + 1])
        zr, zi = mag * jnp.cos(sub * turn[k : k + 1]), mag * jnp.sin(sub * turn[k : k + 1])
        for r in range(4):
            zr_ref[r, 8 * k : 8 * k + 8, :] = zr
            zi_ref[r, 8 * k : 8 * k + 8, :] = zi
            ar, ai = wide(l1r, k), wide(l1i, k)
            zr, zi = zr * ar - zi * ai, zr * ai + zi * ar
    consts = [
        tuple(wide(x, k) for x in (l32r, l32i, 2 * c1r, 2 * c1i, 2 * c2r, 2 * c2i)) for k in range(m)
    ]
    group = fold_matrix(dims)
    for r in range(4):

        def time_step(t, zs):
            at = pl.multiple_of(t * 8, 8)
            k1 = jnp.zeros((8, LANES), f32)
            k2 = jnp.zeros((8, LANES), f32)
            out = []
            for k in range(m):
                zr, zi = zs[2 * k], zs[2 * k + 1]
                ar, ai, b1r, b1i, b2r, b2i = consts[k]
                k1 = k1 + (b1r * zr - b1i * zi)
                k2 = k2 + (b2r * zr - b2i * zi)
                out += [zr * ar - zi * ai, zr * ai + zi * ar]
            wave[pl.ds(at, 8), lanes(0)] = k1
            wave[pl.ds(at, 8), lanes(1)] = k2
            return tuple(out)

        start = []
        for k in range(m):
            start += [zr_ref[r, 8 * k : 8 * k + 8, :], zi_ref[r, 8 * k : 8 * k + 8, :]]
        lax.fori_loop(0, q // 8, time_step, tuple(start), unroll=4)
        for p in range(2):
            both = halves(over_groups(wave[0:q, lanes(p)], group))
            for part in range(2):
                cat[part, :, lanes(2 * r + p)] = both[part]

    forth(tab, cat, wave)

    def spectrum(b, _):
        at = pl.multiple_of(b * STEP, STEP)
        chunk, rows = place_of(b)
        for p in range(2):
            for k, (re, im) in enumerate(butterfly(wave, tw, at, p, 2, dims)):
                spec[chunk, k, rows, lanes(2 * p)] = re * (1.0 / n)
                spec[chunk, k, rows, lanes(2 * p + 1)] = im * (1.0 / n)
        return 0

    lax.fori_loop(0, q // STEP, spectrum, 0)
    outs.append(copy(spec, spec_hbm, sem_spec))
    outs[-1].start()
    for out in outs:
        out.wait()


def lanes(p):
    return slice(p * LANES, (p + 1) * LANES)


def over_groups(x, group):
    return mm(jnp.concatenate(halves(x), axis=1), jnp.concatenate([group, group], axis=0))


def place_of(b):
    return b // PER, pl.ds(pl.multiple_of(b % PER * STEP, STEP), STEP)


def product(table, operand):
    (high, low), (first, second) = table, operand
    return mm(
        jnp.concatenate([high, high, low], axis=1), jnp.concatenate([first, second, first], axis=0)
    )


def forth(tab, cat, wave):
    wave[...] = product((tab[0], tab[1]), (cat[0], cat[1]))


def twiddles(tw, at):
    c1, s1, c2, s2 = [tw[p, pl.ds(at, STEP), :] for p in range(4)]
    return (c2, s2), (c1, s1), None, (c1, -s1)


def times(a, b):
    if b is None:
        return a
    return a[0] * b[0] - a[1] * b[1], a[0] * b[1] + a[1] * b[0]


def plus(a, b):
    return a[0] + b[0], a[1] + b[1]


def minus(a, b):
    return a[0] - b[0], a[1] - b[1]


def turned(a):
    return -a[1], a[0]


def butterfly(wave, tw, at, p, count, dims):
    below = pl.multiple_of(dims.quarter + at, STEP)
    parts = []
    for r, twiddle in enumerate(twiddles(tw, at)):
        re = wave[pl.ds(at, STEP), lanes(r * count + p)]
        im = wave[pl.ds(below, STEP), lanes(r * count + p)]
        parts.append(times((re, -im), twiddle))
    even, odd = plus(parts[0], parts[2]), plus(parts[1], parts[3])
    even_too, odd_too = minus(parts[0], parts[2]), turned(minus(parts[1], parts[3]))
    return plus(even, odd), minus(even_too, odd_too), minus(even, odd), plus(even_too, odd_too)


def unbutterfly(parts, tw, at, cat, p, count, dims):
    even, odd = plus(parts[0], parts[2]), plus(parts[1], parts[3])
    even_too, odd_too = minus(parts[0], parts[2]), turned(minus(parts[1], parts[3]))
    sums = plus(even, odd), plus(even_too, odd_too), minus(even, odd), minus(even_too, odd_too)
    for r, twiddle in enumerate(twiddles(tw, at)):
        if twiddle is not None:
            twiddle = twiddle[0], -twiddle[1]
        re, im = times(sums[r], twiddle)
        for first, value in ((0, re), (dims.quarter, -im)):
            rows = pl.ds(pl.multiple_of(first + at, STEP), STEP)
            for part, half in enumerate(halves(value)):
                cat[part, rows, lanes(r * count + p)] = half


def back(inv, cat):
    return product((inv[0], inv[1]), (cat[0], cat[1]))


def column_sums(x):
    return jnp.sum(x.reshape(x.shape[0] // 8, 8, LANES), axis=0)


def lane_lengths(meta_ref, lens_refs, dims):
    lane = lane_ids((1, LANES)) // dims.chans
    row = jnp.zeros((1, LANES), jnp.int32)
    total = jnp.int32(0)
    for s in range(dims.all_seqs):
        source = s // dims.seqs
        value = lens_refs[source][s % dims.seqs]
        total = total + value
        row = jnp.where(lane == s ^ (meta_ref[0] * dims.seqs), value, row)
    return row, total.astype(f32)


def valid_rows(r, at, rows, lens):
    places = 4 * (lax.broadcasted_iota(jnp.int32, (rows, LANES), 0) + at) + r
    return (places < lens).astype(f32)


def forward_kernel(dims, meta_ref, r_ref, par_ref, tab_hbm, inv_hbm, tw_hbm, spec_hbm, *rest):
    lens_refs, rest = rest[: dims.ni], rest[dims.ni :]
    (send_hbm, mixed_hbm, normed_hbm, seen_hbm, stat_ref), rest = rest[:5], rest[5:]
    tab, inv, tw, spec, seen, x_sc, mix_sc, normed_sc, cat, wave, back_cat, send = rest[:12]
    sem_tab, sem_spec, sem_seen, sem_out, sem_send = rest[12:]
    m, q = dims.mode_rows, dims.quarter
    chunks = q // ROWS
    ins = [copy(tab_hbm, tab, sem_tab.at[0]), copy(tw_hbm, tw, sem_tab.at[1])]
    ins += [copy(spec_hbm.at[c], spec.at[c], sem_spec.at[c]) for c in range(chunks)]
    ins.append(copy(inv_hbm, inv, sem_tab.at[2]))
    for one in ins:
        one.start()
    lens, total = lane_lengths(meta_ref, lens_refs, dims)
    unpack_channels(r_ref, x_sc, dims)
    classes = range(4)

    def add_up(b, acc):
        at = pl.multiple_of(b * ROWS, ROWS)
        for r in classes:
            acc = acc + column_sums(x_sc[r, pl.ds(at, ROWS), :] * valid_rows(r, at, ROWS, lens))
        return acc

    zero = jnp.zeros((8, LANES), f32)
    acc = lax.fori_loop(0, q // ROWS, add_up, zero)
    average = fold(jnp.sum(acc, axis=0, keepdims=True), dims) / total

    def add_squares(b, acc):
        at = pl.multiple_of(b * ROWS, ROWS)
        for r in classes:
            x = (x_sc[r, pl.ds(at, ROWS), :] - average) * valid_rows(r, at, ROWS, lens)
            acc = acc + column_sums(x * x)
        return acc

    acc = lax.fori_loop(0, q // ROWS, add_squares, zero)
    variance = fold(jnp.sum(acc, axis=0, keepdims=True), dims) / total
    inv_scale = lax.rsqrt(variance + EPS)
    gain = par_ref[6 * m + 1 : 6 * m + 2, :]
    shift = par_ref[6 * m + 2 : 6 * m + 3, :]
    skip = par_ref[6 * m + 3 : 6 * m + 4, :]
    stat_ref[0:1, :] = inv_scale
    stat_ref[1:2, :] = jnp.broadcast_to(total, (1, LANES))
    stat_ref[2:3, :] = lens.astype(f32)
    stat_ref[3:8, :] = jnp.zeros((5, LANES), f32)
    first_row = lax.broadcasted_iota(jnp.int32, (ROWS, LANES), 0) == 0

    def normalize(b, last):
        at = pl.multiple_of(b * ROWS, ROWS)
        mixed = []
        for r in classes:
            normed = (x_sc[r, pl.ds(at, ROWS), :] - average) * inv_scale
            mixed.append((gain * normed + shift) * valid_rows(r, at, ROWS, lens))
            normed_sc[r, pl.ds(at, ROWS), :] = normed
            mix_sc[r, pl.ds(at, ROWS), :] = mixed[r]
        earlier = jnp.where(first_row, last, pltpu.roll(mixed[3], 1, 0))
        for r in classes:
            liquid = mixed[r] * (earlier if r == 0 else mixed[r - 1])
            for p, value in enumerate((mixed[r], liquid)):
                for part, half in enumerate(halves(value)):
                    cat[part, pl.ds(at, ROWS), lanes(2 * r + p)] = half
        return mixed[3][ROWS - 1 :, :]

    lax.fori_loop(0, q // ROWS, normalize, jnp.zeros((1, LANES), f32))
    outs = [copy(mix_sc, mixed_hbm, sem_out.at[0]), copy(normed_sc, normed_hbm, sem_out.at[1])]
    for out in outs:
        out.start()
    ins[0].wait()
    forth(tab, cat, wave)
    ins[1].wait()
    for c in range(chunks):
        ins[2 + c].wait()

        def multiply(b, _):
            at = pl.multiple_of(b * STEP, STEP)
            chunk, rows = place_of(b)
            mixed = butterfly(wave, tw, at, 0, 2, dims)
            liquid = butterfly(wave, tw, at, 1, 2, dims)
            parts = []
            for k in range(4):
                for p, value in enumerate(mixed[k] + liquid[k]):
                    seen[chunk, k, rows, lanes(p)] = value
                kr, ki, lr, li = [spec[chunk, k, rows, lanes(p)] for p in range(4)]
                parts.append(plus(times(mixed[k], (kr, ki)), times(liquid[k], (lr, li))))
            unbutterfly(parts, tw, at, back_cat, 0, 1, dims)
            return 0

        lax.fori_loop(PER * c, PER * (c + 1), multiply, 0)
        outs.append(copy(seen.at[c], seen_hbm.at[c], sem_seen.at[c]))
        outs[-1].start()
    ins[-1].wait()

    value = back(inv, back_cat)
    for r in classes:
        x_sc[r] = value[:, lanes(r)] + skip * mix_sc[r]
    pack_channels(
        lambda r, at, size: x_sc[r, pl.ds(at, size), :], send, send_hbm, sem_send, dims
    )
    for out in outs:
        out.wait()


def gate_kernel(dims, meta_ref, r_ref, x_ref, w_ref, b_ref, ct_ref, *rest):
    (send_hbm, out_ref, act_hbm, gj_hbm, bias_ref, wsend_hbm), scratch = rest[:6], rest[6:]
    resp, act, joined, gj, gact, send, weight, wsend, sem_out, sem_send, sem_weight = scratch
    tokens = dims.seqs * dims.places
    width = dims.width
    places = dims.places

    tiles = range(width // LANES)
    if dims.fast:
        unpack_tokens(r_ref, resp, dims)
    else:
        for t in tiles:
            resp[t] = r_ref[:, lanes(t)]
    c0 = math.sqrt(2.0 / math.pi)
    c1 = 0.044715
    rows = 32

    def gelu(b, _):
        at = pl.multiple_of(b * rows, rows)
        for tile in tiles:
            r = resp[tile, pl.ds(at, rows), :]
            t = jnp.tanh(c0 * (r + c1 * r * r * r))
            act[pl.ds(at, rows), lanes(tile)] = (0.5 * r * (1.0 + t)).astype(bf16)
            slope = 0.5 * (1.0 + t) + 0.5 * r * (1.0 - t * t) * (c0 * (1.0 + 3.0 * c1 * r * r))
            resp[tile, pl.ds(at, rows), :] = slope
        return 0

    lax.fori_loop(0, tokens // rows, gelu, 0)
    outs = [copy(act, act_hbm, sem_out.at[0]), copy(gj, gj_hbm, sem_out.at[1])]
    outs[0].start()
    joined[...] = mm(act[...], w_ref[...])
    bias = b_ref[...]
    half = min(16, places)
    for b in range(dims.seqs):

        def gate(k, sums):
            at = pl.multiple_of(k * half, half)
            tok = pl.multiple_of(b * places + k * half, half)
            value = joined[pl.ds(tok, half), :width] + bias[:, :width]
            s = jax.nn.sigmoid(joined[pl.ds(tok, half), width:] + bias[:, width:])
            x = x_ref[b, pl.ds(at, half), :].astype(f32)
            g = ct_ref[b, pl.ds(at, half), :].astype(f32)
            out_ref[b, pl.ds(at, half), :] = (x + value * s).astype(bf16)
            gs = g * s
            first = gs.astype(bf16)
            second = (gs * value * (1.0 - s)).astype(bf16)
            gj[pl.ds(tok, half), :width] = first
            gj[pl.ds(tok, half), width:] = second
            first = jnp.sum(first.astype(f32).reshape(half // 8, 8, width), axis=0)
            second = jnp.sum(second.astype(f32).reshape(half // 8, 8, width), axis=0)
            return sums[0] + first, sums[1] + second

        if b == 0:
            zero = jnp.zeros((8, width), f32)
            sums = (zero, zero)
        sums = lax.fori_loop(0, places // half, gate, sums)
    outs[1].start()
    sums = [jnp.sum(s, axis=0, keepdims=True) for s in sums]
    for p, total in enumerate(sums):
        for t in tiles:
            row = p * (width // LANES) + t
            bias_ref[row : row + 1, :] = total[:, lanes(t)]
    weight_half(dims, meta_ref, 1 - meta_ref[1], act, gj, weight)
    for i in range(dims.ni):
        for z in range(dims.nz):
            for u in range(dims.units):
                wsend[i, z, u, :, :] = weight_unit(dims, meta_ref, weight, i, z, u)
            wsend[i, z, dims.units, :, :] = bias_ref[...]
        outs.append(copy(wsend.at[i], wsend_hbm.at[i], sem_weight.at[i]))
        outs[-1].start()
    grad = lax.dot_general(
        gj[...], w_ref[...], (((1,), (1,)), ((), ())), preferred_element_type=f32
    )
    for t in tiles:
        gact[t] = grad[:, lanes(t)]
    if dims.fast:

        def read(tile, rows):
            return gact[tile, rows, :] * resp[tile, rows, :]

        def put(piece, value):
            send[piece] = value

        def tile_copy(tile):
            some = pl.ds(tile * dims.groups, dims.groups)
            return copy(send.at[some], send_hbm.at[some], sem_send.at[tile])

        pack_tokens(read, put, dims, lambda tile: tile_copy(tile).start())
        outs += [tile_copy(tile) for tile in tiles]
    else:
        for t in tiles:
            send[:, lanes(t)] = gact[t] * resp[t]
        outs.append(copy(send, send_hbm, sem_send.at[0]))
        outs[-1].start()
    for out in outs:
        out.wait()


def weight_half(dims, meta_ref, core, act, gj, weight):
    half = dims.width // 2
    some = act[:, pl.ds(pl.multiple_of(core * half, half), half)]
    weight[...] = lax.dot_general(
        some, gj[...], (((0,), (0,)), ((), ())), preferred_element_type=f32
    )


def weight_unit(dims, meta_ref, weight, i, z, u):
    tiles = 2 * dims.width // LANES
    owner = (meta_ref[0] ^ i) * dims.nz + (meta_ref[2] ^ z)
    if dims.units % tiles == 0:
        row = owner * (dims.units // tiles) + u // tiles
        cols = lanes(u % tiles)
    else:
        unit = owner * dims.units + u
        row = unit // tiles
        cols = pl.ds(pl.multiple_of(unit % tiles * LANES, LANES), LANES)
    return weight[pl.ds(pl.multiple_of(row * 8, 8), 8), cols]


def backward_kernel(dims, r_ref, par_ref, *rest):
    ins_hbm, (stat_ref, send_hbm, grad_hbm, sums_ref) = rest[:6], rest[6:10]
    tab, inv, tw, spec, grads, mix_sc, normed_sc, g_sc, up_sc, cat, wave, back_cat = rest[10:22]
    lead_sc, liquid_sc, send, sem_in, sem_spec, sem_send, sem_grad = rest[22:]
    tab_hbm, inv_hbm, tw_hbm, spec_hbm, mixed_hbm, normed_hbm = ins_hbm
    m, q = dims.mode_rows, dims.quarter
    ins = [
        copy(mixed_hbm, mix_sc, sem_in.at[0]),
        copy(tab_hbm, tab, sem_in.at[1]),
        copy(tw_hbm, tw, sem_in.at[2]),
        copy(normed_hbm, normed_sc, sem_in.at[3]),
        copy(inv_hbm, inv, sem_in.at[4]),
    ]
    chunks = q // ROWS
    for c in range(chunks):
        ins.insert(3 + c, copy(spec_hbm.at[c], spec.at[c], sem_spec.at[c]))
    for one in ins:
        one.start()
    unpack_channels(r_ref, g_sc, dims)
    gain = par_ref[6 * m + 1 : 6 * m + 2, :]
    skip = par_ref[6 * m + 3 : 6 * m + 4, :]
    inv_scale = stat_ref[0:1, :]
    total = stat_ref[1:2, :]
    lens = stat_ref[2:3, :].astype(jnp.int32)
    zero = jnp.zeros((8, LANES), f32)
    classes = range(4)
    ins[0].wait()

    def gather(b, acc):
        at = pl.multiple_of(b * ROWS, ROWS)
        for r in classes:
            g = g_sc[r, pl.ds(at, ROWS), :]
            for part, half in enumerate(halves(g)):
                cat[part, pl.ds(at, ROWS), lanes(r)] = half
            acc = acc + column_sums(g * mix_sc[r, pl.ds(at, ROWS), :])
        return acc

    skip_acc = lax.fori_loop(0, q // ROWS, gather, zero)
    ins[1].wait()
    forth(tab, cat, wave)
    ins[2].wait()
    outs = []
    for c in range(chunks):
        ins[3 + c].wait()

        def multiply(b, _):
            at = pl.multiple_of(b * STEP, STEP)
            chunk, rows = place_of(b)
            grad = butterfly(wave, tw, at, 0, 1, dims)
            for k in range(4):
                for p in range(2):
                    grads[chunk, k, rows, lanes(p)] = grad[k][p]
            for p in range(2):
                products(grad, spec, tw, b, back_cat, p, dims)
            return 0

        lax.fori_loop(PER * c, PER * (c + 1), multiply, 0)
        outs.append(copy(grads.at[c], grad_hbm.at[c], sem_grad.at[c]))
        outs[-1].start()
    for one in ins[3 + chunks :]:
        one.wait()

    value = back(inv, back_cat)
    for r in classes:
        lead_sc[r] = value[:, lanes(2 * r)]
        liquid_sc[r] = value[:, lanes(2 * r + 1)]
        up_sc[r] = value[:, lanes(2 * r + 1)] * mix_sc[r]

    row = lax.broadcasted_iota(jnp.int32, (ROWS, LANES), 0)
    blank = jnp.zeros((1, LANES), f32)
    gain_acc, shift_acc = zero, zero
    for at in range(0, q, ROWS):
        rows = slice(at, at + ROWS)
        for r in classes:
            if r == 0:
                before = blank if at == 0 else mix_sc[3, at - 1 : at, :]
                earlier = jnp.where(row == 0, before, pltpu.roll(mix_sc[3, rows, :], 1, 0))
            else:
                earlier = mix_sc[r - 1, rows, :]
            if r == 3:
                after = blank if at + ROWS == q else up_sc[0, at + ROWS : at + ROWS + 1, :]
                up = jnp.where(row == ROWS - 1, after, pltpu.roll(up_sc[0, rows, :], ROWS - 1, 0))
            else:
                up = up_sc[r + 1, rows, :]
            masked = lead_sc[r, rows, :] + skip * g_sc[r, rows, :] + liquid_sc[r, rows, :] * earlier
            masked = (masked + up) * valid_rows(r, at, ROWS, lens)
            g_sc[r, rows, :] = masked
            gain_acc = gain_acc + column_sums(masked * normed_sc[r, rows, :])
            shift_acc = shift_acc + column_sums(masked)

    def whole(acc):
        return fold(jnp.sum(acc, axis=0, keepdims=True), dims)

    gain_sum, shift_sum, skip_sum = whole(gain_acc), whole(shift_acc), whole(skip_acc)
    scale = gain * inv_scale
    shift_mean = shift_sum / total
    gain_mean = gain_sum / total

    def read(r, at, size):
        normed = normed_sc[r, pl.ds(at, size), :]
        value = g_sc[r, pl.ds(at, size), :] - shift_mean - normed * gain_mean
        return value * scale * valid_rows(r, at, size, lens)

    sums_ref[...] = jnp.zeros_like(sums_ref)
    for p, value in enumerate((gain_sum, shift_sum, skip_sum)):
        sums_ref[p : p + 1, :] = value
    pack_channels(read, send, send_hbm, sem_send, dims)
    for out in outs:
        out.wait()


def products(grad, ref, tw, b, cat, p, dims):
    chunk, rows = place_of(b)
    parts = []
    for k in range(4):
        re = ref[chunk, k, rows, lanes(2 * p)]
        im = ref[chunk, k, rows, lanes(2 * p + 1)]
        parts.append(times(grad[k], (re, -im)))
    unbutterfly(parts, tw, pl.multiple_of(b * STEP, STEP), cat, p, 2, dims)


def modes_kernel(dims, par_ref, inv_hbm, tw_hbm, seen_hbm, grad_hbm, sums_ref, *rest):
    zr_ref, zi_ref, vec_ref, small_ref, inv, tw, seen, grads, back_cat, dk, sem, sem_in = rest
    n, m, q = dims.length, dims.mode_rows, dims.quarter
    chunks = q // ROWS
    ins = [copy(tw_hbm, tw, sem.at[0])]
    for c in range(chunks):
        ins.append(copy(seen_hbm.at[c], seen.at[c], sem_in.at[0, c]))
        ins.append(copy(grad_hbm.at[c], grads.at[c], sem_in.at[1, c]))
    ins.append(copy(inv_hbm, inv, sem.at[1]))
    for one in ins:
        one.start()
    zero = jnp.zeros((8, LANES), f32)
    classes = range(4)
    ins[0].wait()
    for c in range(chunks):
        ins[1 + 2 * c].wait()
        ins[2 + 2 * c].wait()

        def multiply(b, _):
            chunk, rows = place_of(b)
            grad = [tuple(grads[chunk, k, rows, lanes(p)] for p in range(2)) for k in range(4)]
            for p in range(2):
                products(grad, seen, tw, b, back_cat, p, dims)
            return 0

        lax.fori_loop(PER * c, PER * (c + 1), multiply, 0)
    ins[-1].wait()
    group = fold_matrix(dims)

    value = back(inv, back_cat) * (1.0 / n)
    dk[...] = over_groups(jnp.concatenate([value[:, lanes(p)] for p in range(8)], axis=0), group)

    step, log_mag, turn, _, params = mode_constants(par_ref, dims)
    decay, rotation, dr, di, rr, ri = params
    l32r, l32i, c1r, c1i, c2r, c2i = [vec_ref[p * m : (p + 1) * m, :] for p in range(6)]
    sub = 4.0 * lax.broadcasted_iota(jnp.int32, (8, LANES), 0).astype(f32)
    sums = [[] for _ in range(8)]
    for first in range(0, m, 2):
        some = range(first, min(m, first + 2))
        ratio = [
            (
                jnp.broadcast_to(l32r[k : k + 1], (8, LANES)),
                jnp.broadcast_to(l32i[k : k + 1], (8, LANES)),
            )
            for k in some
        ]
        sofar = [zero] * (8 * len(ratio))
        for r in classes:

            def mode_step(t, carry):
                at = pl.multiple_of(t * 8, 8)
                d1 = dk[pl.ds(pl.multiple_of(2 * r * q + at, 8), 8), :]
                d2 = dk[pl.ds(pl.multiple_of((2 * r + 1) * q + at, 8), 8), :]
                place = sub + (32 * t + r).astype(f32)
                e1 = d1 * place
                e2 = d2 * place
                out = []
                for k, (ar, ai) in enumerate(ratio):
                    zr, zi, *acc = carry[10 * k : 10 * (k + 1)]
                    out += [zr * ar - zi * ai, zr * ai + zi * ar]
                    for p, d in enumerate((d1, d2, e1, e2)):
                        out += [acc[2 * p] + d * zr, acc[2 * p + 1] + d * zi]
                return tuple(out)

            carry = []
            for at, k in enumerate(some):
                carry += [zr_ref[r, 8 * k : 8 * k + 8, :], zi_ref[r, 8 * k : 8 * k + 8, :]]
                carry += sofar[8 * at : 8 * at + 8]
            carry = lax.fori_loop(0, q // 8, mode_step, tuple(carry), unroll=4)
            sofar = [v for k in range(len(ratio)) for v in carry[10 * k + 2 : 10 * k + 10]]
        for k in range(len(ratio)):
            for p in range(8):
                sums[p].append(jnp.sum(sofar[8 * k + p], axis=0, keepdims=True))
    a1r, a1i, a2r, a2i, e1r, e1i, e2r, e2i = [
        jnp.concatenate(s, axis=0) if len(s) > 1 else s[0] for s in sums
    ]
    btr = c1r * e1r - c1i * e1i + c2r * e2r - c2i * e2i
    bti = c1r * e1i + c1i * e1r + c2r * e2i + c2i * e2r
    d2r = dr * dr - di * di
    d2i = 2.0 * dr * di
    erd = step * (a1r * dr - a1i * di + a2r * d2r - a2i * d2i)
    eri = step * (a1r * di + a1i * dr + a2r * d2i + a2i * d2r)
    tr = a1r + 2.0 * (a2r * dr - a2i * di)
    ti = a1i + 2.0 * (a2r * di + a2i * dr)
    edr = step * (rr * tr - ri * ti)
    edi = step * (rr * ti + ri * tr)
    by_step = 2.0 * (c1r * a1r - c1i * a1i + c2r * a2r - c2i * a2i) + 2.0 * step * (
        -decay * btr - rotation * bti
    )
    small_ref[...] = jnp.zeros_like(small_ref)
    answers = (-2.0 * step * btr, -2.0 * step * bti, 2.0 * edr, -2.0 * edi, 2.0 * erd, -2.0 * eri)
    for p, value in enumerate(answers):
        small_ref[p * m : (p + 1) * m, :] = value
    small_ref[6 * m : 6 * m + 1, :] = fold(jnp.sum(by_step, axis=0, keepdims=True), dims)
    small_ref[6 * m + 1 : 6 * m + 4, :] = sums_ref[0:3, :]


def first_add_kernel(dims, meta_ref, act_hbm, gj_hbm, bias_ref, other_hbm, *refs):
    out_refs, (act, gj, weight, other, sem_in, sem) = refs[: dims.ni], refs[dims.ni :]
    ins = [copy(act_hbm, act, sem_in.at[0]), copy(gj_hbm, gj, sem_in.at[1])]
    others = [copy(other_hbm.at[i], other.at[i], sem.at[i]) for i in range(dims.ni)]
    for one in ins + others:
        one.start()
    for one in ins:
        one.wait()
    weight_half(dims, meta_ref, meta_ref[1], act, gj, weight)
    for i in range(dims.ni):
        others[i].wait()
        for z in range(dims.nz):
            for u in range(dims.units):
                unit = weight_unit(dims, meta_ref, weight, i, z, u)
                out_refs[i][z, u] = unit + other[i, z, u]
            out_refs[i][z, dims.units] = bias_ref[...] + other[i, z, dims.units]


def add_kernel(count, *refs):
    for p, out_ref in enumerate(refs[count:]):
        total = refs[0][p]
        for ref in refs[1:count]:
            total = total + ref[p]
        out_ref[...] = total


def last_add_kernel(dims, count, small_ref, *refs):
    units_ref, bias_ref = refs[count:]

    def unit(u):
        total = refs[0][u]
        for ref in refs[1:count]:
            total = total + ref[u]
        return total

    for u in range(dims.units):
        units_ref[u] = unit(u)
    for t in range(dims.small_rows // 8):
        units_ref[dims.units + t] = small_ref[8 * t : 8 * t + 8, :]
    bias = unit(dims.units)
    for t in range(2 * dims.width // LANES):
        bias_ref[:, lanes(t)] = bias[t : t + 1, :]


def stack_kernel(meta_at, meta_ref, *refs):
    out_ref = refs[-1]
    for s, ref in enumerate(refs[:-1]):
        out_ref[meta_ref[meta_at] ^ s] = ref[...]


def input_kernel(dims, r_ref, ct_ref, grad_ref, grad):
    unpack_tokens(r_ref, grad, dims, False)
    for b in range(dims.seqs):
        for t in range(dims.width // LANES):
            value = grad[t, b * dims.places : (b + 1) * dims.places, :]
            grad_ref[b, :, lanes(t)] = value + ct_ref[b, :, lanes(t)].astype(f32)


def finish_kernel(dims, meta_ref, *refs):
    ni, nz, m = dims.ni, dims.nz, dims.mode_rows
    planes = refs[:ni], refs[ni : 2 * ni]
    weight_ref, *small_hbm = refs[2 * ni : 2 * ni + 11]
    *small_refs, rows, sem, sem_small = refs[2 * ni + 11 :]
    me, core = meta_ref[0], meta_ref[1]
    tiles = 2 * dims.width // LANES
    per = 8 * dims.units // tiles
    copies = []
    for half, side in ((0, core), (1, 1 - core)):
        for i in range(ni):
            for z in range(nz):
                for u in range(dims.units):
                    at = z * per + u // tiles * 8
                    rows[half, i, at : at + 8, lanes(u % tiles)] = planes[half][i][z, u]
            at = pl.multiple_of((side * ni + (me ^ i)) * nz * per, nz * per)
            target = weight_ref.at[pl.ds(at, nz * per), :]
            copies.append(copy(rows.at[half, i], target, sem.at[half, i]))
            copies[-1].start()
    first = core == 0
    for i in range(ni):
        parts = []
        for z in range(nz):
            a = planes[0][i][z, dims.units :].reshape(dims.small_rows, LANES)
            b = planes[1][i][z, dims.units :].reshape(dims.small_rows, LANES)
            parts += [jnp.where(first, a, b), jnp.where(first, b, a)]
        parts = swap_blocks(parts, dims.chans)
        cols = pl.ds(pl.multiple_of((me ^ i) * LANES, LANES), LANES)
        for q in range(dims.groups):
            for p in range(6):
                small_refs[p][q * m : q * m + m, cols] = parts[q][p * m : p * m + m, :]
        for p in range(4):
            small_refs[6 + p][:, cols] = parts[0][6 * m + p : 6 * m + p + 1, :]
    for p, (ref, hbm) in enumerate(zip(small_refs, small_hbm)):
        copies.append(copy(ref, hbm, sem_small.at[p]))
        copies[-1].start()
    for one in copies:
        one.wait()


def call(kernel, out_shape, in_specs, scratch, limit, us, out_specs=None):
    cost = pl.CostEstimate(flops=int(us * 1.1e9), bytes_accessed=int(us * 3e6), transcendentals=0)
    if out_specs is None:
        out_specs = jax.tree.map(lambda _: VMEM, out_shape)
    else:
        out_shape = tuple(
            pltpu.HBM(out.shape, out.dtype) if spec is HBM else out
            for out, spec in zip(out_shape, out_specs)
        )

    def run(*args):
        args = [
            pltpu.with_memory_space_constraint(x, pltpu.HBM) if spec is HBM else x
            for x, spec in zip(args, in_specs)
        ]
        return pl.pallas_call(
            kernel,
            out_shape=out_shape,
            in_specs=in_specs,
            out_specs=out_specs,
            scratch_shapes=scratch,
            compiler_params=pltpu.CompilerParams(vmem_limit_bytes=limit << 20),
            cost_estimate=cost,
        )(*args)

    return run


def shape(*dims, dtype=f32):
    return jax.ShapeDtypeStruct(dims, dtype)


def local(
    mesh_shape,
    inputs,
    lengths,
    norm_gain,
    norm_shift,
    log_step,
    decay_rate,
    rotation,
    drive_real,
    drive_imag,
    read_real,
    read_imag,
    skip_gain,
    glu_weight,
    glu_bias,
    out_cotangent,
):
    modes = decay_rate.shape[0]
    dims = Dims(inputs.shape, modes, mesh_shape)
    n, nd, m, hc = dims.length, dims.devices, dims.mode_rows, dims.chans
    core = lax.axis_index("core")
    owner = lax.axis_index(ALL)
    meta = jnp.stack([lax.axis_index("batch"), core, lax.axis_index("z")]).astype(jnp.int32)

    def exchange(x):
        return lax.all_to_all(x, ALL, 0, 0, tiled=True)

    some = dims.places // 4

    def to_channels(x):
        x = x.reshape(dims.seqs, some, 4, nd, hc).transpose(3, 2, 1, 0, 4)
        x = exchange(x.reshape(nd, dims.places, dims.piece_width))
        x = x.reshape(dims.ni, dims.nj, 4, some, dims.piece_width).transpose(2, 1, 3, 0, 4)
        x = x.reshape(n, dims.all_seqs * hc)
        return jnp.pad(x, ((0, 0), (0, LANES - x.shape[1])))

    def to_tokens(x):
        x = x[:, : dims.all_seqs * hc].reshape(4, dims.nj, some, dims.ni, dims.piece_width)
        x = x.transpose(3, 1, 0, 2, 4).reshape(nd, dims.places, dims.piece_width)
        x = exchange(x).reshape(nd, 4, some, dims.seqs, hc).transpose(3, 2, 1, 0, 4)
        return x.reshape(dims.seqs * dims.places, dims.width)

    table = jnp.stack([decay_rate, rotation, drive_real, drive_imag, read_real, read_imag])
    table = lax.dynamic_slice_in_dim(table, owner * hc, hc, 2)
    table = jnp.pad(table, ((0, 0), (0, m * dims.groups - modes), (0, 0)))
    table = table.reshape(6, dims.groups, m, hc).transpose(0, 2, 1, 3).reshape(6 * m, LANES)
    rest = jnp.stack([log_step, norm_gain, norm_shift, skip_gain])
    rest = lax.dynamic_slice_in_dim(rest, owner * hc, hc, 1)
    params = jnp.concatenate([table, jnp.tile(rest, (1, dims.groups))], axis=0)
    params, meta = lax.optimization_barrier((params, meta))

    pieces = (nd, dims.piece_rows, LANES) if dims.fast else (n, LANES)
    tokens = dims.seqs * dims.places
    token_pieces = (nd, dims.piece_rows, LANES) if dims.fast else (tokens, dims.width)
    bind = functools.partial
    q = dims.quarter
    tab = (2, 2 * q, q)
    inv = (2, q, 2 * q)
    chunks = q // ROWS
    tw = (4, q, LANES)
    four = (chunks, 4, ROWS, 4 * LANES)
    two = (chunks, 4, ROWS, 2 * LANES)
    sent = (dims.ni, dims.nj, dims.piece_rows, LANES) if dims.fast else (n, LANES)
    plain = (4, q, LANES)
    by_tile = (dims.width // LANES, dims.seqs * dims.places, LANES)

    def vmem(*sizes, dtype=f32):
        return pltpu.VMEM(sizes, dtype)

    if dims.fast:
        packed = call(
            bind(pack_kernel, dims), shape(*pieces), [VMEM], [vmem(*by_tile)], 4, 1.5
        )(inputs)
        received = exchange(packed)
    else:
        received = to_channels(inputs.astype(f32))

    tables, inverse, twiddle, spec, zr, zi, vec = call(
        bind(tables_kernel, dims),
        (
            shape(*tab, dtype=bf16),
            shape(*inv, dtype=bf16),
            shape(*tw),
            shape(*four),
            shape(4, 8 * m, LANES),
            shape(4, 8 * m, LANES),
            shape(6 * m, LANES),
        ),
        [VMEM],
        [
            vmem(*tab, dtype=bf16),
            vmem(*inv, dtype=bf16),
            vmem(*tw),
            vmem(*four),
            vmem(2, q, 8 * LANES, dtype=bf16),
            vmem(2 * q, 8 * LANES),
            DMA((3,)),
            DMA(()),
        ],
        12,
        6,
        (HBM, HBM, HBM, HBM, VMEM, VMEM, VMEM),
    )(params)

    def swap(x, axis, by):
        return lax.ppermute(x, axis, [(i, i ^ by) for i in range(lax.axis_size(axis))])

    def everyone(x, axis, size):
        return [x] + [swap(x, axis, s) for s in range(1, size)]

    lengths, vec = lax.optimization_barrier((lengths, vec))
    lens = everyone(lengths, "batch", dims.ni)
    send, mixed, normed, seen, stat = call(
        bind(forward_kernel, dims),
        (shape(*sent), shape(*plain), shape(*plain), shape(*four), shape(8, LANES)),
        [SMEM, VMEM, VMEM] + [HBM] * 4 + [SMEM] * dims.ni,
        [
            vmem(*tab, dtype=bf16),
            vmem(*inv, dtype=bf16),
            vmem(*tw),
            vmem(*four),
            vmem(*four),
            vmem(*plain),
            vmem(*plain),
            vmem(*plain),
            vmem(2, q, 8 * LANES, dtype=bf16),
            vmem(2 * q, 8 * LANES),
            vmem(2, 2 * q, 4 * LANES, dtype=bf16),
            vmem(*sent),
            DMA((3,)),
            DMA((chunks,)),
            DMA((chunks,)),
            DMA((2,)),
            DMA((dims.nj,)),
        ],
        18,
        7,
        (HBM, HBM, HBM, HBM, VMEM),
    )(meta, received, params, tables, inverse, twiddle, spec, *lens)
    send = send.reshape(pieces)

    received = exchange(send) if dims.fast else to_tokens(send)
    wide = (tokens, dims.width)
    wider = (tokens, 2 * dims.width)
    unit = (dims.units + 1, 8, LANES)
    part = (dims.ni, dims.nz) + unit
    tiles = 2 * dims.width // LANES
    send, result, act, gj, bias, wsend = call(
        bind(gate_kernel, dims),
        (
            shape(*token_pieces),
            shape(*inputs.shape, dtype=bf16),
            shape(*wide, dtype=bf16),
            shape(*wider, dtype=bf16),
            shape(tiles, LANES),
            shape(*part),
        ),
        [SMEM] + [VMEM] * 5,
        [
            vmem(*by_tile),
            vmem(*wide, dtype=bf16),
            vmem(*wider),
            vmem(*wider, dtype=bf16),
            vmem(*by_tile),
            vmem(*token_pieces),
            vmem(dims.width // 2, 2 * dims.width),
            vmem(*part),
            DMA((2,)),
            DMA((max(1, dims.width // LANES),)),
            DMA((dims.ni,)),
        ],
        11,
        5,
        (HBM, VMEM, HBM, HBM, VMEM, HBM),
    )(meta, received, inputs, glu_weight, glu_bias.reshape(1, -1), out_cotangent)
    received = exchange(send) if dims.fast else to_channels(
        send.reshape(dims.seqs, dims.places, dims.width)
    )

    parts = call(
        bind(first_add_kernel, dims),
        (shape(dims.nz, *unit),) * dims.ni,
        [SMEM, HBM, HBM, VMEM, ANY],
        [
            vmem(*wide, dtype=bf16),
            vmem(*wider, dtype=bf16),
            vmem(dims.width // 2, 2 * dims.width),
            vmem(*part),
            DMA((2,)),
            DMA((dims.ni,)),
        ],
        6,
        0.1,
    )(meta, act, gj, bias, swap(wsend, "core", 1))
    parts = [parts[0]] + [swap(parts[s], "batch", s) for s in range(1, dims.ni)]
    send, grads, sums = call(
        bind(backward_kernel, dims),
        (shape(*sent), shape(*two), shape(8, LANES)),
        [VMEM, VMEM] + [HBM] * 6 + [VMEM],
        [
            vmem(*tab, dtype=bf16),
            vmem(*inv, dtype=bf16),
            vmem(*tw),
            vmem(*four),
            vmem(*two),
            vmem(*plain),
            vmem(*plain),
            vmem(*plain),
            vmem(*plain),
            vmem(2, q, 4 * LANES, dtype=bf16),
            vmem(2 * q, 4 * LANES),
            vmem(2, 2 * q, 8 * LANES, dtype=bf16),
            vmem(*plain),
            vmem(*plain),
            vmem(*sent),
            DMA((5,)),
            DMA((chunks,)),
            DMA((dims.nj,)),
            DMA((chunks,)),
        ],
        18,
        9,
        (HBM, HBM, VMEM),
    )(received, params, tables, inverse, twiddle, spec, mixed, normed, stat)
    send = send.reshape(pieces)

    send, parts = lax.optimization_barrier((send, parts))
    parts = call(
        bind(add_kernel, dims.ni), (shape(*unit),) * dims.nz, [VMEM] * dims.ni, [], 2, 0.1
    )(*parts)
    sums, parts = lax.optimization_barrier((sums, parts))
    parts = [parts[0]] + [swap(parts[s], "z", s) for s in range(1, dims.nz)]
    small = call(
        bind(modes_kernel, dims),
        shape(dims.small_rows, LANES),
        [VMEM] + [HBM] * 4 + [VMEM] * 4,
        [
            vmem(*inv, dtype=bf16),
            vmem(*tw),
            vmem(*four),
            vmem(*two),
            vmem(2, 2 * q, 8 * LANES, dtype=bf16),
            vmem(8 * q, LANES),
            DMA((2,)),
            DMA((2, chunks)),
        ],
        12,
        6,
    )(params, inverse, twiddle, seen, grads, sums, zr, zi, vec)

    units = (dims.units + dims.small_rows // 8, 8, LANES)
    units, bias_grad = call(
        bind(last_add_kernel, dims, dims.nz),
        (shape(*units), shape(1, 2 * dims.width)),
        [VMEM] * (1 + dims.nz),
        [],
        2,
        0.7,
    )(small, *parts)
    planes = call(
        bind(stack_kernel, 2),
        shape(dims.nz, *units.shape),
        [SMEM] + [VMEM] * dims.nz,
        [],
        2,
        0.7,
    )(meta, *everyone(units, "z", dims.nz))
    send, planes = lax.optimization_barrier((send, planes))
    received = exchange(send) if dims.fast else to_tokens(send)
    planes = everyone(planes, "batch", dims.ni)
    if dims.fast:
        grad_in = call(
            bind(input_kernel, dims), shape(*inputs.shape), [VMEM] * 2, [vmem(*by_tile)], 4, 1.5
        )(received, out_cotangent)
    else:
        grad_in = out_cotangent.astype(f32) + received.reshape(inputs.shape)
    grad_in, planes = lax.optimization_barrier((grad_in, planes))
    planes_too = [swap(x, "core", 1) for x in planes]

    if dims.fast:
        outs = call(
            bind(finish_kernel, dims),
            (shape(dims.width, 2 * dims.width),)
            + (shape(modes, dims.width),) * 6
            + (shape(1, dims.width),) * 4,
            [SMEM] + [VMEM] * (2 * dims.ni),
            [vmem(modes, dims.width)] * 6
            + [vmem(1, dims.width)] * 4
            + [
                vmem(2, dims.ni, dims.width // 2 // dims.ni, 2 * dims.width),
                DMA((2, dims.ni)),
                DMA((10,)),
            ],
            5,
            3,
            (HBM,) * 11,
        )(meta, *planes, *planes_too)
        weight_grad = outs[0]
        mode_grads = outs[1:7]
        chan_grads = [x.reshape(-1) for x in outs[7:]]
    else:

        def in_order(mine, other):
            both = jnp.where(core == 0, jnp.stack([mine, other]), jnp.stack([other, mine]))
            return jnp.take(both, meta[0] ^ jnp.arange(dims.ni), axis=1)

        both = in_order(jnp.stack(planes), jnp.stack(planes_too))
        weight_grad = both[:, :, :, : dims.units].reshape(dims.width // 8, -1, 8, LANES)
        weight_grad = weight_grad.transpose(0, 2, 1, 3).reshape(dims.width, -1)
        rows = both[:, :, :, dims.units :].transpose(1, 2, 0, 3, 4, 5)
        rows = rows.reshape(nd, dims.small_rows, dims.groups, hc)
        table = rows[:, : 6 * m].reshape(nd, 6, m, dims.groups, hc).transpose(1, 3, 2, 0, 4)
        mode_grads = list(table.reshape(6, m * dims.groups, dims.width)[:, :modes])
        rest = rows[:, 6 * m : 6 * m + 4, 0].transpose(1, 0, 2).reshape(4, dims.width)
        chan_grads = list(rest)
    step_grad, gain_grad, shift_grad, skip_grad = chan_grads
    return (
        result,
        grad_in,
        gain_grad,
        shift_grad,
        step_grad,
        *mode_grads,
        skip_grad,
        weight_grad,
        bias_grad.reshape(-1),
    )


def solution(mesh):
    batch = mesh.shape["batch"]
    fine = Mesh(mesh.devices.reshape(-1, 2, batch), ("z", "core", "batch"))
    tokens = P("batch", ("z", "core"), None)
    return jax.shard_map(
        functools.partial(local, dict(fine.shape)),
        mesh=fine,
        in_specs=(tokens, P("batch")) + (P(),) * 12 + (tokens,),
        out_specs=(tokens, tokens) + (P(),) * 12,
        check_vma=False,
    )
```

```python
import functools
import math

import jax
import jax.numpy as jnp
from jax import lax
from jax.experimental import pallas as pl
from jax.experimental.pallas import tpu as pltpu
from jax.sharding import Mesh
from jax.sharding import PartitionSpec as P


EPS = 1e-05
LANES = 128
ALL = ("batch", "z", "core")
SMEM = pl.BlockSpec(memory_space=pltpu.SMEM)
VMEM = pl.BlockSpec(memory_space=pltpu.VMEM)
HBM = pl.BlockSpec(memory_space=pltpu.HBM)
ANY = pl.BlockSpec(memory_space=pl.ANY)
DMA = pltpu.SemaphoreType.DMA
ROWS = 64
STEP = 16
PER = ROWS // STEP
copy = pltpu.make_async_copy
f32 = jnp.float32
bf16 = jnp.bfloat16


def mm(a, b):
    return jnp.dot(a, b, preferred_element_type=f32)


def halves(x):
    hi = x.astype(bf16)
    return hi, (x - hi.astype(f32)).astype(bf16)


def lane_ids(shape):
    return lax.broadcasted_iota(jnp.int32, shape, len(shape) - 1)


def swap_blocks(tiles, width):
    tiles = list(tiles)
    block = lane_ids(tiles[0].shape) // width
    step = 1
    while step < len(tiles):
        low = (block & step) == 0
        for a in range(len(tiles)):
            if a & step == 0:
                first, second = tiles[a], tiles[a + step]
                tiles[a] = jnp.where(low, first, pltpu.roll(second, step * width, second.ndim - 1))
                tiles[a + step] = jnp.where(
                    low, pltpu.roll(first, LANES - step * width, first.ndim - 1), second
                )
        step *= 2
    return tiles


def fold_matrix(dims):
    rows = lax.broadcasted_iota(jnp.int32, (LANES, LANES), 0) % dims.chans
    cols = lax.broadcasted_iota(jnp.int32, (LANES, LANES), 1) % dims.chans
    return (rows == cols).astype(f32).astype(bf16)


def fold(row, dims):
    shift = dims.chans
    while shift < LANES:
        row = row + pltpu.roll(row, shift, 1)
        shift *= 2
    return row


class Dims:
    def __init__(self, inputs_shape, modes, mesh_shape):
        self.seqs, self.places, self.width = inputs_shape
        self.ni = mesh_shape["batch"]
        self.nz = mesh_shape["z"]
        self.nj = mesh_shape["z"] * mesh_shape["core"]
        self.devices = self.ni * self.nj
        self.length = self.places * self.nj
        self.quarter = self.length // 4
        self.chans = self.width // self.devices
        self.groups = LANES // self.chans
        self.all_seqs = self.seqs * self.ni
        self.modes = modes
        self.mode_rows = -(-modes // self.groups)
        self.small_rows = -(-(6 * self.mode_rows + 4) // 8) * 8
        self.piece_width = self.seqs * self.chans
        self.place_groups = LANES // self.piece_width
        self.piece_rows = self.places // self.place_groups
        self.units = self.width * 2 * self.width // (8 * LANES) // self.devices
        self.fast = (
            self.piece_width * self.ni == LANES
            and self.piece_rows % 8 == 0
            and self.nj == self.groups
            and self.small_rows == 32
            and self.place_groups == 4
        )


def each(count, body, unroll=True):
    lax.fori_loop(0, count, lambda k, _: body(k), None, unroll=unroll)


def class_rows(b, g, dims):
    return pl.ds(b * dims.places + g, dims.piece_rows, stride=4)


def pack_tokens(read, write, dims, done=None):
    def some(tile):
        parts = []
        for g in range(4):
            for b in range(dims.seqs):
                parts.append(read(tile, class_rows(b, g, dims)))
        parts = swap_blocks(parts, dims.chans)
        for e in range(dims.groups):
            write(tile * dims.groups + e, parts[e])
        if done is not None:
            done(tile)

    each(dims.width // LANES, some)


def unpack_tokens(ref, out, dims, unroll=True):
    def some(tile):
        parts = [ref[tile * dims.groups + e] for e in range(dims.groups)]
        parts = swap_blocks(parts, dims.chans)
        for g in range(4):
            for b in range(dims.seqs):
                out[tile, class_rows(b, g, dims), :] = parts[g * dims.seqs + b]

    each(dims.width // LANES, some, unroll)


def pack_kernel(dims, x_ref, out_ref, wide):
    for b in range(dims.seqs):
        for t in range(dims.width // LANES):
            wide[t, b * dims.places : (b + 1) * dims.places, :] = x_ref[b, :, lanes(t)].astype(f32)

    def write(piece, value):
        out_ref[piece] = value

    pack_tokens(lambda tile, rows: wide[tile, rows, :], write, dims)


def unpack_channels(ref, out, dims):
    rows = dims.piece_rows
    if not dims.fast:
        for r in range(4):
            out[r] = ref[r * dims.quarter : (r + 1) * dims.quarter, :]
        return

    def some(j):
        parts = [ref[i * dims.nj + j] for i in range(dims.ni)]
        parts = swap_blocks(parts, dims.piece_width)
        for g in range(4):
            out[g, pl.ds(pl.multiple_of(j * rows, rows), rows), :] = parts[g]

    each(dims.nj, some)


def pack_channels(read, send, send_hbm, sem, dims):
    rows = dims.piece_rows
    if not dims.fast:
        for r in range(4):
            for at in range(0, dims.quarter, ROWS):
                start = r * dims.quarter + at
                send[start : start + ROWS, :] = read(r, at, ROWS)
        whole = copy(send, send_hbm, sem.at[0])
        whole.start()
        whole.wait()
        return

    def pieces(j):
        return copy(send.at[:, j], send_hbm.at[:, j], sem.at[j])

    for j in range(dims.nj):
        parts = swap_blocks([read(g, j * rows, rows) for g in range(4)], dims.piece_width)
        for i in range(dims.ni):
            send[i, j] = parts[i]
        pieces(j).start()
    for j in range(dims.nj):
        pieces(j).wait()


def mode_constants(par_ref, dims):
    m = dims.mode_rows
    decay, rotation, dr, di, rr, ri = [par_ref[p * m : (p + 1) * m, :] for p in range(6)]
    step = jnp.exp(par_ref[6 * m : 6 * m + 1, :])
    log_mag = -step * decay
    turn = step * rotation
    c1r = step * (rr * dr - ri * di)
    c1i = step * (rr * di + ri * dr)
    c2r = c1r * dr - c1i * di
    c2i = c1r * di + c1i * dr
    return step, log_mag, turn, (c1r, c1i, c2r, c2i), (decay, rotation, dr, di, rr, ri)


def waves_kernel(dims, par_ref, zr_ref, zi_ref, vec_ref, cat_ref, wave):
    m, q = dims.mode_rows, dims.quarter
    step, log_mag, turn, coefs, _ = mode_constants(par_ref, dims)
    c1r, c1i, c2r, c2i = coefs
    mag = jnp.exp(log_mag)
    l1r, l1i = mag * jnp.cos(turn), mag * jnp.sin(turn)
    mag = jnp.exp(8.0 * log_mag)
    l32r, l32i = mag * jnp.cos(8.0 * turn), mag * jnp.sin(8.0 * turn)
    for _ in range(2):
        l32r, l32i = l32r * l32r - l32i * l32i, 2.0 * l32r * l32i
    for p, value in enumerate((l32r, l32i, c1r, c1i, c2r, c2i)):
        vec_ref[p * m : (p + 1) * m, :] = value
    sub = 4.0 * lax.broadcasted_iota(jnp.int32, (8, LANES), 0).astype(f32)

    def wide(x, k):
        return jnp.broadcast_to(x[k : k + 1], (8, LANES))

    for k in range(m):
        mag = jnp.exp(sub * log_mag[k : k + 1])
        zr, zi = mag * jnp.cos(sub * turn[k : k + 1]), mag * jnp.sin(sub * turn[k : k + 1])
        for r in range(4):
            zr_ref[r, 8 * k : 8 * k + 8, :] = zr
            zi_ref[r, 8 * k : 8 * k + 8, :] = zi
            ar, ai = wide(l1r, k), wide(l1i, k)
            zr, zi = zr * ar - zi * ai, zr * ai + zi * ar
    consts = [
        tuple(wide(x, k) for x in (l32r, l32i, 2 * c1r, 2 * c1i, 2 * c2r, 2 * c2i)) for k in range(m)
    ]
    group = fold_matrix(dims)
    for r in range(4):

        def time_step(t, zs):
            at = pl.multiple_of(t * 8, 8)
            k1 = jnp.zeros((8, LANES), f32)
            k2 = jnp.zeros((8, LANES), f32)
            out = []
            for k in range(m):
                zr, zi = zs[2 * k], zs[2 * k + 1]
                ar, ai, b1r, b1i, b2r, b2i = consts[k]
                k1 = k1 + (b1r * zr - b1i * zi)
                k2 = k2 + (b2r * zr - b2i * zi)
                out += [zr * ar - zi * ai, zr * ai + zi * ar]
            wave[pl.ds(at, 8), lanes(0)] = k1
            wave[pl.ds(at, 8), lanes(1)] = k2
            return tuple(out)

        start = []
        for k in range(m):
            start += [zr_ref[r, 8 * k : 8 * k + 8, :], zi_ref[r, 8 * k : 8 * k + 8, :]]
        lax.fori_loop(0, q // 8, time_step, tuple(start), unroll=4)
        for p in range(2):
            both = halves(over_groups(wave[0:q, lanes(p)], group))
            for part in range(2):
                cat_ref[part, :, lanes(2 * r + p)] = both[part]


def tables_kernel(dims, cat_ref, tab_hbm, inv_hbm, tw_hbm, spec_hbm, *scratch):
    tab, inv, tw, spec, wave, sem_out, sem_spec = scratch
    n, q = dims.length, dims.quarter

    def angles(b, _):
        at = pl.multiple_of(b * ROWS, ROWS)
        row = 2 * (lax.broadcasted_iota(jnp.int32, (ROWS, q), 0) + at) + 1
        col = 2 * lax.broadcasted_iota(jnp.int32, (ROWS, q), 1) + 1
        turn = ((row * col) & (8 * q - 1)).astype(f32) * (math.pi / (4 * q))
        for first, value in ((0, jnp.cos(turn)), (q, jnp.sin(turn))):
            for part, half in enumerate(halves(value)):
                tab[part, pl.ds(pl.multiple_of(first + at, ROWS), ROWS), :] = half
                inv[part, pl.ds(at, ROWS), first : first + q] = half
        row = 2 * (lax.broadcasted_iota(jnp.int32, (ROWS, LANES), 0) + at) + 1
        turn = row.astype(f32) * (math.pi / (2 * n))
        cos, sin = jnp.cos(turn), jnp.sin(turn)
        for p, value in enumerate((cos, sin, 1.0 - 2.0 * sin * sin, 2.0 * cos * sin)):
            tw[p, pl.ds(at, ROWS), :] = value
        return 0

    lax.fori_loop(0, q // ROWS, angles, 0)
    outs = [copy(tab, tab_hbm, sem_out.at[0]), copy(tw, tw_hbm, sem_out.at[1])]
    outs.append(copy(inv, inv_hbm, sem_out.at[2]))
    for out in outs:
        out.start()
    forth(tab, cat_ref, wave)

    def spectrum(b, _):
        at = pl.multiple_of(b * STEP, STEP)
        chunk, rows = place_of(b)
        for p in range(2):
            for k, (re, im) in enumerate(butterfly(wave, tw, at, p, 2, dims)):
                spec[chunk, k, rows, lanes(2 * p)] = re * (1.0 / n)
                spec[chunk, k, rows, lanes(2 * p + 1)] = im * (1.0 / n)
        return 0

    lax.fori_loop(0, q // STEP, spectrum, 0)
    outs.append(copy(spec, spec_hbm, sem_spec))
    outs[-1].start()
    for out in outs:
        out.wait()


def lanes(p):
    return slice(p * LANES, (p + 1) * LANES)


def over_groups(x, group):
    return mm(jnp.concatenate(halves(x), axis=1), jnp.concatenate([group, group], axis=0))


def place_of(b):
    return b // PER, pl.ds(pl.multiple_of(b % PER * STEP, STEP), STEP)


def product(table, operand):
    (high, low), (first, second) = table, operand
    return mm(
        jnp.concatenate([high, high, low], axis=1), jnp.concatenate([first, second, first], axis=0)
    )


def forth(tab, cat, wave):
    wave[...] = product((tab[0], tab[1]), (cat[0], cat[1]))


def twiddles(tw, at):
    c1, s1, c2, s2 = [tw[p, pl.ds(at, STEP), :] for p in range(4)]
    return (c2, s2), (c1, s1), None, (c1, -s1)


def times(a, b):
    if b is None:
        return a
    return a[0] * b[0] - a[1] * b[1], a[0] * b[1] + a[1] * b[0]


def plus(a, b):
    return a[0] + b[0], a[1] + b[1]


def minus(a, b):
    return a[0] - b[0], a[1] - b[1]


def turned(a):
    return -a[1], a[0]


def butterfly(wave, tw, at, p, count, dims):
    below = pl.multiple_of(dims.quarter + at, STEP)
    parts = []
    for r, twiddle in enumerate(twiddles(tw, at)):
        re = wave[pl.ds(at, STEP), lanes(r * count + p)]
        im = wave[pl.ds(below, STEP), lanes(r * count + p)]
        parts.append(times((re, -im), twiddle))
    even, odd = plus(parts[0], parts[2]), plus(parts[1], parts[3])
    even_too, odd_too = minus(parts[0], parts[2]), turned(minus(parts[1], parts[3]))
    return plus(even, odd), minus(even_too, odd_too), minus(even, odd), plus(even_too, odd_too)


def unbutterfly(parts, tw, at, cat, p, count, dims):
    even, odd = plus(parts[0], parts[2]), plus(parts[1], parts[3])
    even_too, odd_too = minus(parts[0], parts[2]), turned(minus(parts[1], parts[3]))
    sums = plus(even, odd), plus(even_too, odd_too), minus(even, odd), minus(even_too, odd_too)
    for r, twiddle in enumerate(twiddles(tw, at)):
        if twiddle is not None:
            twiddle = twiddle[0], -twiddle[1]
        re, im = times(sums[r], twiddle)
        for first, value in ((0, re), (dims.quarter, -im)):
            rows = pl.ds(pl.multiple_of(first + at, STEP), STEP)
            for part, half in enumerate(halves(value)):
                cat[part, rows, lanes(r * count + p)] = half


def back(inv, cat):
    return product((inv[0], inv[1]), (cat[0], cat[1]))


def column_sums(x):
    return jnp.sum(x.reshape(x.shape[0] // 8, 8, LANES), axis=0)


def lane_lengths(meta_ref, lens_refs, dims):
    lane = lane_ids((1, LANES)) // dims.chans
    row = jnp.zeros((1, LANES), jnp.int32)
    total = jnp.int32(0)
    for s in range(dims.all_seqs):
        source = s // dims.seqs
        value = lens_refs[source][s % dims.seqs]
        total = total + value
        row = jnp.where(lane == s ^ (meta_ref[0] * dims.seqs), value, row)
    return row, total.astype(f32)


def valid_rows(r, at, rows, lens):
    places = 4 * (lax.broadcasted_iota(jnp.int32, (rows, LANES), 0) + at) + r
    return (places < lens).astype(f32)


def forward_kernel(dims, meta_ref, r_ref, par_ref, tab_hbm, inv_hbm, tw_hbm, spec_hbm, *rest):
    lens_refs, rest = rest[: dims.ni], rest[dims.ni :]
    (send_hbm, mixed_hbm, normed_hbm, seen_hbm, stat_ref), rest = rest[:5], rest[5:]
    tab, inv, tw, spec, seen, x_sc, mix_sc, normed_sc, cat, wave, back_cat, send = rest[:12]
    sem_tab, sem_spec, sem_seen, sem_out, sem_send = rest[12:]
    m, q = dims.mode_rows, dims.quarter
    chunks = q // ROWS
    ins = [copy(tab_hbm, tab, sem_tab.at[0]), copy(tw_hbm, tw, sem_tab.at[1])]
    ins += [copy(spec_hbm.at[c], spec.at[c], sem_spec.at[c]) for c in range(chunks)]
    ins.append(copy(inv_hbm, inv, sem_tab.at[2]))
    for one in ins:
        one.start()
    lens, total = lane_lengths(meta_ref, lens_refs, dims)
    unpack_channels(r_ref, x_sc, dims)
    classes = range(4)

    def add_up(b, acc):
        at = pl.multiple_of(b * ROWS, ROWS)
        for r in classes:
            acc = acc + column_sums(x_sc[r, pl.ds(at, ROWS), :] * valid_rows(r, at, ROWS, lens))
        return acc

    zero = jnp.zeros((8, LANES), f32)
    acc = lax.fori_loop(0, q // ROWS, add_up, zero)
    average = fold(jnp.sum(acc, axis=0, keepdims=True), dims) / total

    def add_squares(b, acc):
        at = pl.multiple_of(b * ROWS, ROWS)
        for r in classes:
            x = (x_sc[r, pl.ds(at, ROWS), :] - average) * valid_rows(r, at, ROWS, lens)
            acc = acc + column_sums(x * x)
        return acc

    acc = lax.fori_loop(0, q // ROWS, add_squares, zero)
    variance = fold(jnp.sum(acc, axis=0, keepdims=True), dims) / total
    inv_scale = lax.rsqrt(variance + EPS)
    gain = par_ref[6 * m + 1 : 6 * m + 2, :]
    shift = par_ref[6 * m + 2 : 6 * m + 3, :]
    skip = par_ref[6 * m + 3 : 6 * m + 4, :]
    stat_ref[0:1, :] = inv_scale
    stat_ref[1:2, :] = jnp.broadcast_to(total, (1, LANES))
    stat_ref[2:3, :] = lens.astype(f32)
    stat_ref[3:8, :] = jnp.zeros((5, LANES), f32)
    first_row = lax.broadcasted_iota(jnp.int32, (ROWS, LANES), 0) == 0

    def normalize(b, last):
        at = pl.multiple_of(b * ROWS, ROWS)
        mixed = []
        for r in classes:
            normed = (x_sc[r, pl.ds(at, ROWS), :] - average) * inv_scale
            mixed.append((gain * normed + shift) * valid_rows(r, at, ROWS, lens))
            normed_sc[r, pl.ds(at, ROWS), :] = normed
            mix_sc[r, pl.ds(at, ROWS), :] = mixed[r]
        earlier = jnp.where(first_row, last, pltpu.roll(mixed[3], 1, 0))
        for r in classes:
            liquid = mixed[r] * (earlier if r == 0 else mixed[r - 1])
            for p, value in enumerate((mixed[r], liquid)):
                for part, half in enumerate(halves(value)):
                    cat[part, pl.ds(at, ROWS), lanes(2 * r + p)] = half
        return mixed[3][ROWS - 1 :, :]

    lax.fori_loop(0, q // ROWS, normalize, jnp.zeros((1, LANES), f32))
    outs = [copy(mix_sc, mixed_hbm, sem_out.at[0]), copy(normed_sc, normed_hbm, sem_out.at[1])]
    for out in outs:
        out.start()
    ins[0].wait()
    forth(tab, cat, wave)
    ins[1].wait()
    for c in range(chunks):
        ins[2 + c].wait()

        def multiply(b, _):
            at = pl.multiple_of(b * STEP, STEP)
            chunk, rows = place_of(b)
            mixed = butterfly(wave, tw, at, 0, 2, dims)
            liquid = butterfly(wave, tw, at, 1, 2, dims)
            parts = []
            for k in range(4):
                for p, value in enumerate(mixed[k] + liquid[k]):
                    seen[chunk, k, rows, lanes(p)] = value
                kr, ki, lr, li = [spec[chunk, k, rows, lanes(p)] for p in range(4)]
                parts.append(plus(times(mixed[k], (kr, ki)), times(liquid[k], (lr, li))))
            unbutterfly(parts, tw, at, back_cat, 0, 1, dims)
            return 0

        lax.fori_loop(PER * c, PER * (c + 1), multiply, 0)
        outs.append(copy(seen.at[c], seen_hbm.at[c], sem_seen.at[c]))
        outs[-1].start()
    ins[-1].wait()

    value = back(inv, back_cat)
    for r in classes:
        x_sc[r] = value[:, lanes(r)] + skip * mix_sc[r]
    pack_channels(
        lambda r, at, size: x_sc[r, pl.ds(at, size), :], send, send_hbm, sem_send, dims
    )
    for out in outs:
        out.wait()


def gate_kernel(dims, meta_ref, r_ref, x_ref, w_ref, b_ref, ct_ref, *rest):
    (send_hbm, out_ref, act_hbm, gj_hbm, bias_ref, wsend_hbm), scratch = rest[:6], rest[6:]
    resp, act, joined, gj, gact, send, weight, wsend, sem_out, sem_send, sem_weight = scratch
    tokens = dims.seqs * dims.places
    width = dims.width
    places = dims.places

    tiles = range(width // LANES)
    if dims.fast:
        unpack_tokens(r_ref, resp, dims)
    else:
        for t in tiles:
            resp[t] = r_ref[:, lanes(t)]
    c0 = math.sqrt(2.0 / math.pi)
    c1 = 0.044715
    rows = 32

    def gelu(b, _):
        at = pl.multiple_of(b * rows, rows)
        for tile in tiles:
            r = resp[tile, pl.ds(at, rows), :]
            t = jnp.tanh(c0 * (r + c1 * r * r * r))
            act[pl.ds(at, rows), lanes(tile)] = (0.5 * r * (1.0 + t)).astype(bf16)
            slope = 0.5 * (1.0 + t) + 0.5 * r * (1.0 - t * t) * (c0 * (1.0 + 3.0 * c1 * r * r))
            resp[tile, pl.ds(at, rows), :] = slope
        return 0

    lax.fori_loop(0, tokens // rows, gelu, 0)
    outs = [copy(act, act_hbm, sem_out.at[0]), copy(gj, gj_hbm, sem_out.at[1])]
    outs[0].start()
    joined[...] = mm(act[...], w_ref[...])
    bias = b_ref[...]
    half = min(16, places)
    for b in range(dims.seqs):

        def gate(k, sums):
            at = pl.multiple_of(k * half, half)
            tok = pl.multiple_of(b * places + k * half, half)
            value = joined[pl.ds(tok, half), :width] + bias[:, :width]
            s = jax.nn.sigmoid(joined[pl.ds(tok, half), width:] + bias[:, width:])
            x = x_ref[b, pl.ds(at, half), :].astype(f32)
            g = ct_ref[b, pl.ds(at, half), :].astype(f32)
            out_ref[b, pl.ds(at, half), :] = (x + value * s).astype(bf16)
            gs = g * s
            first = gs.astype(bf16)
            second = (gs * value * (1.0 - s)).astype(bf16)
            gj[pl.ds(tok, half), :width] = first
            gj[pl.ds(tok, half), width:] = second
            first = jnp.sum(first.astype(f32).reshape(half // 8, 8, width), axis=0)
            second = jnp.sum(second.astype(f32).reshape(half // 8, 8, width), axis=0)
            return sums[0] + first, sums[1] + second

        if b == 0:
            zero = jnp.zeros((8, width), f32)
            sums = (zero, zero)
        sums = lax.fori_loop(0, places // half, gate, sums)
    outs[1].start()
    sums = [jnp.sum(s, axis=0, keepdims=True) for s in sums]
    for p, total in enumerate(sums):
        for t in tiles:
            row = p * (width // LANES) + t
            bias_ref[row : row + 1, :] = total[:, lanes(t)]
    weight_half(dims, meta_ref, 1 - meta_ref[1], act, gj, weight)
    for i in range(dims.ni):
        for z in range(dims.nz):
            for u in range(dims.units):
                wsend[i, z, u, :, :] = weight_unit(dims, meta_ref, weight, i, z, u)
            wsend[i, z, dims.units, :, :] = bias_ref[...]
        outs.append(copy(wsend.at[i], wsend_hbm.at[i], sem_weight.at[i]))
        outs[-1].start()
    grad = lax.dot_general(
        gj[...], w_ref[...], (((1,), (1,)), ((), ())), preferred_element_type=f32
    )
    for t in tiles:
        gact[t] = grad[:, lanes(t)]
    if dims.fast:

        def read(tile, rows):
            return gact[tile, rows, :] * resp[tile, rows, :]

        def put(piece, value):
            send[piece] = value

        def tile_copy(tile):
            some = pl.ds(tile * dims.groups, dims.groups)
            return copy(send.at[some], send_hbm.at[some], sem_send.at[tile])

        pack_tokens(read, put, dims, lambda tile: tile_copy(tile).start())
        outs += [tile_copy(tile) for tile in tiles]
    else:
        for t in tiles:
            send[:, lanes(t)] = gact[t] * resp[t]
        outs.append(copy(send, send_hbm, sem_send.at[0]))
        outs[-1].start()
    for out in outs:
        out.wait()


def weight_half(dims, meta_ref, core, act, gj, weight):
    half = dims.width // 2
    some = act[:, pl.ds(pl.multiple_of(core * half, half), half)]
    weight[...] = lax.dot_general(
        some, gj[...], (((0,), (0,)), ((), ())), preferred_element_type=f32
    )


def weight_unit(dims, meta_ref, weight, i, z, u):
    tiles = 2 * dims.width // LANES
    owner = (meta_ref[0] ^ i) * dims.nz + (meta_ref[2] ^ z)
    if dims.units % tiles == 0:
        row = owner * (dims.units // tiles) + u // tiles
        cols = lanes(u % tiles)
    else:
        unit = owner * dims.units + u
        row = unit // tiles
        cols = pl.ds(pl.multiple_of(unit % tiles * LANES, LANES), LANES)
    return weight[pl.ds(pl.multiple_of(row * 8, 8), 8), cols]


def backward_kernel(dims, r_ref, par_ref, *rest):
    ins_hbm, (stat_ref, send_hbm, grad_hbm, sums_ref) = rest[:6], rest[6:10]
    tab, inv, tw, spec, grads, mix_sc, normed_sc, g_sc, up_sc, cat, wave, back_cat = rest[10:22]
    lead_sc, liquid_sc, send, sem_in, sem_spec, sem_send, sem_grad = rest[22:]
    tab_hbm, inv_hbm, tw_hbm, spec_hbm, mixed_hbm, normed_hbm = ins_hbm
    m, q = dims.mode_rows, dims.quarter
    ins = [
        copy(mixed_hbm, mix_sc, sem_in.at[0]),
        copy(tab_hbm, tab, sem_in.at[1]),
        copy(tw_hbm, tw, sem_in.at[2]),
        copy(normed_hbm, normed_sc, sem_in.at[3]),
        copy(inv_hbm, inv, sem_in.at[4]),
    ]
    chunks = q // ROWS
    for c in range(chunks):
        ins.insert(3 + c, copy(spec_hbm.at[c], spec.at[c], sem_spec.at[c]))
    for one in ins:
        one.start()
    unpack_channels(r_ref, g_sc, dims)
    gain = par_ref[6 * m + 1 : 6 * m + 2, :]
    skip = par_ref[6 * m + 3 : 6 * m + 4, :]
    inv_scale = stat_ref[0:1, :]
    total = stat_ref[1:2, :]
    lens = stat_ref[2:3, :].astype(jnp.int32)
    zero = jnp.zeros((8, LANES), f32)
    classes = range(4)
    ins[0].wait()

    def gather(b, acc):
        at = pl.multiple_of(b * ROWS, ROWS)
        for r in classes:
            g = g_sc[r, pl.ds(at, ROWS), :]
            for part, half in enumerate(halves(g)):
                cat[part, pl.ds(at, ROWS), lanes(r)] = half
            acc = acc + column_sums(g * mix_sc[r, pl.ds(at, ROWS), :])
        return acc

    skip_acc = lax.fori_loop(0, q // ROWS, gather, zero)
    ins[1].wait()
    forth(tab, cat, wave)
    ins[2].wait()
    outs = []
    for c in range(chunks):
        ins[3 + c].wait()

        def multiply(b, _):
            at = pl.multiple_of(b * STEP, STEP)
            chunk, rows = place_of(b)
            grad = butterfly(wave, tw, at, 0, 1, dims)
            for k in range(4):
                for p in range(2):
                    grads[chunk, k, rows, lanes(p)] = grad[k][p]
            for p in range(2):
                products(grad, spec, tw, b, back_cat, p, dims)
            return 0

        lax.fori_loop(PER * c, PER * (c + 1), multiply, 0)
        outs.append(copy(grads.at[c], grad_hbm.at[c], sem_grad.at[c]))
        outs[-1].start()
    for one in ins[3 + chunks :]:
        one.wait()

    value = back(inv, back_cat)
    for r in classes:
        lead_sc[r] = value[:, lanes(2 * r)]
        liquid_sc[r] = value[:, lanes(2 * r + 1)]
        up_sc[r] = value[:, lanes(2 * r + 1)] * mix_sc[r]

    row = lax.broadcasted_iota(jnp.int32, (ROWS, LANES), 0)
    blank = jnp.zeros((1, LANES), f32)
    gain_acc, shift_acc = zero, zero
    for at in range(0, q, ROWS):
        rows = slice(at, at + ROWS)
        for r in classes:
            if r == 0:
                before = blank if at == 0 else mix_sc[3, at - 1 : at, :]
                earlier = jnp.where(row == 0, before, pltpu.roll(mix_sc[3, rows, :], 1, 0))
            else:
                earlier = mix_sc[r - 1, rows, :]
            if r == 3:
                after = blank if at + ROWS == q else up_sc[0, at + ROWS : at + ROWS + 1, :]
                up = jnp.where(row == ROWS - 1, after, pltpu.roll(up_sc[0, rows, :], ROWS - 1, 0))
            else:
                up = up_sc[r + 1, rows, :]
            masked = lead_sc[r, rows, :] + skip * g_sc[r, rows, :] + liquid_sc[r, rows, :] * earlier
            masked = (masked + up) * valid_rows(r, at, ROWS, lens)
            g_sc[r, rows, :] = masked
            gain_acc = gain_acc + column_sums(masked * normed_sc[r, rows, :])
            shift_acc = shift_acc + column_sums(masked)

    def whole(acc):
        return fold(jnp.sum(acc, axis=0, keepdims=True), dims)

    gain_sum, shift_sum, skip_sum = whole(gain_acc), whole(shift_acc), whole(skip_acc)
    scale = gain * inv_scale
    shift_mean = shift_sum / total
    gain_mean = gain_sum / total

    def read(r, at, size):
        normed = normed_sc[r, pl.ds(at, size), :]
        value = g_sc[r, pl.ds(at, size), :] - shift_mean - normed * gain_mean
        return value * scale * valid_rows(r, at, size, lens)

    sums_ref[...] = jnp.zeros_like(sums_ref)
    for p, value in enumerate((gain_sum, shift_sum, skip_sum)):
        sums_ref[p : p + 1, :] = value
    pack_channels(read, send, send_hbm, sem_send, dims)
    for out in outs:
        out.wait()


def products(grad, ref, tw, b, cat, p, dims):
    chunk, rows = place_of(b)
    parts = []
    for k in range(4):
        re = ref[chunk, k, rows, lanes(2 * p)]
        im = ref[chunk, k, rows, lanes(2 * p + 1)]
        parts.append(times(grad[k], (re, -im)))
    unbutterfly(parts, tw, pl.multiple_of(b * STEP, STEP), cat, p, 2, dims)


def modes_kernel(dims, par_ref, inv_hbm, tw_hbm, seen_hbm, grad_hbm, sums_ref, *rest):
    zr_ref, zi_ref, vec_ref, small_ref, inv, tw, seen, grads, back_cat, dk, sem, sem_in = rest
    n, m, q = dims.length, dims.mode_rows, dims.quarter
    chunks = q // ROWS
    ins = [copy(tw_hbm, tw, sem.at[0])]
    for c in range(chunks):
        ins.append(copy(seen_hbm.at[c], seen.at[c], sem_in.at[0, c]))
        ins.append(copy(grad_hbm.at[c], grads.at[c], sem_in.at[1, c]))
    ins.append(copy(inv_hbm, inv, sem.at[1]))
    for one in ins:
        one.start()
    zero = jnp.zeros((8, LANES), f32)
    classes = range(4)
    ins[0].wait()
    for c in range(chunks):
        ins[1 + 2 * c].wait()
        ins[2 + 2 * c].wait()

        def multiply(b, _):
            chunk, rows = place_of(b)
            grad = [tuple(grads[chunk, k, rows, lanes(p)] for p in range(2)) for k in range(4)]
            for p in range(2):
                products(grad, seen, tw, b, back_cat, p, dims)
            return 0

        lax.fori_loop(PER * c, PER * (c + 1), multiply, 0)
    ins[-1].wait()
    group = fold_matrix(dims)

    value = back(inv, back_cat) * (1.0 / n)
    dk[...] = over_groups(jnp.concatenate([value[:, lanes(p)] for p in range(8)], axis=0), group)

    step, log_mag, turn, _, params = mode_constants(par_ref, dims)
    decay, rotation, dr, di, rr, ri = params
    l32r, l32i, c1r, c1i, c2r, c2i = [vec_ref[p * m : (p + 1) * m, :] for p in range(6)]
    sub = 4.0 * lax.broadcasted_iota(jnp.int32, (8, LANES), 0).astype(f32)
    sums = [[] for _ in range(8)]
    for first in range(0, m, 2):
        some = range(first, min(m, first + 2))
        ratio = [
            (
                jnp.broadcast_to(l32r[k : k + 1], (8, LANES)),
                jnp.broadcast_to(l32i[k : k + 1], (8, LANES)),
            )
            for k in some
        ]
        sofar = [zero] * (8 * len(ratio))
        for r in classes:

            def mode_step(t, carry):
                at = pl.multiple_of(t * 8, 8)
                d1 = dk[pl.ds(pl.multiple_of(2 * r * q + at, 8), 8), :]
                d2 = dk[pl.ds(pl.multiple_of((2 * r + 1) * q + at, 8), 8), :]
                place = sub + (32 * t + r).astype(f32)
                e1 = d1 * place
                e2 = d2 * place
                out = []
                for k, (ar, ai) in enumerate(ratio):
                    zr, zi, *acc = carry[10 * k : 10 * (k + 1)]
                    out += [zr * ar - zi * ai, zr * ai + zi * ar]
                    for p, d in enumerate((d1, d2, e1, e2)):
                        out += [acc[2 * p] + d * zr, acc[2 * p + 1] + d * zi]
                return tuple(out)

            carry = []
            for at, k in enumerate(some):
                carry += [zr_ref[r, 8 * k : 8 * k + 8, :], zi_ref[r, 8 * k : 8 * k + 8, :]]
                carry += sofar[8 * at : 8 * at + 8]
            carry = lax.fori_loop(0, q // 8, mode_step, tuple(carry), unroll=4)
            sofar = [v for k in range(len(ratio)) for v in carry[10 * k + 2 : 10 * k + 10]]
        for k in range(len(ratio)):
            for p in range(8):
                sums[p].append(jnp.sum(sofar[8 * k + p], axis=0, keepdims=True))
    a1r, a1i, a2r, a2i, e1r, e1i, e2r, e2i = [
        jnp.concatenate(s, axis=0) if len(s) > 1 else s[0] for s in sums
    ]
    btr = c1r * e1r - c1i * e1i + c2r * e2r - c2i * e2i
    bti = c1r * e1i + c1i * e1r + c2r * e2i + c2i * e2r
    d2r = dr * dr - di * di
    d2i = 2.0 * dr * di
    erd = step * (a1r * dr - a1i * di + a2r * d2r - a2i * d2i)
    eri = step * (a1r * di + a1i * dr + a2r * d2i + a2i * d2r)
    tr = a1r + 2.0 * (a2r * dr - a2i * di)
    ti = a1i + 2.0 * (a2r * di + a2i * dr)
    edr = step * (rr * tr - ri * ti)
    edi = step * (rr * ti + ri * tr)
    by_step = 2.0 * (c1r * a1r - c1i * a1i + c2r * a2r - c2i * a2i) + 2.0 * step * (
        -decay * btr - rotation * bti
    )
    small_ref[...] = jnp.zeros_like(small_ref)
    answers = (-2.0 * step * btr, -2.0 * step * bti, 2.0 * edr, -2.0 * edi, 2.0 * erd, -2.0 * eri)
    for p, value in enumerate(answers):
        small_ref[p * m : (p + 1) * m, :] = value
    small_ref[6 * m : 6 * m + 1, :] = fold(jnp.sum(by_step, axis=0, keepdims=True), dims)
    small_ref[6 * m + 1 : 6 * m + 4, :] = sums_ref[0:3, :]


def first_add_kernel(dims, meta_ref, act_hbm, gj_hbm, bias_ref, other_hbm, *refs):
    out_refs, (act, gj, weight, other, sem_in, sem) = refs[: dims.ni], refs[dims.ni :]
    ins = [copy(act_hbm, act, sem_in.at[0]), copy(gj_hbm, gj, sem_in.at[1])]
    others = [copy(other_hbm.at[i], other.at[i], sem.at[i]) for i in range(dims.ni)]
    for one in ins + others:
        one.start()
    for one in ins:
        one.wait()
    weight_half(dims, meta_ref, meta_ref[1], act, gj, weight)
    for i in range(dims.ni):
        others[i].wait()
        for z in range(dims.nz):
            for u in range(dims.units):
                unit = weight_unit(dims, meta_ref, weight, i, z, u)
                out_refs[i][z, u] = unit + other[i, z, u]
            out_refs[i][z, dims.units] = bias_ref[...] + other[i, z, dims.units]


def order_kernel(sums_ref, out_ref):
    out_ref[...] = sums_ref[...]


def add_kernel(count, *refs):
    for p, out_ref in enumerate(refs[count:]):
        total = refs[0][p]
        for ref in refs[1:count]:
            total = total + ref[p]
        out_ref[...] = total


def last_add_kernel(dims, count, small_ref, *refs):
    units_ref, bias_ref = refs[count:]

    def unit(u):
        total = refs[0][u]
        for ref in refs[1:count]:
            total = total + ref[u]
        return total

    for u in range(dims.units):
        units_ref[u] = unit(u)
    for t in range(dims.small_rows // 8):
        units_ref[dims.units + t] = small_ref[8 * t : 8 * t + 8, :]
    bias = unit(dims.units)
    for t in range(2 * dims.width // LANES):
        bias_ref[:, lanes(t)] = bias[t : t + 1, :]


def stack_kernel(meta_at, meta_ref, *refs):
    out_ref = refs[-1]
    for s, ref in enumerate(refs[:-1]):
        out_ref[meta_ref[meta_at] ^ s] = ref[...]


def input_kernel(dims, r_ref, ct_ref, grad_ref, grad):
    unpack_tokens(r_ref, grad, dims, False)
    for b in range(dims.seqs):
        for t in range(dims.width // LANES):
            value = grad[t, b * dims.places : (b + 1) * dims.places, :]
            grad_ref[b, :, lanes(t)] = value + ct_ref[b, :, lanes(t)].astype(f32)


def finish_kernel(dims, meta_ref, *refs):
    ni, nz, m = dims.ni, dims.nz, dims.mode_rows
    planes = refs[:ni], refs[ni : 2 * ni]
    weight_ref, *small_hbm = refs[2 * ni : 2 * ni + 11]
    *small_refs, rows, sem, sem_small = refs[2 * ni + 11 :]
    me, core = meta_ref[0], meta_ref[1]
    tiles = 2 * dims.width // LANES
    per = 8 * dims.units // tiles
    copies = []
    for half, side in ((0, core), (1, 1 - core)):
        for i in range(ni):
            for z in range(nz):
                for u in range(dims.units):
                    at = z * per + u // tiles * 8
                    rows[half, i, at : at + 8, lanes(u % tiles)] = planes[half][i][z, u]
            at = pl.multiple_of((side * ni + (me ^ i)) * nz * per, nz * per)
            target = weight_ref.at[pl.ds(at, nz * per), :]
            copies.append(copy(rows.at[half, i], target, sem.at[half, i]))
            copies[-1].start()
    first = core == 0
    for i in range(ni):
        parts = []
        for z in range(nz):
            a = planes[0][i][z, dims.units :].reshape(dims.small_rows, LANES)
            b = planes[1][i][z, dims.units :].reshape(dims.small_rows, LANES)
            parts += [jnp.where(first, a, b), jnp.where(first, b, a)]
        parts = swap_blocks(parts, dims.chans)
        cols = pl.ds(pl.multiple_of((me ^ i) * LANES, LANES), LANES)
        for q in range(dims.groups):
            for p in range(6):
                small_refs[p][q * m : q * m + m, cols] = parts[q][p * m : p * m + m, :]
        for p in range(4):
            small_refs[6 + p][:, cols] = parts[0][6 * m + p : 6 * m + p + 1, :]
    for p, (ref, hbm) in enumerate(zip(small_refs, small_hbm)):
        copies.append(copy(ref, hbm, sem_small.at[p]))
        copies[-1].start()
    for one in copies:
        one.wait()


def call(kernel, out_shape, in_specs, scratch, limit, us, out_specs=None):
    cost = pl.CostEstimate(flops=int(us * 1.1e9), bytes_accessed=int(us * 3e6), transcendentals=0)
    if out_specs is None:
        out_specs = jax.tree.map(lambda _: VMEM, out_shape)
    else:
        out_shape = tuple(
            pltpu.HBM(out.shape, out.dtype) if spec is HBM else out
            for out, spec in zip(out_shape, out_specs)
        )

    def run(*args):
        args = [
            pltpu.with_memory_space_constraint(x, pltpu.HBM) if spec is HBM else x
            for x, spec in zip(args, in_specs)
        ]
        return pl.pallas_call(
            kernel,
            out_shape=out_shape,
            in_specs=in_specs,
            out_specs=out_specs,
            scratch_shapes=scratch,
            compiler_params=pltpu.CompilerParams(vmem_limit_bytes=limit << 20),
            cost_estimate=cost,
        )(*args)

    return run


def shape(*dims, dtype=f32):
    return jax.ShapeDtypeStruct(dims, dtype)


def local(
    mesh_shape,
    inputs,
    lengths,
    norm_gain,
    norm_shift,
    log_step,
    decay_rate,
    rotation,
    drive_real,
    drive_imag,
    read_real,
    read_imag,
    skip_gain,
    glu_weight,
    glu_bias,
    out_cotangent,
):
    modes = decay_rate.shape[0]
    dims = Dims(inputs.shape, modes, mesh_shape)
    n, nd, m, hc = dims.length, dims.devices, dims.mode_rows, dims.chans
    core = lax.axis_index("core")
    owner = lax.axis_index(ALL)
    meta = jnp.stack([lax.axis_index("batch"), core, lax.axis_index("z")]).astype(jnp.int32)

    def exchange(x):
        return lax.all_to_all(x, ALL, 0, 0, tiled=True)

    some = dims.places // 4

    def to_channels(x):
        x = x.reshape(dims.seqs, some, 4, nd, hc).transpose(3, 2, 1, 0, 4)
        x = exchange(x.reshape(nd, dims.places, dims.piece_width))
        x = x.reshape(dims.ni, dims.nj, 4, some, dims.piece_width).transpose(2, 1, 3, 0, 4)
        x = x.reshape(n, dims.all_seqs * hc)
        return jnp.pad(x, ((0, 0), (0, LANES - x.shape[1])))

    def to_tokens(x):
        x = x[:, : dims.all_seqs * hc].reshape(4, dims.nj, some, dims.ni, dims.piece_width)
        x = x.transpose(3, 1, 0, 2, 4).reshape(nd, dims.places, dims.piece_width)
        x = exchange(x).reshape(nd, 4, some, dims.seqs, hc).transpose(3, 2, 1, 0, 4)
        return x.reshape(dims.seqs * dims.places, dims.width)

    table = jnp.stack([decay_rate, rotation, drive_real, drive_imag, read_real, read_imag])
    table = lax.dynamic_slice_in_dim(table, owner * hc, hc, 2)
    table = jnp.pad(table, ((0, 0), (0, m * dims.groups - modes), (0, 0)))
    table = table.reshape(6, dims.groups, m, hc).transpose(0, 2, 1, 3).reshape(6 * m, LANES)
    rest = jnp.stack([log_step, norm_gain, norm_shift, skip_gain])
    rest = lax.dynamic_slice_in_dim(rest, owner * hc, hc, 1)
    params = jnp.concatenate([table, jnp.tile(rest, (1, dims.groups))], axis=0)
    params, meta = lax.optimization_barrier((params, meta))

    pieces = (nd, dims.piece_rows, LANES) if dims.fast else (n, LANES)
    tokens = dims.seqs * dims.places
    token_pieces = (nd, dims.piece_rows, LANES) if dims.fast else (tokens, dims.width)
    bind = functools.partial
    q = dims.quarter
    tab = (2, 2 * q, q)
    inv = (2, q, 2 * q)
    chunks = q // ROWS
    tw = (4, q, LANES)
    four = (chunks, 4, ROWS, 4 * LANES)
    two = (chunks, 4, ROWS, 2 * LANES)
    sent = (dims.ni, dims.nj, dims.piece_rows, LANES) if dims.fast else (n, LANES)
    plain = (4, q, LANES)
    by_tile = (dims.width // LANES, dims.seqs * dims.places, LANES)

    def vmem(*sizes, dtype=f32):
        return pltpu.VMEM(sizes, dtype)

    if dims.fast:
        packed = call(
            bind(pack_kernel, dims), shape(*pieces), [VMEM], [vmem(*by_tile)], 4, 1.5
        )(inputs)
        received = exchange(packed)
    else:
        received = to_channels(inputs.astype(f32))

    zr, zi, vec, waves = call(
        bind(waves_kernel, dims),
        (
            shape(4, 8 * m, LANES),
            shape(4, 8 * m, LANES),
            shape(6 * m, LANES),
            shape(2, q, 8 * LANES, dtype=bf16),
        ),
        [VMEM],
        [vmem(q, 2 * LANES)],
        4,
        3,
    )(params)
    lengths, waves = lax.optimization_barrier((lengths, waves))
    tables, inverse, twiddle, spec = call(
        bind(tables_kernel, dims),
        (shape(*tab, dtype=bf16), shape(*inv, dtype=bf16), shape(*tw), shape(*four)),
        [VMEM],
        [
            vmem(*tab, dtype=bf16),
            vmem(*inv, dtype=bf16),
            vmem(*tw),
            vmem(*four),
            vmem(2 * q, 8 * LANES),
            DMA((3,)),
            DMA(()),
        ],
        10,
        6,
        (HBM, HBM, HBM, HBM),
    )(waves)

    def swap(x, axis, by):
        return lax.ppermute(x, axis, [(i, i ^ by) for i in range(lax.axis_size(axis))])

    def everyone(x, axis, size):
        return [x] + [swap(x, axis, s) for s in range(1, size)]

    lens = everyone(lengths, "batch", dims.ni)
    send, mixed, normed, seen, stat = call(
        bind(forward_kernel, dims),
        (shape(*sent), shape(*plain), shape(*plain), shape(*four), shape(8, LANES)),
        [SMEM, VMEM, VMEM] + [HBM] * 4 + [SMEM] * dims.ni,
        [
            vmem(*tab, dtype=bf16),
            vmem(*inv, dtype=bf16),
            vmem(*tw),
            vmem(*four),
            vmem(*four),
            vmem(*plain),
            vmem(*plain),
            vmem(*plain),
            vmem(2, q, 8 * LANES, dtype=bf16),
            vmem(2 * q, 8 * LANES),
            vmem(2, 2 * q, 4 * LANES, dtype=bf16),
            vmem(*sent),
            DMA((3,)),
            DMA((chunks,)),
            DMA((chunks,)),
            DMA((2,)),
            DMA((dims.nj,)),
        ],
        18,
        7,
        (HBM, HBM, HBM, HBM, VMEM),
    )(meta, received, params, tables, inverse, twiddle, spec, *lens)
    send = send.reshape(pieces)

    received = exchange(send) if dims.fast else to_tokens(send)
    wide = (tokens, dims.width)
    wider = (tokens, 2 * dims.width)
    unit = (dims.units + 1, 8, LANES)
    part = (dims.ni, dims.nz) + unit
    tiles = 2 * dims.width // LANES
    send, result, act, gj, bias, wsend = call(
        bind(gate_kernel, dims),
        (
            shape(*token_pieces),
            shape(*inputs.shape, dtype=bf16),
            shape(*wide, dtype=bf16),
            shape(*wider, dtype=bf16),
            shape(tiles, LANES),
            shape(*part),
        ),
        [SMEM] + [VMEM] * 5,
        [
            vmem(*by_tile),
            vmem(*wide, dtype=bf16),
            vmem(*wider),
            vmem(*wider, dtype=bf16),
            vmem(*by_tile),
            vmem(*token_pieces),
            vmem(dims.width // 2, 2 * dims.width),
            vmem(*part),
            DMA((2,)),
            DMA((max(1, dims.width // LANES),)),
            DMA((dims.ni,)),
        ],
        11,
        5,
        (HBM, VMEM, HBM, HBM, VMEM, HBM),
    )(meta, received, inputs, glu_weight, glu_bias.reshape(1, -1), out_cotangent)
    received = exchange(send) if dims.fast else to_channels(
        send.reshape(dims.seqs, dims.places, dims.width)
    )

    parts = call(
        bind(first_add_kernel, dims),
        (shape(dims.nz, *unit),) * dims.ni,
        [SMEM, HBM, HBM, VMEM, ANY],
        [
            vmem(*wide, dtype=bf16),
            vmem(*wider, dtype=bf16),
            vmem(dims.width // 2, 2 * dims.width),
            vmem(*part),
            DMA((2,)),
            DMA((dims.ni,)),
        ],
        6,
        0.1,
    )(meta, act, gj, bias, swap(wsend, "core", 1))
    parts = [parts[0]] + [swap(parts[s], "batch", s) for s in range(1, dims.ni)]
    send, grads, sums = call(
        bind(backward_kernel, dims),
        (shape(*sent), shape(*two), shape(8, LANES)),
        [VMEM, VMEM] + [HBM] * 6 + [VMEM],
        [
            vmem(*tab, dtype=bf16),
            vmem(*inv, dtype=bf16),
            vmem(*tw),
            vmem(*four),
            vmem(*two),
            vmem(*plain),
            vmem(*plain),
            vmem(*plain),
            vmem(*plain),
            vmem(2, q, 4 * LANES, dtype=bf16),
            vmem(2 * q, 4 * LANES),
            vmem(2, 2 * q, 8 * LANES, dtype=bf16),
            vmem(*plain),
            vmem(*plain),
            vmem(*sent),
            DMA((5,)),
            DMA((chunks,)),
            DMA((dims.nj,)),
            DMA((chunks,)),
        ],
        18,
        9,
        (HBM, HBM, VMEM),
    )(received, params, tables, inverse, twiddle, spec, mixed, normed, stat)
    send = send.reshape(pieces)

    send, parts = lax.optimization_barrier((send, parts))
    parts = call(
        bind(add_kernel, dims.ni), (shape(*unit),) * dims.nz, [VMEM] * dims.ni, [], 2, 0.1
    )(*parts)
    sums, parts = lax.optimization_barrier((sums, parts))
    sums = call(order_kernel, shape(8, LANES), [VMEM], [], 1, 6)(sums)
    send, sums = lax.optimization_barrier((send, sums))
    received = exchange(send) if dims.fast else to_tokens(send)
    parts = [parts[0]] + [swap(parts[s], "z", s) for s in range(1, dims.nz)]
    small = call(
        bind(modes_kernel, dims),
        shape(dims.small_rows, LANES),
        [VMEM] + [HBM] * 4 + [VMEM] * 4,
        [
            vmem(*inv, dtype=bf16),
            vmem(*tw),
            vmem(*four),
            vmem(*two),
            vmem(2, 2 * q, 8 * LANES, dtype=bf16),
            vmem(8 * q, LANES),
            DMA((2,)),
            DMA((2, chunks)),
        ],
        12,
        6,
    )(params, inverse, twiddle, seen, grads, sums, zr, zi, vec)

    units = (dims.units + dims.small_rows // 8, 8, LANES)
    units, bias_grad = call(
        bind(last_add_kernel, dims, dims.nz),
        (shape(*units), shape(1, 2 * dims.width)),
        [VMEM] * (1 + dims.nz),
        [],
        2,
        0.7,
    )(small, *parts)
    planes = call(
        bind(stack_kernel, 2),
        shape(dims.nz, *units.shape),
        [SMEM] + [VMEM] * dims.nz,
        [],
        2,
        0.7,
    )(meta, *everyone(units, "z", dims.nz))
    planes = everyone(planes, "batch", dims.ni)
    if dims.fast:
        grad_in = call(
            bind(input_kernel, dims), shape(*inputs.shape), [VMEM] * 2, [vmem(*by_tile)], 4, 1.5
        )(received, out_cotangent)
    else:
        grad_in = out_cotangent.astype(f32) + received.reshape(inputs.shape)
    grad_in, planes = lax.optimization_barrier((grad_in, planes))
    planes_too = [swap(x, "core", 1) for x in planes]

    if dims.fast:
        outs = call(
            bind(finish_kernel, dims),
            (shape(dims.width, 2 * dims.width),)
            + (shape(modes, dims.width),) * 6
            + (shape(1, dims.width),) * 4,
            [SMEM] + [VMEM] * (2 * dims.ni),
            [vmem(modes, dims.width)] * 6
            + [vmem(1, dims.width)] * 4
            + [
                vmem(2, dims.ni, dims.width // 2 // dims.ni, 2 * dims.width),
                DMA((2, dims.ni)),
                DMA((10,)),
            ],
            5,
            3,
            (HBM,) * 11,
        )(meta, *planes, *planes_too)
        weight_grad = outs[0]
        mode_grads = outs[1:7]
        chan_grads = [x.reshape(-1) for x in outs[7:]]
    else:

        def in_order(mine, other):
            both = jnp.where(core == 0, jnp.stack([mine, other]), jnp.stack([other, mine]))
            return jnp.take(both, meta[0] ^ jnp.arange(dims.ni), axis=1)

        both = in_order(jnp.stack(planes), jnp.stack(planes_too))
        weight_grad = both[:, :, :, : dims.units].reshape(dims.width // 8, -1, 8, LANES)
        weight_grad = weight_grad.transpose(0, 2, 1, 3).reshape(dims.width, -1)
        rows = both[:, :, :, dims.units :].transpose(1, 2, 0, 3, 4, 5)
        rows = rows.reshape(nd, dims.small_rows, dims.groups, hc)
        table = rows[:, : 6 * m].reshape(nd, 6, m, dims.groups, hc).transpose(1, 3, 2, 0, 4)
        mode_grads = list(table.reshape(6, m * dims.groups, dims.width)[:, :modes])
        rest = rows[:, 6 * m : 6 * m + 4, 0].transpose(1, 0, 2).reshape(4, dims.width)
        chan_grads = list(rest)
    step_grad, gain_grad, shift_grad, skip_grad = chan_grads
    return (
        result,
        grad_in,
        gain_grad,
        shift_grad,
        step_grad,
        *mode_grads,
        skip_grad,
        weight_grad,
        bias_grad.reshape(-1),
    )


def solution(mesh):
    batch = mesh.shape["batch"]
    fine = Mesh(mesh.devices.reshape(-1, 2, batch), ("z", "core", "batch"))
    tokens = P("batch", ("z", "core"), None)
    return jax.shard_map(
        functools.partial(local, dict(fine.shape)),
        mesh=fine,
        in_specs=(tokens, P("batch")) + (P(),) * 12 + (tokens,),
        out_specs=(tokens, tokens) + (P(),) * 12,
        check_vma=False,
    )
```

```python
import functools
import math

import jax
import jax.numpy as jnp
from jax import lax
from jax.experimental import pallas as pl
from jax.experimental.pallas import tpu as pltpu
from jax.sharding import Mesh
from jax.sharding import PartitionSpec as P


EPS = 1e-05
LANES = 128
ALL = ("batch", "z", "core")
SMEM = pl.BlockSpec(memory_space=pltpu.SMEM)
VMEM = pl.BlockSpec(memory_space=pltpu.VMEM)
HBM = pl.BlockSpec(memory_space=pltpu.HBM)
ANY = pl.BlockSpec(memory_space=pl.ANY)
DMA = pltpu.SemaphoreType.DMA
ROWS = 64
STEP = 16
PER = ROWS // STEP
copy = pltpu.make_async_copy
f32 = jnp.float32
bf16 = jnp.bfloat16


def mm(a, b):
    return jnp.dot(a, b, preferred_element_type=f32)


def halves(x):
    hi = x.astype(bf16)
    return hi, (x - hi.astype(f32)).astype(bf16)


def lane_ids(shape):
    return lax.broadcasted_iota(jnp.int32, shape, len(shape) - 1)


def swap_blocks(tiles, width):
    tiles = list(tiles)
    block = lane_ids(tiles[0].shape) // width
    step = 1
    while step < len(tiles):
        low = (block & step) == 0
        for a in range(len(tiles)):
            if a & step == 0:
                first, second = tiles[a], tiles[a + step]
                tiles[a] = jnp.where(low, first, pltpu.roll(second, step * width, second.ndim - 1))
                tiles[a + step] = jnp.where(
                    low, pltpu.roll(first, LANES - step * width, first.ndim - 1), second
                )
        step *= 2
    return tiles


def fold_matrix(dims):
    rows = lax.broadcasted_iota(jnp.int32, (LANES, LANES), 0) % dims.chans
    cols = lax.broadcasted_iota(jnp.int32, (LANES, LANES), 1) % dims.chans
    return (rows == cols).astype(f32).astype(bf16)


def fold(row, dims):
    shift = dims.chans
    while shift < LANES:
        row = row + pltpu.roll(row, shift, 1)
        shift *= 2
    return row


class Dims:
    def __init__(self, inputs_shape, modes, mesh_shape):
        self.seqs, self.places, self.width = inputs_shape
        self.ni = mesh_shape["batch"]
        self.nz = mesh_shape["z"]
        self.nj = mesh_shape["z"] * mesh_shape["core"]
        self.devices = self.ni * self.nj
        self.length = self.places * self.nj
        self.quarter = self.length // 4
        self.chans = self.width // self.devices
        self.groups = LANES // self.chans
        self.all_seqs = self.seqs * self.ni
        self.modes = modes
        self.mode_rows = -(-modes // self.groups)
        self.small_rows = -(-(6 * self.mode_rows + 4) // 8) * 8
        self.piece_width = self.seqs * self.chans
        self.place_groups = LANES // self.piece_width
        self.piece_rows = self.places // self.place_groups
        self.units = self.width * 2 * self.width // (8 * LANES) // self.devices
        self.fast = (
            self.piece_width * self.ni == LANES
            and self.piece_rows % 8 == 0
            and self.nj == self.groups
            and self.small_rows == 32
            and self.place_groups == 4
        )


def each(count, body, unroll=True):
    lax.fori_loop(0, count, lambda k, _: body(k), None, unroll=unroll)


def class_rows(b, g, dims):
    return pl.ds(b * dims.places + g, dims.piece_rows, stride=4)


def pack_tokens(read, write, dims, done=None):
    def some(tile):
        parts = []
        for g in range(4):
            for b in range(dims.seqs):
                parts.append(read(tile, class_rows(b, g, dims)))
        parts = swap_blocks(parts, dims.chans)
        for e in range(dims.groups):
            write(tile * dims.groups + e, parts[e])
        if done is not None:
            done(tile)

    each(dims.width // LANES, some)


def unpack_tokens(ref, out, dims, unroll=True):
    def some(tile):
        parts = [ref[tile * dims.groups + e] for e in range(dims.groups)]
        parts = swap_blocks(parts, dims.chans)
        for g in range(4):
            for b in range(dims.seqs):
                out[tile, class_rows(b, g, dims), :] = parts[g * dims.seqs + b]

    each(dims.width // LANES, some, unroll)


def pack_kernel(dims, x_ref, out_ref, wide):
    for b in range(dims.seqs):
        for t in range(dims.width // LANES):
            wide[t, b * dims.places : (b + 1) * dims.places, :] = x_ref[b, :, lanes(t)].astype(f32)

    def write(piece, value):
        out_ref[piece] = value

    pack_tokens(lambda tile, rows: wide[tile, rows, :], write, dims)


def unpack_channels(ref, out, dims):
    rows = dims.piece_rows
    if not dims.fast:
        for r in range(4):
            out[r] = ref[r * dims.quarter : (r + 1) * dims.quarter, :]
        return

    def some(j):
        parts = [ref[i * dims.nj + j] for i in range(dims.ni)]
        parts = swap_blocks(parts, dims.piece_width)
        for g in range(4):
            out[g, pl.ds(pl.multiple_of(j * rows, rows), rows), :] = parts[g]

    each(dims.nj, some)


def pack_channels(read, send, send_hbm, sem, dims):
    rows = dims.piece_rows
    if not dims.fast:
        for r in range(4):
            for at in range(0, dims.quarter, ROWS):
                start = r * dims.quarter + at
                send[start : start + ROWS, :] = read(r, at, ROWS)
        whole = copy(send, send_hbm, sem.at[0])
        whole.start()
        whole.wait()
        return

    def pieces(j):
        return copy(send.at[:, j], send_hbm.at[:, j], sem.at[j])

    for j in range(dims.nj):
        parts = swap_blocks([read(g, j * rows, rows) for g in range(4)], dims.piece_width)
        for i in range(dims.ni):
            send[i, j] = parts[i]
        pieces(j).start()
    for j in range(dims.nj):
        pieces(j).wait()


def mode_constants(par_ref, dims):
    m = dims.mode_rows
    decay, rotation, dr, di, rr, ri = [par_ref[p * m : (p + 1) * m, :] for p in range(6)]
    step = jnp.exp(par_ref[6 * m : 6 * m + 1, :])
    log_mag = -step * decay
    turn = step * rotation
    c1r = step * (rr * dr - ri * di)
    c1i = step * (rr * di + ri * dr)
    c2r = c1r * dr - c1i * di
    c2i = c1r * di + c1i * dr
    return step, log_mag, turn, (c1r, c1i, c2r, c2i), (decay, rotation, dr, di, rr, ri)


def waves_kernel(dims, par_ref, zr_ref, zi_ref, vec_ref, cat_ref, wave):
    m, q = dims.mode_rows, dims.quarter
    step, log_mag, turn, coefs, _ = mode_constants(par_ref, dims)
    c1r, c1i, c2r, c2i = coefs
    mag = jnp.exp(log_mag)
    l1r, l1i = mag * jnp.cos(turn), mag * jnp.sin(turn)
    mag = jnp.exp(8.0 * log_mag)
    l32r, l32i = mag * jnp.cos(8.0 * turn), mag * jnp.sin(8.0 * turn)
    for _ in range(2):
        l32r, l32i = l32r * l32r - l32i * l32i, 2.0 * l32r * l32i
    for p, value in enumerate((l32r, l32i, c1r, c1i, c2r, c2i)):
        vec_ref[p * m : (p + 1) * m, :] = value
    sub = 4.0 * lax.broadcasted_iota(jnp.int32, (8, LANES), 0).astype(f32)

    def wide(x, k):
        return jnp.broadcast_to(x[k : k + 1], (8, LANES))

    for k in range(m):
        mag = jnp.exp(sub * log_mag[k : k + 1])
        zr, zi = mag * jnp.cos(sub * turn[k : k + 1]), mag * jnp.sin(sub * turn[k : k + 1])
        for r in range(4):
            zr_ref[r, 8 * k : 8 * k + 8, :] = zr
            zi_ref[r, 8 * k : 8 * k + 8, :] = zi
            ar, ai = wide(l1r, k), wide(l1i, k)
            zr, zi = zr * ar - zi * ai, zr * ai + zi * ar
    consts = [
        tuple(wide(x, k) for x in (l32r, l32i, 2 * c1r, 2 * c1i, 2 * c2r, 2 * c2i)) for k in range(m)
    ]
    group = fold_matrix(dims)
    for r in range(4):

        def time_step(t, zs):
            at = pl.multiple_of(t * 8, 8)
            k1 = jnp.zeros((8, LANES), f32)
            k2 = jnp.zeros((8, LANES), f32)
            out = []
            for k in range(m):
                zr, zi = zs[2 * k], zs[2 * k + 1]
                ar, ai, b1r, b1i, b2r, b2i = consts[k]
                k1 = k1 + (b1r * zr - b1i * zi)
                k2 = k2 + (b2r * zr - b2i * zi)
                out += [zr * ar - zi * ai, zr * ai + zi * ar]
            wave[pl.ds(at, 8), lanes(0)] = k1
            wave[pl.ds(at, 8), lanes(1)] = k2
            return tuple(out)

        start = []
        for k in range(m):
            start += [zr_ref[r, 8 * k : 8 * k + 8, :], zi_ref[r, 8 * k : 8 * k + 8, :]]
        lax.fori_loop(0, q // 8, time_step, tuple(start), unroll=4)
        for p in range(2):
            both = halves(over_groups(wave[0:q, lanes(p)], group))
            for part in range(2):
                cat_ref[part, :, lanes(2 * r + p)] = both[part]


def tables_kernel(dims, cat_ref, tab_hbm, inv_hbm, tw_hbm, spec_hbm, *scratch):
    tab, inv, tw, spec, wave, sem_out, sem_spec = scratch
    n, q = dims.length, dims.quarter

    def angles(b, _):
        at = pl.multiple_of(b * ROWS, ROWS)
        row = 2 * (lax.broadcasted_iota(jnp.int32, (ROWS, q), 0) + at) + 1
        col = 2 * lax.broadcasted_iota(jnp.int32, (ROWS, q), 1) + 1
        turn = ((row * col) & (8 * q - 1)).astype(f32) * (math.pi / (4 * q))
        for first, value in ((0, jnp.cos(turn)), (q, jnp.sin(turn))):
            for part, half in enumerate(halves(value)):
                tab[part, pl.ds(pl.multiple_of(first + at, ROWS), ROWS), :] = half
                inv[part, pl.ds(at, ROWS), first : first + q] = half
        row = 2 * (lax.broadcasted_iota(jnp.int32, (ROWS, LANES), 0) + at) + 1
        turn = row.astype(f32) * (math.pi / (2 * n))
        cos, sin = jnp.cos(turn), jnp.sin(turn)
        for p, value in enumerate((cos, sin, 1.0 - 2.0 * sin * sin, 2.0 * cos * sin)):
            tw[p, pl.ds(at, ROWS), :] = value
        return 0

    lax.fori_loop(0, q // ROWS, angles, 0)
    outs = [copy(tab, tab_hbm, sem_out.at[0]), copy(tw, tw_hbm, sem_out.at[1])]
    outs.append(copy(inv, inv_hbm, sem_out.at[2]))
    for out in outs:
        out.start()
    forth(tab, cat_ref, wave)

    def spectrum(b, _):
        at = pl.multiple_of(b * STEP, STEP)
        chunk, rows = place_of(b)
        for p in range(2):
            for k, (re, im) in enumerate(butterfly(wave, tw, at, p, 2, dims)):
                spec[chunk, k, rows, lanes(2 * p)] = re * (1.0 / n)
                spec[chunk, k, rows, lanes(2 * p + 1)] = im * (1.0 / n)
        return 0

    lax.fori_loop(0, q // STEP, spectrum, 0)
    outs.append(copy(spec, spec_hbm, sem_spec))
    outs[-1].start()
    for out in outs:
        out.wait()


def lanes(p):
    return slice(p * LANES, (p + 1) * LANES)


def over_groups(x, group):
    return mm(jnp.concatenate(halves(x), axis=1), jnp.concatenate([group, group], axis=0))


def place_of(b):
    return b // PER, pl.ds(pl.multiple_of(b % PER * STEP, STEP), STEP)


def product(table, operand):
    (high, low), (first, second) = table, operand
    return mm(
        jnp.concatenate([high, high, low], axis=1), jnp.concatenate([first, second, first], axis=0)
    )


def forth(tab, cat, wave):
    wave[...] = product((tab[0], tab[1]), (cat[0], cat[1]))


def twiddles(tw, at):
    c1, s1, c2, s2 = [tw[p, pl.ds(at, STEP), :] for p in range(4)]
    return (c2, s2), (c1, s1), None, (c1, -s1)


def times(a, b):
    if b is None:
        return a
    return a[0] * b[0] - a[1] * b[1], a[0] * b[1] + a[1] * b[0]


def plus(a, b):
    return a[0] + b[0], a[1] + b[1]


def minus(a, b):
    return a[0] - b[0], a[1] - b[1]


def turned(a):
    return -a[1], a[0]


def butterfly(wave, tw, at, p, count, dims):
    below = pl.multiple_of(dims.quarter + at, STEP)
    parts = []
    for r, twiddle in enumerate(twiddles(tw, at)):
        re = wave[pl.ds(at, STEP), lanes(r * count + p)]
        im = wave[pl.ds(below, STEP), lanes(r * count + p)]
        parts.append(times((re, -im), twiddle))
    even, odd = plus(parts[0], parts[2]), plus(parts[1], parts[3])
    even_too, odd_too = minus(parts[0], parts[2]), turned(minus(parts[1], parts[3]))
    return plus(even, odd), minus(even_too, odd_too), minus(even, odd), plus(even_too, odd_too)


def unbutterfly(parts, tw, at, cat, p, count, dims):
    even, odd = plus(parts[0], parts[2]), plus(parts[1], parts[3])
    even_too, odd_too = minus(parts[0], parts[2]), turned(minus(parts[1], parts[3]))
    sums = plus(even, odd), plus(even_too, odd_too), minus(even, odd), minus(even_too, odd_too)
    for r, twiddle in enumerate(twiddles(tw, at)):
        if twiddle is not None:
            twiddle = twiddle[0], -twiddle[1]
        re, im = times(sums[r], twiddle)
        for first, value in ((0, re), (dims.quarter, -im)):
            rows = pl.ds(pl.multiple_of(first + at, STEP), STEP)
            for part, half in enumerate(halves(value)):
                cat[part, rows, lanes(r * count + p)] = half


def back(inv, cat):
    return product((inv[0], inv[1]), (cat[0], cat[1]))


def column_sums(x):
    return jnp.sum(x.reshape(x.shape[0] // 8, 8, LANES), axis=0)


def lane_lengths(meta_ref, lens_refs, dims):
    lane = lane_ids((1, LANES)) // dims.chans
    row = jnp.zeros((1, LANES), jnp.int32)
    total = jnp.int32(0)
    for s in range(dims.all_seqs):
        source = s // dims.seqs
        value = lens_refs[source][s % dims.seqs]
        total = total + value
        row = jnp.where(lane == s ^ (meta_ref[0] * dims.seqs), value, row)
    return row, total.astype(f32)


def valid_rows(r, at, rows, lens):
    places = 4 * (lax.broadcasted_iota(jnp.int32, (rows, LANES), 0) + at) + r
    return (places < lens).astype(f32)


def forward_kernel(dims, meta_ref, r_ref, par_ref, tab_hbm, inv_hbm, tw_hbm, spec_hbm, *rest):
    lens_refs, rest = rest[: dims.ni], rest[dims.ni :]
    (send_hbm, mixed_hbm, normed_hbm, seen_hbm, stat_ref), rest = rest[:5], rest[5:]
    tab, inv, tw, spec, seen, x_sc, mix_sc, normed_sc, cat, wave, back_cat, send = rest[:12]
    sem_tab, sem_spec, sem_seen, sem_out, sem_send = rest[12:]
    m, q = dims.mode_rows, dims.quarter
    chunks = q // ROWS
    ins = [copy(tab_hbm, tab, sem_tab.at[0]), copy(tw_hbm, tw, sem_tab.at[1])]
    ins += [copy(spec_hbm.at[c], spec.at[c], sem_spec.at[c]) for c in range(chunks)]
    ins.append(copy(inv_hbm, inv, sem_tab.at[2]))
    for one in ins:
        one.start()
    lens, total = lane_lengths(meta_ref, lens_refs, dims)
    unpack_channels(r_ref, x_sc, dims)
    classes = range(4)

    def add_up(b, acc):
        at = pl.multiple_of(b * ROWS, ROWS)
        for r in classes:
            acc = acc + column_sums(x_sc[r, pl.ds(at, ROWS), :] * valid_rows(r, at, ROWS, lens))
        return acc

    zero = jnp.zeros((8, LANES), f32)
    acc = lax.fori_loop(0, q // ROWS, add_up, zero)
    average = fold(jnp.sum(acc, axis=0, keepdims=True), dims) / total

    def add_squares(b, acc):
        at = pl.multiple_of(b * ROWS, ROWS)
        for r in classes:
            x = (x_sc[r, pl.ds(at, ROWS), :] - average) * valid_rows(r, at, ROWS, lens)
            acc = acc + column_sums(x * x)
        return acc

    acc = lax.fori_loop(0, q // ROWS, add_squares, zero)
    variance = fold(jnp.sum(acc, axis=0, keepdims=True), dims) / total
    inv_scale = lax.rsqrt(variance + EPS)
    gain = par_ref[6 * m + 1 : 6 * m + 2, :]
    shift = par_ref[6 * m + 2 : 6 * m + 3, :]
    skip = par_ref[6 * m + 3 : 6 * m + 4, :]
    stat_ref[0:1, :] = inv_scale
    stat_ref[1:2, :] = jnp.broadcast_to(total, (1, LANES))
    stat_ref[2:3, :] = lens.astype(f32)
    stat_ref[3:8, :] = jnp.zeros((5, LANES), f32)
    first_row = lax.broadcasted_iota(jnp.int32, (ROWS, LANES), 0) == 0

    def normalize(b, last):
        at = pl.multiple_of(b * ROWS, ROWS)
        mixed = []
        for r in classes:
            normed = (x_sc[r, pl.ds(at, ROWS), :] - average) * inv_scale
            mixed.append((gain * normed + shift) * valid_rows(r, at, ROWS, lens))
            normed_sc[r, pl.ds(at, ROWS), :] = normed
            mix_sc[r, pl.ds(at, ROWS), :] = mixed[r]
        earlier = jnp.where(first_row, last, pltpu.roll(mixed[3], 1, 0))
        for r in classes:
            liquid = mixed[r] * (earlier if r == 0 else mixed[r - 1])
            for p, value in enumerate((mixed[r], liquid)):
                for part, half in enumerate(halves(value)):
                    cat[part, pl.ds(at, ROWS), lanes(2 * r + p)] = half
        return mixed[3][ROWS - 1 :, :]

    lax.fori_loop(0, q // ROWS, normalize, jnp.zeros((1, LANES), f32))
    outs = [copy(mix_sc, mixed_hbm, sem_out.at[0]), copy(normed_sc, normed_hbm, sem_out.at[1])]
    for out in outs:
        out.start()
    ins[0].wait()
    forth(tab, cat, wave)
    ins[1].wait()
    for c in range(chunks):
        ins[2 + c].wait()

        def multiply(b, _):
            at = pl.multiple_of(b * STEP, STEP)
            chunk, rows = place_of(b)
            mixed = butterfly(wave, tw, at, 0, 2, dims)
            liquid = butterfly(wave, tw, at, 1, 2, dims)
            parts = []
            for k in range(4):
                for p, value in enumerate(mixed[k] + liquid[k]):
                    seen[chunk, k, rows, lanes(p)] = value
                kr, ki, lr, li = [spec[chunk, k, rows, lanes(p)] for p in range(4)]
                parts.append(plus(times(mixed[k], (kr, ki)), times(liquid[k], (lr, li))))
            unbutterfly(parts, tw, at, back_cat, 0, 1, dims)
            return 0

        lax.fori_loop(PER * c, PER * (c + 1), multiply, 0)
        outs.append(copy(seen.at[c], seen_hbm.at[c], sem_seen.at[c]))
        outs[-1].start()
    ins[-1].wait()

    value = back(inv, back_cat)
    for r in classes:
        x_sc[r] = value[:, lanes(r)] + skip * mix_sc[r]
    pack_channels(
        lambda r, at, size: x_sc[r, pl.ds(at, size), :], send, send_hbm, sem_send, dims
    )
    for out in outs:
        out.wait()


def gate_kernel(dims, meta_ref, r_ref, x_ref, w_ref, b_ref, ct_ref, *rest):
    (send_hbm, out_ref, act_hbm, gj_hbm, bias_ref, wsend_hbm), scratch = rest[:6], rest[6:]
    resp, act, joined, gj, gact, send, weight, wsend, sem_out, sem_send, sem_weight = scratch
    tokens = dims.seqs * dims.places
    width = dims.width
    places = dims.places

    tiles = range(width // LANES)
    if dims.fast:
        unpack_tokens(r_ref, resp, dims)
    else:
        for t in tiles:
            resp[t] = r_ref[:, lanes(t)]
    c0 = math.sqrt(2.0 / math.pi)
    c1 = 0.044715
    rows = 32

    def gelu(b, _):
        at = pl.multiple_of(b * rows, rows)
        for tile in tiles:
            r = resp[tile, pl.ds(at, rows), :]
            t = jnp.tanh(c0 * (r + c1 * r * r * r))
            act[pl.ds(at, rows), lanes(tile)] = (0.5 * r * (1.0 + t)).astype(bf16)
            slope = 0.5 * (1.0 + t) + 0.5 * r * (1.0 - t * t) * (c0 * (1.0 + 3.0 * c1 * r * r))
            resp[tile, pl.ds(at, rows), :] = slope
        return 0

    lax.fori_loop(0, tokens // rows, gelu, 0)
    outs = [copy(act, act_hbm, sem_out.at[0]), copy(gj, gj_hbm, sem_out.at[1])]
    outs[0].start()
    joined[...] = mm(act[...], w_ref[...])
    bias = b_ref[...]
    half = min(16, places)
    for b in range(dims.seqs):

        def gate(k, sums):
            at = pl.multiple_of(k * half, half)
            tok = pl.multiple_of(b * places + k * half, half)
            value = joined[pl.ds(tok, half), :width] + bias[:, :width]
            s = jax.nn.sigmoid(joined[pl.ds(tok, half), width:] + bias[:, width:])
            x = x_ref[b, pl.ds(at, half), :].astype(f32)
            g = ct_ref[b, pl.ds(at, half), :].astype(f32)
            out_ref[b, pl.ds(at, half), :] = (x + value * s).astype(bf16)
            gs = g * s
            first = gs.astype(bf16)
            second = (gs * value * (1.0 - s)).astype(bf16)
            gj[pl.ds(tok, half), :width] = first
            gj[pl.ds(tok, half), width:] = second
            first = jnp.sum(first.astype(f32).reshape(half // 8, 8, width), axis=0)
            second = jnp.sum(second.astype(f32).reshape(half // 8, 8, width), axis=0)
            return sums[0] + first, sums[1] + second

        if b == 0:
            zero = jnp.zeros((8, width), f32)
            sums = (zero, zero)
        sums = lax.fori_loop(0, places // half, gate, sums)
    outs[1].start()
    sums = [jnp.sum(s, axis=0, keepdims=True) for s in sums]
    for p, total in enumerate(sums):
        for t in tiles:
            row = p * (width // LANES) + t
            bias_ref[row : row + 1, :] = total[:, lanes(t)]
    weight_half(dims, meta_ref, 1 - meta_ref[1], act, gj, weight)
    for i in range(dims.ni):
        for z in range(dims.nz):
            for u in range(dims.units):
                wsend[i, z, u, :, :] = weight_unit(dims, meta_ref, weight, i, z, u)
            wsend[i, z, dims.units, :, :] = bias_ref[...]
        outs.append(copy(wsend.at[i], wsend_hbm.at[i], sem_weight.at[i]))
        outs[-1].start()
    grad = lax.dot_general(
        gj[...], w_ref[...], (((1,), (1,)), ((), ())), preferred_element_type=f32
    )
    for t in tiles:
        gact[t] = grad[:, lanes(t)]
    if dims.fast:

        def read(tile, rows):
            return gact[tile, rows, :] * resp[tile, rows, :]

        def put(piece, value):
            send[piece] = value

        def tile_copy(tile):
            some = pl.ds(tile * dims.groups, dims.groups)
            return copy(send.at[some], send_hbm.at[some], sem_send.at[tile])

        pack_tokens(read, put, dims, lambda tile: tile_copy(tile).start())
        outs += [tile_copy(tile) for tile in tiles]
    else:
        for t in tiles:
            send[:, lanes(t)] = gact[t] * resp[t]
        outs.append(copy(send, send_hbm, sem_send.at[0]))
        outs[-1].start()
    for out in outs:
        out.wait()


def weight_half(dims, meta_ref, core, act, gj, weight):
    half = dims.width // 2
    some = act[:, pl.ds(pl.multiple_of(core * half, half), half)]
    weight[...] = lax.dot_general(
        some, gj[...], (((0,), (0,)), ((), ())), preferred_element_type=f32
    )


def weight_unit(dims, meta_ref, weight, i, z, u):
    tiles = 2 * dims.width // LANES
    owner = (meta_ref[0] ^ i) * dims.nz + (meta_ref[2] ^ z)
    if dims.units % tiles == 0:
        row = owner * (dims.units // tiles) + u // tiles
        cols = lanes(u % tiles)
    else:
        unit = owner * dims.units + u
        row = unit // tiles
        cols = pl.ds(pl.multiple_of(unit % tiles * LANES, LANES), LANES)
    return weight[pl.ds(pl.multiple_of(row * 8, 8), 8), cols]


def backward_kernel(dims, r_ref, par_ref, *rest):
    ins_hbm, (stat_ref, send_hbm, grad_hbm, sums_ref) = rest[:6], rest[6:10]
    tab, inv, tw, spec, grads, mix_sc, normed_sc, g_sc, up_sc, cat, wave, back_cat = rest[10:22]
    lead_sc, liquid_sc, send, sem_in, sem_spec, sem_send, sem_grad = rest[22:]
    tab_hbm, inv_hbm, tw_hbm, spec_hbm, mixed_hbm, normed_hbm = ins_hbm
    m, q = dims.mode_rows, dims.quarter
    ins = [
        copy(mixed_hbm, mix_sc, sem_in.at[0]),
        copy(tab_hbm, tab, sem_in.at[1]),
        copy(tw_hbm, tw, sem_in.at[2]),
        copy(normed_hbm, normed_sc, sem_in.at[3]),
        copy(inv_hbm, inv, sem_in.at[4]),
    ]
    chunks = q // ROWS
    for c in range(chunks):
        ins.insert(3 + c, copy(spec_hbm.at[c], spec.at[c], sem_spec.at[c]))
    for one in ins:
        one.start()
    unpack_channels(r_ref, g_sc, dims)
    gain = par_ref[6 * m + 1 : 6 * m + 2, :]
    skip = par_ref[6 * m + 3 : 6 * m + 4, :]
    inv_scale = stat_ref[0:1, :]
    total = stat_ref[1:2, :]
    lens = stat_ref[2:3, :].astype(jnp.int32)
    zero = jnp.zeros((8, LANES), f32)
    classes = range(4)
    ins[0].wait()

    def gather(b, acc):
        at = pl.multiple_of(b * ROWS, ROWS)
        for r in classes:
            g = g_sc[r, pl.ds(at, ROWS), :]
            for part, half in enumerate(halves(g)):
                cat[part, pl.ds(at, ROWS), lanes(r)] = half
            acc = acc + column_sums(g * mix_sc[r, pl.ds(at, ROWS), :])
        return acc

    skip_acc = lax.fori_loop(0, q // ROWS, gather, zero)
    ins[1].wait()
    forth(tab, cat, wave)
    ins[2].wait()
    outs = []
    for c in range(chunks):
        ins[3 + c].wait()

        def multiply(b, _):
            at = pl.multiple_of(b * STEP, STEP)
            chunk, rows = place_of(b)
            grad = butterfly(wave, tw, at, 0, 1, dims)
            for k in range(4):
                for p in range(2):
                    grads[chunk, k, rows, lanes(p)] = grad[k][p]
            for p in range(2):
                products(grad, spec, tw, b, back_cat, p, dims)
            return 0

        lax.fori_loop(PER * c, PER * (c + 1), multiply, 0)
        outs.append(copy(grads.at[c], grad_hbm.at[c], sem_grad.at[c]))
        outs[-1].start()
    for one in ins[3 + chunks :]:
        one.wait()

    value = back(inv, back_cat)
    for r in classes:
        lead_sc[r] = value[:, lanes(2 * r)]
        liquid_sc[r] = value[:, lanes(2 * r + 1)]
        up_sc[r] = value[:, lanes(2 * r + 1)] * mix_sc[r]

    row = lax.broadcasted_iota(jnp.int32, (ROWS, LANES), 0)
    blank = jnp.zeros((1, LANES), f32)
    gain_acc, shift_acc = zero, zero
    for at in range(0, q, ROWS):
        rows = slice(at, at + ROWS)
        for r in classes:
            if r == 0:
                before = blank if at == 0 else mix_sc[3, at - 1 : at, :]
                earlier = jnp.where(row == 0, before, pltpu.roll(mix_sc[3, rows, :], 1, 0))
            else:
                earlier = mix_sc[r - 1, rows, :]
            if r == 3:
                after = blank if at + ROWS == q else up_sc[0, at + ROWS : at + ROWS + 1, :]
                up = jnp.where(row == ROWS - 1, after, pltpu.roll(up_sc[0, rows, :], ROWS - 1, 0))
            else:
                up = up_sc[r + 1, rows, :]
            masked = lead_sc[r, rows, :] + skip * g_sc[r, rows, :] + liquid_sc[r, rows, :] * earlier
            masked = (masked + up) * valid_rows(r, at, ROWS, lens)
            g_sc[r, rows, :] = masked
            gain_acc = gain_acc + column_sums(masked * normed_sc[r, rows, :])
            shift_acc = shift_acc + column_sums(masked)

    def whole(acc):
        return fold(jnp.sum(acc, axis=0, keepdims=True), dims)

    gain_sum, shift_sum, skip_sum = whole(gain_acc), whole(shift_acc), whole(skip_acc)
    scale = gain * inv_scale
    shift_mean = shift_sum / total
    gain_mean = gain_sum / total

    def read(r, at, size):
        normed = normed_sc[r, pl.ds(at, size), :]
        value = g_sc[r, pl.ds(at, size), :] - shift_mean - normed * gain_mean
        return value * scale * valid_rows(r, at, size, lens)

    sums_ref[...] = jnp.zeros_like(sums_ref)
    for p, value in enumerate((gain_sum, shift_sum, skip_sum)):
        sums_ref[p : p + 1, :] = value
    pack_channels(read, send, send_hbm, sem_send, dims)
    for out in outs:
        out.wait()


def products(grad, ref, tw, b, cat, p, dims):
    chunk, rows = place_of(b)
    parts = []
    for k in range(4):
        re = ref[chunk, k, rows, lanes(2 * p)]
        im = ref[chunk, k, rows, lanes(2 * p + 1)]
        parts.append(times(grad[k], (re, -im)))
    unbutterfly(parts, tw, pl.multiple_of(b * STEP, STEP), cat, p, 2, dims)


def modes_kernel(dims, par_ref, inv_hbm, tw_hbm, seen_hbm, grad_hbm, sums_ref, *rest):
    zr_ref, zi_ref, vec_ref, small_ref, inv, tw, seen, grads, back_cat, dk, sem, sem_in = rest
    n, m, q = dims.length, dims.mode_rows, dims.quarter
    chunks = q // ROWS
    ins = [copy(tw_hbm, tw, sem.at[0])]
    for c in range(chunks):
        ins.append(copy(seen_hbm.at[c], seen.at[c], sem_in.at[0, c]))
        ins.append(copy(grad_hbm.at[c], grads.at[c], sem_in.at[1, c]))
    ins.append(copy(inv_hbm, inv, sem.at[1]))
    for one in ins:
        one.start()
    zero = jnp.zeros((8, LANES), f32)
    classes = range(4)
    ins[0].wait()
    for c in range(chunks):
        ins[1 + 2 * c].wait()
        ins[2 + 2 * c].wait()

        def multiply(b, _):
            chunk, rows = place_of(b)
            grad = [tuple(grads[chunk, k, rows, lanes(p)] for p in range(2)) for k in range(4)]
            for p in range(2):
                products(grad, seen, tw, b, back_cat, p, dims)
            return 0

        lax.fori_loop(PER * c, PER * (c + 1), multiply, 0)
    ins[-1].wait()
    group = fold_matrix(dims)

    value = back(inv, back_cat) * (1.0 / n)
    dk[...] = over_groups(jnp.concatenate([value[:, lanes(p)] for p in range(8)], axis=0), group)

    step, log_mag, turn, _, params = mode_constants(par_ref, dims)
    decay, rotation, dr, di, rr, ri = params
    l32r, l32i, c1r, c1i, c2r, c2i = [vec_ref[p * m : (p + 1) * m, :] for p in range(6)]
    sub = 4.0 * lax.broadcasted_iota(jnp.int32, (8, LANES), 0).astype(f32)
    sums = [[] for _ in range(8)]
    for first in range(0, m, 2):
        some = range(first, min(m, first + 2))
        ratio = [
            (
                jnp.broadcast_to(l32r[k : k + 1], (8, LANES)),
                jnp.broadcast_to(l32i[k : k + 1], (8, LANES)),
            )
            for k in some
        ]
        sofar = [zero] * (8 * len(ratio))
        for r in classes:

            def mode_step(t, carry):
                at = pl.multiple_of(t * 8, 8)
                d1 = dk[pl.ds(pl.multiple_of(2 * r * q + at, 8), 8), :]
                d2 = dk[pl.ds(pl.multiple_of((2 * r + 1) * q + at, 8), 8), :]
                place = sub + (32 * t + r).astype(f32)
                e1 = d1 * place
                e2 = d2 * place
                out = []
                for k, (ar, ai) in enumerate(ratio):
                    zr, zi, *acc = carry[10 * k : 10 * (k + 1)]
                    out += [zr * ar - zi * ai, zr * ai + zi * ar]
                    for p, d in enumerate((d1, d2, e1, e2)):
                        out += [acc[2 * p] + d * zr, acc[2 * p + 1] + d * zi]
                return tuple(out)

            carry = []
            for at, k in enumerate(some):
                carry += [zr_ref[r, 8 * k : 8 * k + 8, :], zi_ref[r, 8 * k : 8 * k + 8, :]]
                carry += sofar[8 * at : 8 * at + 8]
            carry = lax.fori_loop(0, q // 8, mode_step, tuple(carry), unroll=4)
            sofar = [v for k in range(len(ratio)) for v in carry[10 * k + 2 : 10 * k + 10]]
        for k in range(len(ratio)):
            for p in range(8):
                sums[p].append(jnp.sum(sofar[8 * k + p], axis=0, keepdims=True))
    a1r, a1i, a2r, a2i, e1r, e1i, e2r, e2i = [
        jnp.concatenate(s, axis=0) if len(s) > 1 else s[0] for s in sums
    ]
    btr = c1r * e1r - c1i * e1i + c2r * e2r - c2i * e2i
    bti = c1r * e1i + c1i * e1r + c2r * e2i + c2i * e2r
    d2r = dr * dr - di * di
    d2i = 2.0 * dr * di
    erd = step * (a1r * dr - a1i * di + a2r * d2r - a2i * d2i)
    eri = step * (a1r * di + a1i * dr + a2r * d2i + a2i * d2r)
    tr = a1r + 2.0 * (a2r * dr - a2i * di)
    ti = a1i + 2.0 * (a2r * di + a2i * dr)
    edr = step * (rr * tr - ri * ti)
    edi = step * (rr * ti + ri * tr)
    by_step = 2.0 * (c1r * a1r - c1i * a1i + c2r * a2r - c2i * a2i) + 2.0 * step * (
        -decay * btr - rotation * bti
    )
    small_ref[...] = jnp.zeros_like(small_ref)
    answers = (-2.0 * step * btr, -2.0 * step * bti, 2.0 * edr, -2.0 * edi, 2.0 * erd, -2.0 * eri)
    for p, value in enumerate(answers):
        small_ref[p * m : (p + 1) * m, :] = value
    small_ref[6 * m : 6 * m + 1, :] = fold(jnp.sum(by_step, axis=0, keepdims=True), dims)
    small_ref[6 * m + 1 : 6 * m + 4, :] = sums_ref[0:3, :]


def first_add_kernel(dims, meta_ref, act_hbm, gj_hbm, bias_ref, other_hbm, *refs):
    out_refs, (act, gj, weight, other, sem_in, sem) = refs[: dims.ni], refs[dims.ni :]
    ins = [copy(act_hbm, act, sem_in.at[0]), copy(gj_hbm, gj, sem_in.at[1])]
    others = [copy(other_hbm.at[i], other.at[i], sem.at[i]) for i in range(dims.ni)]
    for one in ins + others:
        one.start()
    for one in ins:
        one.wait()
    weight_half(dims, meta_ref, meta_ref[1], act, gj, weight)
    for i in range(dims.ni):
        others[i].wait()
        for z in range(dims.nz):
            for u in range(dims.units):
                unit = weight_unit(dims, meta_ref, weight, i, z, u)
                out_refs[i][z, u] = unit + other[i, z, u]
            out_refs[i][z, dims.units] = bias_ref[...] + other[i, z, dims.units]


def order_kernel(sums_ref, out_ref):
    out_ref[...] = sums_ref[...]


def add_kernel(count, *refs):
    for p, out_ref in enumerate(refs[count:]):
        total = refs[0][p]
        for ref in refs[1:count]:
            total = total + ref[p]
        out_ref[...] = total


def last_add_kernel(dims, count, small_ref, *refs):
    units_ref, bias_ref = refs[count:]

    def unit(u):
        total = refs[0][u]
        for ref in refs[1:count]:
            total = total + ref[u]
        return total

    for u in range(dims.units):
        units_ref[u] = unit(u)
    for t in range(dims.small_rows // 8):
        units_ref[dims.units + t] = small_ref[8 * t : 8 * t + 8, :]
    bias = unit(dims.units)
    for t in range(2 * dims.width // LANES):
        bias_ref[:, lanes(t)] = bias[t : t + 1, :]


def stack_kernel(*refs):
    for k, ref in enumerate(refs[:-1]):
        refs[-1][k] = ref[...]


def input_kernel(dims, r_ref, ct_ref, grad_ref, grad):
    unpack_tokens(r_ref, grad, dims, False)
    for b in range(dims.seqs):
        for t in range(dims.width // LANES):
            value = grad[t, b * dims.places : (b + 1) * dims.places, :]
            grad_ref[b, :, lanes(t)] = value + ct_ref[b, :, lanes(t)].astype(f32)


def finish_kernel(dims, meta_ref, *refs):
    ni, nz, m = dims.ni, dims.nz, dims.mode_rows
    near = refs[:ni], refs[ni : 2 * ni]
    far = refs[2 * ni : 3 * ni], refs[3 * ni : 4 * ni]
    weight_ref, *small_hbm = refs[4 * ni : 4 * ni + 11]
    *small_refs, rows, small, sem, sem_small = refs[4 * ni + 11 :]
    me, core, me_z = meta_ref[0], meta_ref[1], meta_ref[2]
    tiles = 2 * dims.width // LANES
    per = 8 * dims.units // tiles
    copies = []
    for half, side in ((0, core), (1, 1 - core)):
        for i in range(ni):
            for z in range(nz):
                piece = near[half][i] if z == 0 else far[half][i].at[z - 1]
                for u in range(dims.units):
                    at = pl.multiple_of((me_z ^ z) * per + u // tiles * 8, 8)
                    rows[half, i, pl.ds(at, 8), lanes(u % tiles)] = piece[u]
                value = piece[dims.units :].reshape(dims.small_rows, LANES)
                small[half, i, me_z ^ z] = value
            at = pl.multiple_of((side * ni + (me ^ i)) * nz * per, nz * per)
            target = weight_ref.at[pl.ds(at, nz * per), :]
            copies.append(copy(rows.at[half, i], target, sem.at[half, i]))
            copies[-1].start()
    first = core == 0
    for i in range(ni):
        parts = []
        for z in range(nz):
            a, b = small[0, i, z], small[1, i, z]
            parts += [jnp.where(first, a, b), jnp.where(first, b, a)]
        parts = swap_blocks(parts, dims.chans)
        cols = pl.ds(pl.multiple_of((me ^ i) * LANES, LANES), LANES)
        for q in range(dims.groups):
            for p in range(6):
                small_refs[p][q * m : q * m + m, cols] = parts[q][p * m : p * m + m, :]
        for p in range(4):
            small_refs[6 + p][:, cols] = parts[0][6 * m + p : 6 * m + p + 1, :]
    for p, (ref, hbm) in enumerate(zip(small_refs, small_hbm)):
        copies.append(copy(ref, hbm, sem_small.at[p]))
        copies[-1].start()
    for one in copies:
        one.wait()


def call(kernel, out_shape, in_specs, scratch, limit, us, out_specs=None):
    cost = pl.CostEstimate(flops=int(us * 1.1e9), bytes_accessed=int(us * 3e6), transcendentals=0)
    if out_specs is None:
        out_specs = jax.tree.map(lambda _: VMEM, out_shape)
    else:
        out_shape = tuple(
            pltpu.HBM(out.shape, out.dtype) if spec is HBM else out
            for out, spec in zip(out_shape, out_specs)
        )

    def run(*args):
        args = [
            pltpu.with_memory_space_constraint(x, pltpu.HBM) if spec is HBM else x
            for x, spec in zip(args, in_specs)
        ]
        return pl.pallas_call(
            kernel,
            out_shape=out_shape,
            in_specs=in_specs,
            out_specs=out_specs,
            scratch_shapes=scratch,
            compiler_params=pltpu.CompilerParams(vmem_limit_bytes=limit << 20),
            cost_estimate=cost,
        )(*args)

    return run


def shape(*dims, dtype=f32):
    return jax.ShapeDtypeStruct(dims, dtype)


def local(
    mesh_shape,
    inputs,
    lengths,
    norm_gain,
    norm_shift,
    log_step,
    decay_rate,
    rotation,
    drive_real,
    drive_imag,
    read_real,
    read_imag,
    skip_gain,
    glu_weight,
    glu_bias,
    out_cotangent,
):
    modes = decay_rate.shape[0]
    dims = Dims(inputs.shape, modes, mesh_shape)
    n, nd, m, hc = dims.length, dims.devices, dims.mode_rows, dims.chans
    core = lax.axis_index("core")
    owner = lax.axis_index(ALL)
    meta = jnp.stack([lax.axis_index("batch"), core, lax.axis_index("z")]).astype(jnp.int32)

    def exchange(x):
        return lax.all_to_all(x, ALL, 0, 0, tiled=True)

    some = dims.places // 4

    def to_channels(x):
        x = x.reshape(dims.seqs, some, 4, nd, hc).transpose(3, 2, 1, 0, 4)
        x = exchange(x.reshape(nd, dims.places, dims.piece_width))
        x = x.reshape(dims.ni, dims.nj, 4, some, dims.piece_width).transpose(2, 1, 3, 0, 4)
        x = x.reshape(n, dims.all_seqs * hc)
        return jnp.pad(x, ((0, 0), (0, LANES - x.shape[1])))

    def to_tokens(x):
        x = x[:, : dims.all_seqs * hc].reshape(4, dims.nj, some, dims.ni, dims.piece_width)
        x = x.transpose(3, 1, 0, 2, 4).reshape(nd, dims.places, dims.piece_width)
        x = exchange(x).reshape(nd, 4, some, dims.seqs, hc).transpose(3, 2, 1, 0, 4)
        return x.reshape(dims.seqs * dims.places, dims.width)

    table = jnp.stack([decay_rate, rotation, drive_real, drive_imag, read_real, read_imag])
    table = lax.dynamic_slice_in_dim(table, owner * hc, hc, 2)
    table = jnp.pad(table, ((0, 0), (0, m * dims.groups - modes), (0, 0)))
    table = table.reshape(6, dims.groups, m, hc).transpose(0, 2, 1, 3).reshape(6 * m, LANES)
    rest = jnp.stack([log_step, norm_gain, norm_shift, skip_gain])
    rest = lax.dynamic_slice_in_dim(rest, owner * hc, hc, 1)
    params = jnp.concatenate([table, jnp.tile(rest, (1, dims.groups))], axis=0)
    params, meta = lax.optimization_barrier((params, meta))

    pieces = (nd, dims.piece_rows, LANES) if dims.fast else (n, LANES)
    tokens = dims.seqs * dims.places
    token_pieces = (nd, dims.piece_rows, LANES) if dims.fast else (tokens, dims.width)
    bind = functools.partial
    q = dims.quarter
    tab = (2, 2 * q, q)
    inv = (2, q, 2 * q)
    chunks = q // ROWS
    tw = (4, q, LANES)
    four = (chunks, 4, ROWS, 4 * LANES)
    two = (chunks, 4, ROWS, 2 * LANES)
    sent = (dims.ni, dims.nj, dims.piece_rows, LANES) if dims.fast else (n, LANES)
    plain = (4, q, LANES)
    by_tile = (dims.width // LANES, dims.seqs * dims.places, LANES)

    def vmem(*sizes, dtype=f32):
        return pltpu.VMEM(sizes, dtype)

    if dims.fast:
        packed = call(
            bind(pack_kernel, dims), shape(*pieces), [VMEM], [vmem(*by_tile)], 4, 1.5
        )(inputs)
        received = exchange(packed)
    else:
        received = to_channels(inputs.astype(f32))

    zr, zi, vec, waves = call(
        bind(waves_kernel, dims),
        (
            shape(4, 8 * m, LANES),
            shape(4, 8 * m, LANES),
            shape(6 * m, LANES),
            shape(2, q, 8 * LANES, dtype=bf16),
        ),
        [VMEM],
        [vmem(q, 2 * LANES)],
        4,
        3,
    )(params)
    lengths, waves = lax.optimization_barrier((lengths, waves))
    tables, inverse, twiddle, spec = call(
        bind(tables_kernel, dims),
        (shape(*tab, dtype=bf16), shape(*inv, dtype=bf16), shape(*tw), shape(*four)),
        [VMEM],
        [
            vmem(*tab, dtype=bf16),
            vmem(*inv, dtype=bf16),
            vmem(*tw),
            vmem(*four),
            vmem(2 * q, 8 * LANES),
            DMA((3,)),
            DMA(()),
        ],
        10,
        6,
        (HBM, HBM, HBM, HBM),
    )(waves)

    def swap(x, axis, by):
        return lax.ppermute(x, axis, [(i, i ^ by) for i in range(lax.axis_size(axis))])

    def everyone(x, axis, size):
        return [x] + [swap(x, axis, s) for s in range(1, size)]

    lens = everyone(lengths, "batch", dims.ni)
    send, mixed, normed, seen, stat = call(
        bind(forward_kernel, dims),
        (shape(*sent), shape(*plain), shape(*plain), shape(*four), shape(8, LANES)),
        [SMEM, VMEM, VMEM] + [HBM] * 4 + [SMEM] * dims.ni,
        [
            vmem(*tab, dtype=bf16),
            vmem(*inv, dtype=bf16),
            vmem(*tw),
            vmem(*four),
            vmem(*four),
            vmem(*plain),
            vmem(*plain),
            vmem(*plain),
            vmem(2, q, 8 * LANES, dtype=bf16),
            vmem(2 * q, 8 * LANES),
            vmem(2, 2 * q, 4 * LANES, dtype=bf16),
            vmem(*sent),
            DMA((3,)),
            DMA((chunks,)),
            DMA((chunks,)),
            DMA((2,)),
            DMA((dims.nj,)),
        ],
        18,
        7,
        (HBM, HBM, HBM, HBM, VMEM),
    )(meta, received, params, tables, inverse, twiddle, spec, *lens)
    send = send.reshape(pieces)

    received = exchange(send) if dims.fast else to_tokens(send)
    wide = (tokens, dims.width)
    wider = (tokens, 2 * dims.width)
    unit = (dims.units + 1, 8, LANES)
    part = (dims.ni, dims.nz) + unit
    tiles = 2 * dims.width // LANES
    send, result, act, gj, bias, wsend = call(
        bind(gate_kernel, dims),
        (
            shape(*token_pieces),
            shape(*inputs.shape, dtype=bf16),
            shape(*wide, dtype=bf16),
            shape(*wider, dtype=bf16),
            shape(tiles, LANES),
            shape(*part),
        ),
        [SMEM] + [VMEM] * 5,
        [
            vmem(*by_tile),
            vmem(*wide, dtype=bf16),
            vmem(*wider),
            vmem(*wider, dtype=bf16),
            vmem(*by_tile),
            vmem(*token_pieces),
            vmem(dims.width // 2, 2 * dims.width),
            vmem(*part),
            DMA((2,)),
            DMA((max(1, dims.width // LANES),)),
            DMA((dims.ni,)),
        ],
        11,
        5,
        (HBM, VMEM, HBM, HBM, VMEM, HBM),
    )(meta, received, inputs, glu_weight, glu_bias.reshape(1, -1), out_cotangent)
    received = exchange(send) if dims.fast else to_channels(
        send.reshape(dims.seqs, dims.places, dims.width)
    )

    parts = call(
        bind(first_add_kernel, dims),
        (shape(dims.nz, *unit),) * dims.ni,
        [SMEM, HBM, HBM, VMEM, ANY],
        [
            vmem(*wide, dtype=bf16),
            vmem(*wider, dtype=bf16),
            vmem(dims.width // 2, 2 * dims.width),
            vmem(*part),
            DMA((2,)),
            DMA((dims.ni,)),
        ],
        6,
        0.1,
    )(meta, act, gj, bias, swap(wsend, "core", 1))
    parts = [parts[0]] + [swap(parts[s], "batch", s) for s in range(1, dims.ni)]
    send, grads, sums = call(
        bind(backward_kernel, dims),
        (shape(*sent), shape(*two), shape(8, LANES)),
        [VMEM, VMEM] + [HBM] * 6 + [VMEM],
        [
            vmem(*tab, dtype=bf16),
            vmem(*inv, dtype=bf16),
            vmem(*tw),
            vmem(*four),
            vmem(*two),
            vmem(*plain),
            vmem(*plain),
            vmem(*plain),
            vmem(*plain),
            vmem(2, q, 4 * LANES, dtype=bf16),
            vmem(2 * q, 4 * LANES),
            vmem(2, 2 * q, 8 * LANES, dtype=bf16),
            vmem(*plain),
            vmem(*plain),
            vmem(*sent),
            DMA((5,)),
            DMA((chunks,)),
            DMA((dims.nj,)),
            DMA((chunks,)),
        ],
        18,
        9,
        (HBM, HBM, VMEM),
    )(received, params, tables, inverse, twiddle, spec, mixed, normed, stat)
    send = send.reshape(pieces)

    send, parts = lax.optimization_barrier((send, parts))
    parts = call(
        bind(add_kernel, dims.ni), (shape(*unit),) * dims.nz, [VMEM] * dims.ni, [], 2, 0.1
    )(*parts)
    sums, parts = lax.optimization_barrier((sums, parts))
    sums = call(order_kernel, shape(8, LANES), [VMEM], [], 1, 6)(sums)
    send, sums = lax.optimization_barrier((send, sums))
    received = exchange(send) if dims.fast else to_tokens(send)
    parts = [parts[0]] + [swap(parts[s], "z", s) for s in range(1, dims.nz)]
    small = call(
        bind(modes_kernel, dims),
        shape(dims.small_rows, LANES),
        [VMEM] + [HBM] * 4 + [VMEM] * 4,
        [
            vmem(*inv, dtype=bf16),
            vmem(*tw),
            vmem(*four),
            vmem(*two),
            vmem(2, 2 * q, 8 * LANES, dtype=bf16),
            vmem(8 * q, LANES),
            DMA((2,)),
            DMA((2, chunks)),
        ],
        12,
        6,
    )(params, inverse, twiddle, seen, grads, sums, zr, zi, vec)

    units = (dims.units + dims.small_rows // 8, 8, LANES)
    units, bias_grad = call(
        bind(last_add_kernel, dims, dims.nz),
        (shape(*units), shape(1, 2 * dims.width)),
        [VMEM] * (1 + dims.nz),
        [],
        2,
        0.7,
    )(small, *parts)
    pieces_z = everyone(units, "z", dims.nz)
    near = everyone(units, "batch", dims.ni)
    pieces_z, near = lax.optimization_barrier((pieces_z, near))
    near_too = [swap(x, "core", 1) for x in near]
    planes = call(
        stack_kernel, shape(dims.nz - 1, *units.shape), [VMEM] * (dims.nz - 1), [], 2, 0.7
    )(*pieces_z[1:])
    planes = everyone(planes, "batch", dims.ni)
    if dims.fast:
        grad_in = call(
            bind(input_kernel, dims), shape(*inputs.shape), [VMEM] * 2, [vmem(*by_tile)], 4, 1.5
        )(received, out_cotangent)
    else:
        grad_in = out_cotangent.astype(f32) + received.reshape(inputs.shape)
    grad_in, planes = lax.optimization_barrier((grad_in, planes))
    planes_too = [swap(x, "core", 1) for x in planes]

    if dims.fast:
        outs = call(
            bind(finish_kernel, dims),
            (shape(dims.width, 2 * dims.width),)
            + (shape(modes, dims.width),) * 6
            + (shape(1, dims.width),) * 4,
            [SMEM] + [VMEM] * (4 * dims.ni),
            [vmem(modes, dims.width)] * 6
            + [vmem(1, dims.width)] * 4
            + [
                vmem(2, dims.ni, dims.width // 2 // dims.ni, 2 * dims.width),
                vmem(2, dims.ni, dims.nz, dims.small_rows, LANES),
                DMA((2, dims.ni)),
                DMA((10,)),
            ],
            5,
            3,
            (HBM,) * 11,
        )(meta, *near, *near_too, *planes, *planes_too)
        weight_grad = outs[0]
        mode_grads = outs[1:7]
        chan_grads = [x.reshape(-1) for x in outs[7:]]
    else:

        def in_order(mine, other):
            both = jnp.where(core == 0, jnp.stack([mine, other]), jnp.stack([other, mine]))
            both = jnp.take(both, meta[0] ^ jnp.arange(dims.ni), axis=1)
            return jnp.take(both, meta[2] ^ jnp.arange(dims.nz), axis=2)

        def joined(first, rest):
            return jnp.concatenate([jnp.stack(first)[:, None], jnp.stack(rest)], axis=1)

        both = in_order(joined(near, planes), joined(near_too, planes_too))
        weight_grad = both[:, :, :, : dims.units].reshape(dims.width // 8, -1, 8, LANES)
        weight_grad = weight_grad.transpose(0, 2, 1, 3).reshape(dims.width, -1)
        rows = both[:, :, :, dims.units :].transpose(1, 2, 0, 3, 4, 5)
        rows = rows.reshape(nd, dims.small_rows, dims.groups, hc)
        table = rows[:, : 6 * m].reshape(nd, 6, m, dims.groups, hc).transpose(1, 3, 2, 0, 4)
        mode_grads = list(table.reshape(6, m * dims.groups, dims.width)[:, :modes])
        rest = rows[:, 6 * m : 6 * m + 4, 0].transpose(1, 0, 2).reshape(4, dims.width)
        chan_grads = list(rest)
    step_grad, gain_grad, shift_grad, skip_grad = chan_grads
    return (
        result,
        grad_in,
        gain_grad,
        shift_grad,
        step_grad,
        *mode_grads,
        skip_grad,
        weight_grad,
        bias_grad.reshape(-1),
    )


def solution(mesh):
    batch = mesh.shape["batch"]
    fine = Mesh(mesh.devices.reshape(-1, 2, batch), ("z", "core", "batch"))
    tokens = P("batch", ("z", "core"), None)
    return jax.shard_map(
        functools.partial(local, dict(fine.shape)),
        mesh=fine,
        in_specs=(tokens, P("batch")) + (P(),) * 12 + (tokens,),
        out_specs=(tokens, tokens) + (P(),) * 12,
        check_vma=False,
    )
```

```python
import functools
import math

import jax
import jax.numpy as jnp
from jax import lax
from jax.experimental import pallas as pl
from jax.experimental.pallas import tpu as pltpu
from jax.sharding import Mesh
from jax.sharding import PartitionSpec as P


EPS = 1e-05
LANES = 128
ALL = ("batch", "z", "core")
SMEM = pl.BlockSpec(memory_space=pltpu.SMEM)
VMEM = pl.BlockSpec(memory_space=pltpu.VMEM)
HBM = pl.BlockSpec(memory_space=pltpu.HBM)
ANY = pl.BlockSpec(memory_space=pl.ANY)
DMA = pltpu.SemaphoreType.DMA
ROWS = 64
STEP = 16
PER = ROWS // STEP
copy = pltpu.make_async_copy
f32 = jnp.float32
bf16 = jnp.bfloat16


def mm(a, b):
    return jnp.dot(a, b, preferred_element_type=f32)


def halves(x):
    hi = x.astype(bf16)
    return hi, (x - hi.astype(f32)).astype(bf16)


def lane_ids(shape):
    return lax.broadcasted_iota(jnp.int32, shape, len(shape) - 1)


def swap_blocks(tiles, width):
    tiles = list(tiles)
    block = lane_ids(tiles[0].shape) // width
    step = 1
    while step < len(tiles):
        low = (block & step) == 0
        for a in range(len(tiles)):
            if a & step == 0:
                first, second = tiles[a], tiles[a + step]
                tiles[a] = jnp.where(low, first, pltpu.roll(second, step * width, second.ndim - 1))
                tiles[a + step] = jnp.where(
                    low, pltpu.roll(first, LANES - step * width, first.ndim - 1), second
                )
        step *= 2
    return tiles


def fold_matrix(dims):
    rows = lax.broadcasted_iota(jnp.int32, (LANES, LANES), 0) % dims.chans
    cols = lax.broadcasted_iota(jnp.int32, (LANES, LANES), 1) % dims.chans
    return (rows == cols).astype(f32).astype(bf16)


def fold(row, dims):
    shift = dims.chans
    while shift < LANES:
        row = row + pltpu.roll(row, shift, 1)
        shift *= 2
    return row


class Dims:
    def __init__(self, inputs_shape, modes, mesh_shape):
        self.seqs, self.places, self.width = inputs_shape
        self.ni = mesh_shape["batch"]
        self.nz = mesh_shape["z"]
        self.nj = mesh_shape["z"] * mesh_shape["core"]
        self.devices = self.ni * self.nj
        self.length = self.places * self.nj
        self.quarter = self.length // 4
        self.chans = self.width // self.devices
        self.groups = LANES // self.chans
        self.all_seqs = self.seqs * self.ni
        self.modes = modes
        self.mode_rows = -(-modes // self.groups)
        self.small_rows = -(-(6 * self.mode_rows + 4) // 8) * 8
        self.piece_width = self.seqs * self.chans
        self.place_groups = LANES // self.piece_width
        self.piece_rows = self.places // self.place_groups
        self.units = self.width * 2 * self.width // (8 * LANES) // self.devices
        self.fast = (
            self.piece_width * self.ni == LANES
            and self.piece_rows % 8 == 0
            and self.nj == self.groups
            and self.small_rows == 32
            and self.place_groups == 4
        )


def each(count, body, unroll=True):
    lax.fori_loop(0, count, lambda k, _: body(k), None, unroll=unroll)


def class_rows(b, g, dims):
    return pl.ds(b * dims.places + g, dims.piece_rows, stride=4)


def pack_tokens(read, write, dims, done=None):
    def some(tile):
        parts = []
        for g in range(4):
            for b in range(dims.seqs):
                parts.append(read(tile, class_rows(b, g, dims)))
        parts = swap_blocks(parts, dims.chans)
        for e in range(dims.groups):
            write(tile * dims.groups + e, parts[e])
        if done is not None:
            done(tile)

    each(dims.width // LANES, some)


def unpack_tokens(ref, out, dims, unroll=True):
    def some(tile):
        parts = [ref[tile * dims.groups + e] for e in range(dims.groups)]
        parts = swap_blocks(parts, dims.chans)
        for g in range(4):
            for b in range(dims.seqs):
                out[tile, class_rows(b, g, dims), :] = parts[g * dims.seqs + b]

    each(dims.width // LANES, some, unroll)


def pack_kernel(dims, x_ref, out_ref, wide):
    for b in range(dims.seqs):
        for t in range(dims.width // LANES):
            wide[t, b * dims.places : (b + 1) * dims.places, :] = x_ref[b, :, lanes(t)].astype(f32)

    def write(piece, value):
        out_ref[piece] = value

    pack_tokens(lambda tile, rows: wide[tile, rows, :], write, dims)


def unpack_channels(ref, out, dims):
    rows = dims.piece_rows
    if not dims.fast:
        for r in range(4):
            out[r] = ref[r * dims.quarter : (r + 1) * dims.quarter, :]
        return

    def some(j):
        parts = [ref[i * dims.nj + j] for i in range(dims.ni)]
        parts = swap_blocks(parts, dims.piece_width)
        for g in range(4):
            out[g, pl.ds(pl.multiple_of(j * rows, rows), rows), :] = parts[g]

    each(dims.nj, some)


def pack_channels(read, send, send_hbm, sem, dims):
    rows = dims.piece_rows
    if not dims.fast:
        for r in range(4):
            for at in range(0, dims.quarter, ROWS):
                start = r * dims.quarter + at
                send[start : start + ROWS, :] = read(r, at, ROWS)
        whole = copy(send, send_hbm, sem.at[0])
        whole.start()
        whole.wait()
        return

    def pieces(j):
        return copy(send.at[:, j], send_hbm.at[:, j], sem.at[j])

    for j in range(dims.nj):
        parts = swap_blocks([read(g, j * rows, rows) for g in range(4)], dims.piece_width)
        for i in range(dims.ni):
            send[i, j] = parts[i]
        pieces(j).start()
    for j in range(dims.nj):
        pieces(j).wait()


def mode_constants(par_ref, dims):
    m = dims.mode_rows
    decay, rotation, dr, di, rr, ri = [par_ref[p * m : (p + 1) * m, :] for p in range(6)]
    step = jnp.exp(par_ref[6 * m : 6 * m + 1, :])
    log_mag = -step * decay
    turn = step * rotation
    c1r = step * (rr * dr - ri * di)
    c1i = step * (rr * di + ri * dr)
    c2r = c1r * dr - c1i * di
    c2i = c1r * di + c1i * dr
    return step, log_mag, turn, (c1r, c1i, c2r, c2i), (decay, rotation, dr, di, rr, ri)


def waves_kernel(dims, par_ref, zr_ref, zi_ref, vec_ref, cat_ref, wave):
    m, q = dims.mode_rows, dims.quarter
    step, log_mag, turn, coefs, _ = mode_constants(par_ref, dims)
    c1r, c1i, c2r, c2i = coefs
    mag = jnp.exp(log_mag)
    l1r, l1i = mag * jnp.cos(turn), mag * jnp.sin(turn)
    mag = jnp.exp(8.0 * log_mag)
    l32r, l32i = mag * jnp.cos(8.0 * turn), mag * jnp.sin(8.0 * turn)
    for _ in range(2):
        l32r, l32i = l32r * l32r - l32i * l32i, 2.0 * l32r * l32i
    for p, value in enumerate((l32r, l32i, c1r, c1i, c2r, c2i)):
        vec_ref[p * m : (p + 1) * m, :] = value
    sub = 4.0 * lax.broadcasted_iota(jnp.int32, (8, LANES), 0).astype(f32)

    def wide(x, k):
        return jnp.broadcast_to(x[k : k + 1], (8, LANES))

    for k in range(m):
        mag = jnp.exp(sub * log_mag[k : k + 1])
        zr, zi = mag * jnp.cos(sub * turn[k : k + 1]), mag * jnp.sin(sub * turn[k : k + 1])
        for r in range(4):
            zr_ref[r, 8 * k : 8 * k + 8, :] = zr
            zi_ref[r, 8 * k : 8 * k + 8, :] = zi
            ar, ai = wide(l1r, k), wide(l1i, k)
            zr, zi = zr * ar - zi * ai, zr * ai + zi * ar
    consts = [
        tuple(wide(x, k) for x in (l32r, l32i, 2 * c1r, 2 * c1i, 2 * c2r, 2 * c2i)) for k in range(m)
    ]
    group = fold_matrix(dims)
    for r in range(4):

        def time_step(t, zs):
            at = pl.multiple_of(t * 8, 8)
            k1 = jnp.zeros((8, LANES), f32)
            k2 = jnp.zeros((8, LANES), f32)
            out = []
            for k in range(m):
                zr, zi = zs[2 * k], zs[2 * k + 1]
                ar, ai, b1r, b1i, b2r, b2i = consts[k]
                k1 = k1 + (b1r * zr - b1i * zi)
                k2 = k2 + (b2r * zr - b2i * zi)
                out += [zr * ar - zi * ai, zr * ai + zi * ar]
            wave[pl.ds(at, 8), lanes(0)] = k1
            wave[pl.ds(at, 8), lanes(1)] = k2
            return tuple(out)

        start = []
        for k in range(m):
            start += [zr_ref[r, 8 * k : 8 * k + 8, :], zi_ref[r, 8 * k : 8 * k + 8, :]]
        lax.fori_loop(0, q // 8, time_step, tuple(start), unroll=4)
        for p in range(2):
            both = halves(over_groups(wave[0:q, lanes(p)], group))
            for part in range(2):
                cat_ref[part, :, lanes(2 * r + p)] = both[part]


def tables_kernel(dims, cat_ref, tab_hbm, inv_hbm, tw_hbm, spec_hbm, *scratch):
    tab, inv, tw, spec, wave, sem_out, sem_spec = scratch
    n, q = dims.length, dims.quarter

    def angles(b, _):
        at = pl.multiple_of(b * ROWS, ROWS)
        row = 2 * (lax.broadcasted_iota(jnp.int32, (ROWS, q), 0) + at) + 1
        col = 2 * lax.broadcasted_iota(jnp.int32, (ROWS, q), 1) + 1
        turn = ((row * col) & (8 * q - 1)).astype(f32) * (math.pi / (4 * q))
        for first, value in ((0, jnp.cos(turn)), (q, jnp.sin(turn))):
            for part, half in enumerate(halves(value)):
                tab[part, pl.ds(pl.multiple_of(first + at, ROWS), ROWS), :] = half
                inv[part, pl.ds(at, ROWS), first : first + q] = half
        row = 2 * (lax.broadcasted_iota(jnp.int32, (ROWS, LANES), 0) + at) + 1
        turn = row.astype(f32) * (math.pi / (2 * n))
        cos, sin = jnp.cos(turn), jnp.sin(turn)
        for p, value in enumerate((cos, sin, 1.0 - 2.0 * sin * sin, 2.0 * cos * sin)):
            tw[p, pl.ds(at, ROWS), :] = value
        return 0

    lax.fori_loop(0, q // ROWS, angles, 0)
    outs = [copy(tab, tab_hbm, sem_out.at[0]), copy(tw, tw_hbm, sem_out.at[1])]
    outs.append(copy(inv, inv_hbm, sem_out.at[2]))
    for out in outs:
        out.start()
    forth(tab, cat_ref, wave)

    def spectrum(b, _):
        at = pl.multiple_of(b * STEP, STEP)
        chunk, rows = place_of(b)
        for p in range(2):
            for k, (re, im) in enumerate(butterfly(wave, tw, at, p, 2, dims)):
                spec[chunk, k, rows, lanes(2 * p)] = re * (1.0 / n)
                spec[chunk, k, rows, lanes(2 * p + 1)] = im * (1.0 / n)
        return 0

    lax.fori_loop(0, q // STEP, spectrum, 0)
    outs.append(copy(spec, spec_hbm, sem_spec))
    outs[-1].start()
    for out in outs:
        out.wait()


def lanes(p):
    return slice(p * LANES, (p + 1) * LANES)


def over_groups(x, group):
    return mm(jnp.concatenate(halves(x), axis=1), jnp.concatenate([group, group], axis=0))


def place_of(b):
    return b // PER, pl.ds(pl.multiple_of(b % PER * STEP, STEP), STEP)


def product(table, operand):
    (high, low), (first, second) = table, operand
    return mm(
        jnp.concatenate([high, high, low], axis=1), jnp.concatenate([first, second, first], axis=0)
    )


def forth(tab, cat, wave):
    wave[...] = product((tab[0], tab[1]), (cat[0], cat[1]))


def twiddles(tw, at):
    c1, s1, c2, s2 = [tw[p, pl.ds(at, STEP), :] for p in range(4)]
    return (c2, s2), (c1, s1), None, (c1, -s1)


def times(a, b):
    if b is None:
        return a
    return a[0] * b[0] - a[1] * b[1], a[0] * b[1] + a[1] * b[0]


def plus(a, b):
    return a[0] + b[0], a[1] + b[1]


def minus(a, b):
    return a[0] - b[0], a[1] - b[1]


def turned(a):
    return -a[1], a[0]


def butterfly(wave, tw, at, p, count, dims):
    below = pl.multiple_of(dims.quarter + at, STEP)
    parts = []
    for r, twiddle in enumerate(twiddles(tw, at)):
        re = wave[pl.ds(at, STEP), lanes(r * count + p)]
        im = wave[pl.ds(below, STEP), lanes(r * count + p)]
        parts.append(times((re, -im), twiddle))
    even, odd = plus(parts[0], parts[2]), plus(parts[1], parts[3])
    even_too, odd_too = minus(parts[0], parts[2]), turned(minus(parts[1], parts[3]))
    return plus(even, odd), minus(even_too, odd_too), minus(even, odd), plus(even_too, odd_too)


def unbutterfly(parts, tw, at, cat, p, count, dims):
    even, odd = plus(parts[0], parts[2]), plus(parts[1], parts[3])
    even_too, odd_too = minus(parts[0], parts[2]), turned(minus(parts[1], parts[3]))
    sums = plus(even, odd), plus(even_too, odd_too), minus(even, odd), minus(even_too, odd_too)
    for r, twiddle in enumerate(twiddles(tw, at)):
        if twiddle is not None:
            twiddle = twiddle[0], -twiddle[1]
        re, im = times(sums[r], twiddle)
        for first, value in ((0, re), (dims.quarter, -im)):
            rows = pl.ds(pl.multiple_of(first + at, STEP), STEP)
            for part, half in enumerate(halves(value)):
                cat[part, rows, lanes(r * count + p)] = half


def back(inv, cat):
    return product((inv[0], inv[1]), (cat[0], cat[1]))


def column_sums(x):
    return jnp.sum(x.reshape(x.shape[0] // 8, 8, LANES), axis=0)


def lane_lengths(meta_ref, lens_refs, dims):
    lane = lane_ids((1, LANES)) // dims.chans
    row = jnp.zeros((1, LANES), jnp.int32)
    total = jnp.int32(0)
    for s in range(dims.all_seqs):
        source = s // dims.seqs
        value = lens_refs[source][s % dims.seqs]
        total = total + value
        row = jnp.where(lane == s ^ (meta_ref[0] * dims.seqs), value, row)
    return row, total.astype(f32)


def valid_rows(r, at, rows, lens):
    places = 4 * (lax.broadcasted_iota(jnp.int32, (rows, LANES), 0) + at) + r
    return (places < lens).astype(f32)


def forward_kernel(dims, meta_ref, r_ref, par_ref, tab_hbm, inv_hbm, tw_hbm, spec_hbm, *rest):
    lens_refs, rest = rest[: dims.ni], rest[dims.ni :]
    (send_hbm, mixed_hbm, normed_hbm, seen_hbm, stat_ref), rest = rest[:5], rest[5:]
    tab, inv, tw, spec, seen, x_sc, mix_sc, normed_sc, cat, wave, back_cat, send = rest[:12]
    sem_tab, sem_spec, sem_seen, sem_out, sem_send = rest[12:]
    m, q = dims.mode_rows, dims.quarter
    chunks = q // ROWS
    ins = [copy(tab_hbm, tab, sem_tab.at[0]), copy(tw_hbm, tw, sem_tab.at[1])]
    ins += [copy(spec_hbm.at[c], spec.at[c], sem_spec.at[c]) for c in range(chunks)]
    ins.append(copy(inv_hbm, inv, sem_tab.at[2]))
    for one in ins:
        one.start()
    lens, total = lane_lengths(meta_ref, lens_refs, dims)
    unpack_channels(r_ref, x_sc, dims)
    classes = range(4)

    def add_up(b, acc):
        at = pl.multiple_of(b * ROWS, ROWS)
        for r in classes:
            acc = acc + column_sums(x_sc[r, pl.ds(at, ROWS), :] * valid_rows(r, at, ROWS, lens))
        return acc

    zero = jnp.zeros((8, LANES), f32)
    acc = lax.fori_loop(0, q // ROWS, add_up, zero, unroll=True)
    average = fold(jnp.sum(acc, axis=0, keepdims=True), dims) / total

    def add_squares(b, acc):
        at = pl.multiple_of(b * ROWS, ROWS)
        for r in classes:
            x = (x_sc[r, pl.ds(at, ROWS), :] - average) * valid_rows(r, at, ROWS, lens)
            acc = acc + column_sums(x * x)
        return acc

    acc = lax.fori_loop(0, q // ROWS, add_squares, zero, unroll=True)
    variance = fold(jnp.sum(acc, axis=0, keepdims=True), dims) / total
    inv_scale = lax.rsqrt(variance + EPS)
    gain = par_ref[6 * m + 1 : 6 * m + 2, :]
    shift = par_ref[6 * m + 2 : 6 * m + 3, :]
    skip = par_ref[6 * m + 3 : 6 * m + 4, :]
    stat_ref[0:1, :] = inv_scale
    stat_ref[1:2, :] = jnp.broadcast_to(total, (1, LANES))
    stat_ref[2:3, :] = lens.astype(f32)
    stat_ref[3:8, :] = jnp.zeros((5, LANES), f32)
    first_row = lax.broadcasted_iota(jnp.int32, (ROWS, LANES), 0) == 0

    def normalize(b, last):
        at = pl.multiple_of(b * ROWS, ROWS)
        mixed = []
        for r in classes:
            normed = (x_sc[r, pl.ds(at, ROWS), :] - average) * inv_scale
            mixed.append((gain * normed + shift) * valid_rows(r, at, ROWS, lens))
            normed_sc[r, pl.ds(at, ROWS), :] = normed
            mix_sc[r, pl.ds(at, ROWS), :] = mixed[r]
        earlier = jnp.where(first_row, last, pltpu.roll(mixed[3], 1, 0))
        for r in classes:
            liquid = mixed[r] * (earlier if r == 0 else mixed[r - 1])
            for p, value in enumerate((mixed[r], liquid)):
                for part, half in enumerate(halves(value)):
                    cat[part, pl.ds(at, ROWS), lanes(2 * r + p)] = half
        return mixed[3][ROWS - 1 :, :]

    lax.fori_loop(0, q // ROWS, normalize, jnp.zeros((1, LANES), f32))
    outs = [copy(mix_sc, mixed_hbm, sem_out.at[0]), copy(normed_sc, normed_hbm, sem_out.at[1])]
    for out in outs:
        out.start()
    ins[0].wait()
    forth(tab, cat, wave)
    ins[1].wait()
    for c in range(chunks):
        ins[2 + c].wait()

        def multiply(b, _):
            at = pl.multiple_of(b * STEP, STEP)
            chunk, rows = place_of(b)
            mixed = butterfly(wave, tw, at, 0, 2, dims)
            liquid = butterfly(wave, tw, at, 1, 2, dims)
            parts = []
            for k in range(4):
                for p, value in enumerate(mixed[k] + liquid[k]):
                    seen[chunk, k, rows, lanes(p)] = value
                kr, ki, lr, li = [spec[chunk, k, rows, lanes(p)] for p in range(4)]
                parts.append(plus(times(mixed[k], (kr, ki)), times(liquid[k], (lr, li))))
            unbutterfly(parts, tw, at, back_cat, 0, 1, dims)
            return 0

        lax.fori_loop(PER * c, PER * (c + 1), multiply, 0, unroll=PER)
        outs.append(copy(seen.at[c], seen_hbm.at[c], sem_seen.at[c]))
        outs[-1].start()
    ins[-1].wait()

    value = back(inv, back_cat)
    for r in classes:
        x_sc[r] = value[:, lanes(r)] + skip * mix_sc[r]
    pack_channels(
        lambda r, at, size: x_sc[r, pl.ds(at, size), :], send, send_hbm, sem_send, dims
    )
    for out in outs:
        out.wait()


def gate_kernel(dims, meta_ref, r_ref, x_ref, w_ref, b_ref, ct_ref, *rest):
    (send_hbm, out_ref, act_hbm, gj_hbm, bias_ref, wsend_hbm), scratch = rest[:6], rest[6:]
    resp, act, joined, gj, gact, send, weight, wsend, sem_out, sem_send, sem_weight = scratch
    tokens = dims.seqs * dims.places
    width = dims.width
    places = dims.places

    tiles = range(width // LANES)
    if dims.fast:
        unpack_tokens(r_ref, resp, dims)
    else:
        for t in tiles:
            resp[t] = r_ref[:, lanes(t)]
    c0 = math.sqrt(2.0 / math.pi)
    c1 = 0.044715
    rows = 32

    def gelu(b, _):
        at = pl.multiple_of(b * rows, rows)
        for tile in tiles:
            r = resp[tile, pl.ds(at, rows), :]
            t = jnp.tanh(c0 * (r + c1 * r * r * r))
            act[pl.ds(at, rows), lanes(tile)] = (0.5 * r * (1.0 + t)).astype(bf16)
            slope = 0.5 * (1.0 + t) + 0.5 * r * (1.0 - t * t) * (c0 * (1.0 + 3.0 * c1 * r * r))
            resp[tile, pl.ds(at, rows), :] = slope
        return 0

    lax.fori_loop(0, tokens // rows, gelu, 0)
    outs = [copy(act, act_hbm, sem_out.at[0]), copy(gj, gj_hbm, sem_out.at[1])]
    outs[0].start()
    joined[...] = mm(act[...], w_ref[...])
    bias = b_ref[...]
    half = min(16, places)
    for b in range(dims.seqs):

        def gate(k, sums):
            at = pl.multiple_of(k * half, half)
            tok = pl.multiple_of(b * places + k * half, half)
            value = joined[pl.ds(tok, half), :width] + bias[:, :width]
            s = jax.nn.sigmoid(joined[pl.ds(tok, half), width:] + bias[:, width:])
            x = x_ref[b, pl.ds(at, half), :].astype(f32)
            g = ct_ref[b, pl.ds(at, half), :].astype(f32)
            out_ref[b, pl.ds(at, half), :] = (x + value * s).astype(bf16)
            gs = g * s
            first = gs.astype(bf16)
            second = (gs * value * (1.0 - s)).astype(bf16)
            gj[pl.ds(tok, half), :width] = first
            gj[pl.ds(tok, half), width:] = second
            first = jnp.sum(first.astype(f32).reshape(half // 8, 8, width), axis=0)
            second = jnp.sum(second.astype(f32).reshape(half // 8, 8, width), axis=0)
            return sums[0] + first, sums[1] + second

        if b == 0:
            zero = jnp.zeros((8, width), f32)
            sums = (zero, zero)
        sums = lax.fori_loop(0, places // half, gate, sums)
    outs[1].start()
    sums = [jnp.sum(s, axis=0, keepdims=True) for s in sums]
    for p, total in enumerate(sums):
        for t in tiles:
            row = p * (width // LANES) + t
            bias_ref[row : row + 1, :] = total[:, lanes(t)]
    weight_half(dims, meta_ref, 1 - meta_ref[1], act, gj, weight)
    for i in range(dims.ni):
        for z in range(dims.nz):
            for u in range(dims.units):
                wsend[i, z, u, :, :] = weight_unit(dims, meta_ref, weight, i, z, u)
            wsend[i, z, dims.units, :, :] = bias_ref[...]
        outs.append(copy(wsend.at[i], wsend_hbm.at[i], sem_weight.at[i]))
        outs[-1].start()
    grad = lax.dot_general(
        gj[...], w_ref[...], (((1,), (1,)), ((), ())), preferred_element_type=f32
    )
    for t in tiles:
        gact[t] = grad[:, lanes(t)]
    if dims.fast:

        def read(tile, rows):
            return gact[tile, rows, :] * resp[tile, rows, :]

        def put(piece, value):
            send[piece] = value

        def tile_copy(tile):
            some = pl.ds(tile * dims.groups, dims.groups)
            return copy(send.at[some], send_hbm.at[some], sem_send.at[tile])

        pack_tokens(read, put, dims, lambda tile: tile_copy(tile).start())
        outs += [tile_copy(tile) for tile in tiles]
    else:
        for t in tiles:
            send[:, lanes(t)] = gact[t] * resp[t]
        outs.append(copy(send, send_hbm, sem_send.at[0]))
        outs[-1].start()
    for out in outs:
        out.wait()


def weight_half(dims, meta_ref, core, act, gj, weight):
    half = dims.width // 2
    some = act[:, pl.ds(pl.multiple_of(core * half, half), half)]
    weight[...] = lax.dot_general(
        some, gj[...], (((0,), (0,)), ((), ())), preferred_element_type=f32
    )


def weight_unit(dims, meta_ref, weight, i, z, u):
    tiles = 2 * dims.width // LANES
    owner = (meta_ref[0] ^ i) * dims.nz + (meta_ref[2] ^ z)
    if dims.units % tiles == 0:
        row = owner * (dims.units // tiles) + u // tiles
        cols = lanes(u % tiles)
    else:
        unit = owner * dims.units + u
        row = unit // tiles
        cols = pl.ds(pl.multiple_of(unit % tiles * LANES, LANES), LANES)
    return weight[pl.ds(pl.multiple_of(row * 8, 8), 8), cols]


def backward_kernel(dims, r_ref, par_ref, *rest):
    ins_hbm, (stat_ref, send_hbm, grad_hbm, sums_ref) = rest[:6], rest[6:10]
    tab, inv, tw, spec, grads, mix_sc, normed_sc, g_sc, up_sc, cat, wave, back_cat = rest[10:22]
    lead_sc, liquid_sc, send, sem_in, sem_spec, sem_send, sem_grad = rest[22:]
    tab_hbm, inv_hbm, tw_hbm, spec_hbm, mixed_hbm, normed_hbm = ins_hbm
    m, q = dims.mode_rows, dims.quarter
    ins = [
        copy(mixed_hbm, mix_sc, sem_in.at[0]),
        copy(tab_hbm, tab, sem_in.at[1]),
        copy(tw_hbm, tw, sem_in.at[2]),
        copy(normed_hbm, normed_sc, sem_in.at[3]),
        copy(inv_hbm, inv, sem_in.at[4]),
    ]
    chunks = q // ROWS
    for c in range(chunks):
        ins.insert(3 + c, copy(spec_hbm.at[c], spec.at[c], sem_spec.at[c]))
    for one in ins:
        one.start()
    unpack_channels(r_ref, g_sc, dims)
    gain = par_ref[6 * m + 1 : 6 * m + 2, :]
    skip = par_ref[6 * m + 3 : 6 * m + 4, :]
    inv_scale = stat_ref[0:1, :]
    total = stat_ref[1:2, :]
    lens = stat_ref[2:3, :].astype(jnp.int32)
    zero = jnp.zeros((8, LANES), f32)
    classes = range(4)
    ins[0].wait()

    def gather(b, acc):
        at = pl.multiple_of(b * ROWS, ROWS)
        for r in classes:
            g = g_sc[r, pl.ds(at, ROWS), :]
            for part, half in enumerate(halves(g)):
                cat[part, pl.ds(at, ROWS), lanes(r)] = half
            acc = acc + column_sums(g * mix_sc[r, pl.ds(at, ROWS), :])
        return acc

    skip_acc = lax.fori_loop(0, q // ROWS, gather, zero)
    ins[1].wait()
    forth(tab, cat, wave)
    ins[2].wait()
    outs = []
    for c in range(chunks):
        ins[3 + c].wait()

        def multiply(b, _):
            at = pl.multiple_of(b * STEP, STEP)
            chunk, rows = place_of(b)
            grad = butterfly(wave, tw, at, 0, 1, dims)
            for k in range(4):
                for p in range(2):
                    grads[chunk, k, rows, lanes(p)] = grad[k][p]
            for p in range(2):
                products(grad, spec, tw, b, back_cat, p, dims)
            return 0

        lax.fori_loop(PER * c, PER * (c + 1), multiply, 0, unroll=PER)
        outs.append(copy(grads.at[c], grad_hbm.at[c], sem_grad.at[c]))
        outs[-1].start()
    for one in ins[3 + chunks :]:
        one.wait()

    value = back(inv, back_cat)
    for r in classes:
        lead_sc[r] = value[:, lanes(2 * r)]
        liquid_sc[r] = value[:, lanes(2 * r + 1)]
        up_sc[r] = value[:, lanes(2 * r + 1)] * mix_sc[r]

    row = lax.broadcasted_iota(jnp.int32, (ROWS, LANES), 0)
    blank = jnp.zeros((1, LANES), f32)
    gain_acc, shift_acc = zero, zero
    for at in range(0, q, ROWS):
        rows = slice(at, at + ROWS)
        for r in classes:
            if r == 0:
                before = blank if at == 0 else mix_sc[3, at - 1 : at, :]
                earlier = jnp.where(row == 0, before, pltpu.roll(mix_sc[3, rows, :], 1, 0))
            else:
                earlier = mix_sc[r - 1, rows, :]
            if r == 3:
                after = blank if at + ROWS == q else up_sc[0, at + ROWS : at + ROWS + 1, :]
                up = jnp.where(row == ROWS - 1, after, pltpu.roll(up_sc[0, rows, :], ROWS - 1, 0))
            else:
                up = up_sc[r + 1, rows, :]
            masked = lead_sc[r, rows, :] + skip * g_sc[r, rows, :] + liquid_sc[r, rows, :] * earlier
            masked = (masked + up) * valid_rows(r, at, ROWS, lens)
            g_sc[r, rows, :] = masked
            gain_acc = gain_acc + column_sums(masked * normed_sc[r, rows, :])
            shift_acc = shift_acc + column_sums(masked)

    def whole(acc):
        return fold(jnp.sum(acc, axis=0, keepdims=True), dims)

    gain_sum, shift_sum, skip_sum = whole(gain_acc), whole(shift_acc), whole(skip_acc)
    scale = gain * inv_scale
    shift_mean = shift_sum / total
    gain_mean = gain_sum / total

    def read(r, at, size):
        normed = normed_sc[r, pl.ds(at, size), :]
        value = g_sc[r, pl.ds(at, size), :] - shift_mean - normed * gain_mean
        return value * scale * valid_rows(r, at, size, lens)

    sums_ref[...] = jnp.zeros_like(sums_ref)
    for p, value in enumerate((gain_sum, shift_sum, skip_sum)):
        sums_ref[p : p + 1, :] = value
    pack_channels(read, send, send_hbm, sem_send, dims)
    for out in outs:
        out.wait()


def products(grad, ref, tw, b, cat, p, dims):
    chunk, rows = place_of(b)
    parts = []
    for k in range(4):
        re = ref[chunk, k, rows, lanes(2 * p)]
        im = ref[chunk, k, rows, lanes(2 * p + 1)]
        parts.append(times(grad[k], (re, -im)))
    unbutterfly(parts, tw, pl.multiple_of(b * STEP, STEP), cat, p, 2, dims)


def modes_kernel(dims, par_ref, inv_hbm, tw_hbm, seen_hbm, grad_hbm, sums_ref, *rest):
    zr_ref, zi_ref, vec_ref, small_ref, inv, tw, seen, grads, back_cat, dk, sem, sem_in = rest
    n, m, q = dims.length, dims.mode_rows, dims.quarter
    chunks = q // ROWS
    ins = [copy(tw_hbm, tw, sem.at[0])]
    for c in range(chunks):
        ins.append(copy(seen_hbm.at[c], seen.at[c], sem_in.at[0, c]))
        ins.append(copy(grad_hbm.at[c], grads.at[c], sem_in.at[1, c]))
    ins.append(copy(inv_hbm, inv, sem.at[1]))
    for one in ins:
        one.start()
    zero = jnp.zeros((8, LANES), f32)
    classes = range(4)
    ins[0].wait()
    for c in range(chunks):
        ins[1 + 2 * c].wait()
        ins[2 + 2 * c].wait()

        def multiply(b, _):
            chunk, rows = place_of(b)
            grad = [tuple(grads[chunk, k, rows, lanes(p)] for p in range(2)) for k in range(4)]
            for p in range(2):
                products(grad, seen, tw, b, back_cat, p, dims)
            return 0

        lax.fori_loop(PER * c, PER * (c + 1), multiply, 0, unroll=PER)
    ins[-1].wait()
    group = fold_matrix(dims)

    value = back(inv, back_cat) * (1.0 / n)
    dk[...] = over_groups(jnp.concatenate([value[:, lanes(p)] for p in range(8)], axis=0), group)

    step, log_mag, turn, _, params = mode_constants(par_ref, dims)
    decay, rotation, dr, di, rr, ri = params
    l32r, l32i, c1r, c1i, c2r, c2i = [vec_ref[p * m : (p + 1) * m, :] for p in range(6)]
    sub = 4.0 * lax.broadcasted_iota(jnp.int32, (8, LANES), 0).astype(f32)
    sums = [[] for _ in range(8)]
    for first in range(0, m, 2):
        some = range(first, min(m, first + 2))
        ratio = [
            (
                jnp.broadcast_to(l32r[k : k + 1], (8, LANES)),
                jnp.broadcast_to(l32i[k : k + 1], (8, LANES)),
            )
            for k in some
        ]
        sofar = [zero] * (8 * len(ratio))
        for r in classes:

            def mode_step(t, carry):
                at = pl.multiple_of(t * 8, 8)
                d1 = dk[pl.ds(pl.multiple_of(2 * r * q + at, 8), 8), :]
                d2 = dk[pl.ds(pl.multiple_of((2 * r + 1) * q + at, 8), 8), :]
                place = sub + (32 * t + r).astype(f32)
                e1 = d1 * place
                e2 = d2 * place
                out = []
                for k, (ar, ai) in enumerate(ratio):
                    zr, zi, *acc = carry[10 * k : 10 * (k + 1)]
                    out += [zr * ar - zi * ai, zr * ai + zi * ar]
                    for p, d in enumerate((d1, d2, e1, e2)):
                        out += [acc[2 * p] + d * zr, acc[2 * p + 1] + d * zi]
                return tuple(out)

            carry = []
            for at, k in enumerate(some):
                carry += [zr_ref[r, 8 * k : 8 * k + 8, :], zi_ref[r, 8 * k : 8 * k + 8, :]]
                carry += sofar[8 * at : 8 * at + 8]
            carry = lax.fori_loop(0, q // 8, mode_step, tuple(carry), unroll=4)
            sofar = [v for k in range(len(ratio)) for v in carry[10 * k + 2 : 10 * k + 10]]
        for k in range(len(ratio)):
            for p in range(8):
                sums[p].append(jnp.sum(sofar[8 * k + p], axis=0, keepdims=True))
    a1r, a1i, a2r, a2i, e1r, e1i, e2r, e2i = [
        jnp.concatenate(s, axis=0) if len(s) > 1 else s[0] for s in sums
    ]
    btr = c1r * e1r - c1i * e1i + c2r * e2r - c2i * e2i
    bti = c1r * e1i + c1i * e1r + c2r * e2i + c2i * e2r
    d2r = dr * dr - di * di
    d2i = 2.0 * dr * di
    erd = step * (a1r * dr - a1i * di + a2r * d2r - a2i * d2i)
    eri = step * (a1r * di + a1i * dr + a2r * d2i + a2i * d2r)
    tr = a1r + 2.0 * (a2r * dr - a2i * di)
    ti = a1i + 2.0 * (a2r * di + a2i * dr)
    edr = step * (rr * tr - ri * ti)
    edi = step * (rr * ti + ri * tr)
    by_step = 2.0 * (c1r * a1r - c1i * a1i + c2r * a2r - c2i * a2i) + 2.0 * step * (
        -decay * btr - rotation * bti
    )
    small_ref[...] = jnp.zeros_like(small_ref)
    answers = (-2.0 * step * btr, -2.0 * step * bti, 2.0 * edr, -2.0 * edi, 2.0 * erd, -2.0 * eri)
    for p, value in enumerate(answers):
        small_ref[p * m : (p + 1) * m, :] = value
    small_ref[6 * m : 6 * m + 1, :] = fold(jnp.sum(by_step, axis=0, keepdims=True), dims)
    small_ref[6 * m + 1 : 6 * m + 4, :] = sums_ref[0:3, :]


def first_add_kernel(dims, meta_ref, act_hbm, gj_hbm, bias_ref, other_hbm, *refs):
    out_refs, (act, gj, weight, other, sem_in, sem) = refs[: dims.ni], refs[dims.ni :]
    ins = [copy(act_hbm, act, sem_in.at[0]), copy(gj_hbm, gj, sem_in.at[1])]
    others = [copy(other_hbm.at[i], other.at[i], sem.at[i]) for i in range(dims.ni)]
    for one in ins + others:
        one.start()
    for one in ins:
        one.wait()
    weight_half(dims, meta_ref, meta_ref[1], act, gj, weight)
    for i in range(dims.ni):
        others[i].wait()
        for z in range(dims.nz):
            for u in range(dims.units):
                unit = weight_unit(dims, meta_ref, weight, i, z, u)
                out_refs[i][z, u] = unit + other[i, z, u]
            out_refs[i][z, dims.units] = bias_ref[...] + other[i, z, dims.units]


def order_kernel(sums_ref, out_ref):
    out_ref[...] = sums_ref[...]


def add_kernel(count, *refs):
    for p, out_ref in enumerate(refs[count:]):
        total = refs[0][p]
        for ref in refs[1:count]:
            total = total + ref[p]
        out_ref[...] = total


def last_add_kernel(dims, count, small_ref, *refs):
    units_ref, bias_ref = refs[count:]

    def unit(u):
        total = refs[0][u]
        for ref in refs[1:count]:
            total = total + ref[u]
        return total

    for u in range(dims.units):
        units_ref[u] = unit(u)
    for t in range(dims.small_rows // 8):
        units_ref[dims.units + t] = small_ref[8 * t : 8 * t + 8, :]
    bias = unit(dims.units)
    for t in range(2 * dims.width // LANES):
        bias_ref[:, lanes(t)] = bias[t : t + 1, :]


def stack_kernel(*refs):
    for k, ref in enumerate(refs[:-1]):
        refs[-1][k] = ref[...]


def input_kernel(dims, r_ref, ct_ref, grad_ref, grad):
    unpack_tokens(r_ref, grad, dims, False)
    for b in range(dims.seqs):
        for t in range(dims.width // LANES):
            value = grad[t, b * dims.places : (b + 1) * dims.places, :]
            grad_ref[b, :, lanes(t)] = value + ct_ref[b, :, lanes(t)].astype(f32)


def finish_kernel(dims, meta_ref, *refs):
    ni, nz, m = dims.ni, dims.nz, dims.mode_rows
    near = refs[:ni], refs[ni : 2 * ni]
    far = refs[2 * ni : 3 * ni], refs[3 * ni : 4 * ni]
    weight_ref, *small_hbm = refs[4 * ni : 4 * ni + 11]
    *small_refs, rows, small, sem, sem_small = refs[4 * ni + 11 :]
    me, core, me_z = meta_ref[0], meta_ref[1], meta_ref[2]
    tiles = 2 * dims.width // LANES
    per = 8 * dims.units // tiles
    copies = []
    for half, side in ((0, core), (1, 1 - core)):
        for i in range(ni):
            for z in range(nz):
                piece = near[half][i] if z == 0 else far[half][i].at[z - 1]
                for u in range(dims.units):
                    at = pl.multiple_of((me_z ^ z) * per + u // tiles * 8, 8)
                    rows[half, i, pl.ds(at, 8), lanes(u % tiles)] = piece[u]
                value = piece[dims.units :].reshape(dims.small_rows, LANES)
                small[half, i, me_z ^ z] = value
            at = pl.multiple_of((side * ni + (me ^ i)) * nz * per, nz * per)
            target = weight_ref.at[pl.ds(at, nz * per), :]
            copies.append(copy(rows.at[half, i], target, sem.at[half, i]))
            copies[-1].start()
    first = core == 0
    for i in range(ni):
        parts = []
        for z in range(nz):
            a, b = small[0, i, z], small[1, i, z]
            parts += [jnp.where(first, a, b), jnp.where(first, b, a)]
        parts = swap_blocks(parts, dims.chans)
        cols = pl.ds(pl.multiple_of((me ^ i) * LANES, LANES), LANES)
        for q in range(dims.groups):
            for p in range(6):
                small_refs[p][q * m : q * m + m, cols] = parts[q][p * m : p * m + m, :]
        for p in range(4):
            small_refs[6 + p][:, cols] = parts[0][6 * m + p : 6 * m + p + 1, :]
    for p, (ref, hbm) in enumerate(zip(small_refs, small_hbm)):
        copies.append(copy(ref, hbm, sem_small.at[p]))
        copies[-1].start()
    for one in copies:
        one.wait()


def call(kernel, out_shape, in_specs, scratch, limit, us, out_specs=None):
    cost = pl.CostEstimate(flops=int(us * 1.1e9), bytes_accessed=int(us * 3e6), transcendentals=0)
    if out_specs is None:
        out_specs = jax.tree.map(lambda _: VMEM, out_shape)
    else:
        out_shape = tuple(
            pltpu.HBM(out.shape, out.dtype) if spec is HBM else out
            for out, spec in zip(out_shape, out_specs)
        )

    def run(*args):
        args = [
            pltpu.with_memory_space_constraint(x, pltpu.HBM) if spec is HBM else x
            for x, spec in zip(args, in_specs)
        ]
        return pl.pallas_call(
            kernel,
            out_shape=out_shape,
            in_specs=in_specs,
            out_specs=out_specs,
            scratch_shapes=scratch,
            compiler_params=pltpu.CompilerParams(vmem_limit_bytes=limit << 20),
            cost_estimate=cost,
        )(*args)

    return run


def shape(*dims, dtype=f32):
    return jax.ShapeDtypeStruct(dims, dtype)


def local(
    mesh_shape,
    inputs,
    lengths,
    norm_gain,
    norm_shift,
    log_step,
    decay_rate,
    rotation,
    drive_real,
    drive_imag,
    read_real,
    read_imag,
    skip_gain,
    glu_weight,
    glu_bias,
    out_cotangent,
):
    modes = decay_rate.shape[0]
    dims = Dims(inputs.shape, modes, mesh_shape)
    n, nd, m, hc = dims.length, dims.devices, dims.mode_rows, dims.chans
    core = lax.axis_index("core")
    owner = lax.axis_index(ALL)
    meta = jnp.stack([lax.axis_index("batch"), core, lax.axis_index("z")]).astype(jnp.int32)

    def exchange(x):
        return lax.all_to_all(x, ALL, 0, 0, tiled=True)

    some = dims.places // 4

    def to_channels(x):
        x = x.reshape(dims.seqs, some, 4, nd, hc).transpose(3, 2, 1, 0, 4)
        x = exchange(x.reshape(nd, dims.places, dims.piece_width))
        x = x.reshape(dims.ni, dims.nj, 4, some, dims.piece_width).transpose(2, 1, 3, 0, 4)
        x = x.reshape(n, dims.all_seqs * hc)
        return jnp.pad(x, ((0, 0), (0, LANES - x.shape[1])))

    def to_tokens(x):
        x = x[:, : dims.all_seqs * hc].reshape(4, dims.nj, some, dims.ni, dims.piece_width)
        x = x.transpose(3, 1, 0, 2, 4).reshape(nd, dims.places, dims.piece_width)
        x = exchange(x).reshape(nd, 4, some, dims.seqs, hc).transpose(3, 2, 1, 0, 4)
        return x.reshape(dims.seqs * dims.places, dims.width)

    table = jnp.stack([decay_rate, rotation, drive_real, drive_imag, read_real, read_imag])
    table = lax.dynamic_slice_in_dim(table, owner * hc, hc, 2)
    table = jnp.pad(table, ((0, 0), (0, m * dims.groups - modes), (0, 0)))
    table = table.reshape(6, dims.groups, m, hc).transpose(0, 2, 1, 3).reshape(6 * m, LANES)
    rest = jnp.stack([log_step, norm_gain, norm_shift, skip_gain])
    rest = lax.dynamic_slice_in_dim(rest, owner * hc, hc, 1)
    params = jnp.concatenate([table, jnp.tile(rest, (1, dims.groups))], axis=0)
    params, meta = lax.optimization_barrier((params, meta))

    pieces = (nd, dims.piece_rows, LANES) if dims.fast else (n, LANES)
    tokens = dims.seqs * dims.places
    token_pieces = (nd, dims.piece_rows, LANES) if dims.fast else (tokens, dims.width)
    bind = functools.partial
    q = dims.quarter
    tab = (2, 2 * q, q)
    inv = (2, q, 2 * q)
    chunks = q // ROWS
    tw = (4, q, LANES)
    four = (chunks, 4, ROWS, 4 * LANES)
    two = (chunks, 4, ROWS, 2 * LANES)
    sent = (dims.ni, dims.nj, dims.piece_rows, LANES) if dims.fast else (n, LANES)
    plain = (4, q, LANES)
    by_tile = (dims.width // LANES, dims.seqs * dims.places, LANES)

    def vmem(*sizes, dtype=f32):
        return pltpu.VMEM(sizes, dtype)

    if dims.fast:
        packed = call(
            bind(pack_kernel, dims), shape(*pieces), [VMEM], [vmem(*by_tile)], 4, 1.5
        )(inputs)
        received = exchange(packed)
    else:
        received = to_channels(inputs.astype(f32))

    zr, zi, vec, waves = call(
        bind(waves_kernel, dims),
        (
            shape(4, 8 * m, LANES),
            shape(4, 8 * m, LANES),
            shape(6 * m, LANES),
            shape(2, q, 8 * LANES, dtype=bf16),
        ),
        [VMEM],
        [vmem(q, 2 * LANES)],
        4,
        3,
    )(params)
    lengths, waves = lax.optimization_barrier((lengths, waves))
    tables, inverse, twiddle, spec = call(
        bind(tables_kernel, dims),
        (shape(*tab, dtype=bf16), shape(*inv, dtype=bf16), shape(*tw), shape(*four)),
        [VMEM],
        [
            vmem(*tab, dtype=bf16),
            vmem(*inv, dtype=bf16),
            vmem(*tw),
            vmem(*four),
            vmem(2 * q, 8 * LANES),
            DMA((3,)),
            DMA(()),
        ],
        10,
        6,
        (HBM, HBM, HBM, HBM),
    )(waves)

    def swap(x, axis, by):
        return lax.ppermute(x, axis, [(i, i ^ by) for i in range(lax.axis_size(axis))])

    def everyone(x, axis, size):
        return [x] + [swap(x, axis, s) for s in range(1, size)]

    lens = everyone(lengths, "batch", dims.ni)
    send, mixed, normed, seen, stat = call(
        bind(forward_kernel, dims),
        (shape(*sent), shape(*plain), shape(*plain), shape(*four), shape(8, LANES)),
        [SMEM, VMEM, VMEM] + [HBM] * 4 + [SMEM] * dims.ni,
        [
            vmem(*tab, dtype=bf16),
            vmem(*inv, dtype=bf16),
            vmem(*tw),
            vmem(*four),
            vmem(*four),
            vmem(*plain),
            vmem(*plain),
            vmem(*plain),
            vmem(2, q, 8 * LANES, dtype=bf16),
            vmem(2 * q, 8 * LANES),
            vmem(2, 2 * q, 4 * LANES, dtype=bf16),
            vmem(*sent),
            DMA((3,)),
            DMA((chunks,)),
            DMA((chunks,)),
            DMA((2,)),
            DMA((dims.nj,)),
        ],
        18,
        7,
        (HBM, HBM, HBM, HBM, VMEM),
    )(meta, received, params, tables, inverse, twiddle, spec, *lens)
    send = send.reshape(pieces)

    received = exchange(send) if dims.fast else to_tokens(send)
    wide = (tokens, dims.width)
    wider = (tokens, 2 * dims.width)
    unit = (dims.units + 1, 8, LANES)
    part = (dims.ni, dims.nz) + unit
    tiles = 2 * dims.width // LANES
    send, result, act, gj, bias, wsend = call(
        bind(gate_kernel, dims),
        (
            shape(*token_pieces),
            shape(*inputs.shape, dtype=bf16),
            shape(*wide, dtype=bf16),
            shape(*wider, dtype=bf16),
            shape(tiles, LANES),
            shape(*part),
        ),
        [SMEM] + [VMEM] * 5,
        [
            vmem(*by_tile),
            vmem(*wide, dtype=bf16),
            vmem(*wider),
            vmem(*wider, dtype=bf16),
            vmem(*by_tile),
            vmem(*token_pieces),
            vmem(dims.width // 2, 2 * dims.width),
            vmem(*part),
            DMA((2,)),
            DMA((max(1, dims.width // LANES),)),
            DMA((dims.ni,)),
        ],
        11,
        5,
        (HBM, VMEM, HBM, HBM, VMEM, HBM),
    )(meta, received, inputs, glu_weight, glu_bias.reshape(1, -1), out_cotangent)
    received = exchange(send) if dims.fast else to_channels(
        send.reshape(dims.seqs, dims.places, dims.width)
    )

    parts = call(
        bind(first_add_kernel, dims),
        (shape(dims.nz, *unit),) * dims.ni,
        [SMEM, HBM, HBM, VMEM, ANY],
        [
            vmem(*wide, dtype=bf16),
            vmem(*wider, dtype=bf16),
            vmem(dims.width // 2, 2 * dims.width),
            vmem(*part),
            DMA((2,)),
            DMA((dims.ni,)),
        ],
        6,
        0.1,
    )(meta, act, gj, bias, swap(wsend, "core", 1))
    parts = [parts[0]] + [swap(parts[s], "batch", s) for s in range(1, dims.ni)]
    send, grads, sums = call(
        bind(backward_kernel, dims),
        (shape(*sent), shape(*two), shape(8, LANES)),
        [VMEM, VMEM] + [HBM] * 6 + [VMEM],
        [
            vmem(*tab, dtype=bf16),
            vmem(*inv, dtype=bf16),
            vmem(*tw),
            vmem(*four),
            vmem(*two),
            vmem(*plain),
            vmem(*plain),
            vmem(*plain),
            vmem(*plain),
            vmem(2, q, 4 * LANES, dtype=bf16),
            vmem(2 * q, 4 * LANES),
            vmem(2, 2 * q, 8 * LANES, dtype=bf16),
            vmem(*plain),
            vmem(*plain),
            vmem(*sent),
            DMA((5,)),
            DMA((chunks,)),
            DMA((dims.nj,)),
            DMA((chunks,)),
        ],
        18,
        9,
        (HBM, HBM, VMEM),
    )(received, params, tables, inverse, twiddle, spec, mixed, normed, stat)
    send = send.reshape(pieces)

    send, parts = lax.optimization_barrier((send, parts))
    parts = call(
        bind(add_kernel, dims.ni), (shape(*unit),) * dims.nz, [VMEM] * dims.ni, [], 2, 0.1
    )(*parts)
    sums, parts = lax.optimization_barrier((sums, parts))
    sums = call(order_kernel, shape(8, LANES), [VMEM], [], 1, 6)(sums)
    send, sums = lax.optimization_barrier((send, sums))
    received = exchange(send) if dims.fast else to_tokens(send)
    parts = [parts[0]] + [swap(parts[s], "z", s) for s in range(1, dims.nz)]
    small = call(
        bind(modes_kernel, dims),
        shape(dims.small_rows, LANES),
        [VMEM] + [HBM] * 4 + [VMEM] * 4,
        [
            vmem(*inv, dtype=bf16),
            vmem(*tw),
            vmem(*four),
            vmem(*two),
            vmem(2, 2 * q, 8 * LANES, dtype=bf16),
            vmem(8 * q, LANES),
            DMA((2,)),
            DMA((2, chunks)),
        ],
        12,
        6,
    )(params, inverse, twiddle, seen, grads, sums, zr, zi, vec)

    units = (dims.units + dims.small_rows // 8, 8, LANES)
    units, bias_grad = call(
        bind(last_add_kernel, dims, dims.nz),
        (shape(*units), shape(1, 2 * dims.width)),
        [VMEM] * (1 + dims.nz),
        [],
        2,
        0.7,
    )(small, *parts)
    pieces_z = everyone(units, "z", dims.nz)
    near = everyone(units, "batch", dims.ni)
    pieces_z, near = lax.optimization_barrier((pieces_z, near))
    near_too = [swap(x, "core", 1) for x in near]
    planes = call(
        stack_kernel, shape(dims.nz - 1, *units.shape), [VMEM] * (dims.nz - 1), [], 2, 0.7
    )(*pieces_z[1:])
    planes = everyone(planes, "batch", dims.ni)
    if dims.fast:
        grad_in = call(
            bind(input_kernel, dims), shape(*inputs.shape), [VMEM] * 2, [vmem(*by_tile)], 4, 1.5
        )(received, out_cotangent)
    else:
        grad_in = out_cotangent.astype(f32) + received.reshape(inputs.shape)
    grad_in, planes, near_too = lax.optimization_barrier((grad_in, planes, near_too))
    planes_too = [swap(x, "core", 1) for x in planes]

    if dims.fast:
        outs = call(
            bind(finish_kernel, dims),
            (shape(dims.width, 2 * dims.width),)
            + (shape(modes, dims.width),) * 6
            + (shape(1, dims.width),) * 4,
            [SMEM] + [VMEM] * (4 * dims.ni),
            [vmem(modes, dims.width)] * 6
            + [vmem(1, dims.width)] * 4
            + [
                vmem(2, dims.ni, dims.width // 2 // dims.ni, 2 * dims.width),
                vmem(2, dims.ni, dims.nz, dims.small_rows, LANES),
                DMA((2, dims.ni)),
                DMA((10,)),
            ],
            5,
            3,
            (HBM,) * 11,
        )(meta, *near, *near_too, *planes, *planes_too)
        weight_grad = outs[0]
        mode_grads = outs[1:7]
        chan_grads = [x.reshape(-1) for x in outs[7:]]
    else:

        def in_order(mine, other):
            both = jnp.where(core == 0, jnp.stack([mine, other]), jnp.stack([other, mine]))
            both = jnp.take(both, meta[0] ^ jnp.arange(dims.ni), axis=1)
            return jnp.take(both, meta[2] ^ jnp.arange(dims.nz), axis=2)

        def joined(first, rest):
            return jnp.concatenate([jnp.stack(first)[:, None], jnp.stack(rest)], axis=1)

        both = in_order(joined(near, planes), joined(near_too, planes_too))
        weight_grad = both[:, :, :, : dims.units].reshape(dims.width // 8, -1, 8, LANES)
        weight_grad = weight_grad.transpose(0, 2, 1, 3).reshape(dims.width, -1)
        rows = both[:, :, :, dims.units :].transpose(1, 2, 0, 3, 4, 5)
        rows = rows.reshape(nd, dims.small_rows, dims.groups, hc)
        table = rows[:, : 6 * m].reshape(nd, 6, m, dims.groups, hc).transpose(1, 3, 2, 0, 4)
        mode_grads = list(table.reshape(6, m * dims.groups, dims.width)[:, :modes])
        rest = rows[:, 6 * m : 6 * m + 4, 0].transpose(1, 0, 2).reshape(4, dims.width)
        chan_grads = list(rest)
    step_grad, gain_grad, shift_grad, skip_grad = chan_grads
    return (
        result,
        grad_in,
        gain_grad,
        shift_grad,
        step_grad,
        *mode_grads,
        skip_grad,
        weight_grad,
        bias_grad.reshape(-1),
    )


def solution(mesh):
    batch = mesh.shape["batch"]
    fine = Mesh(mesh.devices.reshape(-1, 2, batch), ("z", "core", "batch"))
    tokens = P("batch", ("z", "core"), None)
    return jax.shard_map(
        functools.partial(local, dict(fine.shape)),
        mesh=fine,
        in_specs=(tokens, P("batch")) + (P(),) * 12 + (tokens,),
        out_specs=(tokens, tokens) + (P(),) * 12,
        check_vma=False,
    )
```

```python
import functools
import math

import jax
import jax.numpy as jnp
from jax import lax
from jax.experimental import pallas as pl
from jax.experimental.pallas import tpu as pltpu
from jax.sharding import Mesh
from jax.sharding import PartitionSpec as P


EPS = 1e-05
LANES = 128
ALL = ("batch", "z", "core")
SMEM = pl.BlockSpec(memory_space=pltpu.SMEM)
VMEM = pl.BlockSpec(memory_space=pltpu.VMEM)
HBM = pl.BlockSpec(memory_space=pltpu.HBM)
ANY = pl.BlockSpec(memory_space=pl.ANY)
DMA = pltpu.SemaphoreType.DMA
ROWS = 128
STEP = 16
PER = ROWS // STEP
copy = pltpu.make_async_copy
f32 = jnp.float32
bf16 = jnp.bfloat16


def mm(a, b):
    return jnp.dot(a, b, preferred_element_type=f32)


def halves(x):
    hi = x.astype(bf16)
    return hi, (x - hi.astype(f32)).astype(bf16)


def lane_ids(shape):
    return lax.broadcasted_iota(jnp.int32, shape, len(shape) - 1)


def swap_blocks(tiles, width):
    tiles = list(tiles)
    block = lane_ids(tiles[0].shape) // width
    step = 1
    while step < len(tiles):
        low = (block & step) == 0
        for a in range(len(tiles)):
            if a & step == 0:
                first, second = tiles[a], tiles[a + step]
                tiles[a] = jnp.where(low, first, pltpu.roll(second, step * width, second.ndim - 1))
                tiles[a + step] = jnp.where(
                    low, pltpu.roll(first, LANES - step * width, first.ndim - 1), second
                )
        step *= 2
    return tiles


def fold_matrix(dims):
    rows = lax.broadcasted_iota(jnp.int32, (LANES, LANES), 0) % dims.chans
    cols = lax.broadcasted_iota(jnp.int32, (LANES, LANES), 1) % dims.chans
    return (rows == cols).astype(f32).astype(bf16)


def fold(row, dims):
    shift = dims.chans
    while shift < LANES:
        row = row + pltpu.roll(row, shift, 1)
        shift *= 2
    return row


class Dims:
    def __init__(self, inputs_shape, modes, mesh_shape):
        self.seqs, self.places, self.width = inputs_shape
        self.ni = mesh_shape["batch"]
        self.nz = mesh_shape["z"]
        self.nj = mesh_shape["z"] * mesh_shape["core"]
        self.devices = self.ni * self.nj
        self.length = self.places * self.nj
        self.quarter = self.length // 4
        self.chans = self.width // self.devices
        self.groups = LANES // self.chans
        self.all_seqs = self.seqs * self.ni
        self.modes = modes
        self.mode_rows = -(-modes // self.groups)
        self.small_rows = -(-(6 * self.mode_rows + 4) // 8) * 8
        self.piece_width = self.seqs * self.chans
        self.place_groups = LANES // self.piece_width
        self.piece_rows = self.places // self.place_groups
        self.units = self.width * 2 * self.width // (8 * LANES) // self.devices
        self.fast = (
            self.piece_width * self.ni == LANES
            and self.piece_rows % 8 == 0
            and self.nj == self.groups
            and self.small_rows == 32
            and self.place_groups == 4
        )


def each(count, body, unroll=True):
    lax.fori_loop(0, count, lambda k, _: body(k), None, unroll=unroll)


def class_rows(b, g, dims):
    return pl.ds(b * dims.places + g, dims.piece_rows, stride=4)


def pack_tokens(read, write, dims, done=None):
    def some(tile):
        parts = []
        for g in range(4):
            for b in range(dims.seqs):
                parts.append(read(tile, class_rows(b, g, dims)))
        parts = swap_blocks(parts, dims.chans)
        for e in range(dims.groups):
            write(tile * dims.groups + e, parts[e])
        if done is not None:
            done(tile)

    each(dims.width // LANES, some)


def unpack_tokens(ref, out, dims, unroll=True):
    def some(tile):
        parts = [ref[tile * dims.groups + e] for e in range(dims.groups)]
        parts = swap_blocks(parts, dims.chans)
        for g in range(4):
            for b in range(dims.seqs):
                out[tile, class_rows(b, g, dims), :] = parts[g * dims.seqs + b]

    each(dims.width // LANES, some, unroll)


def pack_kernel(dims, x_ref, out_ref, wide):
    for b in range(dims.seqs):
        for t in range(dims.width // LANES):
            wide[t, b * dims.places : (b + 1) * dims.places, :] = x_ref[b, :, lanes(t)].astype(f32)

    def write(piece, value):
        out_ref[piece] = value

    pack_tokens(lambda tile, rows: wide[tile, rows, :], write, dims)


def unpack_channels(ref, out, dims):
    rows = dims.piece_rows
    if not dims.fast:
        for r in range(4):
            out[r] = ref[r * dims.quarter : (r + 1) * dims.quarter, :]
        return

    def some(j):
        parts = [ref[i * dims.nj + j] for i in range(dims.ni)]
        parts = swap_blocks(parts, dims.piece_width)
        for g in range(4):
            out[g, pl.ds(pl.multiple_of(j * rows, rows), rows), :] = parts[g]

    each(dims.nj, some)


def pack_channels(read, send, send_hbm, sem, dims):
    rows = dims.piece_rows
    if not dims.fast:
        for r in range(4):
            for at in range(0, dims.quarter, ROWS):
                start = r * dims.quarter + at
                send[start : start + ROWS, :] = read(r, at, ROWS)
        whole = copy(send, send_hbm, sem.at[0])
        whole.start()
        whole.wait()
        return

    def pieces(j):
        return copy(send.at[:, j], send_hbm.at[:, j], sem.at[j])

    for j in range(dims.nj):
        parts = swap_blocks([read(g, j * rows, rows) for g in range(4)], dims.piece_width)
        for i in range(dims.ni):
            send[i, j] = parts[i]
        pieces(j).start()
    for j in range(dims.nj):
        pieces(j).wait()


def mode_constants(par_ref, dims):
    m = dims.mode_rows
    decay, rotation, dr, di, rr, ri = [par_ref[p * m : (p + 1) * m, :] for p in range(6)]
    step = jnp.exp(par_ref[6 * m : 6 * m + 1, :])
    log_mag = -step * decay
    turn = step * rotation
    c1r = step * (rr * dr - ri * di)
    c1i = step * (rr * di + ri * dr)
    c2r = c1r * dr - c1i * di
    c2i = c1r * di + c1i * dr
    return step, log_mag, turn, (c1r, c1i, c2r, c2i), (decay, rotation, dr, di, rr, ri)


def waves_kernel(dims, par_ref, zr_ref, zi_ref, vec_ref, cat_ref, wave):
    m, q = dims.mode_rows, dims.quarter
    step, log_mag, turn, coefs, _ = mode_constants(par_ref, dims)
    c1r, c1i, c2r, c2i = coefs
    mag = jnp.exp(log_mag)
    l1r, l1i = mag * jnp.cos(turn), mag * jnp.sin(turn)
    mag = jnp.exp(8.0 * log_mag)
    l32r, l32i = mag * jnp.cos(8.0 * turn), mag * jnp.sin(8.0 * turn)
    for _ in range(2):
        l32r, l32i = l32r * l32r - l32i * l32i, 2.0 * l32r * l32i
    for p, value in enumerate((l32r, l32i, c1r, c1i, c2r, c2i)):
        vec_ref[p * m : (p + 1) * m, :] = value
    sub = 4.0 * lax.broadcasted_iota(jnp.int32, (8, LANES), 0).astype(f32)

    def wide(x, k):
        return jnp.broadcast_to(x[k : k + 1], (8, LANES))

    for k in range(m):
        mag = jnp.exp(sub * log_mag[k : k + 1])
        zr, zi = mag * jnp.cos(sub * turn[k : k + 1]), mag * jnp.sin(sub * turn[k : k + 1])
        for r in range(4):
            zr_ref[r, 8 * k : 8 * k + 8, :] = zr
            zi_ref[r, 8 * k : 8 * k + 8, :] = zi
            ar, ai = wide(l1r, k), wide(l1i, k)
            zr, zi = zr * ar - zi * ai, zr * ai + zi * ar
    consts = [
        tuple(wide(x, k) for x in (l32r, l32i, 2 * c1r, 2 * c1i, 2 * c2r, 2 * c2i)) for k in range(m)
    ]
    group = fold_matrix(dims)
    for r in range(4):

        def time_step(t, zs):
            at = pl.multiple_of(t * 8, 8)
            k1 = jnp.zeros((8, LANES), f32)
            k2 = jnp.zeros((8, LANES), f32)
            out = []
            for k in range(m):
                zr, zi = zs[2 * k], zs[2 * k + 1]
                ar, ai, b1r, b1i, b2r, b2i = consts[k]
                k1 = k1 + (b1r * zr - b1i * zi)
                k2 = k2 + (b2r * zr - b2i * zi)
                out += [zr * ar - zi * ai, zr * ai + zi * ar]
            wave[pl.ds(at, 8), lanes(0)] = k1
            wave[pl.ds(at, 8), lanes(1)] = k2
            return tuple(out)

        start = []
        for k in range(m):
            start += [zr_ref[r, 8 * k : 8 * k + 8, :], zi_ref[r, 8 * k : 8 * k + 8, :]]
        lax.fori_loop(0, q // 8, time_step, tuple(start), unroll=4)
        for p in range(2):
            both = halves(over_groups(wave[0:q, lanes(p)], group))
            for part in range(2):
                cat_ref[part, :, lanes(2 * r + p)] = both[part]


def tables_kernel(dims, cat_ref, tab_hbm, inv_hbm, tw_hbm, spec_hbm, *scratch):
    tab, inv, tw, spec, wave, sem_out, sem_spec = scratch
    n, q = dims.length, dims.quarter

    def angles(b, _):
        at = pl.multiple_of(b * ROWS, ROWS)
        row = 2 * (lax.broadcasted_iota(jnp.int32, (ROWS, q), 0) + at) + 1
        col = 2 * lax.broadcasted_iota(jnp.int32, (ROWS, q), 1) + 1
        turn = ((row * col) & (8 * q - 1)).astype(f32) * (math.pi / (4 * q))
        for first, value in ((0, jnp.cos(turn)), (q, jnp.sin(turn))):
            for part, half in enumerate(halves(value)):
                tab[part, pl.ds(pl.multiple_of(first + at, ROWS), ROWS), :] = half
                inv[part, pl.ds(at, ROWS), first : first + q] = half
        row = 2 * (lax.broadcasted_iota(jnp.int32, (ROWS, LANES), 0) + at) + 1
        turn = row.astype(f32) * (math.pi / (2 * n))
        cos, sin = jnp.cos(turn), jnp.sin(turn)
        for p, value in enumerate((cos, sin, 1.0 - 2.0 * sin * sin, 2.0 * cos * sin)):
            tw[p, pl.ds(at, ROWS), :] = value
        return 0

    lax.fori_loop(0, q // ROWS, angles, 0)
    outs = [copy(tab, tab_hbm, sem_out.at[0]), copy(tw, tw_hbm, sem_out.at[1])]
    outs.append(copy(inv, inv_hbm, sem_out.at[2]))
    for out in outs:
        out.start()
    forth(tab, cat_ref, wave)

    def spectrum(b, _):
        at = pl.multiple_of(b * STEP, STEP)
        chunk, rows = place_of(b)
        for p in range(2):
            for k, (re, im) in enumerate(butterfly(wave, tw, at, p, 2, dims)):
                spec[chunk, k, rows, lanes(2 * p)] = re * (1.0 / n)
                spec[chunk, k, rows, lanes(2 * p + 1)] = im * (1.0 / n)
        return 0

    lax.fori_loop(0, q // STEP, spectrum, 0)
    outs.append(copy(spec, spec_hbm, sem_spec))
    outs[-1].start()
    for out in outs:
        out.wait()


def lanes(p):
    return slice(p * LANES, (p + 1) * LANES)


def over_groups(x, group):
    return mm(jnp.concatenate(halves(x), axis=1), jnp.concatenate([group, group], axis=0))


def place_of(b):
    return b // PER, pl.ds(pl.multiple_of(b % PER * STEP, STEP), STEP)


def product(table, operand):
    (high, low), (first, second) = table, operand
    return mm(
        jnp.concatenate([high, high, low], axis=1), jnp.concatenate([first, second, first], axis=0)
    )


def forth(tab, cat, wave):
    wave[...] = product((tab[0], tab[1]), (cat[0], cat[1]))


def twiddles(tw, at):
    c1, s1, c2, s2 = [tw[p, pl.ds(at, STEP), :] for p in range(4)]
    return (c2, s2), (c1, s1), None, (c1, -s1)


def times(a, b):
    if b is None:
        return a
    return a[0] * b[0] - a[1] * b[1], a[0] * b[1] + a[1] * b[0]


def plus(a, b):
    return a[0] + b[0], a[1] + b[1]


def minus(a, b):
    return a[0] - b[0], a[1] - b[1]


def turned(a):
    return -a[1], a[0]


def butterfly(wave, tw, at, p, count, dims):
    below = pl.multiple_of(dims.quarter + at, STEP)
    parts = []
    for r, twiddle in enumerate(twiddles(tw, at)):
        re = wave[pl.ds(at, STEP), lanes(r * count + p)]
        im = wave[pl.ds(below, STEP), lanes(r * count + p)]
        parts.append(times((re, -im), twiddle))
    even, odd = plus(parts[0], parts[2]), plus(parts[1], parts[3])
    even_too, odd_too = minus(parts[0], parts[2]), turned(minus(parts[1], parts[3]))
    return plus(even, odd), minus(even_too, odd_too), minus(even, odd), plus(even_too, odd_too)


def unbutterfly(parts, tw, at, cat, p, count, dims):
    even, odd = plus(parts[0], parts[2]), plus(parts[1], parts[3])
    even_too, odd_too = minus(parts[0], parts[2]), turned(minus(parts[1], parts[3]))
    sums = plus(even, odd), plus(even_too, odd_too), minus(even, odd), minus(even_too, odd_too)
    for r, twiddle in enumerate(twiddles(tw, at)):
        if twiddle is not None:
            twiddle = twiddle[0], -twiddle[1]
        re, im = times(sums[r], twiddle)
        for first, value in ((0, re), (dims.quarter, -im)):
            rows = pl.ds(pl.multiple_of(first + at, STEP), STEP)
            for part, half in enumerate(halves(value)):
                cat[part, rows, lanes(r * count + p)] = half


def back(inv, cat):
    return product((inv[0], inv[1]), (cat[0], cat[1]))


def column_sums(x):
    return jnp.sum(x.reshape(x.shape[0] // 8, 8, LANES), axis=0)


def lane_lengths(meta_ref, lens_refs, dims):
    lane = lane_ids((1, LANES)) // dims.chans
    row = jnp.zeros((1, LANES), jnp.int32)
    total = jnp.int32(0)
    for s in range(dims.all_seqs):
        source = s // dims.seqs
        value = lens_refs[source][s % dims.seqs]
        total = total + value
        row = jnp.where(lane == s ^ (meta_ref[0] * dims.seqs), value, row)
    return row, total.astype(f32)


def valid_rows(r, at, rows, lens):
    places = 4 * (lax.broadcasted_iota(jnp.int32, (rows, LANES), 0) + at) + r
    return (places < lens).astype(f32)


def forward_kernel(dims, meta_ref, r_ref, par_ref, tab_hbm, inv_hbm, tw_hbm, spec_hbm, *rest):
    lens_refs, rest = rest[: dims.ni], rest[dims.ni :]
    (send_hbm, mixed_hbm, normed_hbm, seen_hbm, stat_ref), rest = rest[:5], rest[5:]
    tab, inv, tw, spec, seen, x_sc, mix_sc, normed_sc, cat, wave, back_cat, send = rest[:12]
    sem_tab, sem_spec, sem_seen, sem_out, sem_send = rest[12:]
    m, q = dims.mode_rows, dims.quarter
    chunks = q // ROWS
    ins = [copy(tab_hbm, tab, sem_tab.at[0]), copy(tw_hbm, tw, sem_tab.at[1])]
    ins += [copy(spec_hbm.at[c], spec.at[c], sem_spec.at[c]) for c in range(chunks)]
    ins.append(copy(inv_hbm, inv, sem_tab.at[2]))
    for one in ins:
        one.start()
    lens, total = lane_lengths(meta_ref, lens_refs, dims)
    unpack_channels(r_ref, x_sc, dims)
    classes = range(4)

    def add_up(b, acc):
        at = pl.multiple_of(b * ROWS, ROWS)
        for r in classes:
            acc = acc + column_sums(x_sc[r, pl.ds(at, ROWS), :] * valid_rows(r, at, ROWS, lens))
        return acc

    zero = jnp.zeros((8, LANES), f32)
    acc = lax.fori_loop(0, q // ROWS, add_up, zero, unroll=True)
    average = fold(jnp.sum(acc, axis=0, keepdims=True), dims) / total

    def add_squares(b, acc):
        at = pl.multiple_of(b * ROWS, ROWS)
        for r in classes:
            x = (x_sc[r, pl.ds(at, ROWS), :] - average) * valid_rows(r, at, ROWS, lens)
            acc = acc + column_sums(x * x)
        return acc

    acc = lax.fori_loop(0, q // ROWS, add_squares, zero, unroll=True)
    variance = fold(jnp.sum(acc, axis=0, keepdims=True), dims) / total
    inv_scale = lax.rsqrt(variance + EPS)
    gain = par_ref[6 * m + 1 : 6 * m + 2, :]
    shift = par_ref[6 * m + 2 : 6 * m + 3, :]
    skip = par_ref[6 * m + 3 : 6 * m + 4, :]
    stat_ref[0:1, :] = inv_scale
    stat_ref[1:2, :] = jnp.broadcast_to(total, (1, LANES))
    stat_ref[2:3, :] = lens.astype(f32)
    stat_ref[3:8, :] = jnp.zeros((5, LANES), f32)
    first_row = lax.broadcasted_iota(jnp.int32, (ROWS, LANES), 0) == 0

    def normalize(b, last):
        at = pl.multiple_of(b * ROWS, ROWS)
        mixed = []
        for r in classes:
            normed = (x_sc[r, pl.ds(at, ROWS), :] - average) * inv_scale
            mixed.append((gain * normed + shift) * valid_rows(r, at, ROWS, lens))
            normed_sc[r, pl.ds(at, ROWS), :] = normed
            mix_sc[r, pl.ds(at, ROWS), :] = mixed[r]
        earlier = jnp.where(first_row, last, pltpu.roll(mixed[3], 1, 0))
        for r in classes:
            liquid = mixed[r] * (earlier if r == 0 else mixed[r - 1])
            for p, value in enumerate((mixed[r], liquid)):
                for part, half in enumerate(halves(value)):
                    cat[part, pl.ds(at, ROWS), lanes(2 * r + p)] = half
        return mixed[3][ROWS - 1 :, :]

    lax.fori_loop(0, q // ROWS, normalize, jnp.zeros((1, LANES), f32))
    outs = [copy(mix_sc, mixed_hbm, sem_out.at[0]), copy(normed_sc, normed_hbm, sem_out.at[1])]
    for out in outs:
        out.start()
    ins[0].wait()
    forth(tab, cat, wave)
    ins[1].wait()
    for c in range(chunks):
        ins[2 + c].wait()

        def multiply(b, _):
            at = pl.multiple_of(b * STEP, STEP)
            chunk, rows = place_of(b)
            mixed = butterfly(wave, tw, at, 0, 2, dims)
            liquid = butterfly(wave, tw, at, 1, 2, dims)
            parts = []
            for k in range(4):
                for p, value in enumerate(mixed[k] + liquid[k]):
                    seen[chunk, k, rows, lanes(p)] = value
                kr, ki, lr, li = [spec[chunk, k, rows, lanes(p)] for p in range(4)]
                parts.append(plus(times(mixed[k], (kr, ki)), times(liquid[k], (lr, li))))
            unbutterfly(parts, tw, at, back_cat, 0, 1, dims)
            return 0

        lax.fori_loop(PER * c, PER * (c + 1), multiply, 0, unroll=PER)
        outs.append(copy(seen.at[c], seen_hbm.at[c], sem_seen.at[c]))
        outs[-1].start()
    ins[-1].wait()

    value = back(inv, back_cat)
    for r in classes:
        x_sc[r] = value[:, lanes(r)] + skip * mix_sc[r]
    pack_channels(
        lambda r, at, size: x_sc[r, pl.ds(at, size), :], send, send_hbm, sem_send, dims
    )
    for out in outs:
        out.wait()


def gate_kernel(dims, meta_ref, r_ref, x_ref, w_ref, b_ref, ct_ref, *rest):
    (send_hbm, out_ref, act_hbm, gj_hbm, bias_ref, wsend_hbm), scratch = rest[:6], rest[6:]
    resp, act, joined, gj, gact, send, weight, wsend, sem_out, sem_send, sem_weight = scratch
    tokens = dims.seqs * dims.places
    width = dims.width
    places = dims.places

    tiles = range(width // LANES)
    if dims.fast:
        unpack_tokens(r_ref, resp, dims)
    else:
        for t in tiles:
            resp[t] = r_ref[:, lanes(t)]
    c0 = math.sqrt(2.0 / math.pi)
    c1 = 0.044715
    rows = 32

    def gelu(b, _):
        at = pl.multiple_of(b * rows, rows)
        for tile in tiles:
            r = resp[tile, pl.ds(at, rows), :]
            t = jnp.tanh(c0 * (r + c1 * r * r * r))
            act[pl.ds(at, rows), lanes(tile)] = (0.5 * r * (1.0 + t)).astype(bf16)
            slope = 0.5 * (1.0 + t) + 0.5 * r * (1.0 - t * t) * (c0 * (1.0 + 3.0 * c1 * r * r))
            resp[tile, pl.ds(at, rows), :] = slope
        return 0

    lax.fori_loop(0, tokens // rows, gelu, 0)
    outs = [copy(act, act_hbm, sem_out.at[0]), copy(gj, gj_hbm, sem_out.at[1])]
    outs[0].start()
    joined[...] = mm(act[...], w_ref[...])
    bias = b_ref[...]
    half = min(16, places)
    for b in range(dims.seqs):

        def gate(k, sums):
            at = pl.multiple_of(k * half, half)
            tok = pl.multiple_of(b * places + k * half, half)
            value = joined[pl.ds(tok, half), :width] + bias[:, :width]
            s = jax.nn.sigmoid(joined[pl.ds(tok, half), width:] + bias[:, width:])
            x = x_ref[b, pl.ds(at, half), :].astype(f32)
            g = ct_ref[b, pl.ds(at, half), :].astype(f32)
            out_ref[b, pl.ds(at, half), :] = (x + value * s).astype(bf16)
            gs = g * s
            first = gs.astype(bf16)
            second = (gs * value * (1.0 - s)).astype(bf16)
            gj[pl.ds(tok, half), :width] = first
            gj[pl.ds(tok, half), width:] = second
            first = jnp.sum(first.astype(f32).reshape(half // 8, 8, width), axis=0)
            second = jnp.sum(second.astype(f32).reshape(half // 8, 8, width), axis=0)
            return sums[0] + first, sums[1] + second

        if b == 0:
            zero = jnp.zeros((8, width), f32)
            sums = (zero, zero)
        sums = lax.fori_loop(0, places // half, gate, sums)
    outs[1].start()
    sums = [jnp.sum(s, axis=0, keepdims=True) for s in sums]
    for p, total in enumerate(sums):
        for t in tiles:
            row = p * (width // LANES) + t
            bias_ref[row : row + 1, :] = total[:, lanes(t)]
    weight_half(dims, meta_ref, 1 - meta_ref[1], act, gj, weight)
    for i in range(dims.ni):
        for z in range(dims.nz):
            for u in range(dims.units):
                wsend[i, z, u, :, :] = weight_unit(dims, meta_ref, weight, i, z, u)
            wsend[i, z, dims.units, :, :] = bias_ref[...]
        outs.append(copy(wsend.at[i], wsend_hbm.at[i], sem_weight.at[i]))
        outs[-1].start()
    grad = lax.dot_general(
        gj[...], w_ref[...], (((1,), (1,)), ((), ())), preferred_element_type=f32
    )
    for t in tiles:
        gact[t] = grad[:, lanes(t)]
    if dims.fast:

        def read(tile, rows):
            return gact[tile, rows, :] * resp[tile, rows, :]

        def put(piece, value):
            send[piece] = value

        def tile_copy(tile):
            some = pl.ds(tile * dims.groups, dims.groups)
            return copy(send.at[some], send_hbm.at[some], sem_send.at[tile])

        pack_tokens(read, put, dims, lambda tile: tile_copy(tile).start())
        outs += [tile_copy(tile) for tile in tiles]
    else:
        for t in tiles:
            send[:, lanes(t)] = gact[t] * resp[t]
        outs.append(copy(send, send_hbm, sem_send.at[0]))
        outs[-1].start()
    for out in outs:
        out.wait()


def weight_half(dims, meta_ref, core, act, gj, weight):
    half = dims.width // 2
    some = act[:, pl.ds(pl.multiple_of(core * half, half), half)]
    weight[...] = lax.dot_general(
        some, gj[...], (((0,), (0,)), ((), ())), preferred_element_type=f32
    )


def weight_unit(dims, meta_ref, weight, i, z, u):
    tiles = 2 * dims.width // LANES
    owner = (meta_ref[0] ^ i) * dims.nz + (meta_ref[2] ^ z)
    if dims.units % tiles == 0:
        row = owner * (dims.units // tiles) + u // tiles
        cols = lanes(u % tiles)
    else:
        unit = owner * dims.units + u
        row = unit // tiles
        cols = pl.ds(pl.multiple_of(unit % tiles * LANES, LANES), LANES)
    return weight[pl.ds(pl.multiple_of(row * 8, 8), 8), cols]


def backward_kernel(dims, r_ref, par_ref, *rest):
    ins_hbm, (stat_ref, send_hbm, grad_hbm, sums_ref) = rest[:6], rest[6:10]
    tab, inv, tw, spec, grads, mix_sc, normed_sc, g_sc, up_sc, cat, wave, back_cat = rest[10:22]
    lead_sc, liquid_sc, send, sem_in, sem_spec, sem_send, sem_grad = rest[22:]
    tab_hbm, inv_hbm, tw_hbm, spec_hbm, mixed_hbm, normed_hbm = ins_hbm
    m, q = dims.mode_rows, dims.quarter
    ins = [
        copy(mixed_hbm, mix_sc, sem_in.at[0]),
        copy(tab_hbm, tab, sem_in.at[1]),
        copy(tw_hbm, tw, sem_in.at[2]),
        copy(normed_hbm, normed_sc, sem_in.at[3]),
        copy(inv_hbm, inv, sem_in.at[4]),
    ]
    chunks = q // ROWS
    for c in range(chunks):
        ins.insert(3 + c, copy(spec_hbm.at[c], spec.at[c], sem_spec.at[c]))
    for one in ins:
        one.start()
    unpack_channels(r_ref, g_sc, dims)
    gain = par_ref[6 * m + 1 : 6 * m + 2, :]
    skip = par_ref[6 * m + 3 : 6 * m + 4, :]
    inv_scale = stat_ref[0:1, :]
    total = stat_ref[1:2, :]
    lens = stat_ref[2:3, :].astype(jnp.int32)
    zero = jnp.zeros((8, LANES), f32)
    classes = range(4)
    ins[0].wait()

    def gather(b, acc):
        at = pl.multiple_of(b * ROWS, ROWS)
        for r in classes:
            g = g_sc[r, pl.ds(at, ROWS), :]
            for part, half in enumerate(halves(g)):
                cat[part, pl.ds(at, ROWS), lanes(r)] = half
            acc = acc + column_sums(g * mix_sc[r, pl.ds(at, ROWS), :])
        return acc

    skip_acc = lax.fori_loop(0, q // ROWS, gather, zero)
    ins[1].wait()
    forth(tab, cat, wave)
    ins[2].wait()
    outs = []
    for c in range(chunks):
        ins[3 + c].wait()

        def multiply(b, _):
            at = pl.multiple_of(b * STEP, STEP)
            chunk, rows = place_of(b)
            grad = butterfly(wave, tw, at, 0, 1, dims)
            for k in range(4):
                for p in range(2):
                    grads[chunk, k, rows, lanes(p)] = grad[k][p]
            for p in range(2):
                products(grad, spec, tw, b, back_cat, p, dims)
            return 0

        lax.fori_loop(PER * c, PER * (c + 1), multiply, 0, unroll=PER)
        outs.append(copy(grads.at[c], grad_hbm.at[c], sem_grad.at[c]))
        outs[-1].start()
    for one in ins[3 + chunks :]:
        one.wait()

    value = back(inv, back_cat)
    for r in classes:
        lead_sc[r] = value[:, lanes(2 * r)]
        liquid_sc[r] = value[:, lanes(2 * r + 1)]
        up_sc[r] = value[:, lanes(2 * r + 1)] * mix_sc[r]

    row = lax.broadcasted_iota(jnp.int32, (ROWS, LANES), 0)
    blank = jnp.zeros((1, LANES), f32)
    gain_acc, shift_acc = zero, zero
    for at in range(0, q, ROWS):
        rows = slice(at, at + ROWS)
        for r in classes:
            if r == 0:
                before = blank if at == 0 else mix_sc[3, at - 1 : at, :]
                earlier = jnp.where(row == 0, before, pltpu.roll(mix_sc[3, rows, :], 1, 0))
            else:
                earlier = mix_sc[r - 1, rows, :]
            if r == 3:
                after = blank if at + ROWS == q else up_sc[0, at + ROWS : at + ROWS + 1, :]
                up = jnp.where(row == ROWS - 1, after, pltpu.roll(up_sc[0, rows, :], ROWS - 1, 0))
            else:
                up = up_sc[r + 1, rows, :]
            masked = lead_sc[r, rows, :] + skip * g_sc[r, rows, :] + liquid_sc[r, rows, :] * earlier
            masked = (masked + up) * valid_rows(r, at, ROWS, lens)
            g_sc[r, rows, :] = masked
            gain_acc = gain_acc + column_sums(masked * normed_sc[r, rows, :])
            shift_acc = shift_acc + column_sums(masked)

    def whole(acc):
        return fold(jnp.sum(acc, axis=0, keepdims=True), dims)

    gain_sum, shift_sum, skip_sum = whole(gain_acc), whole(shift_acc), whole(skip_acc)
    scale = gain * inv_scale
    shift_mean = shift_sum / total
    gain_mean = gain_sum / total

    def read(r, at, size):
        normed = normed_sc[r, pl.ds(at, size), :]
        value = g_sc[r, pl.ds(at, size), :] - shift_mean - normed * gain_mean
        return value * scale * valid_rows(r, at, size, lens)

    sums_ref[...] = jnp.zeros_like(sums_ref)
    for p, value in enumerate((gain_sum, shift_sum, skip_sum)):
        sums_ref[p : p + 1, :] = value
    pack_channels(read, send, send_hbm, sem_send, dims)
    for out in outs:
        out.wait()


def products(grad, ref, tw, b, cat, p, dims):
    chunk, rows = place_of(b)
    parts = []
    for k in range(4):
        re = ref[chunk, k, rows, lanes(2 * p)]
        im = ref[chunk, k, rows, lanes(2 * p + 1)]
        parts.append(times(grad[k], (re, -im)))
    unbutterfly(parts, tw, pl.multiple_of(b * STEP, STEP), cat, p, 2, dims)


def modes_kernel(dims, par_ref, inv_hbm, tw_hbm, seen_hbm, grad_hbm, sums_ref, *rest):
    zr_ref, zi_ref, vec_ref, small_ref, inv, tw, seen, grads, back_cat, dk, sem, sem_in = rest
    n, m, q = dims.length, dims.mode_rows, dims.quarter
    chunks = q // ROWS
    ins = [copy(tw_hbm, tw, sem.at[0])]
    for c in range(chunks):
        ins.append(copy(seen_hbm.at[c], seen.at[c], sem_in.at[0, c]))
        ins.append(copy(grad_hbm.at[c], grads.at[c], sem_in.at[1, c]))
    ins.append(copy(inv_hbm, inv, sem.at[1]))
    for one in ins:
        one.start()
    zero = jnp.zeros((8, LANES), f32)
    classes = range(4)
    ins[0].wait()
    for c in range(chunks):
        ins[1 + 2 * c].wait()
        ins[2 + 2 * c].wait()

        def multiply(b, _):
            chunk, rows = place_of(b)
            grad = [tuple(grads[chunk, k, rows, lanes(p)] for p in range(2)) for k in range(4)]
            for p in range(2):
                products(grad, seen, tw, b, back_cat, p, dims)
            return 0

        lax.fori_loop(PER * c, PER * (c + 1), multiply, 0, unroll=PER)
    ins[-1].wait()
    group = fold_matrix(dims)

    value = back(inv, back_cat) * (1.0 / n)
    dk[...] = over_groups(jnp.concatenate([value[:, lanes(p)] for p in range(8)], axis=0), group)

    step, log_mag, turn, _, params = mode_constants(par_ref, dims)
    decay, rotation, dr, di, rr, ri = params
    l32r, l32i, c1r, c1i, c2r, c2i = [vec_ref[p * m : (p + 1) * m, :] for p in range(6)]
    sub = 4.0 * lax.broadcasted_iota(jnp.int32, (8, LANES), 0).astype(f32)
    sums = [[] for _ in range(8)]
    for first in range(0, m, 2):
        some = range(first, min(m, first + 2))
        ratio = [
            (
                jnp.broadcast_to(l32r[k : k + 1], (8, LANES)),
                jnp.broadcast_to(l32i[k : k + 1], (8, LANES)),
            )
            for k in some
        ]
        sofar = [zero] * (8 * len(ratio))
        for r in classes:

            def mode_step(t, carry):
                at = pl.multiple_of(t * 8, 8)
                d1 = dk[pl.ds(pl.multiple_of(2 * r * q + at, 8), 8), :]
                d2 = dk[pl.ds(pl.multiple_of((2 * r + 1) * q + at, 8), 8), :]
                place = sub + (32 * t + r).astype(f32)
                e1 = d1 * place
                e2 = d2 * place
                out = []
                for k, (ar, ai) in enumerate(ratio):
                    zr, zi, *acc = carry[10 * k : 10 * (k + 1)]
                    out += [zr * ar - zi * ai, zr * ai + zi * ar]
                    for p, d in enumerate((d1, d2, e1, e2)):
                        out += [acc[2 * p] + d * zr, acc[2 * p + 1] + d * zi]
                return tuple(out)

            carry = []
            for at, k in enumerate(some):
                carry += [zr_ref[r, 8 * k : 8 * k + 8, :], zi_ref[r, 8 * k : 8 * k + 8, :]]
                carry += sofar[8 * at : 8 * at + 8]
            carry = lax.fori_loop(0, q // 8, mode_step, tuple(carry), unroll=4)
            sofar = [v for k in range(len(ratio)) for v in carry[10 * k + 2 : 10 * k + 10]]
        for k in range(len(ratio)):
            for p in range(8):
                sums[p].append(jnp.sum(sofar[8 * k + p], axis=0, keepdims=True))
    a1r, a1i, a2r, a2i, e1r, e1i, e2r, e2i = [
        jnp.concatenate(s, axis=0) if len(s) > 1 else s[0] for s in sums
    ]
    btr = c1r * e1r - c1i * e1i + c2r * e2r - c2i * e2i
    bti = c1r * e1i + c1i * e1r + c2r * e2i + c2i * e2r
    d2r = dr * dr - di * di
    d2i = 2.0 * dr * di
    erd = step * (a1r * dr - a1i * di + a2r * d2r - a2i * d2i)
    eri = step * (a1r * di + a1i * dr + a2r * d2i + a2i * d2r)
    tr = a1r + 2.0 * (a2r * dr - a2i * di)
    ti = a1i + 2.0 * (a2r * di + a2i * dr)
    edr = step * (rr * tr - ri * ti)
    edi = step * (rr * ti + ri * tr)
    by_step = 2.0 * (c1r * a1r - c1i * a1i + c2r * a2r - c2i * a2i) + 2.0 * step * (
        -decay * btr - rotation * bti
    )
    small_ref[...] = jnp.zeros_like(small_ref)
    answers = (-2.0 * step * btr, -2.0 * step * bti, 2.0 * edr, -2.0 * edi, 2.0 * erd, -2.0 * eri)
    for p, value in enumerate(answers):
        small_ref[p * m : (p + 1) * m, :] = value
    small_ref[6 * m : 6 * m + 1, :] = fold(jnp.sum(by_step, axis=0, keepdims=True), dims)
    small_ref[6 * m + 1 : 6 * m + 4, :] = sums_ref[0:3, :]


def first_add_kernel(dims, meta_ref, act_hbm, gj_hbm, bias_ref, other_hbm, *refs):
    out_refs, (act, gj, weight, other, sem_in, sem) = refs[: dims.ni], refs[dims.ni :]
    ins = [copy(act_hbm, act, sem_in.at[0]), copy(gj_hbm, gj, sem_in.at[1])]
    others = [copy(other_hbm.at[i], other.at[i], sem.at[i]) for i in range(dims.ni)]
    for one in ins + others:
        one.start()
    for one in ins:
        one.wait()
    weight_half(dims, meta_ref, meta_ref[1], act, gj, weight)
    for i in range(dims.ni):
        others[i].wait()
        for z in range(dims.nz):
            for u in range(dims.units):
                unit = weight_unit(dims, meta_ref, weight, i, z, u)
                out_refs[i][z, u] = unit + other[i, z, u]
            out_refs[i][z, dims.units] = bias_ref[...] + other[i, z, dims.units]


def order_kernel(sums_ref, out_ref):
    out_ref[...] = sums_ref[...]


def add_kernel(count, *refs):
    for p, out_ref in enumerate(refs[count:]):
        total = refs[0][p]
        for ref in refs[1:count]:
            total = total + ref[p]
        out_ref[...] = total


def last_add_kernel(dims, count, small_ref, *refs):
    units_ref, bias_ref = refs[count:]

    def unit(u):
        total = refs[0][u]
        for ref in refs[1:count]:
            total = total + ref[u]
        return total

    for u in range(dims.units):
        units_ref[u] = unit(u)
    for t in range(dims.small_rows // 8):
        units_ref[dims.units + t] = small_ref[8 * t : 8 * t + 8, :]
    bias = unit(dims.units)
    for t in range(2 * dims.width // LANES):
        bias_ref[:, lanes(t)] = bias[t : t + 1, :]


def stack_kernel(*refs):
    for k, ref in enumerate(refs[:-1]):
        refs[-1][k] = ref[...]


def input_kernel(dims, r_ref, ct_ref, grad_ref, grad):
    unpack_tokens(r_ref, grad, dims, False)
    for b in range(dims.seqs):
        for t in range(dims.width // LANES):
            value = grad[t, b * dims.places : (b + 1) * dims.places, :]
            grad_ref[b, :, lanes(t)] = value + ct_ref[b, :, lanes(t)].astype(f32)


def finish_kernel(dims, meta_ref, *refs):
    ni, nz, m = dims.ni, dims.nz, dims.mode_rows
    near = refs[:ni], refs[ni : 2 * ni]
    far = refs[2 * ni : 3 * ni], refs[3 * ni : 4 * ni]
    weight_ref, *small_hbm = refs[4 * ni : 4 * ni + 11]
    *small_refs, rows, small, sem, sem_small = refs[4 * ni + 11 :]
    me, core, me_z = meta_ref[0], meta_ref[1], meta_ref[2]
    tiles = 2 * dims.width // LANES
    per = 8 * dims.units // tiles
    copies = []
    for half, side in ((0, core), (1, 1 - core)):
        for i in range(ni):
            for z in range(nz):
                piece = near[half][i] if z == 0 else far[half][i].at[z - 1]
                for u in range(dims.units):
                    at = pl.multiple_of((me_z ^ z) * per + u // tiles * 8, 8)
                    rows[half, i, pl.ds(at, 8), lanes(u % tiles)] = piece[u]
                value = piece[dims.units :].reshape(dims.small_rows, LANES)
                small[half, i, me_z ^ z] = value
            at = pl.multiple_of((side * ni + (me ^ i)) * nz * per, nz * per)
            target = weight_ref.at[pl.ds(at, nz * per), :]
            copies.append(copy(rows.at[half, i], target, sem.at[half, i]))
            copies[-1].start()
    first = core == 0
    for i in range(ni):
        parts = []
        for z in range(nz):
            a, b = small[0, i, z], small[1, i, z]
            parts += [jnp.where(first, a, b), jnp.where(first, b, a)]
        parts = swap_blocks(parts, dims.chans)
        cols = pl.ds(pl.multiple_of((me ^ i) * LANES, LANES), LANES)
        for q in range(dims.groups):
            for p in range(6):
                small_refs[p][q * m : q * m + m, cols] = parts[q][p * m : p * m + m, :]
        for p in range(4):
            small_refs[6 + p][:, cols] = parts[0][6 * m + p : 6 * m + p + 1, :]
    for p, (ref, hbm) in enumerate(zip(small_refs, small_hbm)):
        copies.append(copy(ref, hbm, sem_small.at[p]))
        copies[-1].start()
    for one in copies:
        one.wait()


def call(kernel, out_shape, in_specs, scratch, limit, us, out_specs=None):
    cost = pl.CostEstimate(flops=int(us * 1.1e9), bytes_accessed=int(us * 3e6), transcendentals=0)
    if out_specs is None:
        out_specs = jax.tree.map(lambda _: VMEM, out_shape)
    else:
        out_shape = tuple(
            pltpu.HBM(out.shape, out.dtype) if spec is HBM else out
            for out, spec in zip(out_shape, out_specs)
        )

    def run(*args):
        args = [
            pltpu.with_memory_space_constraint(x, pltpu.HBM) if spec is HBM else x
            for x, spec in zip(args, in_specs)
        ]
        return pl.pallas_call(
            kernel,
            out_shape=out_shape,
            in_specs=in_specs,
            out_specs=out_specs,
            scratch_shapes=scratch,
            compiler_params=pltpu.CompilerParams(vmem_limit_bytes=limit << 20),
            cost_estimate=cost,
        )(*args)

    return run


def shape(*dims, dtype=f32):
    return jax.ShapeDtypeStruct(dims, dtype)


def local(
    mesh_shape,
    inputs,
    lengths,
    norm_gain,
    norm_shift,
    log_step,
    decay_rate,
    rotation,
    drive_real,
    drive_imag,
    read_real,
    read_imag,
    skip_gain,
    glu_weight,
    glu_bias,
    out_cotangent,
):
    modes = decay_rate.shape[0]
    dims = Dims(inputs.shape, modes, mesh_shape)
    n, nd, m, hc = dims.length, dims.devices, dims.mode_rows, dims.chans
    core = lax.axis_index("core")
    owner = lax.axis_index(ALL)
    meta = jnp.stack([lax.axis_index("batch"), core, lax.axis_index("z")]).astype(jnp.int32)

    def exchange(x):
        return lax.all_to_all(x, ALL, 0, 0, tiled=True)

    some = dims.places // 4

    def to_channels(x):
        x = x.reshape(dims.seqs, some, 4, nd, hc).transpose(3, 2, 1, 0, 4)
        x = exchange(x.reshape(nd, dims.places, dims.piece_width))
        x = x.reshape(dims.ni, dims.nj, 4, some, dims.piece_width).transpose(2, 1, 3, 0, 4)
        x = x.reshape(n, dims.all_seqs * hc)
        return jnp.pad(x, ((0, 0), (0, LANES - x.shape[1])))

    def to_tokens(x):
        x = x[:, : dims.all_seqs * hc].reshape(4, dims.nj, some, dims.ni, dims.piece_width)
        x = x.transpose(3, 1, 0, 2, 4).reshape(nd, dims.places, dims.piece_width)
        x = exchange(x).reshape(nd, 4, some, dims.seqs, hc).transpose(3, 2, 1, 0, 4)
        return x.reshape(dims.seqs * dims.places, dims.width)

    table = jnp.stack([decay_rate, rotation, drive_real, drive_imag, read_real, read_imag])
    table = lax.dynamic_slice_in_dim(table, owner * hc, hc, 2)
    table = jnp.pad(table, ((0, 0), (0, m * dims.groups - modes), (0, 0)))
    table = table.reshape(6, dims.groups, m, hc).transpose(0, 2, 1, 3).reshape(6 * m, LANES)
    rest = jnp.stack([log_step, norm_gain, norm_shift, skip_gain])
    rest = lax.dynamic_slice_in_dim(rest, owner * hc, hc, 1)
    params = jnp.concatenate([table, jnp.tile(rest, (1, dims.groups))], axis=0)
    params, meta = lax.optimization_barrier((params, meta))

    pieces = (nd, dims.piece_rows, LANES) if dims.fast else (n, LANES)
    tokens = dims.seqs * dims.places
    token_pieces = (nd, dims.piece_rows, LANES) if dims.fast else (tokens, dims.width)
    bind = functools.partial
    q = dims.quarter
    tab = (2, 2 * q, q)
    inv = (2, q, 2 * q)
    chunks = q // ROWS
    tw = (4, q, LANES)
    four = (chunks, 4, ROWS, 4 * LANES)
    two = (chunks, 4, ROWS, 2 * LANES)
    sent = (dims.ni, dims.nj, dims.piece_rows, LANES) if dims.fast else (n, LANES)
    plain = (4, q, LANES)
    by_tile = (dims.width // LANES, dims.seqs * dims.places, LANES)

    def vmem(*sizes, dtype=f32):
        return pltpu.VMEM(sizes, dtype)

    if dims.fast:
        packed = call(
            bind(pack_kernel, dims), shape(*pieces), [VMEM], [vmem(*by_tile)], 4, 1.5
        )(inputs)
        received = exchange(packed)
    else:
        received = to_channels(inputs.astype(f32))

    zr, zi, vec, waves = call(
        bind(waves_kernel, dims),
        (
            shape(4, 8 * m, LANES),
            shape(4, 8 * m, LANES),
            shape(6 * m, LANES),
            shape(2, q, 8 * LANES, dtype=bf16),
        ),
        [VMEM],
        [vmem(q, 2 * LANES)],
        4,
        3,
    )(params)
    lengths, waves = lax.optimization_barrier((lengths, waves))
    tables, inverse, twiddle, spec = call(
        bind(tables_kernel, dims),
        (shape(*tab, dtype=bf16), shape(*inv, dtype=bf16), shape(*tw), shape(*four)),
        [VMEM],
        [
            vmem(*tab, dtype=bf16),
            vmem(*inv, dtype=bf16),
            vmem(*tw),
            vmem(*four),
            vmem(2 * q, 8 * LANES),
            DMA((3,)),
            DMA(()),
        ],
        10,
        6,
        (HBM, HBM, HBM, HBM),
    )(waves)

    def swap(x, axis, by):
        return lax.ppermute(x, axis, [(i, i ^ by) for i in range(lax.axis_size(axis))])

    def everyone(x, axis, size):
        return [x] + [swap(x, axis, s) for s in range(1, size)]

    lens = everyone(lengths, "batch", dims.ni)
    send, mixed, normed, seen, stat = call(
        bind(forward_kernel, dims),
        (shape(*sent), shape(*plain), shape(*plain), shape(*four), shape(8, LANES)),
        [SMEM, VMEM, VMEM] + [HBM] * 4 + [SMEM] * dims.ni,
        [
            vmem(*tab, dtype=bf16),
            vmem(*inv, dtype=bf16),
            vmem(*tw),
            vmem(*four),
            vmem(*four),
            vmem(*plain),
            vmem(*plain),
            vmem(*plain),
            vmem(2, q, 8 * LANES, dtype=bf16),
            vmem(2 * q, 8 * LANES),
            vmem(2, 2 * q, 4 * LANES, dtype=bf16),
            vmem(*sent),
            DMA((3,)),
            DMA((chunks,)),
            DMA((chunks,)),
            DMA((2,)),
            DMA((dims.nj,)),
        ],
        18,
        7,
        (HBM, HBM, HBM, HBM, VMEM),
    )(meta, received, params, tables, inverse, twiddle, spec, *lens)
    send = send.reshape(pieces)

    received = exchange(send) if dims.fast else to_tokens(send)
    wide = (tokens, dims.width)
    wider = (tokens, 2 * dims.width)
    unit = (dims.units + 1, 8, LANES)
    part = (dims.ni, dims.nz) + unit
    tiles = 2 * dims.width // LANES
    send, result, act, gj, bias, wsend = call(
        bind(gate_kernel, dims),
        (
            shape(*token_pieces),
            shape(*inputs.shape, dtype=bf16),
            shape(*wide, dtype=bf16),
            shape(*wider, dtype=bf16),
            shape(tiles, LANES),
            shape(*part),
        ),
        [SMEM] + [VMEM] * 5,
        [
            vmem(*by_tile),
            vmem(*wide, dtype=bf16),
            vmem(*wider),
            vmem(*wider, dtype=bf16),
            vmem(*by_tile),
            vmem(*token_pieces),
            vmem(dims.width // 2, 2 * dims.width),
            vmem(*part),
            DMA((2,)),
            DMA((max(1, dims.width // LANES),)),
            DMA((dims.ni,)),
        ],
        11,
        5,
        (HBM, VMEM, HBM, HBM, VMEM, HBM),
    )(meta, received, inputs, glu_weight, glu_bias.reshape(1, -1), out_cotangent)
    received = exchange(send) if dims.fast else to_channels(
        send.reshape(dims.seqs, dims.places, dims.width)
    )

    parts = call(
        bind(first_add_kernel, dims),
        (shape(dims.nz, *unit),) * dims.ni,
        [SMEM, HBM, HBM, VMEM, ANY],
        [
            vmem(*wide, dtype=bf16),
            vmem(*wider, dtype=bf16),
            vmem(dims.width // 2, 2 * dims.width),
            vmem(*part),
            DMA((2,)),
            DMA((dims.ni,)),
        ],
        6,
        0.1,
    )(meta, act, gj, bias, swap(wsend, "core", 1))
    parts = [parts[0]] + [swap(parts[s], "batch", s) for s in range(1, dims.ni)]
    send, grads, sums = call(
        bind(backward_kernel, dims),
        (shape(*sent), shape(*two), shape(8, LANES)),
        [VMEM, VMEM] + [HBM] * 6 + [VMEM],
        [
            vmem(*tab, dtype=bf16),
            vmem(*inv, dtype=bf16),
            vmem(*tw),
            vmem(*four),
            vmem(*two),
            vmem(*plain),
            vmem(*plain),
            vmem(*plain),
            vmem(*plain),
            vmem(2, q, 4 * LANES, dtype=bf16),
            vmem(2 * q, 4 * LANES),
            vmem(2, 2 * q, 8 * LANES, dtype=bf16),
            vmem(*plain),
            vmem(*plain),
            vmem(*sent),
            DMA((5,)),
            DMA((chunks,)),
            DMA((dims.nj,)),
            DMA((chunks,)),
        ],
        18,
        9,
        (HBM, HBM, VMEM),
    )(received, params, tables, inverse, twiddle, spec, mixed, normed, stat)
    send = send.reshape(pieces)

    send, parts = lax.optimization_barrier((send, parts))
    parts = call(
        bind(add_kernel, dims.ni), (shape(*unit),) * dims.nz, [VMEM] * dims.ni, [], 2, 0.1
    )(*parts)
    sums, parts = lax.optimization_barrier((sums, parts))
    sums = call(order_kernel, shape(8, LANES), [VMEM], [], 1, 6)(sums)
    send, sums = lax.optimization_barrier((send, sums))
    received = exchange(send) if dims.fast else to_tokens(send)
    parts = [parts[0]] + [swap(parts[s], "z", s) for s in range(1, dims.nz)]
    small = call(
        bind(modes_kernel, dims),
        shape(dims.small_rows, LANES),
        [VMEM] + [HBM] * 4 + [VMEM] * 4,
        [
            vmem(*inv, dtype=bf16),
            vmem(*tw),
            vmem(*four),
            vmem(*two),
            vmem(2, 2 * q, 8 * LANES, dtype=bf16),
            vmem(8 * q, LANES),
            DMA((2,)),
            DMA((2, chunks)),
        ],
        12,
        6,
    )(params, inverse, twiddle, seen, grads, sums, zr, zi, vec)

    units = (dims.units + dims.small_rows // 8, 8, LANES)
    units, bias_grad = call(
        bind(last_add_kernel, dims, dims.nz),
        (shape(*units), shape(1, 2 * dims.width)),
        [VMEM] * (1 + dims.nz),
        [],
        2,
        0.7,
    )(small, *parts)
    pieces_z = everyone(units, "z", dims.nz)
    near = everyone(units, "batch", dims.ni)
    pieces_z, near = lax.optimization_barrier((pieces_z, near))
    near_too = [swap(x, "core", 1) for x in near]
    planes = call(
        stack_kernel, shape(dims.nz - 1, *units.shape), [VMEM] * (dims.nz - 1), [], 2, 0.7
    )(*pieces_z[1:])
    planes = everyone(planes, "batch", dims.ni)
    if dims.fast:
        grad_in = call(
            bind(input_kernel, dims), shape(*inputs.shape), [VMEM] * 2, [vmem(*by_tile)], 4, 1.5
        )(received, out_cotangent)
    else:
        grad_in = out_cotangent.astype(f32) + received.reshape(inputs.shape)
    grad_in, planes, near_too = lax.optimization_barrier((grad_in, planes, near_too))
    planes_too = [swap(x, "core", 1) for x in planes]

    if dims.fast:
        outs = call(
            bind(finish_kernel, dims),
            (shape(dims.width, 2 * dims.width),)
            + (shape(modes, dims.width),) * 6
            + (shape(1, dims.width),) * 4,
            [SMEM] + [VMEM] * (4 * dims.ni),
            [vmem(modes, dims.width)] * 6
            + [vmem(1, dims.width)] * 4
            + [
                vmem(2, dims.ni, dims.width // 2 // dims.ni, 2 * dims.width),
                vmem(2, dims.ni, dims.nz, dims.small_rows, LANES),
                DMA((2, dims.ni)),
                DMA((10,)),
            ],
            5,
            3,
            (HBM,) * 11,
        )(meta, *near, *near_too, *planes, *planes_too)
        weight_grad = outs[0]
        mode_grads = outs[1:7]
        chan_grads = [x.reshape(-1) for x in outs[7:]]
    else:

        def in_order(mine, other):
            both = jnp.where(core == 0, jnp.stack([mine, other]), jnp.stack([other, mine]))
            both = jnp.take(both, meta[0] ^ jnp.arange(dims.ni), axis=1)
            return jnp.take(both, meta[2] ^ jnp.arange(dims.nz), axis=2)

        def joined(first, rest):
            return jnp.concatenate([jnp.stack(first)[:, None], jnp.stack(rest)], axis=1)

        both = in_order(joined(near, planes), joined(near_too, planes_too))
        weight_grad = both[:, :, :, : dims.units].reshape(dims.width // 8, -1, 8, LANES)
        weight_grad = weight_grad.transpose(0, 2, 1, 3).reshape(dims.width, -1)
        rows = both[:, :, :, dims.units :].transpose(1, 2, 0, 3, 4, 5)
        rows = rows.reshape(nd, dims.small_rows, dims.groups, hc)
        table = rows[:, : 6 * m].reshape(nd, 6, m, dims.groups, hc).transpose(1, 3, 2, 0, 4)
        mode_grads = list(table.reshape(6, m * dims.groups, dims.width)[:, :modes])
        rest = rows[:, 6 * m : 6 * m + 4, 0].transpose(1, 0, 2).reshape(4, dims.width)
        chan_grads = list(rest)
    step_grad, gain_grad, shift_grad, skip_grad = chan_grads
    return (
        result,
        grad_in,
        gain_grad,
        shift_grad,
        step_grad,
        *mode_grads,
        skip_grad,
        weight_grad,
        bias_grad.reshape(-1),
    )


def solution(mesh):
    batch = mesh.shape["batch"]
    fine = Mesh(mesh.devices.reshape(-1, 2, batch), ("z", "core", "batch"))
    tokens = P("batch", ("z", "core"), None)
    return jax.shard_map(
        functools.partial(local, dict(fine.shape)),
        mesh=fine,
        in_specs=(tokens, P("batch")) + (P(),) * 12 + (tokens,),
        out_specs=(tokens, tokens) + (P(),) * 12,
        check_vma=False,
    )
```

```python
import functools
import math

import jax
import jax.numpy as jnp
from jax import lax
from jax.experimental import pallas as pl
from jax.experimental.pallas import tpu as pltpu
from jax.sharding import Mesh
from jax.sharding import PartitionSpec as P


EPS = 1e-05
LANES = 128
ALL = ("batch", "z", "core")
SMEM = pl.BlockSpec(memory_space=pltpu.SMEM)
VMEM = pl.BlockSpec(memory_space=pltpu.VMEM)
HBM = pl.BlockSpec(memory_space=pltpu.HBM)
ANY = pl.BlockSpec(memory_space=pl.ANY)
DMA = pltpu.SemaphoreType.DMA
ROWS = 128
STEP = 16
PER = ROWS // STEP
copy = pltpu.make_async_copy
f32 = jnp.float32
bf16 = jnp.bfloat16


def mm(a, b):
    return jnp.dot(a, b, preferred_element_type=f32)


def halves(x):
    hi = x.astype(bf16)
    return hi, (x - hi.astype(f32)).astype(bf16)


def lane_ids(shape):
    return lax.broadcasted_iota(jnp.int32, shape, len(shape) - 1)


def swap_blocks(tiles, width):
    tiles = list(tiles)
    block = lane_ids(tiles[0].shape) // width
    step = 1
    while step < len(tiles):
        low = (block & step) == 0
        for a in range(len(tiles)):
            if a & step == 0:
                first, second = tiles[a], tiles[a + step]
                tiles[a] = jnp.where(low, first, pltpu.roll(second, step * width, second.ndim - 1))
                tiles[a + step] = jnp.where(
                    low, pltpu.roll(first, LANES - step * width, first.ndim - 1), second
                )
        step *= 2
    return tiles


def fold_matrix(dims):
    rows = lax.broadcasted_iota(jnp.int32, (LANES, LANES), 0) % dims.chans
    cols = lax.broadcasted_iota(jnp.int32, (LANES, LANES), 1) % dims.chans
    return (rows == cols).astype(f32).astype(bf16)


def fold(row, dims):
    shift = dims.chans
    while shift < LANES:
        row = row + pltpu.roll(row, shift, 1)
        shift *= 2
    return row


class Dims:
    def __init__(self, inputs_shape, modes, mesh_shape):
        self.seqs, self.places, self.width = inputs_shape
        self.ni = mesh_shape["batch"]
        self.nz = mesh_shape["z"]
        self.nj = mesh_shape["z"] * mesh_shape["core"]
        self.devices = self.ni * self.nj
        self.length = self.places * self.nj
        self.quarter = self.length // 4
        self.chans = self.width // self.devices
        self.groups = LANES // self.chans
        self.all_seqs = self.seqs * self.ni
        self.modes = modes
        self.mode_rows = -(-modes // self.groups)
        self.small_rows = -(-(6 * self.mode_rows + 4) // 8) * 8
        self.piece_width = self.seqs * self.chans
        self.place_groups = LANES // self.piece_width
        self.piece_rows = self.places // self.place_groups
        self.units = self.width * 2 * self.width // (8 * LANES) // self.devices
        self.fast = (
            self.piece_width * self.ni == LANES
            and self.piece_rows % 8 == 0
            and self.nj == self.groups
            and self.small_rows == 32
            and self.place_groups == 4
        )


def each(count, body, unroll=True):
    lax.fori_loop(0, count, lambda k, _: body(k), None, unroll=unroll)


def class_rows(b, g, dims):
    return pl.ds(b * dims.places + g, dims.piece_rows, stride=4)


def pack_tokens(read, write, dims, done=None):
    def some(tile):
        parts = []
        for g in range(4):
            for b in range(dims.seqs):
                parts.append(read(tile, class_rows(b, g, dims)))
        parts = swap_blocks(parts, dims.chans)
        for e in range(dims.groups):
            write(tile * dims.groups + e, parts[e])
        if done is not None:
            done(tile)

    each(dims.width // LANES, some)


def unpack_tokens(ref, out, dims, unroll=True):
    def some(tile):
        parts = [ref[tile * dims.groups + e] for e in range(dims.groups)]
        parts = swap_blocks(parts, dims.chans)
        for g in range(4):
            for b in range(dims.seqs):
                out[tile, class_rows(b, g, dims), :] = parts[g * dims.seqs + b]

    each(dims.width // LANES, some, unroll)


def pack_kernel(dims, x_ref, out_ref, wide):
    for b in range(dims.seqs):
        for t in range(dims.width // LANES):
            wide[t, b * dims.places : (b + 1) * dims.places, :] = x_ref[b, :, lanes(t)].astype(f32)

    def write(piece, value):
        out_ref[piece] = value

    pack_tokens(lambda tile, rows: wide[tile, rows, :], write, dims)


def unpack_channels(ref, out, dims):
    rows = dims.piece_rows
    if not dims.fast:
        for r in range(4):
            out[r] = ref[r * dims.quarter : (r + 1) * dims.quarter, :]
        return

    def some(j):
        parts = [ref[i * dims.nj + j] for i in range(dims.ni)]
        parts = swap_blocks(parts, dims.piece_width)
        for g in range(4):
            out[g, pl.ds(pl.multiple_of(j * rows, rows), rows), :] = parts[g]

    each(dims.nj, some)


def pack_channels(read, send, send_hbm, sem, dims):
    rows = dims.piece_rows
    if not dims.fast:
        for r in range(4):
            for at in range(0, dims.quarter, ROWS):
                start = r * dims.quarter + at
                send[start : start + ROWS, :] = read(r, at, ROWS)
        whole = copy(send, send_hbm, sem.at[0])
        whole.start()
        whole.wait()
        return

    def pieces(j):
        return copy(send.at[:, j], send_hbm.at[:, j], sem.at[j])

    for j in range(dims.nj):
        parts = swap_blocks([read(g, j * rows, rows) for g in range(4)], dims.piece_width)
        for i in range(dims.ni):
            send[i, j] = parts[i]
        pieces(j).start()
    for j in range(dims.nj):
        pieces(j).wait()


def mode_constants(par_ref, dims):
    m = dims.mode_rows
    decay, rotation, dr, di, rr, ri = [par_ref[p * m : (p + 1) * m, :] for p in range(6)]
    step = jnp.exp(par_ref[6 * m : 6 * m + 1, :])
    log_mag = -step * decay
    turn = step * rotation
    c1r = step * (rr * dr - ri * di)
    c1i = step * (rr * di + ri * dr)
    c2r = c1r * dr - c1i * di
    c2i = c1r * di + c1i * dr
    return step, log_mag, turn, (c1r, c1i, c2r, c2i), (decay, rotation, dr, di, rr, ri)


def waves_kernel(dims, par_ref, zr_ref, zi_ref, vec_ref, cat_ref, wave):
    m, q = dims.mode_rows, dims.quarter
    step, log_mag, turn, coefs, _ = mode_constants(par_ref, dims)
    c1r, c1i, c2r, c2i = coefs
    mag = jnp.exp(log_mag)
    l1r, l1i = mag * jnp.cos(turn), mag * jnp.sin(turn)
    mag = jnp.exp(8.0 * log_mag)
    l32r, l32i = mag * jnp.cos(8.0 * turn), mag * jnp.sin(8.0 * turn)
    for _ in range(2):
        l32r, l32i = l32r * l32r - l32i * l32i, 2.0 * l32r * l32i
    for p, value in enumerate((l32r, l32i, c1r, c1i, c2r, c2i)):
        vec_ref[p * m : (p + 1) * m, :] = value
    sub = 4.0 * lax.broadcasted_iota(jnp.int32, (8, LANES), 0).astype(f32)

    def wide(x, k):
        return jnp.broadcast_to(x[k : k + 1], (8, LANES))

    for k in range(m):
        mag = jnp.exp(sub * log_mag[k : k + 1])
        zr, zi = mag * jnp.cos(sub * turn[k : k + 1]), mag * jnp.sin(sub * turn[k : k + 1])
        for r in range(4):
            zr_ref[r, 8 * k : 8 * k + 8, :] = zr
            zi_ref[r, 8 * k : 8 * k + 8, :] = zi
            ar, ai = wide(l1r, k), wide(l1i, k)
            zr, zi = zr * ar - zi * ai, zr * ai + zi * ar
    consts = [
        tuple(wide(x, k) for x in (l32r, l32i, 2 * c1r, 2 * c1i, 2 * c2r, 2 * c2i)) for k in range(m)
    ]
    group = fold_matrix(dims)
    for r in range(4):

        def time_step(t, zs):
            at = pl.multiple_of(t * 8, 8)
            k1 = jnp.zeros((8, LANES), f32)
            k2 = jnp.zeros((8, LANES), f32)
            out = []
            for k in range(m):
                zr, zi = zs[2 * k], zs[2 * k + 1]
                ar, ai, b1r, b1i, b2r, b2i = consts[k]
                k1 = k1 + (b1r * zr - b1i * zi)
                k2 = k2 + (b2r * zr - b2i * zi)
                out += [zr * ar - zi * ai, zr * ai + zi * ar]
            wave[pl.ds(at, 8), lanes(0)] = k1
            wave[pl.ds(at, 8), lanes(1)] = k2
            return tuple(out)

        start = []
        for k in range(m):
            start += [zr_ref[r, 8 * k : 8 * k + 8, :], zi_ref[r, 8 * k : 8 * k + 8, :]]
        lax.fori_loop(0, q // 8, time_step, tuple(start), unroll=4)
        for p in range(2):
            both = halves(over_groups(wave[0:q, lanes(p)], group))
            for part in range(2):
                cat_ref[part, :, lanes(2 * r + p)] = both[part]


def tables_kernel(dims, cat_ref, tab_hbm, inv_hbm, tw_hbm, spec_hbm, *scratch):
    tab, inv, tw, spec, wave, sem_out, sem_spec = scratch
    n, q = dims.length, dims.quarter

    def angles(b, _):
        at = pl.multiple_of(b * ROWS, ROWS)
        row = 2 * (lax.broadcasted_iota(jnp.int32, (ROWS, q), 0) + at) + 1
        col = 2 * lax.broadcasted_iota(jnp.int32, (ROWS, q), 1) + 1
        turn = ((row * col) & (8 * q - 1)).astype(f32) * (math.pi / (4 * q))
        for first, value in ((0, jnp.cos(turn)), (q, jnp.sin(turn))):
            for part, half in enumerate(halves(value)):
                tab[part, pl.ds(pl.multiple_of(first + at, ROWS), ROWS), :] = half
                inv[part, pl.ds(at, ROWS), first : first + q] = half
        row = 2 * (lax.broadcasted_iota(jnp.int32, (ROWS, LANES), 0) + at) + 1
        turn = row.astype(f32) * (math.pi / (2 * n))
        cos, sin = jnp.cos(turn), jnp.sin(turn)
        for p, value in enumerate((cos, sin, 1.0 - 2.0 * sin * sin, 2.0 * cos * sin)):
            tw[p, pl.ds(at, ROWS), :] = value
        return 0

    lax.fori_loop(0, q // ROWS, angles, 0)
    outs = [copy(tab, tab_hbm, sem_out.at[0]), copy(tw, tw_hbm, sem_out.at[1])]
    outs.append(copy(inv, inv_hbm, sem_out.at[2]))
    for out in outs:
        out.start()
    forth(tab, cat_ref, wave)

    def spectrum(b, _):
        at = pl.multiple_of(b * STEP, STEP)
        chunk, rows = place_of(b)
        for p in range(2):
            for k, (re, im) in enumerate(butterfly(wave, tw, at, p, 2, dims)):
                spec[chunk, k, rows, lanes(2 * p)] = re * (1.0 / n)
                spec[chunk, k, rows, lanes(2 * p + 1)] = im * (1.0 / n)
        return 0

    lax.fori_loop(0, q // STEP, spectrum, 0)
    outs.append(copy(spec, spec_hbm, sem_spec))
    outs[-1].start()
    for out in outs:
        out.wait()


def lanes(p):
    return slice(p * LANES, (p + 1) * LANES)


def over_groups(x, group):
    return mm(jnp.concatenate(halves(x), axis=1), jnp.concatenate([group, group], axis=0))


def place_of(b):
    return b // PER, pl.ds(pl.multiple_of(b % PER * STEP, STEP), STEP)


def product(table, operand):
    (high, low), (first, second) = table, operand
    return mm(
        jnp.concatenate([high, high, low], axis=1), jnp.concatenate([first, second, first], axis=0)
    )


def forth(tab, cat, wave):
    wave[...] = product((tab[0], tab[1]), (cat[0], cat[1]))


def twiddles(tw, at):
    c1, s1, c2, s2 = [tw[p, pl.ds(at, STEP), :] for p in range(4)]
    return (c2, s2), (c1, s1), None, (c1, -s1)


def times(a, b):
    if b is None:
        return a
    return a[0] * b[0] - a[1] * b[1], a[0] * b[1] + a[1] * b[0]


def plus(a, b):
    return a[0] + b[0], a[1] + b[1]


def minus(a, b):
    return a[0] - b[0], a[1] - b[1]


def turned(a):
    return -a[1], a[0]


def butterfly(wave, tw, at, p, count, dims):
    below = pl.multiple_of(dims.quarter + at, STEP)
    parts = []
    for r, twiddle in enumerate(twiddles(tw, at)):
        re = wave[pl.ds(at, STEP), lanes(r * count + p)]
        im = wave[pl.ds(below, STEP), lanes(r * count + p)]
        parts.append(times((re, -im), twiddle))
    even, odd = plus(parts[0], parts[2]), plus(parts[1], parts[3])
    even_too, odd_too = minus(parts[0], parts[2]), turned(minus(parts[1], parts[3]))
    return plus(even, odd), minus(even_too, odd_too), minus(even, odd), plus(even_too, odd_too)


def unbutterfly(parts, tw, at, cat, p, count, dims):
    even, odd = plus(parts[0], parts[2]), plus(parts[1], parts[3])
    even_too, odd_too = minus(parts[0], parts[2]), turned(minus(parts[1], parts[3]))
    sums = plus(even, odd), plus(even_too, odd_too), minus(even, odd), minus(even_too, odd_too)
    for r, twiddle in enumerate(twiddles(tw, at)):
        if twiddle is not None:
            twiddle = twiddle[0], -twiddle[1]
        re, im = times(sums[r], twiddle)
        for first, value in ((0, re), (dims.quarter, -im)):
            rows = pl.ds(pl.multiple_of(first + at, STEP), STEP)
            for part, half in enumerate(halves(value)):
                cat[part, rows, lanes(r * count + p)] = half


def back(inv, cat):
    return product((inv[0], inv[1]), (cat[0], cat[1]))


def column_sums(x):
    return jnp.sum(x.reshape(x.shape[0] // 8, 8, LANES), axis=0)


def lane_lengths(meta_ref, lens_refs, dims):
    lane = lane_ids((1, LANES)) // dims.chans
    row = jnp.zeros((1, LANES), jnp.int32)
    total = jnp.int32(0)
    for s in range(dims.all_seqs):
        source = s // dims.seqs
        value = lens_refs[source][s % dims.seqs]
        total = total + value
        row = jnp.where(lane == s ^ (meta_ref[0] * dims.seqs), value, row)
    return row, total.astype(f32)


def valid_rows(r, at, rows, lens):
    places = 4 * (lax.broadcasted_iota(jnp.int32, (rows, LANES), 0) + at) + r
    return (places < lens).astype(f32)


def forward_kernel(dims, meta_ref, r_ref, par_ref, tab_hbm, inv_hbm, tw_hbm, spec_hbm, *rest):
    lens_refs, rest = rest[: dims.ni], rest[dims.ni :]
    (send_hbm, mixed_hbm, normed_hbm, seen_hbm, stat_ref), rest = rest[:5], rest[5:]
    tab, inv, tw, spec, seen, x_sc, mix_sc, normed_sc, cat, wave, back_cat, send = rest[:12]
    sem_tab, sem_spec, sem_seen, sem_out, sem_send = rest[12:]
    m, q = dims.mode_rows, dims.quarter
    chunks = q // ROWS
    ins = [copy(tab_hbm, tab, sem_tab.at[0]), copy(tw_hbm, tw, sem_tab.at[1])]
    ins += [copy(spec_hbm.at[c], spec.at[c], sem_spec.at[c]) for c in range(chunks)]
    ins.append(copy(inv_hbm, inv, sem_tab.at[2]))
    for one in ins:
        one.start()
    lens, total = lane_lengths(meta_ref, lens_refs, dims)
    unpack_channels(r_ref, x_sc, dims)
    classes = range(4)

    def add_up(b, acc):
        at = pl.multiple_of(b * ROWS, ROWS)
        for r in classes:
            acc = acc + column_sums(x_sc[r, pl.ds(at, ROWS), :] * valid_rows(r, at, ROWS, lens))
        return acc

    zero = jnp.zeros((8, LANES), f32)
    acc = lax.fori_loop(0, q // ROWS, add_up, zero, unroll=True)
    average = fold(jnp.sum(acc, axis=0, keepdims=True), dims) / total

    def add_squares(b, acc):
        at = pl.multiple_of(b * ROWS, ROWS)
        for r in classes:
            x = (x_sc[r, pl.ds(at, ROWS), :] - average) * valid_rows(r, at, ROWS, lens)
            acc = acc + column_sums(x * x)
        return acc

    acc = lax.fori_loop(0, q // ROWS, add_squares, zero, unroll=True)
    variance = fold(jnp.sum(acc, axis=0, keepdims=True), dims) / total
    inv_scale = lax.rsqrt(variance + EPS)
    gain = par_ref[6 * m + 1 : 6 * m + 2, :]
    shift = par_ref[6 * m + 2 : 6 * m + 3, :]
    skip = par_ref[6 * m + 3 : 6 * m + 4, :]
    stat_ref[0:1, :] = inv_scale
    stat_ref[1:2, :] = jnp.broadcast_to(total, (1, LANES))
    stat_ref[2:3, :] = lens.astype(f32)
    stat_ref[3:8, :] = jnp.zeros((5, LANES), f32)
    first_row = lax.broadcasted_iota(jnp.int32, (ROWS, LANES), 0) == 0

    def normalize(b, last):
        at = pl.multiple_of(b * ROWS, ROWS)
        mixed = []
        for r in classes:
            normed = (x_sc[r, pl.ds(at, ROWS), :] - average) * inv_scale
            mixed.append((gain * normed + shift) * valid_rows(r, at, ROWS, lens))
            normed_sc[r, pl.ds(at, ROWS), :] = normed
            mix_sc[r, pl.ds(at, ROWS), :] = mixed[r]
        earlier = jnp.where(first_row, last, pltpu.roll(mixed[3], 1, 0))
        for r in classes:
            liquid = mixed[r] * (earlier if r == 0 else mixed[r - 1])
            for p, value in enumerate((mixed[r], liquid)):
                for part, half in enumerate(halves(value)):
                    cat[part, pl.ds(at, ROWS), lanes(2 * r + p)] = half
        return mixed[3][ROWS - 1 :, :]

    lax.fori_loop(0, q // ROWS, normalize, jnp.zeros((1, LANES), f32))
    outs = [copy(mix_sc, mixed_hbm, sem_out.at[0]), copy(normed_sc, normed_hbm, sem_out.at[1])]
    for out in outs:
        out.start()
    ins[0].wait()
    forth(tab, cat, wave)
    ins[1].wait()
    for c in range(chunks):
        ins[2 + c].wait()

        def multiply(b, _):
            at = pl.multiple_of(b * STEP, STEP)
            chunk, rows = place_of(b)
            mixed = butterfly(wave, tw, at, 0, 2, dims)
            liquid = butterfly(wave, tw, at, 1, 2, dims)
            parts = []
            for k in range(4):
                for p, value in enumerate(mixed[k] + liquid[k]):
                    seen[chunk, k, rows, lanes(p)] = value
                kr, ki, lr, li = [spec[chunk, k, rows, lanes(p)] for p in range(4)]
                parts.append(plus(times(mixed[k], (kr, ki)), times(liquid[k], (lr, li))))
            unbutterfly(parts, tw, at, back_cat, 0, 1, dims)
            return 0

        lax.fori_loop(PER * c, PER * (c + 1), multiply, 0, unroll=PER)
        outs.append(copy(seen.at[c], seen_hbm.at[c], sem_seen.at[c]))
        outs[-1].start()
    ins[-1].wait()

    value = back(inv, back_cat)
    for r in classes:
        x_sc[r] = value[:, lanes(r)] + skip * mix_sc[r]
    pack_channels(
        lambda r, at, size: x_sc[r, pl.ds(at, size), :], send, send_hbm, sem_send, dims
    )
    for out in outs:
        out.wait()


def gate_kernel(dims, meta_ref, r_ref, x_ref, w_ref, b_ref, ct_ref, *rest):
    (send_hbm, out_ref, act_hbm, gj_hbm, bias_ref, wsend_hbm), scratch = rest[:6], rest[6:]
    resp, act, joined, gj, gact, send, weight, wsend, sem_out, sem_send, sem_weight = scratch
    tokens = dims.seqs * dims.places
    width = dims.width
    places = dims.places

    tiles = range(width // LANES)
    if dims.fast:
        unpack_tokens(r_ref, resp, dims)
    else:
        for t in tiles:
            resp[t] = r_ref[:, lanes(t)]
    c0 = math.sqrt(2.0 / math.pi)
    c1 = 0.044715
    rows = 32

    def gelu(b, _):
        at = pl.multiple_of(b * rows, rows)
        for tile in tiles:
            r = resp[tile, pl.ds(at, rows), :]
            t = jnp.tanh(c0 * (r + c1 * r * r * r))
            act[pl.ds(at, rows), lanes(tile)] = (0.5 * r * (1.0 + t)).astype(bf16)
            slope = 0.5 * (1.0 + t) + 0.5 * r * (1.0 - t * t) * (c0 * (1.0 + 3.0 * c1 * r * r))
            resp[tile, pl.ds(at, rows), :] = slope
        return 0

    lax.fori_loop(0, tokens // rows, gelu, 0)
    outs = [copy(act, act_hbm, sem_out.at[0]), copy(gj, gj_hbm, sem_out.at[1])]
    outs[0].start()
    joined[...] = mm(act[...], w_ref[...])
    bias = b_ref[...]
    half = min(16, places)
    for b in range(dims.seqs):

        def gate(k, sums):
            at = pl.multiple_of(k * half, half)
            tok = pl.multiple_of(b * places + k * half, half)
            value = joined[pl.ds(tok, half), :width] + bias[:, :width]
            s = jax.nn.sigmoid(joined[pl.ds(tok, half), width:] + bias[:, width:])
            x = x_ref[b, pl.ds(at, half), :].astype(f32)
            g = ct_ref[b, pl.ds(at, half), :].astype(f32)
            out_ref[b, pl.ds(at, half), :] = (x + value * s).astype(bf16)
            gs = g * s
            first = gs.astype(bf16)
            second = (gs * value * (1.0 - s)).astype(bf16)
            gj[pl.ds(tok, half), :width] = first
            gj[pl.ds(tok, half), width:] = second
            first = jnp.sum(first.astype(f32).reshape(half // 8, 8, width), axis=0)
            second = jnp.sum(second.astype(f32).reshape(half // 8, 8, width), axis=0)
            return sums[0] + first, sums[1] + second

        if b == 0:
            zero = jnp.zeros((8, width), f32)
            sums = (zero, zero)
        sums = lax.fori_loop(0, places // half, gate, sums, unroll=2)
    outs[1].start()
    sums = [jnp.sum(s, axis=0, keepdims=True) for s in sums]
    for p, total in enumerate(sums):
        for t in tiles:
            row = p * (width // LANES) + t
            bias_ref[row : row + 1, :] = total[:, lanes(t)]
    weight_half(dims, meta_ref, 1 - meta_ref[1], act, gj, weight)
    for i in range(dims.ni):
        for z in range(dims.nz):
            for u in range(dims.units):
                wsend[i, z, u, :, :] = weight_unit(dims, meta_ref, weight, i, z, u)
            wsend[i, z, dims.units, :, :] = bias_ref[...]
        outs.append(copy(wsend.at[i], wsend_hbm.at[i], sem_weight.at[i]))
        outs[-1].start()
    grad = lax.dot_general(
        gj[...], w_ref[...], (((1,), (1,)), ((), ())), preferred_element_type=f32
    )
    for t in tiles:
        gact[t] = grad[:, lanes(t)]
    if dims.fast:

        def read(tile, rows):
            return gact[tile, rows, :] * resp[tile, rows, :]

        def put(piece, value):
            send[piece] = value

        def tile_copy(tile):
            some = pl.ds(tile * dims.groups, dims.groups)
            return copy(send.at[some], send_hbm.at[some], sem_send.at[tile])

        pack_tokens(read, put, dims, lambda tile: tile_copy(tile).start())
        outs += [tile_copy(tile) for tile in tiles]
    else:
        for t in tiles:
            send[:, lanes(t)] = gact[t] * resp[t]
        outs.append(copy(send, send_hbm, sem_send.at[0]))
        outs[-1].start()
    for out in outs:
        out.wait()


def weight_half(dims, meta_ref, core, act, gj, weight):
    half = dims.width // 2
    some = act[:, pl.ds(pl.multiple_of(core * half, half), half)]
    weight[...] = lax.dot_general(
        some, gj[...], (((0,), (0,)), ((), ())), preferred_element_type=f32
    )


def weight_unit(dims, meta_ref, weight, i, z, u):
    tiles = 2 * dims.width // LANES
    owner = (meta_ref[0] ^ i) * dims.nz + (meta_ref[2] ^ z)
    if dims.units % tiles == 0:
        row = owner * (dims.units // tiles) + u // tiles
        cols = lanes(u % tiles)
    else:
        unit = owner * dims.units + u
        row = unit // tiles
        cols = pl.ds(pl.multiple_of(unit % tiles * LANES, LANES), LANES)
    return weight[pl.ds(pl.multiple_of(row * 8, 8), 8), cols]


def backward_kernel(dims, r_ref, par_ref, *rest):
    ins_hbm, (stat_ref, send_hbm, grad_hbm, sums_ref) = rest[:6], rest[6:10]
    tab, inv, tw, spec, grads, mix_sc, normed_sc, g_sc, up_sc, cat, wave, back_cat = rest[10:22]
    lead_sc, liquid_sc, send, sem_in, sem_spec, sem_send, sem_grad = rest[22:]
    tab_hbm, inv_hbm, tw_hbm, spec_hbm, mixed_hbm, normed_hbm = ins_hbm
    m, q = dims.mode_rows, dims.quarter
    ins = [
        copy(mixed_hbm, mix_sc, sem_in.at[0]),
        copy(tab_hbm, tab, sem_in.at[1]),
        copy(tw_hbm, tw, sem_in.at[2]),
        copy(normed_hbm, normed_sc, sem_in.at[3]),
        copy(inv_hbm, inv, sem_in.at[4]),
    ]
    chunks = q // ROWS
    for c in range(chunks):
        ins.insert(3 + c, copy(spec_hbm.at[c], spec.at[c], sem_spec.at[c]))
    for one in ins:
        one.start()
    unpack_channels(r_ref, g_sc, dims)
    gain = par_ref[6 * m + 1 : 6 * m + 2, :]
    skip = par_ref[6 * m + 3 : 6 * m + 4, :]
    inv_scale = stat_ref[0:1, :]
    total = stat_ref[1:2, :]
    lens = stat_ref[2:3, :].astype(jnp.int32)
    zero = jnp.zeros((8, LANES), f32)
    classes = range(4)
    ins[0].wait()

    def gather(b, acc):
        at = pl.multiple_of(b * ROWS, ROWS)
        for r in classes:
            g = g_sc[r, pl.ds(at, ROWS), :]
            for part, half in enumerate(halves(g)):
                cat[part, pl.ds(at, ROWS), lanes(r)] = half
            acc = acc + column_sums(g * mix_sc[r, pl.ds(at, ROWS), :])
        return acc

    skip_acc = lax.fori_loop(0, q // ROWS, gather, zero)
    ins[1].wait()
    forth(tab, cat, wave)
    ins[2].wait()
    outs = []
    for c in range(chunks):
        ins[3 + c].wait()

        def multiply(b, _):
            at = pl.multiple_of(b * STEP, STEP)
            chunk, rows = place_of(b)
            grad = butterfly(wave, tw, at, 0, 1, dims)
            for k in range(4):
                for p in range(2):
                    grads[chunk, k, rows, lanes(p)] = grad[k][p]
            for p in range(2):
                products(grad, spec, tw, b, back_cat, p, dims)
            return 0

        lax.fori_loop(PER * c, PER * (c + 1), multiply, 0, unroll=PER)
        outs.append(copy(grads.at[c], grad_hbm.at[c], sem_grad.at[c]))
        outs[-1].start()
    for one in ins[3 + chunks :]:
        one.wait()

    value = back(inv, back_cat)
    for r in classes:
        lead_sc[r] = value[:, lanes(2 * r)]
        liquid_sc[r] = value[:, lanes(2 * r + 1)]
        up_sc[r] = value[:, lanes(2 * r + 1)] * mix_sc[r]

    row = lax.broadcasted_iota(jnp.int32, (ROWS, LANES), 0)
    blank = jnp.zeros((1, LANES), f32)
    gain_acc, shift_acc = zero, zero
    for at in range(0, q, ROWS):
        rows = slice(at, at + ROWS)
        for r in classes:
            if r == 0:
                before = blank if at == 0 else mix_sc[3, at - 1 : at, :]
                earlier = jnp.where(row == 0, before, pltpu.roll(mix_sc[3, rows, :], 1, 0))
            else:
                earlier = mix_sc[r - 1, rows, :]
            if r == 3:
                after = blank if at + ROWS == q else up_sc[0, at + ROWS : at + ROWS + 1, :]
                up = jnp.where(row == ROWS - 1, after, pltpu.roll(up_sc[0, rows, :], ROWS - 1, 0))
            else:
                up = up_sc[r + 1, rows, :]
            masked = lead_sc[r, rows, :] + skip * g_sc[r, rows, :] + liquid_sc[r, rows, :] * earlier
            masked = (masked + up) * valid_rows(r, at, ROWS, lens)
            g_sc[r, rows, :] = masked
            gain_acc = gain_acc + column_sums(masked * normed_sc[r, rows, :])
            shift_acc = shift_acc + column_sums(masked)

    def whole(acc):
        return fold(jnp.sum(acc, axis=0, keepdims=True), dims)

    gain_sum, shift_sum, skip_sum = whole(gain_acc), whole(shift_acc), whole(skip_acc)
    scale = gain * inv_scale
    shift_mean = shift_sum / total
    gain_mean = gain_sum / total

    def read(r, at, size):
        normed = normed_sc[r, pl.ds(at, size), :]
        value = g_sc[r, pl.ds(at, size), :] - shift_mean - normed * gain_mean
        return value * scale * valid_rows(r, at, size, lens)

    sums_ref[...] = jnp.zeros_like(sums_ref)
    for p, value in enumerate((gain_sum, shift_sum, skip_sum)):
        sums_ref[p : p + 1, :] = value
    pack_channels(read, send, send_hbm, sem_send, dims)
    for out in outs:
        out.wait()


def products(grad, ref, tw, b, cat, p, dims):
    chunk, rows = place_of(b)
    parts = []
    for k in range(4):
        re = ref[chunk, k, rows, lanes(2 * p)]
        im = ref[chunk, k, rows, lanes(2 * p + 1)]
        parts.append(times(grad[k], (re, -im)))
    unbutterfly(parts, tw, pl.multiple_of(b * STEP, STEP), cat, p, 2, dims)


def modes_kernel(dims, par_ref, inv_hbm, tw_hbm, seen_hbm, grad_hbm, sums_ref, *rest):
    zr_ref, zi_ref, vec_ref, small_ref, inv, tw, seen, grads, back_cat, dk, sem, sem_in = rest
    n, m, q = dims.length, dims.mode_rows, dims.quarter
    chunks = q // ROWS
    ins = [copy(tw_hbm, tw, sem.at[0])]
    for c in range(chunks):
        ins.append(copy(seen_hbm.at[c], seen.at[c], sem_in.at[0, c]))
        ins.append(copy(grad_hbm.at[c], grads.at[c], sem_in.at[1, c]))
    ins.append(copy(inv_hbm, inv, sem.at[1]))
    for one in ins:
        one.start()
    zero = jnp.zeros((8, LANES), f32)
    classes = range(4)
    ins[0].wait()
    for c in range(chunks):
        ins[1 + 2 * c].wait()
        ins[2 + 2 * c].wait()

        def multiply(b, _):
            chunk, rows = place_of(b)
            grad = [tuple(grads[chunk, k, rows, lanes(p)] for p in range(2)) for k in range(4)]
            for p in range(2):
                products(grad, seen, tw, b, back_cat, p, dims)
            return 0

        lax.fori_loop(PER * c, PER * (c + 1), multiply, 0, unroll=PER)
    ins[-1].wait()
    group = fold_matrix(dims)

    value = back(inv, back_cat) * (1.0 / n)
    dk[...] = over_groups(jnp.concatenate([value[:, lanes(p)] for p in range(8)], axis=0), group)

    step, log_mag, turn, _, params = mode_constants(par_ref, dims)
    decay, rotation, dr, di, rr, ri = params
    l32r, l32i, c1r, c1i, c2r, c2i = [vec_ref[p * m : (p + 1) * m, :] for p in range(6)]
    sub = 4.0 * lax.broadcasted_iota(jnp.int32, (8, LANES), 0).astype(f32)
    sums = [[] for _ in range(8)]
    for first in range(0, m, 2):
        some = range(first, min(m, first + 2))
        ratio = [
            (
                jnp.broadcast_to(l32r[k : k + 1], (8, LANES)),
                jnp.broadcast_to(l32i[k : k + 1], (8, LANES)),
            )
            for k in some
        ]
        sofar = [zero] * (8 * len(ratio))
        for r in classes:

            def mode_step(t, carry):
                at = pl.multiple_of(t * 8, 8)
                d1 = dk[pl.ds(pl.multiple_of(2 * r * q + at, 8), 8), :]
                d2 = dk[pl.ds(pl.multiple_of((2 * r + 1) * q + at, 8), 8), :]
                place = sub + (32 * t + r).astype(f32)
                e1 = d1 * place
                e2 = d2 * place
                out = []
                for k, (ar, ai) in enumerate(ratio):
                    zr, zi, *acc = carry[10 * k : 10 * (k + 1)]
                    out += [zr * ar - zi * ai, zr * ai + zi * ar]
                    for p, d in enumerate((d1, d2, e1, e2)):
                        out += [acc[2 * p] + d * zr, acc[2 * p + 1] + d * zi]
                return tuple(out)

            carry = []
            for at, k in enumerate(some):
                carry += [zr_ref[r, 8 * k : 8 * k + 8, :], zi_ref[r, 8 * k : 8 * k + 8, :]]
                carry += sofar[8 * at : 8 * at + 8]
            carry = lax.fori_loop(0, q // 8, mode_step, tuple(carry), unroll=8)
            sofar = [v for k in range(len(ratio)) for v in carry[10 * k + 2 : 10 * k + 10]]
        for k in range(len(ratio)):
            for p in range(8):
                sums[p].append(jnp.sum(sofar[8 * k + p], axis=0, keepdims=True))
    a1r, a1i, a2r, a2i, e1r, e1i, e2r, e2i = [
        jnp.concatenate(s, axis=0) if len(s) > 1 else s[0] for s in sums
    ]
    btr = c1r * e1r - c1i * e1i + c2r * e2r - c2i * e2i
    bti = c1r * e1i + c1i * e1r + c2r * e2i + c2i * e2r
    d2r = dr * dr - di * di
    d2i = 2.0 * dr * di
    erd = step * (a1r * dr - a1i * di + a2r * d2r - a2i * d2i)
    eri = step * (a1r * di + a1i * dr + a2r * d2i + a2i * d2r)
    tr = a1r + 2.0 * (a2r * dr - a2i * di)
    ti = a1i + 2.0 * (a2r * di + a2i * dr)
    edr = step * (rr * tr - ri * ti)
    edi = step * (rr * ti + ri * tr)
    by_step = 2.0 * (c1r * a1r - c1i * a1i + c2r * a2r - c2i * a2i) + 2.0 * step * (
        -decay * btr - rotation * bti
    )
    small_ref[...] = jnp.zeros_like(small_ref)
    answers = (-2.0 * step * btr, -2.0 * step * bti, 2.0 * edr, -2.0 * edi, 2.0 * erd, -2.0 * eri)
    for p, value in enumerate(answers):
        small_ref[p * m : (p + 1) * m, :] = value
    small_ref[6 * m : 6 * m + 1, :] = fold(jnp.sum(by_step, axis=0, keepdims=True), dims)
    small_ref[6 * m + 1 : 6 * m + 4, :] = sums_ref[0:3, :]


def first_add_kernel(dims, meta_ref, act_hbm, gj_hbm, bias_ref, other_hbm, *refs):
    out_refs, (act, gj, weight, other, sem_in, sem) = refs[: dims.ni], refs[dims.ni :]
    ins = [copy(act_hbm, act, sem_in.at[0]), copy(gj_hbm, gj, sem_in.at[1])]
    others = [copy(other_hbm.at[i], other.at[i], sem.at[i]) for i in range(dims.ni)]
    for one in ins + others:
        one.start()
    for one in ins:
        one.wait()
    weight_half(dims, meta_ref, meta_ref[1], act, gj, weight)
    for i in range(dims.ni):
        others[i].wait()
        for z in range(dims.nz):
            for u in range(dims.units):
                unit = weight_unit(dims, meta_ref, weight, i, z, u)
                out_refs[i][z, u] = unit + other[i, z, u]
            out_refs[i][z, dims.units] = bias_ref[...] + other[i, z, dims.units]


def order_kernel(sums_ref, out_ref):
    out_ref[...] = sums_ref[...]


def add_kernel(count, *refs):
    for p, out_ref in enumerate(refs[count:]):
        total = refs[0][p]
        for ref in refs[1:count]:
            total = total + ref[p]
        out_ref[...] = total


def last_add_kernel(dims, count, small_ref, *refs):
    units_ref, bias_ref = refs[count:]

    def unit(u):
        total = refs[0][u]
        for ref in refs[1:count]:
            total = total + ref[u]
        return total

    for u in range(dims.units):
        units_ref[u] = unit(u)
    for t in range(dims.small_rows // 8):
        units_ref[dims.units + t] = small_ref[8 * t : 8 * t + 8, :]
    bias = unit(dims.units)
    for t in range(2 * dims.width // LANES):
        bias_ref[:, lanes(t)] = bias[t : t + 1, :]


def stack_kernel(*refs):
    for k, ref in enumerate(refs[:-1]):
        refs[-1][k] = ref[...]


def input_kernel(dims, r_ref, ct_ref, grad_ref, grad):
    unpack_tokens(r_ref, grad, dims, False)
    for b in range(dims.seqs):
        for t in range(dims.width // LANES):
            value = grad[t, b * dims.places : (b + 1) * dims.places, :]
            grad_ref[b, :, lanes(t)] = value + ct_ref[b, :, lanes(t)].astype(f32)


def finish_kernel(dims, meta_ref, *refs):
    ni, nz, m = dims.ni, dims.nz, dims.mode_rows
    near = refs[:ni], refs[ni : 2 * ni]
    far = refs[2 * ni : 3 * ni], refs[3 * ni : 4 * ni]
    weight_ref, *small_hbm = refs[4 * ni : 4 * ni + 11]
    *small_refs, rows, small, sem, sem_small = refs[4 * ni + 11 :]
    me, core, me_z = meta_ref[0], meta_ref[1], meta_ref[2]
    tiles = 2 * dims.width // LANES
    per = 8 * dims.units // tiles
    copies = []
    for half, side in ((0, core), (1, 1 - core)):
        for i in range(ni):
            for z in range(nz):
                piece = near[half][i] if z == 0 else far[half][i].at[z - 1]
                for u in range(dims.units):
                    at = pl.multiple_of((me_z ^ z) * per + u // tiles * 8, 8)
                    rows[half, i, pl.ds(at, 8), lanes(u % tiles)] = piece[u]
                value = piece[dims.units :].reshape(dims.small_rows, LANES)
                small[half, i, me_z ^ z] = value
            at = pl.multiple_of((side * ni + (me ^ i)) * nz * per, nz * per)
            target = weight_ref.at[pl.ds(at, nz * per), :]
            copies.append(copy(rows.at[half, i], target, sem.at[half, i]))
            copies[-1].start()
    first = core == 0
    for i in range(ni):
        parts = []
        for z in range(nz):
            a, b = small[0, i, z], small[1, i, z]
            parts += [jnp.where(first, a, b), jnp.where(first, b, a)]
        parts = swap_blocks(parts, dims.chans)
        cols = pl.ds(pl.multiple_of((me ^ i) * LANES, LANES), LANES)
        for q in range(dims.groups):
            for p in range(6):
                small_refs[p][q * m : q * m + m, cols] = parts[q][p * m : p * m + m, :]
        for p in range(4):
            small_refs[6 + p][:, cols] = parts[0][6 * m + p : 6 * m + p + 1, :]
    for p, (ref, hbm) in enumerate(zip(small_refs, small_hbm)):
        copies.append(copy(ref, hbm, sem_small.at[p]))
        copies[-1].start()
    for one in copies:
        one.wait()


def call(kernel, out_shape, in_specs, scratch, limit, us, out_specs=None):
    cost = pl.CostEstimate(flops=int(us * 1.1e9), bytes_accessed=int(us * 3e6), transcendentals=0)
    if out_specs is None:
        out_specs = jax.tree.map(lambda _: VMEM, out_shape)
    else:
        out_shape = tuple(
            pltpu.HBM(out.shape, out.dtype) if spec is HBM else out
            for out, spec in zip(out_shape, out_specs)
        )

    def run(*args):
        args = [
            pltpu.with_memory_space_constraint(x, pltpu.HBM) if spec is HBM else x
            for x, spec in zip(args, in_specs)
        ]
        return pl.pallas_call(
            kernel,
            out_shape=out_shape,
            in_specs=in_specs,
            out_specs=out_specs,
            scratch_shapes=scratch,
            compiler_params=pltpu.CompilerParams(vmem_limit_bytes=limit << 20),
            cost_estimate=cost,
        )(*args)

    return run


def shape(*dims, dtype=f32):
    return jax.ShapeDtypeStruct(dims, dtype)


def local(
    mesh_shape,
    inputs,
    lengths,
    norm_gain,
    norm_shift,
    log_step,
    decay_rate,
    rotation,
    drive_real,
    drive_imag,
    read_real,
    read_imag,
    skip_gain,
    glu_weight,
    glu_bias,
    out_cotangent,
):
    modes = decay_rate.shape[0]
    dims = Dims(inputs.shape, modes, mesh_shape)
    n, nd, m, hc = dims.length, dims.devices, dims.mode_rows, dims.chans
    core = lax.axis_index("core")
    owner = lax.axis_index(ALL)
    meta = jnp.stack([lax.axis_index("batch"), core, lax.axis_index("z")]).astype(jnp.int32)

    def exchange(x):
        return lax.all_to_all(x, ALL, 0, 0, tiled=True)

    some = dims.places // 4

    def to_channels(x):
        x = x.reshape(dims.seqs, some, 4, nd, hc).transpose(3, 2, 1, 0, 4)
        x = exchange(x.reshape(nd, dims.places, dims.piece_width))
        x = x.reshape(dims.ni, dims.nj, 4, some, dims.piece_width).transpose(2, 1, 3, 0, 4)
        x = x.reshape(n, dims.all_seqs * hc)
        return jnp.pad(x, ((0, 0), (0, LANES - x.shape[1])))

    def to_tokens(x):
        x = x[:, : dims.all_seqs * hc].reshape(4, dims.nj, some, dims.ni, dims.piece_width)
        x = x.transpose(3, 1, 0, 2, 4).reshape(nd, dims.places, dims.piece_width)
        x = exchange(x).reshape(nd, 4, some, dims.seqs, hc).transpose(3, 2, 1, 0, 4)
        return x.reshape(dims.seqs * dims.places, dims.width)

    table = jnp.stack([decay_rate, rotation, drive_real, drive_imag, read_real, read_imag])
    table = lax.dynamic_slice_in_dim(table, owner * hc, hc, 2)
    table = jnp.pad(table, ((0, 0), (0, m * dims.groups - modes), (0, 0)))
    table = table.reshape(6, dims.groups, m, hc).transpose(0, 2, 1, 3).reshape(6 * m, LANES)
    rest = jnp.stack([log_step, norm_gain, norm_shift, skip_gain])
    rest = lax.dynamic_slice_in_dim(rest, owner * hc, hc, 1)
    params = jnp.concatenate([table, jnp.tile(rest, (1, dims.groups))], axis=0)
    params, meta = lax.optimization_barrier((params, meta))

    pieces = (nd, dims.piece_rows, LANES) if dims.fast else (n, LANES)
    tokens = dims.seqs * dims.places
    token_pieces = (nd, dims.piece_rows, LANES) if dims.fast else (tokens, dims.width)
    bind = functools.partial
    q = dims.quarter
    tab = (2, 2 * q, q)
    inv = (2, q, 2 * q)
    chunks = q // ROWS
    tw = (4, q, LANES)
    four = (chunks, 4, ROWS, 4 * LANES)
    two = (chunks, 4, ROWS, 2 * LANES)
    sent = (dims.ni, dims.nj, dims.piece_rows, LANES) if dims.fast else (n, LANES)
    plain = (4, q, LANES)
    by_tile = (dims.width // LANES, dims.seqs * dims.places, LANES)

    def vmem(*sizes, dtype=f32):
        return pltpu.VMEM(sizes, dtype)

    if dims.fast:
        packed = call(
            bind(pack_kernel, dims), shape(*pieces), [VMEM], [vmem(*by_tile)], 4, 1.5
        )(inputs)
        received = exchange(packed)
    else:
        received = to_channels(inputs.astype(f32))

    zr, zi, vec, waves = call(
        bind(waves_kernel, dims),
        (
            shape(4, 8 * m, LANES),
            shape(4, 8 * m, LANES),
            shape(6 * m, LANES),
            shape(2, q, 8 * LANES, dtype=bf16),
        ),
        [VMEM],
        [vmem(q, 2 * LANES)],
        4,
        3,
    )(params)
    lengths, waves = lax.optimization_barrier((lengths, waves))
    tables, inverse, twiddle, spec = call(
        bind(tables_kernel, dims),
        (shape(*tab, dtype=bf16), shape(*inv, dtype=bf16), shape(*tw), shape(*four)),
        [VMEM],
        [
            vmem(*tab, dtype=bf16),
            vmem(*inv, dtype=bf16),
            vmem(*tw),
            vmem(*four),
            vmem(2 * q, 8 * LANES),
            DMA((3,)),
            DMA(()),
        ],
        10,
        6,
        (HBM, HBM, HBM, HBM),
    )(waves)

    def swap(x, axis, by):
        return lax.ppermute(x, axis, [(i, i ^ by) for i in range(lax.axis_size(axis))])

    def everyone(x, axis, size):
        return [x] + [swap(x, axis, s) for s in range(1, size)]

    lens = everyone(lengths, "batch", dims.ni)
    send, mixed, normed, seen, stat = call(
        bind(forward_kernel, dims),
        (shape(*sent), shape(*plain), shape(*plain), shape(*four), shape(8, LANES)),
        [SMEM, VMEM, VMEM] + [HBM] * 4 + [SMEM] * dims.ni,
        [
            vmem(*tab, dtype=bf16),
            vmem(*inv, dtype=bf16),
            vmem(*tw),
            vmem(*four),
            vmem(*four),
            vmem(*plain),
            vmem(*plain),
            vmem(*plain),
            vmem(2, q, 8 * LANES, dtype=bf16),
            vmem(2 * q, 8 * LANES),
            vmem(2, 2 * q, 4 * LANES, dtype=bf16),
            vmem(*sent),
            DMA((3,)),
            DMA((chunks,)),
            DMA((chunks,)),
            DMA((2,)),
            DMA((dims.nj,)),
        ],
        18,
        7,
        (HBM, HBM, HBM, HBM, VMEM),
    )(meta, received, params, tables, inverse, twiddle, spec, *lens)
    send = send.reshape(pieces)

    received = exchange(send) if dims.fast else to_tokens(send)
    wide = (tokens, dims.width)
    wider = (tokens, 2 * dims.width)
    unit = (dims.units + 1, 8, LANES)
    part = (dims.ni, dims.nz) + unit
    tiles = 2 * dims.width // LANES
    send, result, act, gj, bias, wsend = call(
        bind(gate_kernel, dims),
        (
            shape(*token_pieces),
            shape(*inputs.shape, dtype=bf16),
            shape(*wide, dtype=bf16),
            shape(*wider, dtype=bf16),
            shape(tiles, LANES),
            shape(*part),
        ),
        [SMEM] + [VMEM] * 5,
        [
            vmem(*by_tile),
            vmem(*wide, dtype=bf16),
            vmem(*wider),
            vmem(*wider, dtype=bf16),
            vmem(*by_tile),
            vmem(*token_pieces),
            vmem(dims.width // 2, 2 * dims.width),
            vmem(*part),
            DMA((2,)),
            DMA((max(1, dims.width // LANES),)),
            DMA((dims.ni,)),
        ],
        11,
        5,
        (HBM, VMEM, HBM, HBM, VMEM, HBM),
    )(meta, received, inputs, glu_weight, glu_bias.reshape(1, -1), out_cotangent)
    received = exchange(send) if dims.fast else to_channels(
        send.reshape(dims.seqs, dims.places, dims.width)
    )

    parts = call(
        bind(first_add_kernel, dims),
        (shape(dims.nz, *unit),) * dims.ni,
        [SMEM, HBM, HBM, VMEM, ANY],
        [
            vmem(*wide, dtype=bf16),
            vmem(*wider, dtype=bf16),
            vmem(dims.width // 2, 2 * dims.width),
            vmem(*part),
            DMA((2,)),
            DMA((dims.ni,)),
        ],
        6,
        0.1,
    )(meta, act, gj, bias, swap(wsend, "core", 1))
    parts = [parts[0]] + [swap(parts[s], "batch", s) for s in range(1, dims.ni)]
    send, grads, sums = call(
        bind(backward_kernel, dims),
        (shape(*sent), shape(*two), shape(8, LANES)),
        [VMEM, VMEM] + [HBM] * 6 + [VMEM],
        [
            vmem(*tab, dtype=bf16),
            vmem(*inv, dtype=bf16),
            vmem(*tw),
            vmem(*four),
            vmem(*two),
            vmem(*plain),
            vmem(*plain),
            vmem(*plain),
            vmem(*plain),
            vmem(2, q, 4 * LANES, dtype=bf16),
            vmem(2 * q, 4 * LANES),
            vmem(2, 2 * q, 8 * LANES, dtype=bf16),
            vmem(*plain),
            vmem(*plain),
            vmem(*sent),
            DMA((5,)),
            DMA((chunks,)),
            DMA((dims.nj,)),
            DMA((chunks,)),
        ],
        18,
        9,
        (HBM, HBM, VMEM),
    )(received, params, tables, inverse, twiddle, spec, mixed, normed, stat)
    send = send.reshape(pieces)

    send, parts = lax.optimization_barrier((send, parts))
    parts = call(
        bind(add_kernel, dims.ni), (shape(*unit),) * dims.nz, [VMEM] * dims.ni, [], 2, 0.1
    )(*parts)
    sums, parts = lax.optimization_barrier((sums, parts))
    sums = call(order_kernel, shape(8, LANES), [VMEM], [], 1, 6)(sums)
    send, sums = lax.optimization_barrier((send, sums))
    received = exchange(send) if dims.fast else to_tokens(send)
    parts = [parts[0]] + [swap(parts[s], "z", s) for s in range(1, dims.nz)]
    small = call(
        bind(modes_kernel, dims),
        shape(dims.small_rows, LANES),
        [VMEM] + [HBM] * 4 + [VMEM] * 4,
        [
            vmem(*inv, dtype=bf16),
            vmem(*tw),
            vmem(*four),
            vmem(*two),
            vmem(2, 2 * q, 8 * LANES, dtype=bf16),
            vmem(8 * q, LANES),
            DMA((2,)),
            DMA((2, chunks)),
        ],
        12,
        6,
    )(params, inverse, twiddle, seen, grads, sums, zr, zi, vec)

    units = (dims.units + dims.small_rows // 8, 8, LANES)
    units, bias_grad = call(
        bind(last_add_kernel, dims, dims.nz),
        (shape(*units), shape(1, 2 * dims.width)),
        [VMEM] * (1 + dims.nz),
        [],
        2,
        0.7,
    )(small, *parts)
    pieces_z = everyone(units, "z", dims.nz)
    near = everyone(units, "batch", dims.ni)
    pieces_z, near = lax.optimization_barrier((pieces_z, near))
    near_too = [swap(x, "core", 1) for x in near]
    planes = call(
        stack_kernel, shape(dims.nz - 1, *units.shape), [VMEM] * (dims.nz - 1), [], 2, 0.7
    )(*pieces_z[1:])
    planes = everyone(planes, "batch", dims.ni)
    if dims.fast:
        grad_in = call(
            bind(input_kernel, dims), shape(*inputs.shape), [VMEM] * 2, [vmem(*by_tile)], 4, 1.5
        )(received, out_cotangent)
    else:
        grad_in = out_cotangent.astype(f32) + received.reshape(inputs.shape)
    grad_in, planes, near_too = lax.optimization_barrier((grad_in, planes, near_too))
    planes_too = [swap(x, "core", 1) for x in planes]

    if dims.fast:
        outs = call(
            bind(finish_kernel, dims),
            (shape(dims.width, 2 * dims.width),)
            + (shape(modes, dims.width),) * 6
            + (shape(1, dims.width),) * 4,
            [SMEM] + [VMEM] * (4 * dims.ni),
            [vmem(modes, dims.width)] * 6
            + [vmem(1, dims.width)] * 4
            + [
                vmem(2, dims.ni, dims.width // 2 // dims.ni, 2 * dims.width),
                vmem(2, dims.ni, dims.nz, dims.small_rows, LANES),
                DMA((2, dims.ni)),
                DMA((10,)),
            ],
            5,
            3,
            (HBM,) * 11,
        )(meta, *near, *near_too, *planes, *planes_too)
        weight_grad = outs[0]
        mode_grads = outs[1:7]
        chan_grads = [x.reshape(-1) for x in outs[7:]]
    else:

        def in_order(mine, other):
            both = jnp.where(core == 0, jnp.stack([mine, other]), jnp.stack([other, mine]))
            both = jnp.take(both, meta[0] ^ jnp.arange(dims.ni), axis=1)
            return jnp.take(both, meta[2] ^ jnp.arange(dims.nz), axis=2)

        def joined(first, rest):
            return jnp.concatenate([jnp.stack(first)[:, None], jnp.stack(rest)], axis=1)

        both = in_order(joined(near, planes), joined(near_too, planes_too))
        weight_grad = both[:, :, :, : dims.units].reshape(dims.width // 8, -1, 8, LANES)
        weight_grad = weight_grad.transpose(0, 2, 1, 3).reshape(dims.width, -1)
        rows = both[:, :, :, dims.units :].transpose(1, 2, 0, 3, 4, 5)
        rows = rows.reshape(nd, dims.small_rows, dims.groups, hc)
        table = rows[:, : 6 * m].reshape(nd, 6, m, dims.groups, hc).transpose(1, 3, 2, 0, 4)
        mode_grads = list(table.reshape(6, m * dims.groups, dims.width)[:, :modes])
        rest = rows[:, 6 * m : 6 * m + 4, 0].transpose(1, 0, 2).reshape(4, dims.width)
        chan_grads = list(rest)
    step_grad, gain_grad, shift_grad, skip_grad = chan_grads
    return (
        result,
        grad_in,
        gain_grad,
        shift_grad,
        step_grad,
        *mode_grads,
        skip_grad,
        weight_grad,
        bias_grad.reshape(-1),
    )


def solution(mesh):
    batch = mesh.shape["batch"]
    fine = Mesh(mesh.devices.reshape(-1, 2, batch), ("z", "core", "batch"))
    tokens = P("batch", ("z", "core"), None)
    return jax.shard_map(
        functools.partial(local, dict(fine.shape)),
        mesh=fine,
        in_specs=(tokens, P("batch")) + (P(),) * 12 + (tokens,),
        out_specs=(tokens, tokens) + (P(),) * 12,
        check_vma=False,
    )
```
